32 devices in a mesh: dp: 2 (over x), gx: 4 (over y, core), gy: 4 (over z).
Axes of the slice: x: 2, y: 2, z: 4, core: 2. Of those that a mesh axis runs over, the one named last changes fastest.
Arguments:
- block_input: bfloat16 [64, 529, 768], P(('dp', 'gx', 'gy')), may hold values from -6 to 6
- segment_ids: int32 [64, 529], P(('dp', 'gx', 'gy')), may hold values from 0 to 5, never falling along the last dimension, each value on 1 to 264 neighbouring positions
- out_grad: bfloat16 [64, 529, 768], P(('dp', 'gx', 'gy')), may hold values from -6 to 6
- query_weight: bfloat16 [768, 768], P(('dp', 'gx', 'gy')), may hold values from -0.21875 to 0.21875
- key_weight: bfloat16 [768, 768], P(('dp', 'gx', 'gy')), may hold values from -0.21875 to 0.21875
- value_weight: bfloat16 [768, 768], P(('dp', 'gx', 'gy')), may hold values from -0.21875 to 0.21875
- output_weight: bfloat16 [768, 768], P(('dp', 'gx', 'gy')), may hold values from -0.875 to 0.875
- first_gain: bfloat16 [768], P(('dp', 'gx', 'gy')), may hold values from 0.25 to 1.75
- first_shift: bfloat16 [768], P(('dp', 'gx', 'gy')), may hold values from -3 to 3
- query_bias: bfloat16 [768], P(('dp', 'gx', 'gy')), may hold values from -3 to 3
- value_bias: bfloat16 [768], P(('dp', 'gx', 'gy')), may hold values from -3 to 3
- output_bias: bfloat16 [768], P(('dp', 'gx', 'gy')), may hold values from -3 to 3
- second_gain: bfloat16 [768], P(('dp', 'gx', 'gy')), may hold values from 0.25 to 1.75
- second_shift: bfloat16 [768], P(('dp', 'gx', 'gy')), may hold values from -3 to 3
- up_weight: bfloat16 [768, 3072], P(('dp', 'gy'), 'gx'), may hold values from -0.21875 to 0.21875
- up_bias: bfloat16 [3072], P(('dp', 'gx', 'gy')), may hold values from -3 to 3
- down_weight: bfloat16 [768, 3072], P(('dp', 'gy'), 'gx'), may hold values from -0.15625 to 0.15625
- down_bias: bfloat16 [768], P(('dp', 'gx', 'gy')), may hold values from -3 to 3
Outputs:
- block_output: bfloat16 [64, 529, 768], P(('dp', 'gx', 'gy'))
- input_grad: bfloat16 [64, 529, 768], P(('dp', 'gx', 'gy'))
- query_weight_grad: float32 [768, 768], P(('dp', 'gx', 'gy'))
- key_weight_grad: float32 [768, 768], P(('dp', 'gx', 'gy'))
- value_weight_grad: float32 [768, 768], P(('dp', 'gx', 'gy'))
- output_weight_grad: float32 [768, 768], P(('dp', 'gx', 'gy'))
- first_gain_grad: float32 [768], P(('dp', 'gx', 'gy'))
- first_shift_grad: float32 [768], P(('dp', 'gx', 'gy'))
- query_bias_grad: float32 [768], P(('dp', 'gx', 'gy'))
- value_bias_grad: float32 [768], P(('dp', 'gx', 'gy'))
- output_bias_grad: float32 [768], P(('dp', 'gx', 'gy'))
- second_gain_grad: float32 [768], P(('dp', 'gx', 'gy'))
- second_shift_grad: float32 [768], P(('dp', 'gx', 'gy'))
- up_weight_grad: float32 [768, 3072], P(('dp', 'gy'), 'gx')
- up_bias_grad: float32 [3072], P(('dp', 'gx', 'gy'))
- down_weight_grad: float32 [768, 3072], P(('dp', 'gy'), 'gx')
- down_bias_grad: float32 [768], P(('dp', 'gx', 'gy'))
The draws below stay inside these ranges and needn't reach their ends.
Inputs may be any that keep to these rules, and one draw needn't show every extreme that they name: `segment_ids`: in each strip the document numbers never fall and every one of the 6 documents takes one or more slots; none takes more than half of 529 (rounded down) slots, and one takes exactly that many.
All inputs are finite; a program needn't handle non-finite values.
Results may differ from the reference program's by a relative error of at most 0.017.
Values may be sent and summed in bfloat16 or wider, within the bound.
A program may use at most 192 MiB of HBM per device.

```python
import math
import jax
import jax.numpy as jnp
import numpy as np
from jax import lax

D = 768
H = 12
HD = 64
FF = 3072
LEN = 529
DOCS = 6
STRIPS = 64


def with_spikes(values, rng, source, target, parts, factor):
    def block_of(dim):
        return (jnp.arange(values.shape[dim]) // (values.shape[dim] // parts)).reshape((-1,) + (1,) * (values.ndim - 1 - dim))

    one_side = jax.random.permutation(rng, parts)[block_of(target)]
    other_side = (block_of(target) + parts // 2) % parts
    return jnp.where((block_of(source) == one_side) | (block_of(source) == other_side), factor * values, values)


def level_of(stream_key, dims, cuts, least, high):
    loudness, own = 1.0, jax.random.fold_in(stream_key, 6)
    for position, shards_of in cuts:
        steps = jnp.exp(jax.random.uniform(jax.random.fold_in(own, position), (shards_of,), jnp.float32, least / len(cuts), high / len(cuts)))
        loudness = loudness * jnp.repeat(steps, dims[position] // shards_of).reshape([-1 if axis == position else 1 for axis in range(len(dims))])
    return loudness


def profile(count, total, most, skew):
    weights = [(1 << 20) // math.isqrt(grade ** skew) + 1 for grade in range(2, count + 1)]
    rest, counts = total - most - (count - 1), [1] * (count - 1)
    while rest > 0:
        free = [i for i in range(count - 1) if counts[i] < most]
        whole, budget = sum([weights[i] for i in free]), rest
        for i in free:
            more = min(most - counts[i], max(1, budget * weights[i] // whole), rest)
            counts[i] = counts[i] + more
            rest = rest - more
    return np.array([most] + counts)


def uneven(own_key, count, total, bound, slope):
    if count == 2:
        one = jax.random.randint(own_key, (), max(1, total - bound), min(bound, total - 1) + 1)
        return jnp.stack([one, total - one])
    lengths = jnp.asarray(profile(count, total, bound, slope), jnp.int32)
    pairs = (count - 1) // 2
    donor, taker = lengths[1:1 + 2 * pairs:2], lengths[2:2 + 2 * pairs:2]
    margin = jnp.minimum(donor - 1, bound - taker)
    shifted = jax.random.randint(jax.random.fold_in(own_key, 1), (pairs,), 0, 1 << 20) % (margin + 1)
    lengths = lengths.at[1:1 + 2 * pairs:2].set(donor - shifted).at[2:2 + 2 * pairs:2].set(taker + shifted)
    return lengths[jax.random.permutation(jax.random.fold_in(own_key, 2), count)]


def gaussian(own_key, extent, scale, limit, shards=(), held_as=jnp.bfloat16):
    entries = scale * jax.random.normal(own_key, extent, jnp.float32)
    if shards:
        entries = entries * level_of(own_key, extent, shards, -0.22, 0.18)
    return jnp.clip(entries, -limit, limit).astype(held_as)


def noise_with(stream_key, shape, scale, most, pieces, heavy, dtype=jnp.bfloat16):
    array = scale * jax.random.normal(stream_key, shape, jnp.float32)
    if pieces:
        array = array * level_of(stream_key, shape, pieces, -0.22, 0.18)
    return jnp.clip(with_spikes(array, jax.random.fold_in(stream_key, 3), *heavy), -most, most).astype(dtype)


def setup_inputs(seed: int = 0) -> dict:
    arg_keys = jax.random.split(jax.random.key(seed), 19)
    block_input = noise_with(arg_keys[0], (STRIPS, LEN, D), 1.0, 6.0, ((0, 32),), (0, 2, 32, 2.75))
    segment_ids = jax.vmap(lambda own: jnp.searchsorted(jnp.cumsum(uneven(own, DOCS, LEN, LEN // 2, 2)), jnp.arange(LEN), side="right"))(jax.random.split(arg_keys[1], STRIPS)).reshape((STRIPS, LEN)).astype(jnp.int32)
    out_grad = noise_with(arg_keys[2], (STRIPS, LEN, D), 1.0, 6.0, ((0, 32),), (0, 2, 32, 2.75))
    query_weight = gaussian(arg_keys[3], (D, D), D ** -0.5, 0.21875, ((0, 32),))
    key_weight = gaussian(arg_keys[4], (D, D), D ** -0.5, 0.21875, ((0, 32),))
    value_weight = gaussian(arg_keys[5], (D, D), D ** -0.5, 0.21875, ((0, 32),))
    output_weight = gaussian(arg_keys[6], (D, D), (D // 16) ** -0.5, 0.875, ((0, 32),))
    first_gain = jnp.clip(1.0 + 0.15 * jax.random.normal(arg_keys[7], (D,), jnp.float32), 0.25, 1.75).astype(jnp.bfloat16)
    first_shift = gaussian(arg_keys[8], (D,), 0.5, 3.0, ((0, 32),))
    query_bias = gaussian(arg_keys[9], (D,), 0.5, 3.0, ((0, 32),))
    value_bias = gaussian(arg_keys[10], (D,), 0.5, 3.0, ((0, 32),))
    output_bias = gaussian(arg_keys[11], (D,), 0.5, 3.0, ((0, 32),))
    second_gain = jnp.clip(1.0 + 0.15 * jax.random.normal(arg_keys[12], (D,), jnp.float32), 0.25, 1.75).astype(jnp.bfloat16)
    second_shift = gaussian(arg_keys[13], (D,), 0.5, 3.0, ((0, 32),))
    up_weight = gaussian(arg_keys[14], (D, FF), D ** -0.5, 0.21875, ((0, 8), (1, 4)))
    up_bias = gaussian(arg_keys[15], (FF,), 0.5, 3.0, ((0, 32),))
    down_weight = gaussian(arg_keys[16], (D, FF), (FF // 2) ** -0.5, 0.15625, ((0, 8), (1, 4)))
    down_bias = gaussian(arg_keys[17], (D,), 0.5, 3.0, ((0, 32),))
    return dict(block_input=block_input, segment_ids=segment_ids, out_grad=out_grad, query_weight=query_weight, key_weight=key_weight, value_weight=value_weight, output_weight=output_weight, first_gain=first_gain, first_shift=first_shift, query_bias=query_bias, value_bias=value_bias, output_bias=output_bias, second_gain=second_gain, second_shift=second_shift, up_weight=up_weight, up_bias=up_bias, down_weight=down_weight, down_bias=down_bias)


@jax.custom_vjp
def low(v):
    return lax.optimization_barrier(v.astype(jnp.bfloat16)).astype(jnp.float32)

@jax.custom_vjp
def low_back(v):
    return v

def low_keep(v):
    return (low(v), None)

def low_pass(kept, grad):
    return (grad,)

def back_keep(v):
    return (v, None)

def back_low(kept, grad):
    return (low(grad),)
low.defvjp(low_keep, low_pass)
low_back.defvjp(back_keep, back_low)

def product(left, right):
    return jnp.dot(left, right, precision=lax.Precision.HIGHEST)

def norm_rows(in_rows, norm_gain, norm_shift):
    centred = in_rows - lax.optimization_barrier(jnp.mean(in_rows, axis=-1, keepdims=True))
    variance = lax.optimization_barrier(jnp.mean(centred * centred, axis=-1, keepdims=True))
    return centred * lax.rsqrt(variance + 1e-06) * norm_gain + norm_shift

def strip_forward(params, in_rows, seg_row):
    query_weight, key_weight, value_weight, output_weight, first_gain, first_shift, query_bias, value_bias, output_bias, second_gain, second_shift, up_weight, up_bias, down_weight, down_bias = params
    length = in_rows.shape[0]
    normed = low(norm_rows(in_rows, first_gain, first_shift))
    query_rows = low(low_back(product(normed, query_weight) + query_bias))
    key_rows = low(low_back(product(normed, key_weight)))
    value_rows = low(low_back(product(normed, value_weight) + value_bias))
    query_heads = query_rows.reshape(length, H, HD)
    key_heads = key_rows.reshape(length, H, HD)
    value_heads = value_rows.reshape(length, H, HD)
    raw_scores = jnp.einsum('qhd,khd->hqk', query_heads, key_heads, precision=lax.Precision.HIGHEST) * 0.125
    same_doc = seg_row[:, None] == seg_row[None, :]
    scores = jnp.where(same_doc[None], low_back(raw_scores), -1e+30)
    row_max = lax.optimization_barrier(jnp.max(scores, axis=-1, keepdims=True))
    exp_rows = jnp.exp(scores - row_max)
    prob_rows = low(exp_rows / lax.optimization_barrier(jnp.sum(exp_rows, axis=-1, keepdims=True)))
    head_mix = jnp.einsum('hqk,khd->qhd', prob_rows, value_heads, precision=lax.Precision.HIGHEST)
    mixed_low = low(low_back(head_mix.reshape(length, H * HD)))
    residual = in_rows + low_back(product(mixed_low, output_weight) + output_bias)
    second = low(norm_rows(residual, second_gain, second_shift))
    hidden = low(jax.nn.gelu(low_back(product(second, up_weight) + up_bias), approximate=False))
    return residual + (product(hidden, down_weight.T) + down_bias)

def reference(block_input, segment_ids, out_grad, query_weight, key_weight, value_weight, output_weight, first_gain, first_shift, query_bias, value_bias, output_bias, second_gain, second_shift, up_weight, up_bias, down_weight, down_bias):
    params = tuple((weight.astype(jnp.float32) for weight in (query_weight, key_weight, value_weight, output_weight, first_gain, first_shift, query_bias, value_bias, output_bias, second_gain, second_shift, up_weight, up_bias, down_weight, down_bias)))
    groups = STRIPS // 4
    in_rows = block_input.astype(jnp.float32).reshape(groups, 4, LEN, D)
    seg_rows = segment_ids.reshape(groups, 4, LEN)

    def whole(params, in_rows):

        def one_group(item):
            return jax.vmap(strip_forward, in_axes=(None, 0, 0))(params, item[0], item[1])
        return lax.map(jax.checkpoint(one_group), (in_rows, seg_rows))
    result, pull_back = jax.vjp(whole, params, in_rows)
    param_grads, input_grad = pull_back(out_grad.astype(jnp.float32).reshape(groups, 4, LEN, D))
    block_output = result.reshape(STRIPS, LEN, D).astype(jnp.bfloat16)
    input_grad = input_grad.reshape(STRIPS, LEN, D).astype(jnp.bfloat16)
    return (block_output, input_grad, param_grads[0], param_grads[1], param_grads[2], param_grads[3], param_grads[4], param_grads[5], param_grads[6], param_grads[7], param_grads[8], param_grads[9], param_grads[10], param_grads[11], param_grads[12], param_grads[13], param_grads[14])
```

```python
import functools
import math

import jax
import jax.numpy as jnp
from jax import lax
from jax.experimental import pallas as pl
from jax.experimental.pallas import tpu as pltpu
from jax.sharding import PartitionSpec as P

H = 12
HD = 64
BF = jnp.bfloat16
F32 = jnp.float32
ALL = ("dp", "gx", "gy")
MESH = pl.DeviceIdType.MESH
LOG2E = 1.4426950408889634
INV_SQRT2 = 0.7071067811865476
INV_SQRT_2PI = 0.3989422804014327
ANY = pl.BlockSpec(memory_space=pl.ANY)
VM = pl.BlockSpec(memory_space=pltpu.VMEM)
LIMIT = 60 << 20

G1, S1, QB, VB, OB, G2, S2, DB, UB0 = 0, 1, 2, 3, 4, 5, 6, 7, 8


def nn(a, b):
    return lax.dot_general(a, b, (((1,), (0,)), ((), ())), preferred_element_type=F32)


def nt(a, b):
    return lax.dot_general(a, b, (((1,), (1,)), ((), ())), preferred_element_type=F32)


def padded(length):
    return (length + 31) // 32 * 32


def row_pieces(length, step):
    return [(lo, min(step, length - lo)) for lo in range(0, length, step)]


def normalise(rows):
    centred = rows - jnp.mean(rows, axis=-1, keepdims=True)
    scale = lax.rsqrt(jnp.mean(centred * centred, axis=-1, keepdims=True) + 1e-06)
    return centred * scale, scale


def norm_back(grad, gain, xhat, scale):
    t = grad * gain
    return scale * (
        t
        - jnp.mean(t, axis=-1, keepdims=True)
        - xhat * jnp.mean(t * xhat, axis=-1, keepdims=True)
    )


def colsum(rows):
    return jnp.sum(rows, axis=0, keepdims=True)


def place(d, x, g):
    return (d, x, g)


def remote(src, dst, send, recv, dev):
    return pltpu.make_async_remote_copy(
        src_ref=src, dst_ref=dst, send_sem=send, recv_sem=recv, device_id=dev, device_id_type=MESH
    )


def greet(d, x, g, ny):
    h, c = x // 2, x % 2
    barrier = pltpu.get_barrier_semaphore()
    peers = [(d, x, lax.rem(g + k, ny)) for k in range(1, ny)]
    peers += [(1 - d, x, g), (d, (1 - h) * 2 + c, g), (d, h * 2 + 1 - c, g)]
    for peer in peers:
        pl.semaphore_signal(barrier, inc=1, device_id=peer, device_id_type=MESH)
    pl.semaphore_wait(barrier, len(peers))


def block(ref, units_first, d, h, c):
    return ref.at[h, c, d] if units_first else ref.at[d, h, c]


def gather_kernel(orders, ny, *refs):
    n = len(orders)
    shards, outs = refs[:n], refs[n : 2 * n]
    loc, zsend, zrecv, bsend, brecv = refs[2 * n :]
    d, x, g = lax.axis_index("dp"), lax.axis_index("gx"), lax.axis_index("gy")
    h, c = x // 2, x % 2
    greet(d, x, g, ny)
    ydev, xdev, cdev = (d, (1 - h) * 2 + c, g), (1 - d, x, g), (d, h * 2 + 1 - c, g)
    half = ny // 2

    def start_z(t):
        own = block(outs[t], orders[t], d, h, c).at[g]
        local = pltpu.make_async_copy(shards[t], own, loc.at[t])
        local.start()
        copies = []
        for k in range(1, ny):
            dev = (d, x, lax.rem(g + k, ny))
            cp = remote(shards[t], own, zsend.at[t, k - 1], zrecv.at[t, k - 1], dev)
            cp.start()
            copies.append(cp)
        return local, copies

    def start_b(t, zs):
        local, copies = zs
        local.wait()
        for cp in copies:
            cp.wait_recv()
        b = block(outs[t], orders[t], d, h, c)
        res = []
        for i, dev in enumerate((ydev, xdev, cdev)):
            cp = remote(b, b, bsend.at[t, i], brecv.at[t, i], dev)
            cp.start()
            res.append(cp)
        return res

    def start_f(t, bs):
        y, xx, _ = bs
        y.wait_recv()
        by = block(outs[t], orders[t], d, 1 - h, c)
        lo, hi = pl.ds(0, half), pl.ds(half, ny - half)
        f1 = remote(by.at[lo], by.at[lo], bsend.at[t, 3], brecv.at[t, 3], xdev)
        f1.start()
        c1 = remote(by, by, bsend.at[t, 4], brecv.at[t, 4], cdev)
        c1.start()
        xx.wait_recv()
        bx = block(outs[t], orders[t], 1 - d, h, c)
        f2 = remote(bx.at[hi], bx.at[hi], bsend.at[t, 5], brecv.at[t, 5], ydev)
        f2.start()
        c2 = remote(bx, bx, bsend.at[t, 6], brecv.at[t, 6], cdev)
        c2.start()
        return [f1, c1, f2, c2]

    def start_c(t, fs):
        fs[0].wait_recv()
        fs[2].wait_recv()
        bd = block(outs[t], orders[t], 1 - d, 1 - h, c)
        cp = remote(bd, bd, bsend.at[t, 7], brecv.at[t, 7], cdev)
        cp.start()
        return cp

    zs, bs, fs, cs = {}, {}, {}, {}
    for step in range(n + 3):
        if step < n:
            zs[step] = start_z(step)
        if 0 <= step - 1 < n:
            bs[step - 1] = start_b(step - 1, zs[step - 1])
        if 0 <= step - 2 < n:
            fs[step - 2] = start_f(step - 2, bs[step - 2])
        if 0 <= step - 3 < n:
            cs[step - 3] = start_c(step - 3, fs[step - 3])
    for t in range(n):
        for cp in (bs[t][2], fs[t][1], fs[t][3], cs[t]):
            cp.wait_recv()
        for cp in zs[t][1] + bs[t] + fs[t] + [cs[t]]:
            cp.wait_send()


def gather(shards, orders, nd, nh, ny):
    n = len(shards)

    def shape(s, units_first):
        lead = (nh, 2, nd, ny) if units_first else (nd, nh, 2, ny)
        return jax.ShapeDtypeStruct(lead + s.shape, s.dtype)

    return pl.pallas_call(
        functools.partial(gather_kernel, orders, ny),
        out_shape=[shape(s, o) for s, o in zip(shards, orders)],
        in_specs=[ANY] * n,
        out_specs=[ANY] * n,
        scratch_shapes=[
            pltpu.SemaphoreType.DMA((n,)),
            pltpu.SemaphoreType.DMA((n, ny - 1)),
            pltpu.SemaphoreType.DMA((n, ny - 1)),
            pltpu.SemaphoreType.DMA((n, 8)),
            pltpu.SemaphoreType.DMA((n, 8)),
        ],
        compiler_params=pltpu.CompilerParams(collective_id=0, has_side_effects=True),
    )(*shards)


def scatter_kernel(orders, nd, nh, ny, *refs):
    n = len(orders)
    parts, outs = refs[:n], refs[n : 2 * n]
    rest = refs[2 * n :]
    sums, rc, rs, rl, rz = (rest[i * n : (i + 1) * n] for i in range(5))
    lsem, csend, crecv, bsend, brecv, zsend, zrecv = rest[5 * n :]
    d, x, g = lax.axis_index("dp"), lax.axis_index("gx"), lax.axis_index("gy")
    h, c = x // 2, x % 2
    greet(d, x, g, ny)
    ydev, xdev, cdev = (d, (1 - h) * 2 + c, g), (1 - d, x, g), (d, h * 2 + 1 - c, g)
    half = ny // 2
    lo, hi = pl.ds(0, half), pl.ds(half, ny - half)
    quads = [(1 - d, 1 - h), (d, 1 - h), (1 - d, h), (d, h)]

    def start_core(t):
        res = []
        for q, (bd, bh) in enumerate(quads):
            cp = remote(
                block(parts[t], orders[t], bd, bh, 1 - c), rc[t].at[q], csend.at[t, q], crecv.at[t, q], cdev
            )
            cp.start()
            lc = pltpu.make_async_copy(
                block(parts[t], orders[t], bd, bh, c), sums[t].at[q], lsem.at[t, q]
            )
            lc.start()
            res.append((cp, lc))
        return res

    def add(dst, src, lead):
        def body(i, carry):
            dst[i] = (dst[i].astype(F32) + src[i].astype(F32)).astype(dst.dtype)
            return carry

        lax.fori_loop(0, lead, body, 0)

    def start_far(t, cs):
        for q in range(4):
            cs[q][0].wait_recv()
            cs[q][1].wait()
            add(sums[t].at[q], rc[t].at[q], ny)
        a = remote(sums[t].at[0, lo], rs[t].at[0], bsend.at[t, 0], brecv.at[t, 0], xdev)
        b = remote(sums[t].at[0, hi], rs[t].at[1], bsend.at[t, 1], brecv.at[t, 1], ydev)
        a.start()
        b.start()
        return a, b

    def start_near(t, far):
        far[0].wait_recv()
        add(sums[t].at[1, lo], rs[t].at[0], half)
        y = remote(sums[t].at[1], rl[t].at[0], bsend.at[t, 2], brecv.at[t, 2], ydev)
        y.start()
        far[1].wait_recv()
        add(sums[t].at[2, hi], rs[t].at[1], half)
        xx = remote(sums[t].at[2], rl[t].at[1], bsend.at[t, 3], brecv.at[t, 3], xdev)
        xx.start()
        return y, xx

    def start_z(t, near):
        for i in range(2):
            near[i].wait_recv()
            add(sums[t].at[3], rl[t].at[i], ny)
        res = []
        for k in range(1, ny):
            to = lax.rem(g + k, ny)
            cp = remote(
                sums[t].at[3, to], rz[t].at[k - 1], zsend.at[t, k - 1], zrecv.at[t, k - 1], (d, x, to)
            )
            cp.start()
            res.append(cp)
        return res

    def finish(t, zs):
        total = sums[t][3, g].astype(F32)
        for k in range(ny - 1):
            zs[k].wait_recv()
            total = total + rz[t][k].astype(F32)
        outs[t][...] = total

    cs, far, near, zs = {}, {}, {}, {}
    for step in range(n + 4):
        if step < n:
            cs[step] = start_core(step)
        if 0 <= step - 1 < n:
            far[step - 1] = start_far(step - 1, cs[step - 1])
        if 0 <= step - 2 < n:
            near[step - 2] = start_near(step - 2, far[step - 2])
        if 0 <= step - 3 < n:
            zs[step - 3] = start_z(step - 3, near[step - 3])
        if 0 <= step - 4 < n:
            finish(step - 4, zs[step - 4])
    for t in range(n):
        for q in range(4):
            cs[t][q][0].wait_send()
        for cp in far[t] + near[t] + tuple(zs[t]):
            cp.wait_send()


def scatter(parts, orders, nd, nh, ny):
    n = len(parts)
    tails = [p.shape[4:] for p in parts]

    def buffers(lead):
        return [pltpu.VMEM(lead + t, p.dtype) for t, p in zip(tails, parts)]

    return pl.pallas_call(
        functools.partial(scatter_kernel, orders, nd, nh, ny),
        out_shape=[jax.ShapeDtypeStruct(t, F32) for t in tails],
        in_specs=[ANY] * n,
        out_specs=[VM] * n,
        scratch_shapes=buffers((4, ny))
        + buffers((4, ny))
        + buffers((2, ny // 2))
        + buffers((2, ny))
        + buffers((ny - 1,))
        + [
            pltpu.SemaphoreType.DMA((n, 4)),
            pltpu.SemaphoreType.DMA((n, 4)),
            pltpu.SemaphoreType.DMA((n, 4)),
            pltpu.SemaphoreType.DMA((n, 4)),
            pltpu.SemaphoreType.DMA((n, 4)),
            pltpu.SemaphoreType.DMA((n, ny - 1)),
            pltpu.SemaphoreType.DMA((n, ny - 1)),
        ],
        compiler_params=pltpu.CompilerParams(
            collective_id=1, has_side_effects=True, vmem_limit_bytes=LIMIT
        ),
    )(*parts)


def qkv_kernel(x_ref, w_ref, v_ref, qkv_ref, n_ref, bias_ref):
    strips, length, width = x_ref.shape
    lp = n_ref.shape[1]
    gain, shift = v_ref[G1 : G1 + 1, :], v_ref[S1 : S1 + 1, :]
    for s in range(strips):
        for lo, size in row_pieces(length, 136):
            xhat, _ = normalise(x_ref[s, lo : lo + size, :].astype(F32))
            n_ref[s, lo : lo + size, :] = (xhat * gain + shift).astype(BF)
        n_ref[s, length:lp, :] = jnp.zeros((lp - length, width), BF)
    bias_ref[0:1, 0:width] = v_ref[QB : QB + 1, :]
    bias_ref[0:1, width : 2 * width] = jnp.zeros((1, width), F32)
    bias_ref[0:1, 2 * width : 3 * width] = v_ref[VB : VB + 1, :]
    step = 256

    def body(i, carry):
        cols = pl.ds(pl.multiple_of(i * step, step), step)
        w = w_ref[:, cols]
        for s in range(strips):
            qkv_ref[s, :, cols] = (nn(n_ref[s], w) + bias_ref[0:1, cols]).astype(BF)
        return carry

    lax.fori_loop(0, 3 * width // step, body, 0)


def fill_bias(bias_ref, row, col):
    bias_ref[...] = jnp.where(row == col, 0.0, -1e30).astype(F32)


def attend_kernel(qkv_ref, sr_ref, sc_ref, o_ref, lse_ref, bias_ref):
    strips, lp, width = o_ref.shape
    qrows = lp // 2
    first = lax.broadcasted_iota(jnp.int32, (qrows, 128), 1) < HD
    lane = lax.broadcasted_iota(jnp.int32, (qrows, 128), 1)
    scale = 0.125 * LOG2E
    for s in range(strips):
        fill_bias(bias_ref, sc_ref[s], sr_ref[s])
        lse_ref[s] = jnp.zeros((lp, 128), F32)

        def body(p, carry):
            cq = pl.ds(pl.multiple_of(p * 128, 128), 128)
            ck = pl.ds(pl.multiple_of(width + p * 128, 128), 128)
            cv = pl.ds(pl.multiple_of(2 * width + p * 128, 128), 128)
            k, v = qkv_ref[s, :, ck], qkv_ref[s, :, cv]
            for part in range(2):
                rows = pl.ds(part * qrows, qrows)
                q = qkv_ref[s, rows, cq]
                lse = lse_ref[s, rows, :]
                res = []
                for j in range(2):
                    keep = first if j == 0 else jnp.logical_not(first)
                    z = nt(jnp.where(keep, q, jnp.zeros_like(q)), k) * scale + bias_ref[rows, :]
                    top = jnp.max(z, axis=-1, keepdims=True)
                    e = jnp.exp2(z - top)
                    total = jnp.sum(e, axis=-1, keepdims=True)
                    res.append(nn(e.astype(BF), v) / total)
                    lse = jnp.where(lane == 2 * p + j, top + jnp.log2(total), lse)
                o_ref[s, rows, cq] = jnp.where(first, res[0], res[1]).astype(BF)
                lse_ref[s, rows, :] = lse
            return carry

        lax.fori_loop(0, H // 2, body, 0)


def transpose_into(dst_ref, src_ref, lp):
    strips, _, width = src_ref.shape
    for s in range(strips):

        def body(i, carry):
            cols = pl.ds(pl.multiple_of(i * 128, 128), 128)
            dst_ref[s, cols, :] = src_ref[s, :, cols].astype(F32).T.astype(BF)
            return carry

        lax.fori_loop(0, width // 128, body, 0)


def ff_kernel(
    x_ref, mix_ref, dout_in_ref, wo_ref, up_ref, down_ref, v_ref,
    y_ref, rg_ref, mg_ref, gup_ref, gdown_ref, gwo_ref, gv_ref,
    dout_ref, doutT_ref, sec_ref, secT_ref, res_ref, acc_ref, sg_ref, hid_ref, pre_ref,
):
    strips, length, width = x_ref.shape
    lp = mix_ref.shape[1]
    groups = up_ref.shape[0]
    units = up_ref.shape[2]
    gv_ref[...] = jnp.zeros(gv_ref.shape, F32)
    bias_o, gain, shift = v_ref[OB : OB + 1, :], v_ref[G2 : G2 + 1, :], v_ref[S2 : S2 + 1, :]
    step = 256
    for s in range(strips):
        dout_ref[s, 0:length, :] = dout_in_ref[s]
        dout_ref[s, length:lp, :] = jnp.zeros((lp - length, width), BF)

        def proj(i, carry):
            cols = pl.ds(pl.multiple_of(i * step, step), step)
            acc_ref[s, :, cols] = nn(mix_ref[s], wo_ref[:, cols])
            return carry

        lax.fori_loop(0, width // step, proj, 0)
        for lo, size in row_pieces(length, 136):
            rows = pl.ds(lo, size)
            residual = x_ref[s, rows, :].astype(F32) + (acc_ref[s, rows, :] + bias_o)
            res_ref[s, rows, :] = residual
            xhat, _ = normalise(residual)
            sec_ref[s, rows, :] = (xhat * gain + shift).astype(BF)
            acc_ref[s, rows, :] = residual + v_ref[DB : DB + 1, :]
        sec_ref[s, length:lp, :] = jnp.zeros((lp - length, width), BF)
        res_ref[s, length:lp, :] = jnp.zeros((lp - length, width), F32)
        gv_ref[DB : DB + 1, :] += colsum(dout_in_ref[s].astype(F32))
    sg_ref[...] = jnp.zeros(sg_ref.shape, F32)
    transpose_into(doutT_ref, dout_ref, lp)
    transpose_into(secT_ref, sec_ref, lp)

    def group(gi, carry):
        def hidden(i, carry):
            cols = pl.ds(pl.multiple_of(i * step, step), step)
            up, down = up_ref[gi, :, cols], down_ref[gi, :, cols]
            ub = v_ref[pl.ds(UB0 + gi, 1), cols]
            total = jnp.zeros((1, step), F32)
            for s in range(strips):
                pre = nn(sec_ref[s], up) + ub
                hg = nn(dout_ref[s], down)
                cdf = 0.5 + 0.5 * lax.erf(pre * INV_SQRT2)
                pdf = jnp.exp(-0.5 * pre * pre) * INV_SQRT_2PI
                hid_ref[s, :, cols] = (pre * cdf).astype(BF)
                pg = (hg * (cdf + pre * pdf)).astype(BF)
                pre_ref[s, :, cols] = pg
                total = total + colsum(pg.astype(F32))
            gv_ref[pl.ds(UB0 + gi, 1), cols] = total
            return carry

        lax.fori_loop(0, units // step, hidden, 0)

        def back(i, carry):
            rows = pl.ds(pl.multiple_of(i * step, step), step)
            for s in range(strips):
                acc_ref[s, :, rows] += nt(hid_ref[s], down_ref[gi, rows, :])
                sg_ref[s, :, rows] += nt(pre_ref[s], up_ref[gi, rows, :])
            gd = nn(doutT_ref[0, rows, :], hid_ref[0])
            gu = nn(secT_ref[0, rows, :], pre_ref[0])
            for s in range(1, strips):
                gd = gd + nn(doutT_ref[s, rows, :], hid_ref[s])
                gu = gu + nn(secT_ref[s, rows, :], pre_ref[s])
            gdown_ref[gi, rows, :] = gd.astype(BF)
            gup_ref[gi, rows, :] = gu.astype(BF)
            return carry

        lax.fori_loop(0, width // step, back, 0)
        return carry

    lax.fori_loop(0, groups, group, 0)
    for s in range(strips):
        for lo, size in row_pieces(length, 136):
            rows = pl.ds(lo, size)
            y_ref[s, rows, :] = acc_ref[s, rows, :].astype(BF)
            xhat, scale = normalise(res_ref[s, rows, :])
            grad = sg_ref[s, rows, :]
            gv_ref[G2 : G2 + 1, :] += colsum(grad * xhat)
            gv_ref[S2 : S2 + 1, :] += colsum(grad)
            rg = dout_ref[s, rows, :].astype(F32) + norm_back(grad, gain, xhat, scale)
            rg_ref[s, rows, :] = rg
            low = rg.astype(BF)
            sec_ref[s, rows, :] = low
            gv_ref[OB : OB + 1, :] += colsum(low.astype(F32))
        sec_ref[s, length:lp, :] = jnp.zeros((lp - length, width), BF)
        rg_ref[s, length:lp, :] = jnp.zeros((lp - length, width), F32)
    transpose_into(secT_ref, mix_ref, lp)

    def last(i, carry):
        rows = pl.ds(pl.multiple_of(i * step, step), step)
        for s in range(strips):
            mg_ref[s, :, rows] = nt(sec_ref[s], wo_ref[rows, :]).astype(BF)
        gw = nn(secT_ref[0, rows, :], sec_ref[0])
        for s in range(1, strips):
            gw = gw + nn(secT_ref[s, rows, :], sec_ref[s])
        gwo_ref[rows, :] = gw.astype(BF)
        return carry

    lax.fori_loop(0, width // step, last, 0)


def attend_back_kernel(
    qkv_ref, mg_ref, mix_ref, lse_ref, sr_ref, sc_ref, dqkv_ref, bias_ref, lt_ref, dt_ref, kt_ref
):
    strips, lp, width = mg_ref.shape
    krows = lp // 2
    first = lax.broadcasted_iota(jnp.int32, (krows, 128), 1) < HD
    scale = 0.125 * LOG2E
    heads = lax.broadcasted_iota(jnp.int32, (16, width), 0)
    owner = lax.broadcasted_iota(jnp.int32, (16, width), 1) // HD
    pick = jnp.where(heads == owner, 1.0, 0.0).astype(BF)
    for s in range(strips):
        fill_bias(bias_ref, sc_ref[s], sr_ref[s])
        lt_ref[...] = lse_ref[s].T
        prod = mg_ref[s].astype(F32) * mix_ref[s].astype(F32)
        high = prod.astype(BF)
        rest = (prod - high.astype(F32)).astype(BF)
        dt_ref[...] = nt(pick, high) + nt(pick, rest)

        def body(p, carry):
            cq = pl.ds(pl.multiple_of(p * 128, 128), 128)
            ck = pl.ds(pl.multiple_of(width + p * 128, 128), 128)
            cv = pl.ds(pl.multiple_of(2 * width + p * 128, 128), 128)
            q, do = qkv_ref[s, :, cq], mg_ref[s, :, cq]
            kt_ref[...] = qkv_ref[s, :, ck].astype(F32).T.astype(BF)
            dq = [jnp.zeros((HD, lp), F32), jnp.zeros((HD, lp), F32)]
            for part in range(2):
                rows = pl.ds(part * krows, krows)
                k, v = qkv_ref[s, rows, ck], qkv_ref[s, rows, cv]
                dv, dk = [], []
                for j in range(2):
                    keep = first if j == 0 else jnp.logical_not(first)
                    lse = lt_ref[pl.ds(2 * p + j, 1), :]
                    delta = dt_ref[pl.ds(2 * p + j, 1), :]
                    z = nt(jnp.where(keep, k, jnp.zeros_like(k)), q) * scale + bias_ref[rows, :]
                    prob = jnp.exp2(z - lse)
                    pg = nt(jnp.where(keep, v, jnp.zeros_like(v)), do)
                    sg = (prob * (pg - delta)).astype(BF)
                    dv.append(nn(prob.astype(BF), do))
                    dk.append(nn(sg, q))
                    dq[j] = dq[j] + nn(kt_ref[j * HD : (j + 1) * HD, part * krows : (part + 1) * krows], sg)
                dqkv_ref[s, rows, cv] = jnp.where(first, dv[0], dv[1]).astype(BF)
                dqkv_ref[s, rows, ck] = (0.125 * jnp.where(first, dk[0], dk[1])).astype(BF)
            dqkv_ref[s, :, cq] = (0.125 * jnp.concatenate(dq, axis=0)).T.astype(BF)
            return carry

        lax.fori_loop(0, H // 2, body, 0)


def qkv_back_kernel(
    x_ref, n_ref, dqkv_ref, rg_ref, w_ref, v_ref, gx_ref, gw_ref, gv_ref, nT_ref, ng_ref
):
    strips, length, width = x_ref.shape
    lp = n_ref.shape[1]
    step = 256
    gv_ref[...] = jnp.zeros(gv_ref.shape, F32)
    gain = v_ref[G1 : G1 + 1, :]
    transpose_into(nT_ref, n_ref, lp)
    for s in range(strips):
        gv_ref[QB : QB + 1, :] += colsum(dqkv_ref[s, :, 0:width].astype(F32))
        gv_ref[VB : VB + 1, :] += colsum(dqkv_ref[s, :, 2 * width : 3 * width].astype(F32))

        def body(i, carry):
            rows = pl.ds(pl.multiple_of(i * step, step), step)
            ng_ref[s, :, rows] = nt(dqkv_ref[s], w_ref[rows, :])
            return carry

        lax.fori_loop(0, width // step, body, 0)

    def grads(i, carry):
        cols = pl.ds(pl.multiple_of(i * step, step), step)
        gw = nn(nT_ref[0], dqkv_ref[0, :, cols])
        for s in range(1, strips):
            gw = gw + nn(nT_ref[s], dqkv_ref[s, :, cols])
        gw_ref[:, cols] = gw.astype(BF)
        return carry

    lax.fori_loop(0, 3 * width // step, grads, 0)
    for s in range(strips):
        for lo, size in row_pieces(length, 136):
            rows = pl.ds(lo, size)
            xhat, scale = normalise(x_ref[s, rows, :].astype(F32))
            grad = ng_ref[s, rows, :]
            gv_ref[G1 : G1 + 1, :] += colsum(grad * xhat)
            gv_ref[S1 : S1 + 1, :] += colsum(grad)
            term = norm_back(grad, gain, xhat, scale)
            gx_ref[s, rows, :] = (rg_ref[s, rows, :] + term).astype(BF)


def call(kernel, outs, n_in, scratch=()):
    return pl.pallas_call(
        kernel,
        out_shape=outs,
        in_specs=[VM] * n_in,
        out_specs=[VM] * len(outs),
        scratch_shapes=list(scratch),
        compiler_params=pltpu.CompilerParams(vmem_limit_bytes=LIMIT),
    )


def sds(shape, dtype):
    return jax.ShapeDtypeStruct(shape, dtype)


def per_device(
    sizes, block_input, segment_ids, out_grad, query_weight, key_weight, value_weight, output_weight,
    first_gain, first_shift, query_bias, value_bias, output_bias, second_gain, second_shift,
    up_weight, up_bias, down_weight, down_bias,
):
    nd, nx, ny = sizes
    n_dev = nd * nx * ny
    strips, length, width = block_input.shape
    lp = padded(length)
    units = up_weight.shape[1]
    att_rows, ff_rows = query_weight.shape[0], up_weight.shape[0]
    own = nd == 2 and nx == 4 and att_rows % 8 == 0 and ff_rows % 8 == 0

    att = jnp.concatenate([query_weight, key_weight, value_weight, output_weight], axis=1)
    vecs = [first_gain, first_shift, query_bias, value_bias, output_bias, second_gain, second_shift, down_bias]
    n_vec = len(vecs)
    small = jnp.concatenate(vecs + [up_bias])
    n_small = small.shape[0]
    lanes = (n_small + 127) // 128
    small = jnp.pad(small.astype(F32), (0, lanes * 128 - n_small)).reshape(lanes, 128)
    if own:
        att, up, down, small = gather(
            [att, up_weight, down_weight, small], [False, True, True, False], nd, nx // 2, ny
        )
    else:
        att, small = (lax.all_gather(a, ALL, axis=0) for a in (att, small))
        up, down = (
            lax.all_gather(lax.all_gather(a, ("dp", "gy"), axis=0), "gx", axis=0)
            for a in (up_weight, down_weight)
        )
    att = att.reshape(width, 4 * width)
    up, down = up.reshape(nx, width, units), down.reshape(nx, width, units)
    small = small.reshape(n_dev, lanes * 128)
    cut = n_vec * att_rows
    table = small[:, :cut].reshape(n_dev, n_vec, att_rows).transpose(1, 0, 2).reshape(n_vec, width)
    table = jnp.concatenate([table, small[:, cut:n_small].reshape(-1, width)])
    w_qkv, w_out = att[:, : 3 * width], att[:, 3 * width :]

    seg = jnp.pad(segment_ids, ((0, 0), (0, lp - length)), constant_values=-1)
    seg_row, seg_col = seg[:, None, :], seg[:, :, None]
    full = (strips, lp, width)
    wide = (strips, lp, 3 * width)
    turned = (strips, width, lp)
    qkv, normed = call(
        qkv_kernel, [sds(wide, BF), sds(full, BF)], 3, [pltpu.VMEM((8, 3 * width), F32)]
    )(block_input, w_qkv, table)
    mixed, lse = call(
        attend_kernel, [sds(full, BF), sds((strips, lp, 128), F32)], 3, [pltpu.VMEM((lp, lp), F32)]
    )(qkv, seg_row, seg_col)
    n_tab = table.shape[0]
    y, res_grad, mixed_grad, g_up, g_down, g_out, g_tab = call(
        ff_kernel,
        [
            sds(block_input.shape, BF), sds(full, F32), sds(full, BF), sds(up.shape, BF),
            sds(down.shape, BF), sds((width, width), BF), sds((n_tab, width), F32),
        ],
        7,
        [
            pltpu.VMEM(full, BF), pltpu.VMEM(turned, BF), pltpu.VMEM(full, BF), pltpu.VMEM(turned, BF),
            pltpu.VMEM(full, F32), pltpu.VMEM(full, F32), pltpu.VMEM(full, F32),
            pltpu.VMEM((strips, lp, units), BF), pltpu.VMEM((strips, lp, units), BF),
        ],
    )(block_input, mixed, out_grad, w_out, up, down, table)
    (dqkv,) = call(
        attend_back_kernel,
        [sds(wide, BF)],
        6,
        [
            pltpu.VMEM((lp, lp), F32), pltpu.VMEM((128, lp), F32), pltpu.VMEM((16, lp), F32),
            pltpu.VMEM((128, lp), BF),
        ],
    )(qkv, mixed_grad, mixed, lse, seg_row, seg_col)
    x_grad, g_qkv, g_tab1 = call(
        qkv_back_kernel,
        [sds(block_input.shape, BF), sds((width, 3 * width), BF), sds((n_tab, width), F32)],
        6,
        [pltpu.VMEM(turned, BF), pltpu.VMEM(full, F32)],
    )(block_input, normed, dqkv, res_grad, w_qkv, table)

    g_tab = g_tab + g_tab1
    g_small = jnp.concatenate(
        [
            g_tab[:n_vec].reshape(n_vec, n_dev, att_rows).transpose(1, 0, 2).reshape(n_dev, cut),
            g_tab[n_vec:].reshape(n_dev, n_small - cut),
        ],
        axis=1,
    )
    g_small = jnp.pad(g_small, ((0, 0), (0, lanes * 128 - n_small)))
    if own:
        nh = nx // 2
        g_qkv, g_out, g_up, g_down, g_small = scatter(
            [
                g_qkv.reshape(nd, nh, 2, ny, att_rows, 3 * width),
                g_out.reshape(nd, nh, 2, ny, att_rows, width),
                g_up.reshape(nh, 2, nd, ny, ff_rows, units),
                g_down.reshape(nh, 2, nd, ny, ff_rows, units),
                g_small.reshape(nd, nh, 2, ny, lanes, 128),
            ],
            [False, False, True, True, False],
            nd,
            nh,
            ny,
        )
    else:
        g_qkv, g_out, g_small = (
            lax.psum_scatter(a.astype(F32), ALL, scatter_dimension=0, tiled=True)
            for a in (g_qkv, g_out, g_small)
        )
        gx = lax.axis_index("gx")
        g_up, g_down = (
            lax.psum_scatter(
                lax.psum_scatter(a.astype(F32), "gx", scatter_dimension=0, tiled=True)[0],
                ("dp", "gy"),
                scatter_dimension=0,
                tiled=True,
            )
            for a in (g_up, g_down)
        )
    g_small = g_small.reshape(lanes * 128)
    gv = [g_small[i * att_rows : (i + 1) * att_rows] for i in range(n_vec)]
    return (
        y,
        x_grad,
        g_qkv[:, :width],
        g_qkv[:, width : 2 * width],
        g_qkv[:, 2 * width :],
        g_out,
        gv[G1],
        gv[S1],
        gv[QB],
        gv[VB],
        gv[OB],
        gv[G2],
        gv[S2],
        g_up,
        g_small[cut:n_small],
        g_down,
        gv[DB],
    )


def solution(mesh):
    rows, cols = P(ALL, None), P(ALL)
    cube = P(ALL, None, None)
    ff = P(("dp", "gy"), "gx")
    sizes = (mesh.shape["dp"], mesh.shape["gx"], mesh.shape["gy"])
    return jax.shard_map(
        functools.partial(per_device, sizes),
        mesh=mesh,
        in_specs=(cube, rows, cube) + (rows,) * 4 + (cols,) * 7 + (ff, cols, ff, cols),
        out_specs=(cube, cube) + (rows,) * 4 + (cols,) * 7 + (ff, cols, ff, cols),
        check_vma=False,
    )
```

```python
import functools
import math

import jax
import jax.numpy as jnp
from jax import lax
from jax.experimental import pallas as pl
from jax.experimental.pallas import tpu as pltpu
from jax.sharding import PartitionSpec as P

H = 12
HD = 64
BF = jnp.bfloat16
F32 = jnp.float32
ALL = ("dp", "gx", "gy")
MESH = pl.DeviceIdType.MESH
LOG2E = 1.4426950408889634
INV_SQRT2 = 0.7071067811865476
INV_SQRT_2PI = 0.3989422804014327
ANY = pl.BlockSpec(memory_space=pl.ANY)
VM = pl.BlockSpec(memory_space=pltpu.VMEM)
LIMIT = 60 << 20

G1, S1, QB, VB, OB, G2, S2, DB, UB0 = 0, 1, 2, 3, 4, 5, 6, 7, 8


def nn(a, b):
    return lax.dot_general(a, b, (((1,), (0,)), ((), ())), preferred_element_type=F32)


def nt(a, b):
    return lax.dot_general(a, b, (((1,), (1,)), ((), ())), preferred_element_type=F32)


def padded(length):
    return (length + 31) // 32 * 32


def row_pieces(length, step):
    return [(lo, min(step, length - lo)) for lo in range(0, length, step)]


def normalise(rows):
    centred = rows - jnp.mean(rows, axis=-1, keepdims=True)
    scale = lax.rsqrt(jnp.mean(centred * centred, axis=-1, keepdims=True) + 1e-06)
    return centred * scale, scale


def norm_back(grad, gain, xhat, scale):
    t = grad * gain
    return scale * (
        t
        - jnp.mean(t, axis=-1, keepdims=True)
        - xhat * jnp.mean(t * xhat, axis=-1, keepdims=True)
    )


def colsum(rows):
    return jnp.sum(rows, axis=0, keepdims=True)


def qkv_kernel(x_ref, w_ref, v_ref, qkv_ref, n_ref, bias_ref):
    strips, length, width = x_ref.shape
    lp = n_ref.shape[1]
    gain, shift = v_ref[G1 : G1 + 1, :], v_ref[S1 : S1 + 1, :]
    for s in range(strips):
        for lo, size in row_pieces(length, 136):
            xhat, _ = normalise(x_ref[s, lo : lo + size, :].astype(F32))
            n_ref[s, lo : lo + size, :] = (xhat * gain + shift).astype(BF)
        n_ref[s, length:lp, :] = jnp.zeros((lp - length, width), BF)
    bias_ref[0:1, 0:width] = v_ref[QB : QB + 1, :]
    bias_ref[0:1, width : 2 * width] = jnp.zeros((1, width), F32)
    bias_ref[0:1, 2 * width : 3 * width] = v_ref[VB : VB + 1, :]
    step = 256

    def body(i, carry):
        cols = pl.ds(pl.multiple_of(i * step, step), step)
        w = w_ref[:, cols]
        for s in range(strips):
            qkv_ref[s, :, cols] = (nn(n_ref[s], w) + bias_ref[0:1, cols]).astype(BF)
        return carry

    lax.fori_loop(0, 3 * width // step, body, 0)


def fill_bias(bias_ref, row, col):
    bias_ref[...] = jnp.where(row == col, 0.0, -1e30).astype(F32)


def attend_kernel(qkv_ref, sr_ref, sc_ref, o_ref, lse_ref, bias_ref):
    strips, lp, width = o_ref.shape
    qrows = lp // 2
    first = lax.broadcasted_iota(jnp.int32, (qrows, 128), 1) < HD
    lane = lax.broadcasted_iota(jnp.int32, (qrows, 128), 1)
    scale = 0.125 * LOG2E
    for s in range(strips):
        fill_bias(bias_ref, sc_ref[s], sr_ref[s])
        lse_ref[s] = jnp.zeros((lp, 128), F32)

        def body(p, carry):
            cq = pl.ds(pl.multiple_of(p * 128, 128), 128)
            ck = pl.ds(pl.multiple_of(width + p * 128, 128), 128)
            cv = pl.ds(pl.multiple_of(2 * width + p * 128, 128), 128)
            k, v = qkv_ref[s, :, ck], qkv_ref[s, :, cv]
            for part in range(2):
                rows = pl.ds(part * qrows, qrows)
                q = qkv_ref[s, rows, cq]
                lse = lse_ref[s, rows, :]
                res = []
                for j in range(2):
                    keep = first if j == 0 else jnp.logical_not(first)
                    z = nt(jnp.where(keep, q, jnp.zeros_like(q)), k) * scale + bias_ref[rows, :]
                    top = jnp.max(z, axis=-1, keepdims=True)
                    e = jnp.exp2(z - top)
                    total = jnp.sum(e, axis=-1, keepdims=True)
                    res.append(nn(e.astype(BF), v) / total)
                    lse = jnp.where(lane == 2 * p + j, top + jnp.log2(total), lse)
                o_ref[s, rows, cq] = jnp.where(first, res[0], res[1]).astype(BF)
                lse_ref[s, rows, :] = lse
            return carry

        lax.fori_loop(0, H // 2, body, 0)


def transpose_into(dst_ref, src_ref, lp):
    strips, _, width = src_ref.shape
    for s in range(strips):

        def body(i, carry):
            cols = pl.ds(pl.multiple_of(i * 128, 128), 128)
            dst_ref[s, cols, :] = src_ref[s, :, cols].astype(F32).T.astype(BF)
            return carry

        lax.fori_loop(0, width // 128, body, 0)


def ff_kernel(
    x_ref, mix_ref, dout_in_ref, wo_ref, up_ref, down_ref, v_ref,
    y_ref, rg_ref, mg_ref, gup_ref, gdown_ref, gwo_ref, gv_ref,
    dout_ref, doutT_ref, sec_ref, secT_ref, res_ref, acc_ref, sg_ref, hid_ref, pre_ref,
):
    strips, length, width = x_ref.shape
    lp = mix_ref.shape[1]
    groups = up_ref.shape[0]
    units = up_ref.shape[2]
    gv_ref[...] = jnp.zeros(gv_ref.shape, F32)
    bias_o, gain, shift = v_ref[OB : OB + 1, :], v_ref[G2 : G2 + 1, :], v_ref[S2 : S2 + 1, :]
    step = 256
    for s in range(strips):
        dout_ref[s, 0:length, :] = dout_in_ref[s]
        dout_ref[s, length:lp, :] = jnp.zeros((lp - length, width), BF)

        def proj(i, carry):
            cols = pl.ds(pl.multiple_of(i * step, step), step)
            acc_ref[s, :, cols] = nn(mix_ref[s], wo_ref[:, cols])
            return carry

        lax.fori_loop(0, width // step, proj, 0)
        for lo, size in row_pieces(length, 136):
            rows = pl.ds(lo, size)
            residual = x_ref[s, rows, :].astype(F32) + (acc_ref[s, rows, :] + bias_o)
            res_ref[s, rows, :] = residual
            xhat, _ = normalise(residual)
            sec_ref[s, rows, :] = (xhat * gain + shift).astype(BF)
            acc_ref[s, rows, :] = residual + v_ref[DB : DB + 1, :]
        sec_ref[s, length:lp, :] = jnp.zeros((lp - length, width), BF)
        res_ref[s, length:lp, :] = jnp.zeros((lp - length, width), F32)
        gv_ref[DB : DB + 1, :] += colsum(dout_in_ref[s].astype(F32))
    sg_ref[...] = jnp.zeros(sg_ref.shape, F32)
    transpose_into(doutT_ref, dout_ref, lp)
    transpose_into(secT_ref, sec_ref, lp)

    def group(gi, carry):
        def hidden(i, carry):
            cols = pl.ds(pl.multiple_of(i * step, step), step)
            up, down = up_ref[gi, :, cols], down_ref[gi, :, cols]
            ub = v_ref[pl.ds(UB0 + gi, 1), cols]
            total = jnp.zeros((1, step), F32)
            for s in range(strips):
                pre = nn(sec_ref[s], up) + ub
                hg = nn(dout_ref[s], down)
                cdf = 0.5 + 0.5 * lax.erf(pre * INV_SQRT2)
                pdf = jnp.exp(-0.5 * pre * pre) * INV_SQRT_2PI
                hid_ref[s, :, cols] = (pre * cdf).astype(BF)
                pg = (hg * (cdf + pre * pdf)).astype(BF)
                pre_ref[s, :, cols] = pg
                total = total + colsum(pg.astype(F32))
            gv_ref[pl.ds(UB0 + gi, 1), cols] = total
            return carry

        lax.fori_loop(0, units // step, hidden, 0)

        def back(i, carry):
            rows = pl.ds(pl.multiple_of(i * step, step), step)
            for s in range(strips):
                acc_ref[s, :, rows] += nt(hid_ref[s], down_ref[gi, rows, :])
                sg_ref[s, :, rows] += nt(pre_ref[s], up_ref[gi, rows, :])
            gd = nn(doutT_ref[0, rows, :], hid_ref[0])
            gu = nn(secT_ref[0, rows, :], pre_ref[0])
            for s in range(1, strips):
                gd = gd + nn(doutT_ref[s, rows, :], hid_ref[s])
                gu = gu + nn(secT_ref[s, rows, :], pre_ref[s])
            gdown_ref[gi, rows, :] = gd.astype(BF)
            gup_ref[gi, rows, :] = gu.astype(BF)
            return carry

        lax.fori_loop(0, width // step, back, 0)
        return carry

    lax.fori_loop(0, groups, group, 0)
    for s in range(strips):
        for lo, size in row_pieces(length, 136):
            rows = pl.ds(lo, size)
            y_ref[s, rows, :] = acc_ref[s, rows, :].astype(BF)
            xhat, scale = normalise(res_ref[s, rows, :])
            grad = sg_ref[s, rows, :]
            gv_ref[G2 : G2 + 1, :] += colsum(grad * xhat)
            gv_ref[S2 : S2 + 1, :] += colsum(grad)
            rg = dout_ref[s, rows, :].astype(F32) + norm_back(grad, gain, xhat, scale)
            rg_ref[s, rows, :] = rg
            low = rg.astype(BF)
            sec_ref[s, rows, :] = low
            gv_ref[OB : OB + 1, :] += colsum(low.astype(F32))
        sec_ref[s, length:lp, :] = jnp.zeros((lp - length, width), BF)
        rg_ref[s, length:lp, :] = jnp.zeros((lp - length, width), F32)
    transpose_into(secT_ref, mix_ref, lp)

    def last(i, carry):
        rows = pl.ds(pl.multiple_of(i * step, step), step)
        for s in range(strips):
            mg_ref[s, :, rows] = nt(sec_ref[s], wo_ref[rows, :]).astype(BF)
        gw = nn(secT_ref[0, rows, :], sec_ref[0])
        for s in range(1, strips):
            gw = gw + nn(secT_ref[s, rows, :], sec_ref[s])
        gwo_ref[rows, :] = gw.astype(BF)
        return carry

    lax.fori_loop(0, width // step, last, 0)


def attend_back_kernel(
    qkv_ref, mg_ref, mix_ref, lse_ref, sr_ref, sc_ref, dqkv_ref, bias_ref, lt_ref, dt_ref, kt_ref
):
    strips, lp, width = mg_ref.shape
    krows = lp // 2
    first = lax.broadcasted_iota(jnp.int32, (krows, 128), 1) < HD
    scale = 0.125 * LOG2E
    heads = lax.broadcasted_iota(jnp.int32, (16, width), 0)
    owner = lax.broadcasted_iota(jnp.int32, (16, width), 1) // HD
    pick = jnp.where(heads == owner, 1.0, 0.0).astype(BF)
    for s in range(strips):
        fill_bias(bias_ref, sc_ref[s], sr_ref[s])
        lt_ref[...] = lse_ref[s].T
        prod = mg_ref[s].astype(F32) * mix_ref[s].astype(F32)
        high = prod.astype(BF)
        rest = (prod - high.astype(F32)).astype(BF)
        dt_ref[...] = nt(pick, high) + nt(pick, rest)

        def body(p, carry):
            cq = pl.ds(pl.multiple_of(p * 128, 128), 128)
            ck = pl.ds(pl.multiple_of(width + p * 128, 128), 128)
            cv = pl.ds(pl.multiple_of(2 * width + p * 128, 128), 128)
            q, do = qkv_ref[s, :, cq], mg_ref[s, :, cq]
            kt_ref[...] = qkv_ref[s, :, ck].astype(F32).T.astype(BF)
            dq = [jnp.zeros((HD, lp), F32), jnp.zeros((HD, lp), F32)]
            for part in range(2):
                rows = pl.ds(part * krows, krows)
                k, v = qkv_ref[s, rows, ck], qkv_ref[s, rows, cv]
                dv, dk = [], []
                for j in range(2):
                    keep = first if j == 0 else jnp.logical_not(first)
                    lse = lt_ref[pl.ds(2 * p + j, 1), :]
                    delta = dt_ref[pl.ds(2 * p + j, 1), :]
                    z = nt(jnp.where(keep, k, jnp.zeros_like(k)), q) * scale + bias_ref[rows, :]
                    prob = jnp.exp2(z - lse)
                    pg = nt(jnp.where(keep, v, jnp.zeros_like(v)), do)
                    sg = (prob * (pg - delta)).astype(BF)
                    dv.append(nn(prob.astype(BF), do))
                    dk.append(nn(sg, q))
                    dq[j] = dq[j] + nn(kt_ref[j * HD : (j + 1) * HD, part * krows : (part + 1) * krows], sg)
                dqkv_ref[s, rows, cv] = jnp.where(first, dv[0], dv[1]).astype(BF)
                dqkv_ref[s, rows, ck] = (0.125 * jnp.where(first, dk[0], dk[1])).astype(BF)
            dqkv_ref[s, :, cq] = (0.125 * jnp.concatenate(dq, axis=0)).T.astype(BF)
            return carry

        lax.fori_loop(0, H // 2, body, 0)


def qkv_back_kernel(
    x_ref, n_ref, dqkv_ref, rg_ref, w_ref, v_ref, gx_ref, gw_ref, gv_ref, nT_ref, ng_ref
):
    strips, length, width = x_ref.shape
    lp = n_ref.shape[1]
    step = 256
    gv_ref[...] = jnp.zeros(gv_ref.shape, F32)
    gain = v_ref[G1 : G1 + 1, :]
    transpose_into(nT_ref, n_ref, lp)
    for s in range(strips):
        gv_ref[QB : QB + 1, :] += colsum(dqkv_ref[s, :, 0:width].astype(F32))
        gv_ref[VB : VB + 1, :] += colsum(dqkv_ref[s, :, 2 * width : 3 * width].astype(F32))

        def body(i, carry):
            rows = pl.ds(pl.multiple_of(i * step, step), step)
            ng_ref[s, :, rows] = nt(dqkv_ref[s], w_ref[rows, :])
            return carry

        lax.fori_loop(0, width // step, body, 0)

    def grads(i, carry):
        cols = pl.ds(pl.multiple_of(i * step, step), step)
        gw = nn(nT_ref[0], dqkv_ref[0, :, cols])
        for s in range(1, strips):
            gw = gw + nn(nT_ref[s], dqkv_ref[s, :, cols])
        gw_ref[:, cols] = gw.astype(BF)
        return carry

    lax.fori_loop(0, 3 * width // step, grads, 0)
    for s in range(strips):
        for lo, size in row_pieces(length, 136):
            rows = pl.ds(lo, size)
            xhat, scale = normalise(x_ref[s, rows, :].astype(F32))
            grad = ng_ref[s, rows, :]
            gv_ref[G1 : G1 + 1, :] += colsum(grad * xhat)
            gv_ref[S1 : S1 + 1, :] += colsum(grad)
            term = norm_back(grad, gain, xhat, scale)
            gx_ref[s, rows, :] = (rg_ref[s, rows, :] + term).astype(BF)


def call(kernel, outs, n_in, scratch=()):
    return pl.pallas_call(
        kernel,
        out_shape=outs,
        in_specs=[VM] * n_in,
        out_specs=[VM] * len(outs),
        scratch_shapes=list(scratch),
        compiler_params=pltpu.CompilerParams(vmem_limit_bytes=LIMIT),
    )


def sds(shape, dtype):
    return jax.ShapeDtypeStruct(shape, dtype)


def remote(src, dst, send, recv, dev):
    return pltpu.make_async_remote_copy(
        src_ref=src, dst_ref=dst, send_sem=send, recv_sem=recv, device_id=dev, device_id_type=MESH
    )


class Place:
    def __init__(self, ny):
        self.ny = ny
        self.d, x, self.g = lax.axis_index("dp"), lax.axis_index("gx"), lax.axis_index("gy")
        self.h, self.c = x // 2, x % 2
        self.z = [(self.d, x, lax.rem(self.g + k, ny)) for k in range(1, ny)]
        self.y = (self.d, (1 - self.h) * 2 + self.c, self.g)
        self.x = (1 - self.d, x, self.g)
        self.core = (self.d, self.h * 2 + 1 - self.c, self.g)

    def greet(self):
        barrier = pltpu.get_barrier_semaphore()
        peers = self.z + [self.y, self.x, self.core]
        for peer in peers:
            pl.semaphore_signal(barrier, inc=1, device_id=peer, device_id_type=MESH)
        pl.semaphore_wait(barrier, len(peers))


class Gather:
    def __init__(self, at, shards, views, sems):
        self.at, self.shards, self.views, self.n = at, shards, views, len(shards)
        self.loc, self.zsend, self.zrecv, self.bsend, self.brecv = sems
        self.zs, self.bs, self.fs, self.cs = {}, {}, {}, {}

    @staticmethod
    def semaphores(n, ny):
        return [pltpu.SemaphoreType.DMA(s) for s in ((n,), (n, ny - 1), (n, ny - 1), (n, 8), (n, 8))]

    def push(self, t, i, ref, dev):
        cp = remote(ref, ref, self.bsend.at[t, i], self.brecv.at[t, i], dev)
        cp.start()
        return cp

    def start_z(self, t):
        at = self.at
        own = self.views[t](at.d, at.h, at.c, at.g, 1)
        local = pltpu.make_async_copy(self.shards[t], own, self.loc.at[t])
        local.start()
        copies = []
        for k, dev in enumerate(at.z):
            cp = remote(self.shards[t], own, self.zsend.at[t, k], self.zrecv.at[t, k], dev)
            cp.start()
            copies.append(cp)
        self.zs[t] = local, copies

    def start_b(self, t):
        at = self.at
        self.zs[t][0].wait()
        for cp in self.zs[t][1]:
            cp.wait_recv()
        b = self.views[t](at.d, at.h, at.c, 0, at.ny)
        self.bs[t] = [self.push(t, i, b, dev) for i, dev in enumerate((at.y, at.x, at.core))]

    def start_f(self, t):
        at, view = self.at, self.views[t]
        half = at.ny // 2
        self.bs[t][0].wait_recv()
        f1 = self.push(t, 3, view(at.d, 1 - at.h, at.c, 0, half), at.x)
        c1 = self.push(t, 4, view(at.d, 1 - at.h, at.c, 0, at.ny), at.core)
        self.bs[t][1].wait_recv()
        f2 = self.push(t, 5, view(1 - at.d, at.h, at.c, half, at.ny - half), at.y)
        c2 = self.push(t, 6, view(1 - at.d, at.h, at.c, 0, at.ny), at.core)
        self.fs[t] = [f1, c1, f2, c2]

    def start_c(self, t):
        at = self.at
        self.fs[t][0].wait_recv()
        self.fs[t][2].wait_recv()
        self.cs[t] = self.push(t, 7, self.views[t](1 - at.d, 1 - at.h, at.c, 0, at.ny), at.core)

    def arrived(self, t):
        for cp in (self.bs[t][2], self.fs[t][1], self.fs[t][3], self.cs[t]):
            cp.wait_recv()

    def sent(self, t):
        for cp in self.zs[t][1] + self.bs[t] + self.fs[t] + [self.cs[t]]:
            cp.wait_send()

    def step(self, k):
        for lag, stage in enumerate((self.start_z, self.start_b, self.start_f, self.start_c)):
            if 0 <= k - lag < self.n:
                stage(k - lag)


class Table:
    def __init__(self, at, total, landing, send, recv, order):
        self.at, self.total, self.landing, self.send, self.recv = at, total, landing, send, recv
        self.stages = [at.z if o == "z" else [getattr(at, o)] for o in order]
        self.flight, self.slot = [], 0

    @staticmethod
    def scratch(shape, ny):
        return [
            pltpu.VMEM((ny + 2,) + shape, F32), pltpu.VMEM((4,) + shape, F32),
            pltpu.SemaphoreType.DMA((ny + 2,)), pltpu.SemaphoreType.DMA((ny + 2,)),
        ]

    def step(self, k):
        if k > 0:
            value = self.total[k - 1]
            for cp, slot in self.flight[k - 1]:
                cp.wait_recv()
                value = value + self.landing[slot]
            if k < len(self.stages):
                self.total[k] = value
            else:
                return value
        copies = []
        for dev in self.stages[k]:
            slot = self.slot
            self.slot += 1
            cp = remote(self.total.at[k], self.landing.at[slot], self.send.at[slot], self.recv.at[slot], dev)
            cp.start()
            copies.append((cp, slot))
        self.flight.append(copies)
        return None

    def sent(self):
        for copies in self.flight:
            for cp, _ in copies:
                cp.wait_send()


class Scatter:
    def __init__(self, at, units, buffers, sems):
        self.at, self.units, self.n = at, units, len(units)
        self.bufs = buffers
        self.lsem, self.csend, self.crecv, self.bsend, self.brecv, self.zsend, self.zrecv = sems
        d, h = at.d, at.h
        self.quads = [(1 - d, 1 - h), (d, 1 - h), (1 - d, h), (d, h)]
        self.cs, self.far, self.near, self.zs = {}, {}, {}, {}

    @staticmethod
    def buffers(k, rows, cols, ny):
        return [
            pltpu.VMEM((lead, n * k, rows, cols), BF)
            for lead, n in ((4, ny), (4, ny), (2, ny // 2), (2, ny), (ny - 1, 1))
        ]

    @staticmethod
    def semaphores(n, ny):
        lead = (4, 4, 4, 4, 4, ny - 1, ny - 1)
        return [pltpu.SemaphoreType.DMA((n, k)) for k in lead]

    def add(self, dst, src, pieces):
        lead = dst.shape[0] // pieces

        def body(i, carry):
            part = pl.ds(i * lead, lead)
            dst[part] = (dst[part].astype(F32) + src[part].astype(F32)).astype(dst.dtype)
            return carry

        lax.fori_loop(0, pieces, body, 0)

    def start_core(self, t):
        view, (sums, rc) = self.units[t][0], self.bufs[t][:2]
        c = self.at.c
        res = []
        for q, (d, h) in enumerate(self.quads):
            cp = remote(
                view(d, h, 1 - c), rc.at[q], self.csend.at[t, q], self.crecv.at[t, q], self.at.core
            )
            cp.start()
            lc = pltpu.make_async_copy(view(d, h, c), sums.at[q], self.lsem.at[t, q])
            lc.start()
            res.append((cp, lc))
        self.cs[t] = res

    def start_far(self, t):
        sums, rc, rs = self.bufs[t][:3]
        ny, k = self.at.ny, self.units[t][1]
        cut = ny // 2 * k
        res = []
        for q in range(4):
            self.cs[t][q][0].wait_recv()
            self.cs[t][q][1].wait()
            self.add(sums.at[q], rc.at[q], ny)
            if q == 0:
                for i, (lo, dev) in enumerate(((0, self.at.x), (cut, self.at.y))):
                    cp = remote(
                        sums.at[0, lo : lo + cut], rs.at[i], self.bsend.at[t, i], self.brecv.at[t, i], dev
                    )
                    cp.start()
                    res.append(cp)
        self.far[t] = res

    def start_near(self, t):
        sums, _, rs, rl = self.bufs[t][:4]
        ny, k = self.at.ny, self.units[t][1]
        cut = ny // 2 * k
        res = []
        for i, (lo, dev) in enumerate(((0, self.at.y), (cut, self.at.x))):
            self.far[t][i].wait_recv()
            self.add(sums.at[1 + i, lo : lo + cut], rs.at[i], ny // 2)
            cp = remote(sums.at[1 + i], rl.at[i], self.bsend.at[t, 2 + i], self.brecv.at[t, 2 + i], dev)
            cp.start()
            res.append(cp)
        self.near[t] = res

    def start_z(self, t):
        sums, rl, rz = self.bufs[t][0], self.bufs[t][3], self.bufs[t][4]
        at, n = self.at, self.units[t][1]
        for i in range(2):
            self.near[t][i].wait_recv()
            self.add(sums.at[3], rl.at[i], at.ny)
        res = []
        for k, dev in enumerate(at.z):
            cp = remote(
                sums.at[3, pl.ds(dev[2] * n, n)], rz.at[k], self.zsend.at[t, k], self.zrecv.at[t, k], dev
            )
            cp.start()
            res.append(cp)
        self.zs[t] = res

    def finish(self, t):
        sums, rz = self.bufs[t][0], self.bufs[t][4]
        n = self.units[t][1]
        total = sums[3, pl.ds(self.at.g * n, n)].astype(F32)
        for k, cp in enumerate(self.zs[t]):
            cp.wait_recv()
            total = total + rz[k].astype(F32)
        self.units[t][2](total)

    def sent(self, t):
        for q in range(4):
            self.cs[t][q][0].wait_send()
        for cp in self.far[t] + self.near[t] + self.zs[t]:
            cp.wait_send()

    def step(self, k):
        stages = (self.start_core, self.start_far, self.start_near, self.start_z, self.finish)
        for lag, stage in enumerate(stages):
            if 0 <= k - lag < self.n:
                stage(k - lag)


GROUPS = 3
GW = 256
PARTS = 3


def att_view(ref, tiles, sizes):
    nd, nh, ny = sizes

    def view(d, h, c, lo, n):
        return ref.at[pl.ds((((d * nh + h) * 2 + c) * ny + lo) * tiles, n * tiles)]

    return view


def ff_view(ref, cols):
    def view(d, h, c, lo, n):
        return ref.at[h, c, d, pl.ds(lo, n), :, cols]

    return view


def columns_of(seg_row):
    return jnp.broadcast_to(seg_row, (128, seg_row.shape[1])).T[:, 0:1]


def transpose_rows(dst_ref, src_ref):
    total, width = src_ref.shape
    for lo, size in row_pieces(total, 128):

        def body(i, carry):
            cols = pl.ds(pl.multiple_of(i * 128, 128), 128)
            dst_ref[cols, lo : lo + size] = src_ref[lo : lo + size, cols].astype(F32).T.astype(BF)
            return carry

        lax.fori_loop(0, width // 128, body, 0)


def mask_into(bias_ref, segp_ref, s):
    row = segp_ref[s : s + 1, :]
    bias_ref[...] = jnp.where(columns_of(row) == row, 0.0, -1e30).astype(F32)


def segments_into(segp_ref, seg_ref):
    strips, length = seg_ref.shape
    segp_ref[...] = jnp.full(segp_ref.shape, -1.0, F32)
    segp_ref[0:strips, 0:length] = seg_ref[...].astype(F32)


def attend_pair(qkv_ref, o_ref, lse_ref, bias_ref, s, lp, base, out_col, head):
    qrows = lp // 2
    lane = lax.broadcasted_iota(jnp.int32, (qrows, 128), 1)
    first = lane < HD
    scale = 0.125 * LOG2E
    off = s * lp
    k = qkv_ref[off : off + lp, base + GW : base + GW + 128]
    v = qkv_ref[off : off + lp, base + 2 * GW : base + 2 * GW + 128]
    for part in range(2):
        lo = part * qrows
        q = qkv_ref[off + lo : off + lo + qrows, base : base + 128]
        lse = lse_ref[s, lo : lo + qrows, :]
        res = []
        for j in range(2):
            keep = first if j == 0 else jnp.logical_not(first)
            z = nt(jnp.where(keep, q, jnp.zeros_like(q)), k) * scale + bias_ref[s, lo : lo + qrows, :]
            top = jnp.max(z, axis=-1, keepdims=True)
            e = jnp.exp2(z - top)
            total = jnp.sum(e, axis=-1, keepdims=True)
            res.append(nn(e.astype(BF), v) / total)
            lse = jnp.where(lane == head + j, top + jnp.log2(total), lse)
        o_ref[off + lo : off + lo + qrows, out_col : out_col + 128] = jnp.where(first, res[0], res[1]).astype(BF)
        lse_ref[s, lo : lo + qrows, :] = lse


def front_kernel(
    sizes, x_hbm, do_hbm, seg_ref, wq, wk, wv, wo, up, down, small_ref,
    qkv_ref, mixed_ref, nT_ref, dout_ref, doutT_ref, lt_ref, table_ref, gsum_ref,
    watt_out, wo_out, up_out, down_out,
    x_ref, do_ref, xhat_ref, norm_ref, shard_ref, land_w, watt_ref, bias_row, lse_ref, bias_ref, segp_ref,
    land_ref, tot_ref, tsend, trecv, lsem, s_loc, s_zs, s_zr, s_bs, s_br,
):
    nd, nh, ny = sizes
    strips, length, width = x_ref.shape
    lp = norm_ref.shape[0] // strips
    tiles = wq.shape[0]
    at = Place(ny)
    loads = [pltpu.make_async_copy(x_hbm, x_ref, lsem.at[0]), pltpu.make_async_copy(do_hbm, do_ref, lsem.at[1])]
    pieces = []
    for i in range(GROUPS):
        for j, w in enumerate((wq, wk, wv)):
            pieces.append(
                pltpu.make_async_copy(
                    w.at[:, :, i * GW : (i + 1) * GW], shard_ref.at[i, :, :, j * GW : (j + 1) * GW],
                    lsem.at[2 + 3 * i + j],
                )
            )
    for cp in pieces + loads:
        cp.start()
    at.greet()
    for cp in pieces:
        cp.wait()
    views = [att_view(land_w.at[i], tiles, sizes) for i in range(GROUPS)] + [att_view(wo_out, tiles, sizes)]
    shards = [shard_ref.at[i] for i in range(GROUPS)] + [wo]
    pw = up.shape[-1] // PARTS
    for i in range(PARTS):
        cols = slice(i * pw, (i + 1) * pw)
        for w, out in ((up, up_out), (down, down_out)):
            shards.append(w.at[:, :, cols])
            views.append(ff_view(out, cols))
    gat = Gather(at, shards, views, (s_loc, s_zs, s_zr, s_bs, s_br))
    tab = Table(at, tot_ref, land_ref, tsend, trecv, ("z", "y", "x", "core"))
    tot_ref[0] = small_ref[...]

    gat.step(0)
    tab.step(0)
    for cp in loads:
        cp.wait()
    segments_into(segp_ref, seg_ref)
    for s in range(strips):
        mask_into(bias_ref.at[s], segp_ref, s)
    lse_ref[...] = jnp.zeros(lse_ref.shape, F32)
    gat.step(1)
    tab.step(1)
    for s in range(strips):
        for lo, size in row_pieces(length, 136):
            xhat, _ = normalise(x_ref[s, lo : lo + size, :].astype(F32))
            xhat_ref[s * lp + lo : s * lp + lo + size, :] = xhat
        if s == 0:
            gat.step(2)
            tab.step(2)
    gat.step(3)
    tab.step(3)
    gsum = jnp.zeros((1, width), F32)
    for s in range(strips):
        dout_ref[s * lp : s * lp + length, :] = do_ref[s]
        dout_ref[s * lp + length : (s + 1) * lp, :] = jnp.zeros((lp - length, width), BF)
        gsum = gsum + colsum(do_ref[s].astype(F32))
    gsum_ref[...] = jnp.broadcast_to(gsum, gsum_ref.shape)
    transpose_rows(doutT_ref, dout_ref)
    gat.step(4)
    table = tab.step(4)
    table_ref[...] = table
    gain, shift = table[G1 : G1 + 1, :], table[S1 : S1 + 1, :]
    for s in range(strips):
        for lo, size in row_pieces(length, 136):
            part = slice(s * lp + lo, s * lp + lo + size)
            norm_ref[part, :] = (xhat_ref[part, :] * gain + shift).astype(BF)
        norm_ref[s * lp + length : (s + 1) * lp, :] = jnp.zeros((lp - length, width), BF)
    for i in range(GROUPS):
        cols = slice(i * GW, (i + 1) * GW)
        bias_row[i : i + 1, 0:GW] = table[QB : QB + 1, cols]
        bias_row[i : i + 1, GW : 2 * GW] = jnp.zeros((1, GW), F32)
        bias_row[i : i + 1, 2 * GW : 3 * GW] = table[VB : VB + 1, cols]

    done = 5
    after = (2, 2, 2)
    for i in range(GROUPS):
        gat.arrived(i)

        def settle(n, carry):
            part = pl.ds(n * 8, 8)
            rows = pl.ds(pl.multiple_of(n * 64, 64), 64)
            watt_ref[i, rows, :] = land_w[i, part].astype(F32).reshape(64, width).astype(BF)
            return carry

        lax.fori_loop(0, width // 64, settle, 0)

        def project(n, carry):
            cols = pl.ds(pl.multiple_of(n * GW, GW), GW)
            dst = pl.ds(pl.multiple_of(i * 3 * GW + n * GW, GW), GW)
            qkv_ref[:, dst] = (nn(norm_ref[...], watt_ref[i, :, cols]) + bias_row[i : i + 1, cols]).astype(BF)
            return carry

        lax.fori_loop(0, 3, project, 0)
        for s in range(strips):
            for p in range(GW // 128):
                attend_pair(
                    qkv_ref, mixed_ref, lse_ref, bias_ref, s, lp,
                    i * 3 * GW + p * 128, i * GW + p * 128, i * (GW // HD) + 2 * p,
                )
                if done < gat.n + 3 and p % 2 == 1:
                    gat.step(done)
                    done += 1
        if i == 0:
            transpose_rows(nT_ref, norm_ref)
    for s in range(strips):
        lt_ref[s] = lse_ref[s].T[0:16, :]
    copies = [pltpu.make_async_copy(watt_ref, watt_out, lsem.at[0])]
    copies[0].start()
    while done < gat.n + 3:
        gat.step(done)
        done += 1
    for t in range(GROUPS, gat.n):
        gat.arrived(t)
    for t in range(gat.n):
        gat.sent(t)
    tab.sent()
    copies[0].wait()


def middle_kernel(
    x_ref, mix_ref, dout_ref, doutT_ref, wo_ref, v_ref, gsum_ref, up_ref, down_ref,
    y_ref, rg_ref, mg_ref, gwo_ref, gv_ref, gup_ref, gdown_ref,
    sec_ref, secT_ref, res_ref, acc_ref, sg_ref, hid_ref, pre_ref,
):
    strips, length, width = x_ref.shape
    lp = mix_ref.shape[0] // strips
    units = up_ref.shape[1]
    gi = pl.program_id(0)
    step = 256
    bias_o, gain, shift = v_ref[OB : OB + 1, :], v_ref[G2 : G2 + 1, :], v_ref[S2 : S2 + 1, :]

    @pl.when(gi == 0)
    def _():
        gv_ref[...] = jnp.zeros(gv_ref.shape, F32)
        gv_ref[DB : DB + 1, :] = gsum_ref[0:1, :]

        def proj(i, carry):
            cols = pl.ds(pl.multiple_of(i * step, step), step)
            acc_ref[:, cols] = nn(mix_ref[...], wo_ref[:, cols])
            return carry

        lax.fori_loop(0, width // step, proj, 0)
        for s in range(strips):
            for lo, size in row_pieces(length, 136):
                part = slice(s * lp + lo, s * lp + lo + size)
                residual = x_ref[s, lo : lo + size, :].astype(F32) + (acc_ref[part, :] + bias_o)
                res_ref[part, :] = residual
                xhat, _ = normalise(residual)
                sec_ref[part, :] = (xhat * gain + shift).astype(BF)
                acc_ref[part, :] = residual + v_ref[DB : DB + 1, :]
            sec_ref[s * lp + length : (s + 1) * lp, :] = jnp.zeros((lp - length, width), BF)
        sg_ref[...] = jnp.zeros(sg_ref.shape, F32)
        transpose_rows(secT_ref, sec_ref)

    def hidden(i, carry):
        cols = pl.ds(pl.multiple_of(i * step, step), step)
        pre = nn(sec_ref[...], up_ref[:, cols]) + v_ref[pl.ds(UB0 + gi, 1), cols]
        hg = nn(dout_ref[...], down_ref[:, cols])
        cdf = 0.5 + 0.5 * lax.erf(pre * INV_SQRT2)
        pdf = jnp.exp(-0.5 * pre * pre) * INV_SQRT_2PI
        hid_ref[:, cols] = (pre * cdf).astype(BF)
        pg = (hg * (cdf + pre * pdf)).astype(BF)
        pre_ref[:, cols] = pg
        gv_ref[pl.ds(UB0 + gi, 1), cols] = colsum(pg.astype(F32))
        return carry

    lax.fori_loop(0, units // step, hidden, 0)

    def back(i, carry):
        rows = pl.ds(pl.multiple_of(i * step, step), step)
        acc_ref[:, rows] += nt(hid_ref[...], down_ref[rows, :])
        sg_ref[:, rows] += nt(pre_ref[...], up_ref[rows, :])
        gdown_ref[rows, :] = nn(doutT_ref[rows, :], hid_ref[...]).astype(BF)
        gup_ref[rows, :] = nn(secT_ref[rows, :], pre_ref[...]).astype(BF)
        return carry

    lax.fori_loop(0, width // step, back, 0)

    @pl.when(gi == pl.num_programs(0) - 1)
    def _():
        for s in range(strips):
            for lo, size in row_pieces(length, 136):
                part = slice(s * lp + lo, s * lp + lo + size)
                y_ref[s, lo : lo + size, :] = acc_ref[part, :].astype(BF)
                xhat, scale = normalise(res_ref[part, :])
                grad = sg_ref[part, :]
                gv_ref[G2 : G2 + 1, :] += colsum(grad * xhat)
                gv_ref[S2 : S2 + 1, :] += colsum(grad)
                rg = dout_ref[part, :].astype(F32) + norm_back(grad, gain, xhat, scale)
                rg_ref[part, :] = rg
                low = rg.astype(BF)
                sec_ref[part, :] = low
                gv_ref[OB : OB + 1, :] += colsum(low.astype(F32))
            tail = slice(s * lp + length, (s + 1) * lp)
            sec_ref[tail, :] = jnp.zeros((lp - length, width), BF)
            rg_ref[tail, :] = jnp.zeros((lp - length, width), F32)
        transpose_rows(secT_ref, mix_ref)

        def last(i, carry):
            rows = pl.ds(pl.multiple_of(i * step, step), step)
            mg_ref[:, rows] = nt(sec_ref[...], wo_ref[rows, :]).astype(BF)
            gwo_ref[rows, :] = nn(secT_ref[rows, :], sec_ref[...]).astype(BF)
            return carry

        lax.fori_loop(0, width // step, last, 0)


def attend_back_pair(
    qkv_ref, mg_ref, dz_ref, bias_ref, lt_ref, dt_ref, kt_ref, s, lp, base, out_col, head, dst
):
    krows = lp // 2
    first = lax.broadcasted_iota(jnp.int32, (krows, 128), 1) < HD
    scale = 0.125 * LOG2E
    off = s * lp
    q = qkv_ref[off : off + lp, base : base + 128]
    do = mg_ref[off : off + lp, out_col : out_col + 128]
    kt_ref[...] = qkv_ref[off : off + lp, base + GW : base + GW + 128].astype(F32).T.astype(BF)
    dq = [jnp.zeros((HD, lp), F32), jnp.zeros((HD, lp), F32)]
    for part in range(2):
        lo = off + part * krows
        k = qkv_ref[lo : lo + krows, base + GW : base + GW + 128]
        v = qkv_ref[lo : lo + krows, base + 2 * GW : base + 2 * GW + 128]
        dv, dk = [], []
        for j in range(2):
            keep = first if j == 0 else jnp.logical_not(first)
            lse = lt_ref[s, head + j : head + j + 1, :]
            delta = dt_ref[s, head + j : head + j + 1, :]
            mask = bias_ref[s, part * krows : (part + 1) * krows, :]
            z = nt(jnp.where(keep, k, jnp.zeros_like(k)), q) * scale + mask
            prob = jnp.exp2(z - lse)
            pg = nt(jnp.where(keep, v, jnp.zeros_like(v)), do)
            sg = (prob * (pg - delta)).astype(BF)
            dv.append(nn(prob.astype(BF), do))
            dk.append(nn(sg, q))
            dq[j] = dq[j] + nn(kt_ref[j * HD : (j + 1) * HD, part * krows : (part + 1) * krows], sg)
        dz_ref[lo : lo + krows, dst + 2 * GW : dst + 2 * GW + 128] = jnp.where(first, dv[0], dv[1]).astype(BF)
        dz_ref[lo : lo + krows, dst + GW : dst + GW + 128] = (0.125 * jnp.where(first, dk[0], dk[1])).astype(BF)
    dz_ref[off : off + lp, dst : dst + 128] = (0.125 * jnp.concatenate(dq, axis=0)).T.astype(BF)


def back_kernel(
    sizes, gup, gdown, gwo, qkv_ref, mg_ref, mix_ref, lt_ref, seg_ref, nT_ref, x_ref, rg_ref,
    watt_ref, v_ref, gvm_ref,
    gx_ref, gq_ref, gk_ref, gv_ref, go_ref, gu_ref, gd_ref, gtab_ref,
    dz_ref, ng_ref, part_ref, bias_ref, segp_ref, dt_ref, kt_ref, tab_ref,
    land_ref, tot_ref, tsend, trecv,
    *rest,
):
    nd, nh, ny = sizes
    strips, length, width = x_ref.shape
    lp = qkv_ref.shape[0] // strips
    at = Place(ny)
    at.greet()
    n_ff = 2 * PARTS
    n = n_ff + 1 + GROUPS
    bufs = [rest[5 * t : 5 * t + 5] for t in range(n)]
    sems = rest[5 * n :]
    pw = gup.shape[-1] // PARTS
    units = []

    def ff_unit(src, dst, cols):
        def view(d, h, c):
            return src.at[h, c, d, :, :, cols]

        def put(total):
            dst[:, cols] = total[0]

        return view, 1, put

    for i in range(PARTS):
        cols = slice(i * pw, (i + 1) * pw)
        units += [ff_unit(gup, gu_ref, cols), ff_unit(gdown, gd_ref, cols)]
    tiles = gq_ref.shape[0] // 8

    def att_unit(src, put):
        inner = att_view(src, tiles, sizes)
        return lambda d, h, c: inner(d, h, c, 0, ny), tiles, put

    def put_out(total):
        go_ref[...] = total.reshape(go_ref.shape)

    units.append(att_unit(gwo, put_out))
    for i in range(GROUPS):

        def put_group(total, i=i):
            for j, ref in enumerate((gq_ref, gk_ref, gv_ref)):
                ref[:, i * GW : (i + 1) * GW] = total[:, :, j * GW : (j + 1) * GW].reshape(-1, GW)

        units.append(att_unit(part_ref.at[i], put_group))
    sca = Scatter(at, units, bufs, sems)
    tab = Table(at, tot_ref, land_ref, tsend, trecv, ("core", "x", "y", "z"))

    sca.step(0)
    done = 1
    tab_ref[...] = gvm_ref[...]
    segments_into(segp_ref, seg_ref)
    heads = lax.broadcasted_iota(jnp.int32, (16, width), 0)
    pick = jnp.where(heads == lax.broadcasted_iota(jnp.int32, (16, width), 1) // HD, 1.0, 0.0).astype(BF)
    for s in range(strips):
        mask_into(bias_ref.at[s], segp_ref, s)
        part = slice(s * lp, (s + 1) * lp)
        prod = mg_ref[part, :].astype(F32) * mix_ref[part, :].astype(F32)
        high = prod.astype(BF)
        dt_ref[s] = nt(pick, high) + nt(pick, (prod - high.astype(F32)).astype(BF))
    schedule = ((1, 1, 1, 1), (1, 1, 1, 1), (1, 1, 1, 1))
    limit = (n_ff + 1, n_ff + 2, n_ff + 3)
    for i in range(GROUPS):
        body = 0
        for s in range(strips):
            for p in range(GW // 128):
                attend_back_pair(
                    qkv_ref, mg_ref, dz_ref, bias_ref, lt_ref, dt_ref, kt_ref, s, lp,
                    i * 3 * GW + p * 128, i * GW + p * 128, i * (GW // HD) + 2 * p, p * 128,
                )
                for _ in range(schedule[i][body]):
                    if done < limit[i]:
                        sca.step(done)
                        done += 1
                body += 1
        cols = slice(i * GW, (i + 1) * GW)
        tab_ref[QB : QB + 1, cols] = colsum(dz_ref[:, 0:GW].astype(F32))
        tab_ref[VB : VB + 1, cols] = colsum(dz_ref[:, 2 * GW : 3 * GW].astype(F32))

        def grads(j, carry):
            c = pl.ds(pl.multiple_of(j * GW, GW), GW)
            part_ref[i, :, :, c] = nn(nT_ref[...], dz_ref[:, c]).reshape(width // 8, 8, GW).astype(BF)
            return carry

        lax.fori_loop(0, 3, grads, 0)
        while done < n_ff + 1 + i:
            sca.step(done)
            done += 1
        if done == n_ff + 1 + i:
            sca.step(done)
            done += 1

        def to_norm(j, carry):
            c = pl.ds(pl.multiple_of(j * GW, GW), GW)
            value = nt(dz_ref[...], watt_ref[i, c, :])
            ng_ref[:, c] = value if i == 0 else ng_ref[:, c] + value
            return carry

        lax.fori_loop(0, width // GW, to_norm, 0)
    gain = v_ref[G1 : G1 + 1, :]
    for s in range(strips):
        for lo, size in row_pieces(length, 136):
            part = slice(s * lp + lo, s * lp + lo + size)
            xhat, scale = normalise(x_ref[s, lo : lo + size, :].astype(F32))
            grad = ng_ref[part, :]
            tab_ref[G1 : G1 + 1, :] += colsum(grad * xhat)
            tab_ref[S1 : S1 + 1, :] += colsum(grad)
            term = norm_back(grad, gain, xhat, scale)
            gx_ref[s, lo : lo + size, :] = (rg_ref[part, :] + term).astype(BF)
        if s == 0:
            sca.step(done)
            done += 1
    tot_ref[0] = tab_ref[...]
    k = 0
    while done < n + 4 or k < 5:
        if k < 5:
            res = tab.step(k)
            if res is not None:
                gtab_ref[...] = res
            k += 1
        if done < n + 4:
            sca.step(done)
            done += 1
    for t in range(n):
        sca.sent(t)
    tab.sent()


def own_path(sizes, args):
    (
        block_input, segment_ids, out_grad, query_weight, key_weight, value_weight, output_weight, small,
        up_weight, down_weight,
    ) = args
    nd, nx, ny = sizes
    nh = nx // 2
    grid3 = (nd, nh, ny)
    strips, length, width = block_input.shape
    units = up_weight.shape[1]
    att_rows, ff_rows = query_weight.shape[0], up_weight.shape[0]
    lp = padded(length)
    tiles = att_rows // 8
    full, wide, turned = (strips * lp, width), (strips * lp, 3 * width), (width, strips * lp)
    n_tab = small.shape[0]
    n_units = GROUPS + 1 + 2 * PARTS
    ff_shape = (nh, 2, nd, ny, ff_rows, units)
    dma = pltpu.SemaphoreType.DMA
    (
        qkv, mixed, nT, dout, doutT, lt, table, gsum, watt, wo, up, down,
    ) = pl.pallas_call(
        functools.partial(front_kernel, grid3),
        out_shape=[
            sds(wide, BF), sds(full, BF), sds(turned, BF), sds(full, BF), sds(turned, BF),
            sds((strips, 16, lp), F32), sds((n_tab, width), F32), sds((8, width), F32),
            sds((GROUPS, width, width), BF), sds((width // 8, 8, width), BF), sds(ff_shape, BF), sds(ff_shape, BF),
        ],
        in_specs=[ANY, ANY, VM] + [ANY] * 6 + [VM],
        out_specs=[VM] * 8 + [ANY] * 4,
        scratch_shapes=[
            pltpu.VMEM(block_input.shape, BF), pltpu.VMEM(block_input.shape, BF),
            pltpu.VMEM(full, F32), pltpu.VMEM(full, BF),
            pltpu.VMEM((GROUPS, tiles, 8, width), BF), pltpu.VMEM((GROUPS, width // 8, 8, width), BF),
            pltpu.VMEM((GROUPS, width, width), BF), pltpu.VMEM((8, width), F32), pltpu.VMEM((strips, lp, 128), F32),
            pltpu.VMEM((strips, lp, lp), F32), pltpu.VMEM((8, lp), F32),
        ]
        + Table.scratch((n_tab, width), ny)
        + [dma((2 + 3 * GROUPS,))]
        + Gather.semaphores(n_units, ny),
        compiler_params=pltpu.CompilerParams(collective_id=0, has_side_effects=True, vmem_limit_bytes=LIMIT),
    )(
        block_input, out_grad, segment_ids,
        *(w.reshape(tiles, 8, width) for w in (query_weight, key_weight, value_weight, output_weight)),
        up_weight[None], down_weight[None], small,
    )

    def once(shape):
        return pl.BlockSpec(shape, lambda i: (0,) * len(shape), pipeline_mode=pl.Buffered(1))

    group = pl.BlockSpec((None, width, units), lambda i: (i, 0, 0))
    x_shape = block_input.shape
    y, rg, mg, gwo, gvm, gup, gdown = pl.pallas_call(
        middle_kernel,
        grid=(nx,),
        out_shape=[
            sds(x_shape, BF), sds(full, F32), sds(full, BF), sds((width, width), BF), sds((n_tab, width), F32),
            sds((nx, width, units), BF), sds((nx, width, units), BF),
        ],
        in_specs=[
            once(x_shape), once(full), once(full), once(turned), once((width, width)), once((n_tab, width)),
            once((8, width)), group, group,
        ],
        out_specs=[
            once(x_shape), once(full), once(full), once((width, width)), once((n_tab, width)), group, group,
        ],
        scratch_shapes=[
            pltpu.VMEM(full, BF), pltpu.VMEM(turned, BF), pltpu.VMEM(full, F32), pltpu.VMEM(full, F32),
            pltpu.VMEM(full, F32), pltpu.VMEM((strips * lp, units), BF), pltpu.VMEM((strips * lp, units), BF),
        ],
        compiler_params=pltpu.CompilerParams(vmem_limit_bytes=LIMIT),
    )(
        block_input, mixed, dout, doutT, wo.reshape(width, width), table, gsum, up.reshape(nx, width, units),
        down.reshape(nx, width, units),
    )

    ff6 = (nh, 2, nd, ny, ff_rows, units)
    buffers = []
    for _ in range(2 * PARTS):
        buffers += Scatter.buffers(1, ff_rows, units // PARTS, ny)
    for _ in range(1 + GROUPS):
        buffers += Scatter.buffers(tiles, 8, width, ny)
    gx, gq, gk, gv, go, gu, gd, gtab = pl.pallas_call(
        functools.partial(back_kernel, grid3),
        out_shape=[sds(x_shape, BF)] + [sds((att_rows, width), F32)] * 4 + [sds((ff_rows, units), F32)] * 2
        + [sds((n_tab, width), F32)],
        in_specs=[ANY] * 3 + [VM] * 11,
        out_specs=[VM] * 8,
        scratch_shapes=[
            pltpu.VMEM(full, BF), pltpu.VMEM(full, F32), pltpu.VMEM((GROUPS, width // 8, 8, width), BF),
            pltpu.VMEM((strips, lp, lp), F32), pltpu.VMEM((8, lp), F32), pltpu.VMEM((strips, 16, lp), F32),
            pltpu.VMEM((128, lp), BF), pltpu.VMEM((n_tab, width), F32),
        ]
        + Table.scratch((n_tab, width), ny)
        + buffers
        + Scatter.semaphores(n_units, ny),
        compiler_params=pltpu.CompilerParams(collective_id=1, has_side_effects=True, vmem_limit_bytes=LIMIT),
    )(
        gup.reshape(ff6), gdown.reshape(ff6), gwo.reshape(width // 8, 8, width), qkv, mg, mixed, lt, segment_ids, nT, block_input, rg,
        watt, table, gvm,
    )
    return y, gx, gq, gk, gv, go, gu, gd, gtab


def wide_path(sizes, args):
    (
        block_input, segment_ids, out_grad, query_weight, key_weight, value_weight, output_weight, table,
        up_weight, down_weight,
    ) = args
    nd, nx, ny = sizes
    strips, length, width = block_input.shape
    units = up_weight.shape[1]
    lp = padded(length)
    att = jnp.concatenate([query_weight, key_weight, value_weight, output_weight], axis=1)
    att = lax.all_gather(att, ALL, axis=0, tiled=True)
    up, down = (
        lax.all_gather(lax.all_gather(a, ("dp", "gy"), axis=0, tiled=True), "gx", axis=0)
        for a in (up_weight, down_weight)
    )
    w_qkv, w_out = att[:, : 3 * width], att[:, 3 * width :]
    seg = jnp.pad(segment_ids, ((0, 0), (0, lp - length)), constant_values=-1)
    seg_row, seg_col = seg[:, None, :], seg[:, :, None]
    full = (strips, lp, width)
    wide = (strips, lp, 3 * width)
    turned = (strips, width, lp)
    qkv, normed = call(
        qkv_kernel, [sds(wide, BF), sds(full, BF)], 3, [pltpu.VMEM((8, 3 * width), F32)]
    )(block_input, w_qkv, table)
    mixed, lse = call(
        attend_kernel, [sds(full, BF), sds((strips, lp, 128), F32)], 3, [pltpu.VMEM((lp, lp), F32)]
    )(qkv, seg_row, seg_col)
    y, res_grad, mixed_grad, g_up, g_down, g_out, g_tab = call(
        ff_kernel,
        [
            sds(block_input.shape, BF), sds(full, F32), sds(full, BF), sds(up.shape, BF),
            sds(down.shape, BF), sds((width, width), BF), sds(table.shape, F32),
        ],
        7,
        [
            pltpu.VMEM(full, BF), pltpu.VMEM(turned, BF), pltpu.VMEM(full, BF), pltpu.VMEM(turned, BF),
            pltpu.VMEM(full, F32), pltpu.VMEM(full, F32), pltpu.VMEM(full, F32),
            pltpu.VMEM((strips, lp, units), BF), pltpu.VMEM((strips, lp, units), BF),
        ],
    )(block_input, mixed, out_grad, w_out, up, down, table)
    (dqkv,) = call(
        attend_back_kernel,
        [sds(wide, BF)],
        6,
        [
            pltpu.VMEM((lp, lp), F32), pltpu.VMEM((128, lp), F32), pltpu.VMEM((16, lp), F32),
            pltpu.VMEM((128, lp), BF),
        ],
    )(qkv, mixed_grad, mixed, lse, seg_row, seg_col)
    x_grad, g_qkv, g_tab1 = call(
        qkv_back_kernel,
        [sds(block_input.shape, BF), sds((width, 3 * width), BF), sds(table.shape, F32)],
        6,
        [pltpu.VMEM(turned, BF), pltpu.VMEM(full, F32)],
    )(block_input, normed, dqkv, res_grad, w_qkv, table)
    g_tab = lax.psum(g_tab + g_tab1, ALL)
    g_qkv, g_out = (
        lax.psum_scatter(a.astype(F32), ALL, scatter_dimension=0, tiled=True) for a in (g_qkv, g_out)
    )
    g_up, g_down = (
        lax.psum_scatter(
            lax.psum_scatter(a.astype(F32), "gx", scatter_dimension=0, tiled=True)[0],
            ("dp", "gy"),
            scatter_dimension=0,
            tiled=True,
        )
        for a in (g_up, g_down)
    )
    g_att = (g_qkv[:, :width], g_qkv[:, width : 2 * width], g_qkv[:, 2 * width :], g_out)
    return y, x_grad, g_att, g_up, g_down, g_tab


def per_device(
    sizes, block_input, segment_ids, out_grad, query_weight, key_weight, value_weight, output_weight,
    first_gain, first_shift, query_bias, value_bias, output_bias, second_gain, second_shift,
    up_weight, up_bias, down_weight, down_bias,
):
    nd, nx, ny = sizes
    n_dev = nd * nx * ny
    strips, length, width = block_input.shape
    units = up_weight.shape[1]
    att_rows, ff_rows = query_weight.shape[0], up_weight.shape[0]
    own = nd == 2 and nx == 4 and ny % 2 == 0 and att_rows % 8 == 0 and ff_rows % 8 == 0

    vecs = [first_gain, first_shift, query_bias, value_bias, output_bias, second_gain, second_shift, down_bias]
    n_vec = len(vecs)
    me = (lax.axis_index("dp") * nx + lax.axis_index("gx")) * ny + lax.axis_index("gy")
    n_tab = n_vec + up_bias.shape[0] * n_dev // width
    pieces = jnp.stack(vecs).astype(F32)
    lane = lax.broadcasted_iota(jnp.int32, (n_vec, width), 1) // att_rows
    top = jnp.where(lane == me, jnp.tile(pieces, (1, n_dev)), 0.0)
    flat = jnp.tile(up_bias.astype(F32), n_dev).reshape(n_tab - n_vec, width)
    index = lax.broadcasted_iota(jnp.int32, flat.shape, 0) * width + lax.broadcasted_iota(jnp.int32, flat.shape, 1)
    small = jnp.concatenate([top, jnp.where(index // up_bias.shape[0] == me, flat, 0.0)])
    rows_up = (n_tab + 7) // 8 * 8
    small = jnp.pad(small, ((0, rows_up - n_tab), (0, 0)))
    if own:
        y, x_grad, gq, gk, gv_, go, g_up, g_down, g_tab = own_path(
            sizes,
            (
                block_input, segment_ids, out_grad, query_weight, key_weight, value_weight, output_weight,
                small, up_weight, down_weight,
            ),
        )
        g_att = (gq, gk, gv_, go)
    else:
        table = lax.psum(small, ALL)
        y, x_grad, g_att, g_up, g_down, g_tab = wide_path(
            sizes,
            (
                block_input, segment_ids, out_grad, query_weight, key_weight, value_weight, output_weight,
                table, up_weight, down_weight,
            ),
        )
    mine = lax.dynamic_slice(g_tab, (0, me * att_rows), (n_vec, att_rows))
    g_bias = lax.dynamic_slice(
        g_tab[n_vec:n_tab].reshape(-1), (me * up_bias.shape[0],), (up_bias.shape[0],)
    )
    return (
        y, x_grad, *g_att, mine[G1], mine[S1], mine[QB], mine[VB], mine[OB], mine[G2], mine[S2],
        g_up, g_bias, g_down, mine[DB],
    )


def solution(mesh):
    rows, cols = P(ALL, None), P(ALL)
    cube = P(ALL, None, None)
    ff = P(("dp", "gy"), "gx")
    sizes = (mesh.shape["dp"], mesh.shape["gx"], mesh.shape["gy"])
    return jax.shard_map(
        functools.partial(per_device, sizes),
        mesh=mesh,
        in_specs=(cube, rows, cube) + (rows,) * 4 + (cols,) * 7 + (ff, cols, ff, cols),
        out_specs=(cube, cube) + (rows,) * 4 + (cols,) * 7 + (ff, cols, ff, cols),
        check_vma=False,
    )
```

```python
import functools
import math

import jax
import jax.numpy as jnp
from jax import lax
from jax.experimental import pallas as pl
from jax.experimental.pallas import tpu as pltpu
from jax.sharding import PartitionSpec as P

H = 12
HD = 64
BF = jnp.bfloat16
F32 = jnp.float32
ALL = ("dp", "gx", "gy")
MESH = pl.DeviceIdType.MESH
LOG2E = 1.4426950408889634
INV_SQRT2 = 0.7071067811865476
INV_SQRT_2PI = 0.3989422804014327
ANY = pl.BlockSpec(memory_space=pl.ANY)
VM = pl.BlockSpec(memory_space=pltpu.VMEM)
LIMIT = 61 << 20

G1, S1, QB, VB, OB, G2, S2, DB, UB0 = 0, 1, 2, 3, 4, 5, 6, 7, 8


def nn(a, b):
    return lax.dot_general(a, b, (((1,), (0,)), ((), ())), preferred_element_type=F32)


def nt(a, b):
    return lax.dot_general(a, b, (((1,), (1,)), ((), ())), preferred_element_type=F32)


def padded(length):
    return (length + 31) // 32 * 32


def row_pieces(length, step):
    return [(lo, min(step, length - lo)) for lo in range(0, length, step)]


def normalise(rows):
    centred = rows - jnp.mean(rows, axis=-1, keepdims=True)
    scale = lax.rsqrt(jnp.mean(centred * centred, axis=-1, keepdims=True) + 1e-06)
    return centred * scale, scale


def norm_back(grad, gain, xhat, scale):
    t = grad * gain
    return scale * (
        t
        - jnp.mean(t, axis=-1, keepdims=True)
        - xhat * jnp.mean(t * xhat, axis=-1, keepdims=True)
    )


def colsum(rows):
    return jnp.sum(rows, axis=0, keepdims=True)


def qkv_kernel(x_ref, w_ref, v_ref, qkv_ref, n_ref, bias_ref):
    strips, length, width = x_ref.shape
    lp = n_ref.shape[1]
    gain, shift = v_ref[G1 : G1 + 1, :], v_ref[S1 : S1 + 1, :]
    for s in range(strips):
        for lo, size in row_pieces(length, 136):
            xhat, _ = normalise(x_ref[s, lo : lo + size, :].astype(F32))
            n_ref[s, lo : lo + size, :] = (xhat * gain + shift).astype(BF)
        n_ref[s, length:lp, :] = jnp.zeros((lp - length, width), BF)
    bias_ref[0:1, 0:width] = v_ref[QB : QB + 1, :]
    bias_ref[0:1, width : 2 * width] = jnp.zeros((1, width), F32)
    bias_ref[0:1, 2 * width : 3 * width] = v_ref[VB : VB + 1, :]
    step = 256

    def body(i, carry):
        cols = pl.ds(pl.multiple_of(i * step, step), step)
        w = w_ref[:, cols]
        for s in range(strips):
            qkv_ref[s, :, cols] = (nn(n_ref[s], w) + bias_ref[0:1, cols]).astype(BF)
        return carry

    lax.fori_loop(0, 3 * width // step, body, 0)


def fill_bias(bias_ref, row, col):
    bias_ref[...] = jnp.where(row == col, 0.0, -1e30).astype(F32)


def attend_kernel(qkv_ref, sr_ref, sc_ref, o_ref, lse_ref, bias_ref):
    strips, lp, width = o_ref.shape
    qrows = lp // 2
    first = lax.broadcasted_iota(jnp.int32, (qrows, 128), 1) < HD
    lane = lax.broadcasted_iota(jnp.int32, (qrows, 128), 1)
    scale = 0.125 * LOG2E
    for s in range(strips):
        fill_bias(bias_ref, sc_ref[s], sr_ref[s])
        lse_ref[s] = jnp.zeros((lp, 128), F32)

        def body(p, carry):
            cq = pl.ds(pl.multiple_of(p * 128, 128), 128)
            ck = pl.ds(pl.multiple_of(width + p * 128, 128), 128)
            cv = pl.ds(pl.multiple_of(2 * width + p * 128, 128), 128)
            k, v = qkv_ref[s, :, ck], qkv_ref[s, :, cv]
            for part in range(2):
                rows = pl.ds(part * qrows, qrows)
                q = qkv_ref[s, rows, cq]
                lse = lse_ref[s, rows, :]
                res = []
                for j in range(2):
                    keep = first if j == 0 else jnp.logical_not(first)
                    z = nt(jnp.where(keep, q, jnp.zeros_like(q)), k) * scale + bias_ref[rows, :]
                    top = jnp.max(z, axis=-1, keepdims=True)
                    e = jnp.exp2(z - top)
                    total = jnp.sum(e, axis=-1, keepdims=True)
                    res.append(nn(e.astype(BF), v) / total)
                    lse = jnp.where(lane == 2 * p + j, top + jnp.log2(total), lse)
                o_ref[s, rows, cq] = jnp.where(first, res[0], res[1]).astype(BF)
                lse_ref[s, rows, :] = lse
            return carry

        lax.fori_loop(0, H // 2, body, 0)


def transpose_into(dst_ref, src_ref, lp):
    strips, _, width = src_ref.shape
    for s in range(strips):

        def body(i, carry):
            cols = pl.ds(pl.multiple_of(i * 128, 128), 128)
            dst_ref[s, cols, :] = src_ref[s, :, cols].astype(F32).T.astype(BF)
            return carry

        lax.fori_loop(0, width // 128, body, 0)


def ff_kernel(
    x_ref, mix_ref, dout_in_ref, wo_ref, up_ref, down_ref, v_ref,
    y_ref, rg_ref, mg_ref, gup_ref, gdown_ref, gwo_ref, gv_ref,
    dout_ref, doutT_ref, sec_ref, secT_ref, res_ref, acc_ref, sg_ref, hid_ref, pre_ref,
):
    strips, length, width = x_ref.shape
    lp = mix_ref.shape[1]
    groups = up_ref.shape[0]
    units = up_ref.shape[2]
    gv_ref[...] = jnp.zeros(gv_ref.shape, F32)
    bias_o, gain, shift = v_ref[OB : OB + 1, :], v_ref[G2 : G2 + 1, :], v_ref[S2 : S2 + 1, :]
    step = 256
    for s in range(strips):
        dout_ref[s, 0:length, :] = dout_in_ref[s]
        dout_ref[s, length:lp, :] = jnp.zeros((lp - length, width), BF)

        def proj(i, carry):
            cols = pl.ds(pl.multiple_of(i * step, step), step)
            acc_ref[s, :, cols] = nn(mix_ref[s], wo_ref[:, cols])
            return carry

        lax.fori_loop(0, width // step, proj, 0)
        for lo, size in row_pieces(length, 136):
            rows = pl.ds(lo, size)
            residual = x_ref[s, rows, :].astype(F32) + (acc_ref[s, rows, :] + bias_o)
            res_ref[s, rows, :] = residual
            xhat, _ = normalise(residual)
            sec_ref[s, rows, :] = (xhat * gain + shift).astype(BF)
            acc_ref[s, rows, :] = residual + v_ref[DB : DB + 1, :]
        sec_ref[s, length:lp, :] = jnp.zeros((lp - length, width), BF)
        res_ref[s, length:lp, :] = jnp.zeros((lp - length, width), F32)
        gv_ref[DB : DB + 1, :] += colsum(dout_in_ref[s].astype(F32))
    sg_ref[...] = jnp.zeros(sg_ref.shape, F32)
    transpose_into(doutT_ref, dout_ref, lp)
    transpose_into(secT_ref, sec_ref, lp)

    def group(gi, carry):
        def hidden(i, carry):
            cols = pl.ds(pl.multiple_of(i * step, step), step)
            up, down = up_ref[gi, :, cols], down_ref[gi, :, cols]
            ub = v_ref[pl.ds(UB0 + gi, 1), cols]
            total = jnp.zeros((1, step), F32)
            for s in range(strips):
                pre = nn(sec_ref[s], up) + ub
                hg = nn(dout_ref[s], down)
                cdf = 0.5 + 0.5 * lax.erf(pre * INV_SQRT2)
                pdf = jnp.exp(-0.5 * pre * pre) * INV_SQRT_2PI
                hid_ref[s, :, cols] = (pre * cdf).astype(BF)
                pg = (hg * (cdf + pre * pdf)).astype(BF)
                pre_ref[s, :, cols] = pg
                total = total + colsum(pg.astype(F32))
            gv_ref[pl.ds(UB0 + gi, 1), cols] = total
            return carry

        lax.fori_loop(0, units // step, hidden, 0)

        def back(i, carry):
            rows = pl.ds(pl.multiple_of(i * step, step), step)
            for s in range(strips):
                acc_ref[s, :, rows] += nt(hid_ref[s], down_ref[gi, rows, :])
                sg_ref[s, :, rows] += nt(pre_ref[s], up_ref[gi, rows, :])
            gd = nn(doutT_ref[0, rows, :], hid_ref[0])
            gu = nn(secT_ref[0, rows, :], pre_ref[0])
            for s in range(1, strips):
                gd = gd + nn(doutT_ref[s, rows, :], hid_ref[s])
                gu = gu + nn(secT_ref[s, rows, :], pre_ref[s])
            gdown_ref[gi, rows, :] = gd.astype(BF)
            gup_ref[gi, rows, :] = gu.astype(BF)
            return carry

        lax.fori_loop(0, width // step, back, 0)
        return carry

    lax.fori_loop(0, groups, group, 0)
    for s in range(strips):
        for lo, size in row_pieces(length, 136):
            rows = pl.ds(lo, size)
            y_ref[s, rows, :] = acc_ref[s, rows, :].astype(BF)
            xhat, scale = normalise(res_ref[s, rows, :])
            grad = sg_ref[s, rows, :]
            gv_ref[G2 : G2 + 1, :] += colsum(grad * xhat)
            gv_ref[S2 : S2 + 1, :] += colsum(grad)
            rg = dout_ref[s, rows, :].astype(F32) + norm_back(grad, gain, xhat, scale)
            rg_ref[s, rows, :] = rg
            low = rg.astype(BF)
            sec_ref[s, rows, :] = low
            gv_ref[OB : OB + 1, :] += colsum(low.astype(F32))
        sec_ref[s, length:lp, :] = jnp.zeros((lp - length, width), BF)
        rg_ref[s, length:lp, :] = jnp.zeros((lp - length, width), F32)
    transpose_into(secT_ref, mix_ref, lp)

    def last(i, carry):
        rows = pl.ds(pl.multiple_of(i * step, step), step)
        for s in range(strips):
            mg_ref[s, :, rows] = nt(sec_ref[s], wo_ref[rows, :]).astype(BF)
        gw = nn(secT_ref[0, rows, :], sec_ref[0])
        for s in range(1, strips):
            gw = gw + nn(secT_ref[s, rows, :], sec_ref[s])
        gwo_ref[rows, :] = gw.astype(BF)
        return carry

    lax.fori_loop(0, width // step, last, 0)


def attend_back_kernel(
    qkv_ref, mg_ref, mix_ref, lse_ref, sr_ref, sc_ref, dqkv_ref, bias_ref, lt_ref, dt_ref, kt_ref
):
    strips, lp, width = mg_ref.shape
    krows = lp // 2
    first = lax.broadcasted_iota(jnp.int32, (krows, 128), 1) < HD
    scale = 0.125 * LOG2E
    heads = lax.broadcasted_iota(jnp.int32, (16, width), 0)
    owner = lax.broadcasted_iota(jnp.int32, (16, width), 1) // HD
    pick = jnp.where(heads == owner, 1.0, 0.0).astype(BF)
    for s in range(strips):
        fill_bias(bias_ref, sc_ref[s], sr_ref[s])
        lt_ref[...] = lse_ref[s].T
        prod = mg_ref[s].astype(F32) * mix_ref[s].astype(F32)
        high = prod.astype(BF)
        rest = (prod - high.astype(F32)).astype(BF)
        dt_ref[...] = nt(pick, high) + nt(pick, rest)

        def body(p, carry):
            cq = pl.ds(pl.multiple_of(p * 128, 128), 128)
            ck = pl.ds(pl.multiple_of(width + p * 128, 128), 128)
            cv = pl.ds(pl.multiple_of(2 * width + p * 128, 128), 128)
            q, do = qkv_ref[s, :, cq], mg_ref[s, :, cq]
            kt_ref[...] = qkv_ref[s, :, ck].astype(F32).T.astype(BF)
            dq = [jnp.zeros((HD, lp), F32), jnp.zeros((HD, lp), F32)]
            for part in range(2):
                rows = pl.ds(part * krows, krows)
                k, v = qkv_ref[s, rows, ck], qkv_ref[s, rows, cv]
                dv, dk = [], []
                for j in range(2):
                    keep = first if j == 0 else jnp.logical_not(first)
                    lse = lt_ref[pl.ds(2 * p + j, 1), :]
                    delta = dt_ref[pl.ds(2 * p + j, 1), :]
                    z = nt(jnp.where(keep, k, jnp.zeros_like(k)), q) * scale + bias_ref[rows, :]
                    prob = jnp.exp2(z - lse)
                    pg = nt(jnp.where(keep, v, jnp.zeros_like(v)), do)
                    sg = (prob * (pg - delta)).astype(BF)
                    dv.append(nn(prob.astype(BF), do))
                    dk.append(nn(sg, q))
                    dq[j] = dq[j] + nn(kt_ref[j * HD : (j + 1) * HD, part * krows : (part + 1) * krows], sg)
                dqkv_ref[s, rows, cv] = jnp.where(first, dv[0], dv[1]).astype(BF)
                dqkv_ref[s, rows, ck] = (0.125 * jnp.where(first, dk[0], dk[1])).astype(BF)
            dqkv_ref[s, :, cq] = (0.125 * jnp.concatenate(dq, axis=0)).T.astype(BF)
            return carry

        lax.fori_loop(0, H // 2, body, 0)


def qkv_back_kernel(
    x_ref, n_ref, dqkv_ref, rg_ref, w_ref, v_ref, gx_ref, gw_ref, gv_ref, nT_ref, ng_ref
):
    strips, length, width = x_ref.shape
    lp = n_ref.shape[1]
    step = 256
    gv_ref[...] = jnp.zeros(gv_ref.shape, F32)
    gain = v_ref[G1 : G1 + 1, :]
    transpose_into(nT_ref, n_ref, lp)
    for s in range(strips):
        gv_ref[QB : QB + 1, :] += colsum(dqkv_ref[s, :, 0:width].astype(F32))
        gv_ref[VB : VB + 1, :] += colsum(dqkv_ref[s, :, 2 * width : 3 * width].astype(F32))

        def body(i, carry):
            rows = pl.ds(pl.multiple_of(i * step, step), step)
            ng_ref[s, :, rows] = nt(dqkv_ref[s], w_ref[rows, :])
            return carry

        lax.fori_loop(0, width // step, body, 0)

    def grads(i, carry):
        cols = pl.ds(pl.multiple_of(i * step, step), step)
        gw = nn(nT_ref[0], dqkv_ref[0, :, cols])
        for s in range(1, strips):
            gw = gw + nn(nT_ref[s], dqkv_ref[s, :, cols])
        gw_ref[:, cols] = gw.astype(BF)
        return carry

    lax.fori_loop(0, 3 * width // step, grads, 0)
    for s in range(strips):
        for lo, size in row_pieces(length, 136):
            rows = pl.ds(lo, size)
            xhat, scale = normalise(x_ref[s, rows, :].astype(F32))
            grad = ng_ref[s, rows, :]
            gv_ref[G1 : G1 + 1, :] += colsum(grad * xhat)
            gv_ref[S1 : S1 + 1, :] += colsum(grad)
            term = norm_back(grad, gain, xhat, scale)
            gx_ref[s, rows, :] = (rg_ref[s, rows, :] + term).astype(BF)


def call(kernel, outs, n_in, scratch=()):
    return pl.pallas_call(
        kernel,
        out_shape=outs,
        in_specs=[VM] * n_in,
        out_specs=[VM] * len(outs),
        scratch_shapes=list(scratch),
        compiler_params=pltpu.CompilerParams(vmem_limit_bytes=LIMIT),
    )


def sds(shape, dtype):
    return jax.ShapeDtypeStruct(shape, dtype)


def remote(src, dst, send, recv, dev):
    return pltpu.make_async_remote_copy(
        src_ref=src, dst_ref=dst, send_sem=send, recv_sem=recv, device_id=dev, device_id_type=MESH
    )


class Place:
    def __init__(self, ny):
        self.ny = ny
        self.d, x, self.g = lax.axis_index("dp"), lax.axis_index("gx"), lax.axis_index("gy")
        self.h, self.c = x // 2, x % 2
        self.z = [(self.d, x, lax.rem(self.g + k, ny)) for k in range(1, ny)]
        self.y = (self.d, (1 - self.h) * 2 + self.c, self.g)
        self.x = (1 - self.d, x, self.g)
        self.core = (self.d, self.h * 2 + 1 - self.c, self.g)
        h, c = (self.h, 1 - self.h), (self.c, 1 - self.c)
        every = [(d, hh * 2 + cc, self.g) for d in (self.d, 1 - self.d) for hh in h for cc in c]
        self.plane = every[1:]

    def greet(self):
        barrier = pltpu.get_barrier_semaphore()
        peers = self.z + self.plane
        for peer in peers:
            pl.semaphore_signal(barrier, inc=1, device_id=peer, device_id_type=MESH)
        pl.semaphore_wait(barrier, len(peers))


class Gather:
    def __init__(self, at, shards, views, sems):
        self.at, self.shards, self.views, self.n = at, shards, views, len(shards)
        self.loc, self.zsend, self.zrecv, self.bsend, self.brecv = sems
        self.zs, self.bs, self.fs, self.cs = {}, {}, {}, {}

    @staticmethod
    def semaphores(n, ny):
        return [pltpu.SemaphoreType.DMA(s) for s in ((n,), (n, ny - 1), (n, ny - 1), (n, 8), (n, 8))]

    def push(self, t, i, ref, dev):
        cp = remote(ref, ref, self.bsend.at[t, i], self.brecv.at[t, i], dev)
        cp.start()
        return cp

    def z(self, t):
        at = self.at
        own = self.views[t](at.d, at.h, at.c, at.g, 1)
        local = pltpu.make_async_copy(self.shards[t], own, self.loc.at[t])
        local.start()
        copies = []
        for k, dev in enumerate(at.z):
            cp = remote(self.shards[t], own, self.zsend.at[t, k], self.zrecv.at[t, k], dev)
            cp.start()
            copies.append(cp)
        self.zs[t] = local, copies

    def b(self, t):
        at = self.at
        self.zs[t][0].wait()
        for cp in self.zs[t][1]:
            cp.wait_recv()
        b = self.views[t](at.d, at.h, at.c, 0, at.ny)
        self.bs[t] = [self.push(t, i, b, dev) for i, dev in enumerate((at.y, at.x, at.core))]

    def f(self, t):
        at, view = self.at, self.views[t]
        half = at.ny // 2
        self.bs[t][0].wait_recv()
        f1 = self.push(t, 3, view(at.d, 1 - at.h, at.c, 0, half), at.x)
        c1 = self.push(t, 4, view(at.d, 1 - at.h, at.c, 0, at.ny), at.core)
        self.bs[t][1].wait_recv()
        f2 = self.push(t, 5, view(1 - at.d, at.h, at.c, half, at.ny - half), at.y)
        c2 = self.push(t, 6, view(1 - at.d, at.h, at.c, 0, at.ny), at.core)
        self.fs[t] = [f1, c1, f2, c2]

    def c(self, t):
        at = self.at
        self.fs[t][0].wait_recv()
        self.fs[t][2].wait_recv()
        self.cs[t] = self.push(t, 7, self.views[t](1 - at.d, 1 - at.h, at.c, 0, at.ny), at.core)

    def arrived(self, t):
        for cp in (self.bs[t][2], self.fs[t][1], self.fs[t][3], self.cs[t]):
            cp.wait_recv()

    def sent(self, t):
        for cp in self.zs[t][1] + self.bs[t] + self.fs[t] + [self.cs[t]]:
            cp.wait_send()


class Table:
    def __init__(self, at, total, landing, send, recv):
        self.at, self.total, self.landing, self.send, self.recv = at, total, landing, send, recv
        self.stages = [at.plane, at.z]
        self.flight, self.slot = [], 0

    @staticmethod
    def scratch(shape, ny, dtype):
        return [
            pltpu.VMEM((ny + 6,) + shape, dtype), pltpu.VMEM((2,) + shape, dtype),
            pltpu.SemaphoreType.DMA((ny + 6,)), pltpu.SemaphoreType.DMA((ny + 6,)),
        ]

    def step(self, k):
        if k > 0:
            value = self.total[k - 1].astype(F32)
            for cp, slot in self.flight[k - 1]:
                cp.wait_recv()
                value = value + self.landing[slot].astype(F32)
            if k < len(self.stages):
                self.total[k] = value.astype(self.total.dtype)
            else:
                return value
        copies = []
        for dev in self.stages[k]:
            slot = self.slot
            self.slot += 1
            cp = remote(self.total.at[k], self.landing.at[slot], self.send.at[slot], self.recv.at[slot], dev)
            cp.start()
            copies.append((cp, slot))
        self.flight.append(copies)
        return None

    def sent(self):
        for copies in self.flight:
            for cp, _ in copies:
                cp.wait_send()


class Scatter:
    def __init__(self, at, units, buffers, sems):
        self.at, self.units, self.n = at, units, len(units)
        self.bufs = buffers
        self.lsem, self.csend, self.crecv, self.bsend, self.brecv, self.zsend, self.zrecv = sems
        d, h = at.d, at.h
        self.quads = [(1 - d, 1 - h), (d, 1 - h), (1 - d, h), (d, h)]
        self.cs, self.fars, self.nears, self.zs = {}, {}, {}, {}

    @staticmethod
    def buffers(k, rows, cols, ny):
        return [
            pltpu.VMEM((lead, n * k, rows, cols), BF)
            for lead, n in ((4, ny), (4, ny), (2, ny // 2), (2, ny), (ny - 1, 1))
        ]

    @staticmethod
    def semaphores(n, ny):
        lead = (4, 4, 4, 4, 4, ny - 1, ny - 1)
        return [pltpu.SemaphoreType.DMA((n, k)) for k in lead]

    def add(self, dst, src, pieces):
        lead = dst.shape[0] // pieces

        def body(i, carry):
            part = pl.ds(i * lead, lead)
            dst[part] = (dst[part].astype(F32) + src[part].astype(F32)).astype(dst.dtype)
            return carry

        lax.fori_loop(0, pieces, body, 0)

    def core(self, t):
        view, (sums, rc) = self.units[t][0], self.bufs[t][:2]
        c = self.at.c
        res = []
        for q, (d, h) in enumerate(self.quads):
            cp = remote(
                view(d, h, 1 - c), rc.at[q], self.csend.at[t, q], self.crecv.at[t, q], self.at.core
            )
            cp.start()
            lc = pltpu.make_async_copy(view(d, h, c), sums.at[q], self.lsem.at[t, q])
            lc.start()
            res.append((cp, lc))
        self.cs[t] = res

    def far(self, t):
        sums, rc, rs = self.bufs[t][:3]
        ny, k = self.at.ny, self.units[t][1]
        cut = ny // 2 * k
        res = []
        for q in range(4):
            self.cs[t][q][0].wait_recv()
            self.cs[t][q][1].wait()
            self.add(sums.at[q], rc.at[q], ny)
            if q == 0:
                for i, (lo, dev) in enumerate(((0, self.at.x), (cut, self.at.y))):
                    cp = remote(
                        sums.at[0, lo : lo + cut], rs.at[i], self.bsend.at[t, i], self.brecv.at[t, i], dev
                    )
                    cp.start()
                    res.append(cp)
        self.fars[t] = res

    def near(self, t):
        sums, _, rs, rl = self.bufs[t][:4]
        ny, k = self.at.ny, self.units[t][1]
        cut = ny // 2 * k
        res = []
        for i, (lo, dev) in enumerate(((0, self.at.y), (cut, self.at.x))):
            self.fars[t][i].wait_recv()
            self.add(sums.at[1 + i, lo : lo + cut], rs.at[i], ny // 2)
            cp = remote(sums.at[1 + i], rl.at[i], self.bsend.at[t, 2 + i], self.brecv.at[t, 2 + i], dev)
            cp.start()
            res.append(cp)
        self.nears[t] = res

    def z(self, t):
        sums, rl, rz = self.bufs[t][0], self.bufs[t][3], self.bufs[t][4]
        at, n = self.at, self.units[t][1]
        for i in range(2):
            self.nears[t][i].wait_recv()
            self.add(sums.at[3], rl.at[i], at.ny)
        res = []
        for k, dev in enumerate(at.z):
            cp = remote(
                sums.at[3, pl.ds(dev[2] * n, n)], rz.at[k], self.zsend.at[t, k], self.zrecv.at[t, k], dev
            )
            cp.start()
            res.append(cp)
        self.zs[t] = res

    def finish(self, t):
        sums, rz = self.bufs[t][0], self.bufs[t][4]
        n = self.units[t][1]
        total = sums[3, pl.ds(self.at.g * n, n)].astype(F32)
        for k, cp in enumerate(self.zs[t]):
            cp.wait_recv()
            total = total + rz[k].astype(F32)
        self.units[t][2](total)

    def sent(self, t):
        for q in range(4):
            self.cs[t][q][0].wait_send()
        for cp in self.fars[t] + self.nears[t] + self.zs[t]:
            cp.wait_send()


GROUPS = ((0, 128), (128, 256), (384, 256), (640, 128))
NG = len(GROUPS)
PARTS = 3


def att_view(ref, tiles, sizes):
    nd, nh, ny = sizes

    def view(d, h, c, lo, n):
        return ref.at[pl.ds((((d * nh + h) * 2 + c) * ny + lo) * tiles, n * tiles)]

    return view


def ff_view(ref, part):
    def view(d, h, c, lo, n):
        start = pl.multiple_of((h * 2 + c) * part, part)
        return ref.at[d, pl.ds(lo, n), :, pl.ds(start, part)]

    return view


def copies_of(sem, *pairs):
    made = [pltpu.make_async_copy(a, b, sem.at[i]) for i, (a, b) in enumerate(pairs)]
    for cp in made:
        cp.start()
    return made


def columns_of(seg_row):
    return jnp.broadcast_to(seg_row, (128, seg_row.shape[1])).T[:, 0:1]


def turn(dst_ref, src_ref):
    total, width = src_ref.shape
    step = 256
    eye = jnp.where(
        lax.broadcasted_iota(jnp.int32, (step, step), 0) == lax.broadcasted_iota(jnp.int32, (step, step), 1), 1.0, 0.0
    ).astype(BF)
    for lo, size in row_pieces(total, step):
        for j in range(width // step):
            cols = slice(j * step, (j + 1) * step)
            dst_ref[cols, lo : lo + size] = nt(eye, src_ref[lo : lo + size, cols]).astype(BF)


def mask_into(bias_ref, segp_ref, s):
    row = segp_ref[s : s + 1, :]
    bias_ref[...] = jnp.where(columns_of(row) == row, 0.0, -1e30).astype(F32)


def segments_into(segp_ref, seg_ref):
    strips, length = seg_ref.shape
    segp_ref[...] = jnp.full(segp_ref.shape, -1.0, F32)
    segp_ref[0:strips, 0:length] = seg_ref[...].astype(F32)


def attend_pair(qkv_ref, o_ref, lse_ref, bias_ref, s, lp, base, gw, out_col):
    head = out_col // HD
    qrows = lp // 2
    lane = lax.broadcasted_iota(jnp.int32, (qrows, 128), 1)
    first = lane < HD
    scale = 0.125 * LOG2E
    off = s * lp
    k = qkv_ref[off : off + lp, base + gw : base + gw + 128]
    v = qkv_ref[off : off + lp, base + 2 * gw : base + 2 * gw + 128]
    for part in range(2):
        lo = part * qrows
        q = qkv_ref[off + lo : off + lo + qrows, base : base + 128]
        lse = lse_ref[s, lo : lo + qrows, :]
        res = []
        for j in range(2):
            keep = first if j == 0 else jnp.logical_not(first)
            z = nt(jnp.where(keep, q, jnp.zeros_like(q)), k) * scale + bias_ref[s, lo : lo + qrows, :]
            top = jnp.max(z, axis=-1, keepdims=True)
            e = jnp.exp2(z - top)
            total = jnp.sum(e, axis=-1, keepdims=True)
            res.append(nn(e.astype(BF), v) / total)
            lse = jnp.where(lane == head + j, top + jnp.log2(total), lse)
        o_ref[off + lo : off + lo + qrows, out_col : out_col + 128] = jnp.where(first, res[0], res[1]).astype(BF)
        lse_ref[s, lo : lo + qrows, :] = lse


def front_kernel(
    sizes, x_hbm, do_hbm, seg_ref, wq, wk, wv, wo, up, down, small_ref,
    lt_ref, table_ref, gsum_ref, qkv_out, mixed_out, nT_out, dout_out, doutT_out, watt_out, wo_out, up_out, down_out,
    x_ref, do_ref, xhat_ref, norm_ref, shard_ref, watt_ref, bias_row, lse_ref, bias_ref, segp_ref,
    qkv_ref, mixed_ref, nT_ref, dout_ref, doutT_ref,
    land_ref, tot_ref, tsend, trecv, lsem, osem, s_loc, s_zs, s_zr, s_bs, s_br, *land_w,
):
    nd, nh, ny = sizes
    strips, length, width = x_ref.shape
    lp = norm_ref.shape[0] // strips
    tiles = wq.shape[0]
    at = Place(ny)
    loads = [pltpu.make_async_copy(x_hbm, x_ref, lsem.at[0]), pltpu.make_async_copy(do_hbm, do_ref, lsem.at[1])]
    pieces = []
    for i, (first, gw) in enumerate(GROUPS):
        for j, w in enumerate((wq, wk, wv)):
            to = 3 * first + j * gw
            pieces.append(
                pltpu.make_async_copy(
                    w.at[:, :, first : first + gw], shard_ref.at[:, :, to : to + gw], lsem.at[2 + 3 * i + j]
                )
            )
    for cp in pieces + loads:
        cp.start()
    at.greet()
    tab = Table(at, tot_ref, land_ref, tsend, trecv)
    tot_ref[0] = small_ref[...].astype(BF)
    for cp in pieces:
        cp.wait()
    pw = up.shape[-1] // PARTS
    views = [att_view(land, tiles, sizes) for land in land_w] + [att_view(wo_out, tiles, sizes)]
    shards = [shard_ref.at[:, :, 3 * first : 3 * (first + gw)] for first, gw in GROUPS]
    shards += [wo, up.at[:, :, 0:pw], down.at[:, :, 0:pw]]
    views += [ff_view(up_out, pw), ff_view(down_out, pw)]
    gat = Gather(at, shards, views, (s_loc, s_zs, s_zr, s_bs, s_br))

    gat.z(0)
    tab.step(0)
    for cp in loads:
        cp.wait()

    def hats(s):
        for lo, size in row_pieces(length, 136):
            xhat, _ = normalise(x_ref[s, lo : lo + size, :].astype(F32))
            xhat_ref[s * lp + lo : s * lp + lo + size, :] = xhat

    hats(0)
    gat.z(1)
    hats(1)
    for s in range(2, strips):
        hats(s)
    gat.b(0)
    gat.z(2)
    segments_into(segp_ref, seg_ref)
    for s in range(strips):
        mask_into(bias_ref.at[s], segp_ref, s)
    lse_ref[...] = jnp.zeros(lse_ref.shape, F32)
    tab.step(1)
    gsum = jnp.zeros((1, width), F32)
    for s in range(strips):
        dout_ref[s * lp : s * lp + length, :] = do_ref[s]
        dout_ref[s * lp + length : (s + 1) * lp, :] = jnp.zeros((lp - length, width), BF)
        gsum = gsum + colsum(do_ref[s].astype(F32))
    gsum_ref[...] = jnp.broadcast_to(gsum, gsum_ref.shape)
    gat.b(1)
    gat.z(3)
    gat.f(0)
    turn(doutT_ref, dout_ref)
    outs = copies_of(osem, (dout_ref, dout_out), (doutT_ref, doutT_out))
    gat.b(2)
    gat.z(4)
    gat.c(0)
    table = tab.step(2)
    table_ref[...] = table
    gain, shift = table[G1 : G1 + 1, :], table[S1 : S1 + 1, :]
    for s in range(strips):
        for lo, size in row_pieces(length, 136):
            part = slice(s * lp + lo, s * lp + lo + size)
            norm_ref[part, :] = (xhat_ref[part, :] * gain + shift).astype(BF)
        norm_ref[s * lp + length : (s + 1) * lp, :] = jnp.zeros((lp - length, width), BF)
    for first, gw in GROUPS:
        cols = slice(first, first + gw)
        bias_row[0:1, 3 * first : 3 * first + gw] = table[QB : QB + 1, cols]
        bias_row[0:1, 3 * first + gw : 3 * first + 2 * gw] = jnp.zeros((1, gw), F32)
        bias_row[0:1, 3 * first + 2 * gw : 3 * (first + gw)] = table[VB : VB + 1, cols]
    plan = iter(front_plan(gat))
    for i, (first, gw) in enumerate(GROUPS):
        gat.arrived(i)
        wide = slice(3 * first, 3 * (first + gw))
        step = 3 * gw // 3

        def settle(n, carry):
            rows = pl.ds(pl.multiple_of(n * 64, 64), 64)
            watt_ref[rows, wide] = land_w[i][pl.ds(n * 8, 8)].astype(F32).reshape(64, 3 * gw).astype(BF)
            return carry

        lax.fori_loop(0, width // 64, settle, 0)

        def project(n, carry):
            cols = pl.ds(pl.multiple_of(3 * first + n * step, 128), step)
            qkv_ref[:, cols] = (nn(norm_ref[...], watt_ref[:, cols]) + bias_row[0:1, cols]).astype(BF)
            return carry

        lax.fori_loop(0, 3, project, 0)
        outs += copies_of(
            osem.at[2 + 2 * i : 4 + 2 * i],
            (qkv_ref.at[:, wide], qkv_out.at[:, wide]), (watt_ref.at[:, wide], watt_out.at[:, wide]),
        )
        next(plan)
        for s in range(strips):
            for p in range(gw // 128):
                attend_pair(
                    qkv_ref, mixed_ref, lse_ref, bias_ref, s, lp, 3 * first + p * 128, gw, first + p * 128
                )
                next(plan)
        if i == 0:
            turn(nT_ref, norm_ref)
            outs += copies_of(osem.at[2 + 2 * NG : 3 + 2 * NG], (nT_ref, nT_out))
    outs += copies_of(osem.at[3 + 2 * NG :], (mixed_ref, mixed_out))
    for s in range(strips):
        lt_ref[s] = lse_ref[s].T[0:16, :]
    for _ in plan:
        pass
    for t in range(NG, gat.n):
        gat.arrived(t)
    for t in range(gat.n):
        gat.sent(t)
    tab.sent()
    for cp in outs:
        cp.wait()


def front_plan(gat):
    z, b, f, c = gat.z, gat.b, gat.f, gat.c
    stops = (
        ((f, 1), (b, 3), (z, 5)), ((c, 1),), ((f, 2), (b, 4)),
        ((z, 6), (c, 2)), ((f, 3), (b, 5)), (), ((f, 4), (c, 3)), (),
        ((b, 6),), ((f, 5), (c, 4)), (), (), ((f, 6), (c, 5)),
        (), ((c, 6),),
    )
    for stop in stops:
        for stage, t in stop:
            stage(t)
        yield
    for _ in range(64):
        yield


def middle_plan(gat, sca):
    return (
        (
            ((gat.f, 0),), ((gat.f, 1),), ((gat.c, 0), (sca.core, 0), (sca.core, 1), (gat.b, 2)),
            ((gat.c, 1), (sca.far, 0), (gat.b, 3)), ((sca.far, 1),),
        ),
        (
            ((gat.f, 2), (sca.near, 0)), ((gat.f, 3), (sca.near, 1)),
            ((gat.c, 2), (sca.core, 2), (sca.core, 3), (sca.z, 0)), ((gat.c, 3), (sca.far, 2), (sca.z, 1)),
            ((sca.far, 3),),
        ),
        (
            ((sca.finish, 0), (sca.near, 2)), ((sca.finish, 1), (sca.near, 3)), ((sca.z, 2),), ((sca.z, 3),), (),
        ),
    )


def middle_kernel(
    sizes, x_ref, mix_ref, wo_ref, v_ref, gsum_ref, dout_hbm, doutT_hbm, u0, d0, up, down,
    mg_ref, gwo_ref, gv_ref, gu_ref, gd_ref, y_out, rg_out, gu2, gd2,
    dout_ref, doutT_ref, sec_ref, secT_ref, res_ref, acc_ref, rg_ref, hid_ref, pre_ref, y_ref, wu, wd, pu, pd,
    lsem, osem, s_loc, s_zs, s_zr, s_bs, s_br, *rest,
):
    nd, nh, ny = sizes
    nq = nh * 2
    strips, length, width = x_ref.shape
    lp = mix_ref.shape[0] // strips
    rows, part = up.shape[1], up.shape[2] // PARTS
    at = Place(ny)
    loads = copies_of(lsem, (dout_hbm, dout_ref), (doutT_hbm, doutT_ref), (u0, wu.at[0]), (d0, wd.at[0]))
    at.greet()
    n_sc = 2 * (PARTS - 1)
    shards, views, units = [], [], []
    for b in range(1, PARTS):
        cols = slice(b * part, (b + 1) * part)
        shards += [up.at[:, :, cols], down.at[:, :, cols]]
        views += [ff_view(wu.at[b], part), ff_view(wd.at[b], part)]
    for b in range(PARTS - 1):
        for src, dst in ((pu, gu_ref), (pd, gd_ref)):

            def put(total, dst=dst, cols=slice(b * part, (b + 1) * part)):
                dst[:, cols] = total[0]

            whole = ff_view(src.at[b], part)
            units.append(((lambda d, h, c, whole=whole: whole(d, h, c, 0, ny)), 1, put))
    gat = Gather(at, shards, views, (s_loc, s_zs, s_zr, s_bs, s_br))
    sca = Scatter(at, units, [rest[5 * t : 5 * t + 5] for t in range(n_sc)], rest[5 * n_sc :])
    gat.z(0)
    gat.z(1)

    step = 256
    bias_o, gain, shift = v_ref[OB : OB + 1, :], v_ref[G2 : G2 + 1, :], v_ref[S2 : S2 + 1, :]
    gv_ref[...] = jnp.zeros(gv_ref.shape, F32)
    gv_ref[DB : DB + 1, :] = gsum_ref[0:1, :]

    def proj(i, carry):
        cols = pl.ds(pl.multiple_of(i * step, step), step)
        acc_ref[:, cols] = nn(mix_ref[...], wo_ref[:, cols])
        return carry

    lax.fori_loop(0, width // step, proj, 0)
    for s in range(strips):
        if s == 1:
            gat.b(0)
            gat.z(2)
        for lo, size in row_pieces(length, 136):
            sel = slice(s * lp + lo, s * lp + lo + size)
            residual = x_ref[s, lo : lo + size, :].astype(F32) + (acc_ref[sel, :] + bias_o)
            res_ref[sel, :] = residual
            xhat, _ = normalise(residual)
            sec_ref[sel, :] = (xhat * gain + shift).astype(BF)
            acc_ref[sel, :] = residual + v_ref[DB : DB + 1, :]
        sec_ref[s * lp + length : (s + 1) * lp, :] = jnp.zeros((lp - length, width), BF)
    turn(secT_ref, sec_ref)
    gat.b(1)
    gat.z(3)
    for cp in loads:
        cp.wait()

    def stop(b, k):
        for stage, t in middle_plan(gat, sca)[b][k]:
            stage(t)

    for b in range(PARTS):
        if b > 0:
            gat.arrived(2 * b - 2)
            gat.arrived(2 * b - 1)

        def hidden(q, carry):
            cols = pl.ds(pl.multiple_of(q * part, part), part)
            w_up = wu[b, :, :, :, cols].reshape(width, part)
            w_down = wd[b, :, :, :, cols].reshape(width, part)
            pre = nn(sec_ref[...], w_up) + v_ref[pl.ds(UB0 + q, 1), b * part : (b + 1) * part]
            hg = nn(dout_ref[...], w_down)
            cdf = 0.5 + 0.5 * lax.erf(pre * INV_SQRT2)
            pdf = jnp.exp(-0.5 * pre * pre) * INV_SQRT_2PI
            hid_ref[:, cols] = (pre * cdf).astype(BF)
            pg = (hg * (cdf + pre * pdf)).astype(BF)
            pre_ref[:, cols] = pg
            gv_ref[pl.ds(UB0 + q, 1), b * part : (b + 1) * part] = colsum(pg.astype(F32))
            return carry

        g_up, g_down = (pu.at[b], pd.at[b]) if b < PARTS - 1 else (wu.at[0], wd.at[0])

        def grads(q, carry):
            cols = pl.ds(pl.multiple_of(q * part, part), part)
            shape = (nd, ny, rows, part)
            g_down[:, :, :, cols] = nn(doutT_ref[...], hid_ref[:, cols]).astype(BF).reshape(shape)
            g_up[:, :, :, cols] = nn(secT_ref[...], pre_ref[:, cols]).astype(BF).reshape(shape)
            return carry

        lax.fori_loop(0, nq // 2, hidden, 0)
        stop(b, 0)
        lax.fori_loop(nq // 2, nq, hidden, 0)
        stop(b, 1)
        lax.fori_loop(0, nq, grads, 0)
        if b == PARTS - 1:
            outs = copies_of(osem, (g_up, gu2), (g_down, gd2))
        stop(b, 2)
        w_down = wd[b].reshape(width, nq * part)
        for n in range(width // step):
            cols = slice(n * step, (n + 1) * step)
            acc_ref[:, cols] += nt(hid_ref[...], w_down[cols, :])
        stop(b, 3)
        w_up = wu[b].reshape(width, nq * part)
        for n in range(width // step):
            cols = slice(n * step, (n + 1) * step)
            value = nt(pre_ref[...], w_up[cols, :])
            rg_ref[:, cols] = value if b == 0 else rg_ref[:, cols] + value
        stop(b, 4)

    for s in range(strips):
        for lo, size in row_pieces(length, 136):
            sel = slice(s * lp + lo, s * lp + lo + size)
            y_ref[s, lo : lo + size, :] = acc_ref[sel, :].astype(BF)
            xhat, scale = normalise(res_ref[sel, :])
            grad = rg_ref[sel, :]
            gv_ref[G2 : G2 + 1, :] += colsum(grad * xhat)
            gv_ref[S2 : S2 + 1, :] += colsum(grad)
            rg = dout_ref[sel, :].astype(F32) + norm_back(grad, gain, xhat, scale)
            rg_ref[sel, :] = rg
            low = rg.astype(BF)
            sec_ref[sel, :] = low
            gv_ref[OB : OB + 1, :] += colsum(low.astype(F32))
        tail = slice(s * lp + length, (s + 1) * lp)
        sec_ref[tail, :] = jnp.zeros((lp - length, width), BF)
        rg_ref[tail, :] = jnp.zeros((lp - length, width), F32)
    outs += copies_of(osem.at[2:4], (rg_ref, rg_out), (y_ref, y_out))
    sca.finish(2)
    sca.finish(3)
    turn(secT_ref, mix_ref)

    def last(i, carry):
        sel = pl.ds(pl.multiple_of(i * step, step), step)
        mg_ref[:, sel] = nt(sec_ref[...], wo_ref[sel, :]).astype(BF)
        gwo_ref[sel, :] = nn(secT_ref[sel, :], sec_ref[...]).astype(BF)
        return carry

    lax.fori_loop(0, width // step, last, 0)
    for t in range(gat.n):
        gat.sent(t)
    for t in range(n_sc):
        sca.sent(t)
    for cp in outs:
        cp.wait()


def attend_back_pair(
    qkv_ref, mg_ref, dz_ref, bias_ref, lt_ref, dt_ref, kt_ref, s, lp, base, gw, out_col, dst
):
    head = out_col // HD
    krows = lp // 2
    first = lax.broadcasted_iota(jnp.int32, (krows, 128), 1) < HD
    scale = 0.125 * LOG2E
    off = s * lp
    q = qkv_ref[off : off + lp, base : base + 128]
    do = mg_ref[off : off + lp, out_col : out_col + 128]
    kt_ref[...] = qkv_ref[off : off + lp, base + gw : base + gw + 128].astype(F32).T.astype(BF)
    dq = [jnp.zeros((HD, lp), F32), jnp.zeros((HD, lp), F32)]
    for part in range(2):
        lo = off + part * krows
        k = qkv_ref[lo : lo + krows, base + gw : base + gw + 128]
        v = qkv_ref[lo : lo + krows, base + 2 * gw : base + 2 * gw + 128]
        dv, dk = [], []
        for j in range(2):
            keep = first if j == 0 else jnp.logical_not(first)
            lse = lt_ref[s, head + j : head + j + 1, :]
            delta = dt_ref[s, head + j : head + j + 1, :]
            mask = bias_ref[s, part * krows : (part + 1) * krows, :]
            z = nt(jnp.where(keep, k, jnp.zeros_like(k)), q) * scale + mask
            prob = jnp.exp2(z - lse)
            pg = nt(jnp.where(keep, v, jnp.zeros_like(v)), do)
            sg = (prob * (pg - delta)).astype(BF)
            dv.append(nn(prob.astype(BF), do))
            dk.append(nn(sg, q))
            dq[j] = dq[j] + nn(kt_ref[j * HD : (j + 1) * HD, part * krows : (part + 1) * krows], sg)
        dz_ref[lo : lo + krows, dst + 2 * gw : dst + 2 * gw + 128] = jnp.where(first, dv[0], dv[1]).astype(BF)
        dz_ref[lo : lo + krows, dst + gw : dst + gw + 128] = (0.125 * jnp.where(first, dk[0], dk[1])).astype(BF)
    dz_ref[off : off + lp, dst : dst + 128] = (0.125 * jnp.concatenate(dq, axis=0)).T.astype(BF)


def back_plan(sca):
    core, far, near, z, end = sca.core, sca.far, sca.near, sca.z, sca.finish
    return iter((
        ((far, 0),),
        ((far, 1), (far, 2)), ((near, 0),), ((core, 3), (near, 1)),
        ((far, 3), (z, 0)), ((near, 2),), ((z, 1), (near, 3)), ((end, 0), (z, 2)), ((core, 4), (end, 1)),
        ((far, 4), (z, 3)), ((end, 2),), ((near, 4), (end, 3)), (), ((core, 5), (z, 4)),
        ((far, 5),), ((near, 5), (end, 4)), ((core, 6), (z, 5)),
    ))


def back_kernel(
    sizes, gup, gdown, gwo, seg_ref, lt_ref, v_ref, gvm_ref, gu01_ref, gd01_ref,
    mg_hbm, mix_hbm, qkv_hbm, nT_hbm, watt_hbm, x_hbm, rg_hbm,
    gx_ref, gq_ref, gk_ref, gv_ref, go_ref, gu_ref, gd_ref, gtab_ref,
    mg_ref, mix_ref, qkv_ref, nT_ref, watt_ref, x_ref, rg_ref,
    dz_ref, ng_ref, bias_ref, segp_ref, dt_ref, kt_ref, tab_ref,
    land_ref, tot_ref, tsend, trecv, land2_ref, tot2_ref, tsend2, trecv2, isem,
    *rest,
):
    nd, nh, ny = sizes
    strips, length, width = x_ref.shape
    lp = qkv_ref.shape[0] // strips
    parts, rest = rest[:NG], rest[NG:]
    loads = copies_of(
        isem, (mg_hbm, mg_ref), (mix_hbm, mix_ref),
        *[
            (qkv_hbm.at[:, 3 * first : 3 * (first + gw)], qkv_ref.at[:, 3 * first : 3 * (first + gw)])
            for first, gw in GROUPS
        ],
        (nT_hbm, nT_ref), (watt_hbm, watt_ref), (x_hbm, x_ref), (rg_hbm, rg_ref),
    )
    at = Place(ny)
    at.greet()
    n = 3 + NG
    bufs = [rest[5 * t : 5 * t + 5] for t in range(n)]
    sems = rest[5 * n :]
    pw = gup.shape[-1] // (2 * nh)
    units = []

    def ff_unit(src, dst, cols):
        whole = ff_view(src, pw)

        def put(total):
            dst[:, cols] = total[0]

        return lambda d, h, c: whole(d, h, c, 0, ny), 1, put

    last = slice((PARTS - 1) * pw, PARTS * pw)
    units += [ff_unit(gup, gu_ref, last), ff_unit(gdown, gd_ref, last)]
    tiles = gq_ref.shape[0] // 8

    def att_unit(src, put):
        inner = att_view(src, tiles, sizes)
        return lambda d, h, c: inner(d, h, c, 0, ny), tiles, put

    def put_out(total):
        go_ref[...] = total.reshape(go_ref.shape)

    units.append(att_unit(gwo, put_out))
    for i, (first, gw) in enumerate(GROUPS):

        def put_group(total, first=first, gw=gw):
            for j, ref in enumerate((gq_ref, gk_ref, gv_ref)):
                ref[:, first : first + gw] = total[:, :, j * gw : (j + 1) * gw].reshape(-1, gw)

        units.append(att_unit(parts[i], put_group))
    sca = Scatter(at, units, bufs, sems)
    early = Table(at, tot_ref, land_ref, tsend, trecv)
    late = Table(at, tot2_ref, land2_ref, tsend2, trecv2)
    plan = back_plan(sca)

    def stop():
        for stage, t in next(plan):
            stage(t)

    for t in range(3):
        sca.core(t)
    gu_ref[:, 0 : last.start] = gu01_ref[...]
    gd_ref[:, 0 : last.start] = gd01_ref[...]
    tab_ref[...] = gvm_ref[...]
    segments_into(segp_ref, seg_ref)
    heads = lax.broadcasted_iota(jnp.int32, (16, width), 0)
    pick = jnp.where(heads == lax.broadcasted_iota(jnp.int32, (16, width), 1) // HD, 1.0, 0.0).astype(BF)
    for s in range(strips):
        mask_into(bias_ref.at[s], segp_ref, s)
    loads[0].wait()
    loads[1].wait()
    for s in range(strips):
        part = slice(s * lp, (s + 1) * lp)
        prod = mg_ref[part, :].astype(F32) * mix_ref[part, :].astype(F32)
        high = prod.astype(BF)
        dt_ref[s] = nt(pick, high) + nt(pick, (prod - high.astype(F32)).astype(BF))
    stop()
    for i, (first, gw) in enumerate(GROUPS):
        loads[2 + i].wait()
        for s in range(strips):
            for p in range(gw // 128):
                attend_back_pair(
                    qkv_ref, mg_ref, dz_ref, bias_ref, lt_ref, dt_ref, kt_ref, s, lp,
                    3 * first + p * 128, gw, first + p * 128, p * 128,
                )
                stop()
        cols = slice(first, first + gw)
        tab_ref[QB : QB + 1, cols] = colsum(dz_ref[:, 0:gw].astype(F32))
        tab_ref[VB : VB + 1, cols] = colsum(dz_ref[:, 2 * gw : 3 * gw].astype(F32))
        if i == 0:
            loads[2 + NG].wait()
            loads[3 + NG].wait()

        def grads(j, carry):
            c = pl.ds(pl.multiple_of(j * gw, gw), gw)
            parts[i][:, :, c] = nn(nT_ref[...], dz_ref[:, c]).reshape(width // 8, 8, gw).astype(BF)
            return carry

        lax.fori_loop(0, 3, grads, 0)
        stop()
        if i == NG - 1:
            tot_ref[0] = tab_ref[...]
            early.step(0)

        def to_norm(j, carry):
            c = pl.ds(pl.multiple_of(j * 256, 256), 256)
            value = nt(dz_ref[:, 0 : 3 * gw], watt_ref[c, 3 * first : 3 * (first + gw)])
            ng_ref[:, c] = value if i == 0 else ng_ref[:, c] + value
            return carry

        lax.fori_loop(0, width // 256, to_norm, 0)
    end = n - 1
    sca.far(end)
    gain = v_ref[G1 : G1 + 1, :]
    loads[4 + NG].wait()
    loads[5 + NG].wait()
    g_gain, g_shift = jnp.zeros((1, width), F32), jnp.zeros((1, width), F32)
    for s in range(strips):
        for lo, size in row_pieces(length, 136):
            part = slice(s * lp + lo, s * lp + lo + size)
            xhat, scale = normalise(x_ref[s, lo : lo + size, :].astype(F32))
            grad = ng_ref[part, :]
            g_gain = g_gain + colsum(grad * xhat)
            g_shift = g_shift + colsum(grad)
            term = norm_back(grad, gain, xhat, scale)
            gx_ref[s, lo : lo + size, :] = (rg_ref[part, :] + term).astype(BF)
        if s == 0:
            early.step(1)
            sca.finish(end - 1)
            sca.near(end)
    tot2_ref[0, 0:1, :] = g_gain
    tot2_ref[0, 1:2, :] = g_shift
    late.step(0)
    gtab_ref[...] = early.step(2)
    sca.z(end)
    late.step(1)
    sca.finish(end)
    gtab_ref[0:2, :] = late.step(2)
    for t in range(n):
        sca.sent(t)
    early.sent()
    late.sent()


def own_path(sizes, args):
    (
        block_input, segment_ids, out_grad, query_weight, key_weight, value_weight, output_weight, small,
        up_weight, down_weight,
    ) = args
    nd, nx, ny = sizes
    nh = nx // 2
    grid3 = (nd, nh, ny)
    strips, length, width = block_input.shape
    units = up_weight.shape[1]
    att_rows, ff_rows = query_weight.shape[0], up_weight.shape[0]
    lp = padded(length)
    tiles = att_rows // 8
    part = units // PARTS
    total = strips * lp
    full, wide, turned = (total, width), (total, 3 * width), (width, total)
    n_tab = small.shape[0]
    ff_shape = (nd, ny, ff_rows, nx * part)
    x_shape = block_input.shape
    watt_shape = (width, 3 * width)
    lt_shape = (strips, 16, lp)
    dma = pltpu.SemaphoreType.DMA
    ups, downs = up_weight[None], down_weight[None]
    (
        lt, table, gsum, qkv, mixed, nT, dout, doutT, watt, wo, u0, d0,
    ) = pl.pallas_call(
        functools.partial(front_kernel, grid3),
        out_shape=[
            sds(lt_shape, F32), sds((n_tab, width), F32), sds((8, width), F32), sds(wide, BF), sds(full, BF),
            sds(turned, BF), sds(full, BF), sds(turned, BF), sds(watt_shape, BF), sds((width // 8, 8, width), BF),
            sds(ff_shape, BF), sds(ff_shape, BF),
        ],
        in_specs=[ANY, ANY, VM] + [ANY] * 6 + [VM],
        out_specs=[VM] * 3 + [ANY] * 9,
        scratch_shapes=[
            pltpu.VMEM(x_shape, BF), pltpu.VMEM(x_shape, BF), pltpu.VMEM(full, F32), pltpu.VMEM(full, BF),
            pltpu.VMEM((tiles, 8, 3 * width), BF), pltpu.VMEM(watt_shape, BF), pltpu.VMEM((8, 3 * width), F32), pltpu.VMEM((strips, lp, 128), F32),
            pltpu.VMEM((strips, lp, lp), F32), pltpu.VMEM((8, lp), F32),
            pltpu.VMEM(wide, BF), pltpu.VMEM(full, BF), pltpu.VMEM(turned, BF), pltpu.VMEM(full, BF),
            pltpu.VMEM(turned, BF),
        ]
        + Table.scratch((n_tab, width), ny, BF)
        + [dma((2 + 3 * NG,)), dma((4 + 2 * NG,))]
        + Gather.semaphores(NG + 3, ny)
        + [pltpu.VMEM((width // 8, 8, 3 * gw), BF) for _, gw in GROUPS],
        compiler_params=pltpu.CompilerParams(collective_id=0, has_side_effects=True, vmem_limit_bytes=LIMIT),
    )(
        block_input, out_grad, segment_ids,
        *(w.reshape(tiles, 8, width) for w in (query_weight, key_weight, value_weight, output_weight)),
        ups, downs, small,
    )

    n_sc = 2 * (PARTS - 1)
    some = (ff_rows, units - part)
    buffers = []
    for _ in range(n_sc):
        buffers += Scatter.buffers(1, ff_rows, part, ny)
    mg, gwo, gvm, gu01, gd01, y, rg, gu2, gd2 = pl.pallas_call(
        functools.partial(middle_kernel, grid3),
        out_shape=[
            sds(full, BF), sds((width, width), BF), sds((n_tab, width), F32), sds(some, F32), sds(some, F32),
            sds(x_shape, BF), sds(full, F32), sds(ff_shape, BF), sds(ff_shape, BF),
        ],
        in_specs=[VM] * 5 + [ANY] * 6,
        out_specs=[VM] * 5 + [ANY] * 4,
        scratch_shapes=[
            pltpu.VMEM(full, BF), pltpu.VMEM(turned, BF), pltpu.VMEM(full, BF), pltpu.VMEM(turned, BF),
            pltpu.VMEM(full, F32), pltpu.VMEM(full, F32), pltpu.VMEM(full, F32),
            pltpu.VMEM((total, nx * part), BF), pltpu.VMEM((total, nx * part), BF), pltpu.VMEM(x_shape, BF),
        ]
        + [pltpu.VMEM((PARTS,) + ff_shape, BF)] * 2
        + [pltpu.VMEM((PARTS - 1,) + ff_shape, BF)] * 2
        + [dma((4,)), dma((4,))]
        + Gather.semaphores(n_sc, ny)
        + buffers
        + Scatter.semaphores(n_sc, ny),
        compiler_params=pltpu.CompilerParams(collective_id=1, has_side_effects=True, vmem_limit_bytes=LIMIT),
    )(block_input, mixed, wo.reshape(width, width), table, gsum, dout, doutT, u0, d0, ups, downs)

    n_units = 3 + NG
    buffers = []
    for _ in range(2):
        buffers += Scatter.buffers(1, ff_rows, part, ny)
    for cols in [width] + [3 * gw for _, gw in GROUPS]:
        buffers += Scatter.buffers(tiles, 8, cols, ny)
    gx, gq, gk, gv, go, gu, gd, gtab = pl.pallas_call(
        functools.partial(back_kernel, grid3),
        out_shape=[sds(x_shape, BF)] + [sds((att_rows, width), F32)] * 4 + [sds((ff_rows, units), F32)] * 2
        + [sds((n_tab, width), F32)],
        in_specs=[ANY] * 3 + [VM] * 6 + [ANY] * 7,
        out_specs=[VM] * 8,
        scratch_shapes=[
            pltpu.VMEM(full, BF), pltpu.VMEM(full, BF), pltpu.VMEM(wide, BF), pltpu.VMEM(turned, BF),
            pltpu.VMEM(watt_shape, BF), pltpu.VMEM(x_shape, BF), pltpu.VMEM(full, F32),
            pltpu.VMEM(full, BF), pltpu.VMEM(full, F32), pltpu.VMEM((strips, lp, lp), F32), pltpu.VMEM((8, lp), F32), pltpu.VMEM(lt_shape, F32),
            pltpu.VMEM((128, lp), BF), pltpu.VMEM((n_tab, width), F32),
        ]
        + Table.scratch((n_tab, width), ny, F32)
        + Table.scratch((2, width), ny, F32)
        + [dma((6 + NG,))]
        + [pltpu.VMEM((width // 8, 8, 3 * gw), BF) for _, gw in GROUPS]
        + buffers
        + Scatter.semaphores(n_units, ny),
        compiler_params=pltpu.CompilerParams(collective_id=2, has_side_effects=True, vmem_limit_bytes=LIMIT),
    )(
        gu2, gd2, gwo.reshape(width // 8, 8, width), segment_ids, lt, table, gvm, gu01, gd01,
        mg, mixed, qkv, nT, watt, block_input, rg,
    )
    return y, gx, gq, gk, gv, go, gu, gd, gtab


def wide_path(sizes, args):
    (
        block_input, segment_ids, out_grad, query_weight, key_weight, value_weight, output_weight, table,
        up_weight, down_weight,
    ) = args
    nd, nx, ny = sizes
    strips, length, width = block_input.shape
    units = up_weight.shape[1]
    lp = padded(length)
    att = jnp.concatenate([query_weight, key_weight, value_weight, output_weight], axis=1)
    att = lax.all_gather(att, ALL, axis=0, tiled=True)
    up, down = (
        lax.all_gather(lax.all_gather(a, ("dp", "gy"), axis=0, tiled=True), "gx", axis=0)
        for a in (up_weight, down_weight)
    )
    w_qkv, w_out = att[:, : 3 * width], att[:, 3 * width :]
    seg = jnp.pad(segment_ids, ((0, 0), (0, lp - length)), constant_values=-1)
    seg_row, seg_col = seg[:, None, :], seg[:, :, None]
    full = (strips, lp, width)
    wide = (strips, lp, 3 * width)
    turned = (strips, width, lp)
    qkv, normed = call(
        qkv_kernel, [sds(wide, BF), sds(full, BF)], 3, [pltpu.VMEM((8, 3 * width), F32)]
    )(block_input, w_qkv, table)
    mixed, lse = call(
        attend_kernel, [sds(full, BF), sds((strips, lp, 128), F32)], 3, [pltpu.VMEM((lp, lp), F32)]
    )(qkv, seg_row, seg_col)
    y, res_grad, mixed_grad, g_up, g_down, g_out, g_tab = call(
        ff_kernel,
        [
            sds(block_input.shape, BF), sds(full, F32), sds(full, BF), sds(up.shape, BF),
            sds(down.shape, BF), sds((width, width), BF), sds(table.shape, F32),
        ],
        7,
        [
            pltpu.VMEM(full, BF), pltpu.VMEM(turned, BF), pltpu.VMEM(full, BF), pltpu.VMEM(turned, BF),
            pltpu.VMEM(full, F32), pltpu.VMEM(full, F32), pltpu.VMEM(full, F32),
            pltpu.VMEM((strips, lp, units), BF), pltpu.VMEM((strips, lp, units), BF),
        ],
    )(block_input, mixed, out_grad, w_out, up, down, table)
    (dqkv,) = call(
        attend_back_kernel,
        [sds(wide, BF)],
        6,
        [
            pltpu.VMEM((lp, lp), F32), pltpu.VMEM((128, lp), F32), pltpu.VMEM((16, lp), F32),
            pltpu.VMEM((128, lp), BF),
        ],
    )(qkv, mixed_grad, mixed, lse, seg_row, seg_col)
    x_grad, g_qkv, g_tab1 = call(
        qkv_back_kernel,
        [sds(block_input.shape, BF), sds((width, 3 * width), BF), sds(table.shape, F32)],
        6,
        [pltpu.VMEM(turned, BF), pltpu.VMEM(full, F32)],
    )(block_input, normed, dqkv, res_grad, w_qkv, table)
    g_tab = lax.psum(g_tab + g_tab1, ALL)
    g_qkv, g_out = (
        lax.psum_scatter(a.astype(F32), ALL, scatter_dimension=0, tiled=True) for a in (g_qkv, g_out)
    )
    g_up, g_down = (
        lax.psum_scatter(
            lax.psum_scatter(a.astype(F32), "gx", scatter_dimension=0, tiled=True)[0],
            ("dp", "gy"),
            scatter_dimension=0,
            tiled=True,
        )
        for a in (g_up, g_down)
    )
    g_att = (g_qkv[:, :width], g_qkv[:, width : 2 * width], g_qkv[:, 2 * width :], g_out)
    return y, x_grad, g_att, g_up, g_down, g_tab


def per_device(
    sizes, block_input, segment_ids, out_grad, query_weight, key_weight, value_weight, output_weight,
    first_gain, first_shift, query_bias, value_bias, output_bias, second_gain, second_shift,
    up_weight, up_bias, down_weight, down_bias,
):
    nd, nx, ny = sizes
    n_dev = nd * nx * ny
    strips, length, width = block_input.shape
    units = up_weight.shape[1]
    att_rows, ff_rows = query_weight.shape[0], up_weight.shape[0]
    own = nd == 2 and nx == 4 and ny % 2 == 0 and att_rows % 8 == 0 and ff_rows % 8 == 0

    vecs = [first_gain, first_shift, query_bias, value_bias, output_bias, second_gain, second_shift, down_bias]
    n_vec = len(vecs)
    me = (lax.axis_index("dp") * nx + lax.axis_index("gx")) * ny + lax.axis_index("gy")
    n_tab = n_vec + up_bias.shape[0] * n_dev // width
    pieces = jnp.stack(vecs).astype(F32)
    lane = lax.broadcasted_iota(jnp.int32, (n_vec, width), 1) // att_rows
    top = jnp.where(lane == me, jnp.tile(pieces, (1, n_dev)), 0.0)
    flat = jnp.tile(up_bias.astype(F32), n_dev).reshape(n_tab - n_vec, width)
    index = lax.broadcasted_iota(jnp.int32, flat.shape, 0) * width + lax.broadcasted_iota(jnp.int32, flat.shape, 1)
    small = jnp.concatenate([top, jnp.where(index // up_bias.shape[0] == me, flat, 0.0)])
    rows_up = (n_tab + 7) // 8 * 8
    small = jnp.pad(small, ((0, rows_up - n_tab), (0, 0)))
    if own:
        y, x_grad, gq, gk, gv_, go, g_up, g_down, g_tab = own_path(
            sizes,
            (
                block_input, segment_ids, out_grad, query_weight, key_weight, value_weight, output_weight,
                small, up_weight, down_weight,
            ),
        )
        g_att = (gq, gk, gv_, go)
    else:
        table = lax.psum(small, ALL)
        y, x_grad, g_att, g_up, g_down, g_tab = wide_path(
            sizes,
            (
                block_input, segment_ids, out_grad, query_weight, key_weight, value_weight, output_weight,
                table, up_weight, down_weight,
            ),
        )
    mine = lax.dynamic_slice(g_tab, (0, me * att_rows), (n_vec, att_rows))
    g_bias = lax.dynamic_slice(
        g_tab[n_vec:n_tab].reshape(-1), (me * up_bias.shape[0],), (up_bias.shape[0],)
    )
    return (
        y, x_grad, *g_att, mine[G1], mine[S1], mine[QB], mine[VB], mine[OB], mine[G2], mine[S2],
        g_up, g_bias, g_down, mine[DB],
    )


def solution(mesh):
    rows, cols = P(ALL, None), P(ALL)
    cube = P(ALL, None, None)
    ff = P(("dp", "gy"), "gx")
    sizes = (mesh.shape["dp"], mesh.shape["gx"], mesh.shape["gy"])
    return jax.shard_map(
        functools.partial(per_device, sizes),
        mesh=mesh,
        in_specs=(cube, rows, cube) + (rows,) * 4 + (cols,) * 7 + (ff, cols, ff, cols),
        out_specs=(cube, cube) + (rows,) * 4 + (cols,) * 7 + (ff, cols, ff, cols),
        check_vma=False,
    )
```

```python
import functools
import math

import jax
import jax.numpy as jnp
from jax import lax
from jax.experimental import pallas as pl
from jax.experimental.pallas import tpu as pltpu
from jax.sharding import PartitionSpec as P

H = 12
HD = 64
BF = jnp.bfloat16
F32 = jnp.float32
ALL = ("dp", "gx", "gy")
MESH = pl.DeviceIdType.MESH
LOG2E = 1.4426950408889634
INV_SQRT2 = 0.7071067811865476
INV_SQRT_2PI = 0.3989422804014327
ANY = pl.BlockSpec(memory_space=pl.ANY)
VM = pl.BlockSpec(memory_space=pltpu.VMEM)
LIMIT = 61 << 20

G1, S1, QB, VB, OB, G2, S2, DB, UB0 = 0, 1, 2, 3, 4, 5, 6, 7, 8


def nn(a, b):
    return lax.dot_general(a, b, (((1,), (0,)), ((), ())), preferred_element_type=F32)


def nt(a, b):
    return lax.dot_general(a, b, (((1,), (1,)), ((), ())), preferred_element_type=F32)


def padded(length):
    return (length + 31) // 32 * 32


def row_pieces(length, step):
    return [(lo, min(step, length - lo)) for lo in range(0, length, step)]


def normalise(rows):
    centred = rows - jnp.mean(rows, axis=-1, keepdims=True)
    scale = lax.rsqrt(jnp.mean(centred * centred, axis=-1, keepdims=True) + 1e-06)
    return centred * scale, scale


def norm_back(grad, gain, xhat, scale):
    t = grad * gain
    return scale * (
        t
        - jnp.mean(t, axis=-1, keepdims=True)
        - xhat * jnp.mean(t * xhat, axis=-1, keepdims=True)
    )


def colsum(rows):
    return jnp.sum(rows, axis=0, keepdims=True)


def qkv_kernel(x_ref, w_ref, v_ref, qkv_ref, n_ref, bias_ref):
    strips, length, width = x_ref.shape
    lp = n_ref.shape[1]
    gain, shift = v_ref[G1 : G1 + 1, :], v_ref[S1 : S1 + 1, :]
    for s in range(strips):
        for lo, size in row_pieces(length, 136):
            xhat, _ = normalise(x_ref[s, lo : lo + size, :].astype(F32))
            n_ref[s, lo : lo + size, :] = (xhat * gain + shift).astype(BF)
        n_ref[s, length:lp, :] = jnp.zeros((lp - length, width), BF)
    bias_ref[0:1, 0:width] = v_ref[QB : QB + 1, :]
    bias_ref[0:1, width : 2 * width] = jnp.zeros((1, width), F32)
    bias_ref[0:1, 2 * width : 3 * width] = v_ref[VB : VB + 1, :]
    step = 256

    def body(i, carry):
        cols = pl.ds(pl.multiple_of(i * step, step), step)
        w = w_ref[:, cols]
        for s in range(strips):
            qkv_ref[s, :, cols] = (nn(n_ref[s], w) + bias_ref[0:1, cols]).astype(BF)
        return carry

    lax.fori_loop(0, 3 * width // step, body, 0)


def fill_bias(bias_ref, row, col):
    bias_ref[...] = jnp.where(row == col, 0.0, -1e30).astype(F32)


def attend_kernel(qkv_ref, sr_ref, sc_ref, o_ref, lse_ref, bias_ref):
    strips, lp, width = o_ref.shape
    qrows = lp // 2
    first = lax.broadcasted_iota(jnp.int32, (qrows, 128), 1) < HD
    lane = lax.broadcasted_iota(jnp.int32, (qrows, 128), 1)
    scale = 0.125 * LOG2E
    for s in range(strips):
        fill_bias(bias_ref, sc_ref[s], sr_ref[s])
        lse_ref[s] = jnp.zeros((lp, 128), F32)

        def body(p, carry):
            cq = pl.ds(pl.multiple_of(p * 128, 128), 128)
            ck = pl.ds(pl.multiple_of(width + p * 128, 128), 128)
            cv = pl.ds(pl.multiple_of(2 * width + p * 128, 128), 128)
            k, v = qkv_ref[s, :, ck], qkv_ref[s, :, cv]
            for part in range(2):
                rows = pl.ds(part * qrows, qrows)
                q = qkv_ref[s, rows, cq]
                lse = lse_ref[s, rows, :]
                res = []
                for j in range(2):
                    keep = first if j == 0 else jnp.logical_not(first)
                    z = nt(jnp.where(keep, q, jnp.zeros_like(q)), k) * scale + bias_ref[rows, :]
                    top = jnp.max(z, axis=-1, keepdims=True)
                    e = jnp.exp2(z - top)
                    total = jnp.sum(e, axis=-1, keepdims=True)
                    res.append(nn(e.astype(BF), v) / total)
                    lse = jnp.where(lane == 2 * p + j, top + jnp.log2(total), lse)
                o_ref[s, rows, cq] = jnp.where(first, res[0], res[1]).astype(BF)
                lse_ref[s, rows, :] = lse
            return carry

        lax.fori_loop(0, H // 2, body, 0)


def transpose_into(dst_ref, src_ref, lp):
    strips, _, width = src_ref.shape
    for s in range(strips):

        def body(i, carry):
            cols = pl.ds(pl.multiple_of(i * 128, 128), 128)
            dst_ref[s, cols, :] = src_ref[s, :, cols].astype(F32).T.astype(BF)
            return carry

        lax.fori_loop(0, width // 128, body, 0)


def ff_kernel(
    x_ref, mix_ref, dout_in_ref, wo_ref, up_ref, down_ref, v_ref,
    y_ref, rg_ref, mg_ref, gup_ref, gdown_ref, gwo_ref, gv_ref,
    dout_ref, doutT_ref, sec_ref, secT_ref, res_ref, acc_ref, sg_ref, hid_ref, pre_ref,
):
    strips, length, width = x_ref.shape
    lp = mix_ref.shape[1]
    groups = up_ref.shape[0]
    units = up_ref.shape[2]
    gv_ref[...] = jnp.zeros(gv_ref.shape, F32)
    bias_o, gain, shift = v_ref[OB : OB + 1, :], v_ref[G2 : G2 + 1, :], v_ref[S2 : S2 + 1, :]
    step = 256
    for s in range(strips):
        dout_ref[s, 0:length, :] = dout_in_ref[s]
        dout_ref[s, length:lp, :] = jnp.zeros((lp - length, width), BF)

        def proj(i, carry):
            cols = pl.ds(pl.multiple_of(i * step, step), step)
            acc_ref[s, :, cols] = nn(mix_ref[s], wo_ref[:, cols])
            return carry

        lax.fori_loop(0, width // step, proj, 0)
        for lo, size in row_pieces(length, 136):
            rows = pl.ds(lo, size)
            residual = x_ref[s, rows, :].astype(F32) + (acc_ref[s, rows, :] + bias_o)
            res_ref[s, rows, :] = residual
            xhat, _ = normalise(residual)
            sec_ref[s, rows, :] = (xhat * gain + shift).astype(BF)
            acc_ref[s, rows, :] = residual + v_ref[DB : DB + 1, :]
        sec_ref[s, length:lp, :] = jnp.zeros((lp - length, width), BF)
        res_ref[s, length:lp, :] = jnp.zeros((lp - length, width), F32)
        gv_ref[DB : DB + 1, :] += colsum(dout_in_ref[s].astype(F32))
    sg_ref[...] = jnp.zeros(sg_ref.shape, F32)
    transpose_into(doutT_ref, dout_ref, lp)
    transpose_into(secT_ref, sec_ref, lp)

    def group(gi, carry):
        def hidden(i, carry):
            cols = pl.ds(pl.multiple_of(i * step, step), step)
            up, down = up_ref[gi, :, cols], down_ref[gi, :, cols]
            ub = v_ref[pl.ds(UB0 + gi, 1), cols]
            total = jnp.zeros((1, step), F32)
            for s in range(strips):
                pre = nn(sec_ref[s], up) + ub
                hg = nn(dout_ref[s], down)
                cdf = 0.5 + 0.5 * lax.erf(pre * INV_SQRT2)
                pdf = jnp.exp(-0.5 * pre * pre) * INV_SQRT_2PI
                hid_ref[s, :, cols] = (pre * cdf).astype(BF)
                pg = (hg * (cdf + pre * pdf)).astype(BF)
                pre_ref[s, :, cols] = pg
                total = total + colsum(pg.astype(F32))
            gv_ref[pl.ds(UB0 + gi, 1), cols] = total
            return carry

        lax.fori_loop(0, units // step, hidden, 0)

        def back(i, carry):
            rows = pl.ds(pl.multiple_of(i * step, step), step)
            for s in range(strips):
                acc_ref[s, :, rows] += nt(hid_ref[s], down_ref[gi, rows, :])
                sg_ref[s, :, rows] += nt(pre_ref[s], up_ref[gi, rows, :])
            gd = nn(doutT_ref[0, rows, :], hid_ref[0])
            gu = nn(secT_ref[0, rows, :], pre_ref[0])
            for s in range(1, strips):
                gd = gd + nn(doutT_ref[s, rows, :], hid_ref[s])
                gu = gu + nn(secT_ref[s, rows, :], pre_ref[s])
            gdown_ref[gi, rows, :] = gd.astype(BF)
            gup_ref[gi, rows, :] = gu.astype(BF)
            return carry

        lax.fori_loop(0, width // step, back, 0)
        return carry

    lax.fori_loop(0, groups, group, 0)
    for s in range(strips):
        for lo, size in row_pieces(length, 136):
            rows = pl.ds(lo, size)
            y_ref[s, rows, :] = acc_ref[s, rows, :].astype(BF)
            xhat, scale = normalise(res_ref[s, rows, :])
            grad = sg_ref[s, rows, :]
            gv_ref[G2 : G2 + 1, :] += colsum(grad * xhat)
            gv_ref[S2 : S2 + 1, :] += colsum(grad)
            rg = dout_ref[s, rows, :].astype(F32) + norm_back(grad, gain, xhat, scale)
            rg_ref[s, rows, :] = rg
            low = rg.astype(BF)
            sec_ref[s, rows, :] = low
            gv_ref[OB : OB + 1, :] += colsum(low.astype(F32))
        sec_ref[s, length:lp, :] = jnp.zeros((lp - length, width), BF)
        rg_ref[s, length:lp, :] = jnp.zeros((lp - length, width), F32)
    transpose_into(secT_ref, mix_ref, lp)

    def last(i, carry):
        rows = pl.ds(pl.multiple_of(i * step, step), step)
        for s in range(strips):
            mg_ref[s, :, rows] = nt(sec_ref[s], wo_ref[rows, :]).astype(BF)
        gw = nn(secT_ref[0, rows, :], sec_ref[0])
        for s in range(1, strips):
            gw = gw + nn(secT_ref[s, rows, :], sec_ref[s])
        gwo_ref[rows, :] = gw.astype(BF)
        return carry

    lax.fori_loop(0, width // step, last, 0)


def attend_back_kernel(
    qkv_ref, mg_ref, mix_ref, lse_ref, sr_ref, sc_ref, dqkv_ref, bias_ref, lt_ref, dt_ref, kt_ref
):
    strips, lp, width = mg_ref.shape
    krows = lp // 2
    first = lax.broadcasted_iota(jnp.int32, (krows, 128), 1) < HD
    scale = 0.125 * LOG2E
    heads = lax.broadcasted_iota(jnp.int32, (16, width), 0)
    owner = lax.broadcasted_iota(jnp.int32, (16, width), 1) // HD
    pick = jnp.where(heads == owner, 1.0, 0.0).astype(BF)
    for s in range(strips):
        fill_bias(bias_ref, sc_ref[s], sr_ref[s])
        lt_ref[...] = lse_ref[s].T
        prod = mg_ref[s].astype(F32) * mix_ref[s].astype(F32)
        high = prod.astype(BF)
        rest = (prod - high.astype(F32)).astype(BF)
        dt_ref[...] = nt(pick, high) + nt(pick, rest)

        def body(p, carry):
            cq = pl.ds(pl.multiple_of(p * 128, 128), 128)
            ck = pl.ds(pl.multiple_of(width + p * 128, 128), 128)
            cv = pl.ds(pl.multiple_of(2 * width + p * 128, 128), 128)
            q, do = qkv_ref[s, :, cq], mg_ref[s, :, cq]
            kt_ref[...] = qkv_ref[s, :, ck].astype(F32).T.astype(BF)
            dq = [jnp.zeros((HD, lp), F32), jnp.zeros((HD, lp), F32)]
            for part in range(2):
                rows = pl.ds(part * krows, krows)
                k, v = qkv_ref[s, rows, ck], qkv_ref[s, rows, cv]
                dv, dk = [], []
                for j in range(2):
                    keep = first if j == 0 else jnp.logical_not(first)
                    lse = lt_ref[pl.ds(2 * p + j, 1), :]
                    delta = dt_ref[pl.ds(2 * p + j, 1), :]
                    z = nt(jnp.where(keep, k, jnp.zeros_like(k)), q) * scale + bias_ref[rows, :]
                    prob = jnp.exp2(z - lse)
                    pg = nt(jnp.where(keep, v, jnp.zeros_like(v)), do)
                    sg = (prob * (pg - delta)).astype(BF)
                    dv.append(nn(prob.astype(BF), do))
                    dk.append(nn(sg, q))
                    dq[j] = dq[j] + nn(kt_ref[j * HD : (j + 1) * HD, part * krows : (part + 1) * krows], sg)
                dqkv_ref[s, rows, cv] = jnp.where(first, dv[0], dv[1]).astype(BF)
                dqkv_ref[s, rows, ck] = (0.125 * jnp.where(first, dk[0], dk[1])).astype(BF)
            dqkv_ref[s, :, cq] = (0.125 * jnp.concatenate(dq, axis=0)).T.astype(BF)
            return carry

        lax.fori_loop(0, H // 2, body, 0)


def qkv_back_kernel(
    x_ref, n_ref, dqkv_ref, rg_ref, w_ref, v_ref, gx_ref, gw_ref, gv_ref, nT_ref, ng_ref
):
    strips, length, width = x_ref.shape
    lp = n_ref.shape[1]
    step = 256
    gv_ref[...] = jnp.zeros(gv_ref.shape, F32)
    gain = v_ref[G1 : G1 + 1, :]
    transpose_into(nT_ref, n_ref, lp)
    for s in range(strips):
        gv_ref[QB : QB + 1, :] += colsum(dqkv_ref[s, :, 0:width].astype(F32))
        gv_ref[VB : VB + 1, :] += colsum(dqkv_ref[s, :, 2 * width : 3 * width].astype(F32))

        def body(i, carry):
            rows = pl.ds(pl.multiple_of(i * step, step), step)
            ng_ref[s, :, rows] = nt(dqkv_ref[s], w_ref[rows, :])
            return carry

        lax.fori_loop(0, width // step, body, 0)

    def grads(i, carry):
        cols = pl.ds(pl.multiple_of(i * step, step), step)
        gw = nn(nT_ref[0], dqkv_ref[0, :, cols])
        for s in range(1, strips):
            gw = gw + nn(nT_ref[s], dqkv_ref[s, :, cols])
        gw_ref[:, cols] = gw.astype(BF)
        return carry

    lax.fori_loop(0, 3 * width // step, grads, 0)
    for s in range(strips):
        for lo, size in row_pieces(length, 136):
            rows = pl.ds(lo, size)
            xhat, scale = normalise(x_ref[s, rows, :].astype(F32))
            grad = ng_ref[s, rows, :]
            gv_ref[G1 : G1 + 1, :] += colsum(grad * xhat)
            gv_ref[S1 : S1 + 1, :] += colsum(grad)
            term = norm_back(grad, gain, xhat, scale)
            gx_ref[s, rows, :] = (rg_ref[s, rows, :] + term).astype(BF)


def call(kernel, outs, n_in, scratch=()):
    return pl.pallas_call(
        kernel,
        out_shape=outs,
        in_specs=[VM] * n_in,
        out_specs=[VM] * len(outs),
        scratch_shapes=list(scratch),
        compiler_params=pltpu.CompilerParams(vmem_limit_bytes=LIMIT),
    )


def sds(shape, dtype):
    return jax.ShapeDtypeStruct(shape, dtype)


def remote(src, dst, send, recv, dev):
    return pltpu.make_async_remote_copy(
        src_ref=src, dst_ref=dst, send_sem=send, recv_sem=recv, device_id=dev, device_id_type=MESH
    )


class Place:
    def __init__(self, ny):
        self.ny = ny
        self.d, x, self.g = lax.axis_index("dp"), lax.axis_index("gx"), lax.axis_index("gy")
        self.h, self.c = x // 2, x % 2
        self.z = [(self.d, x, lax.rem(self.g + k, ny)) for k in range(1, ny)]
        self.y = (self.d, (1 - self.h) * 2 + self.c, self.g)
        self.x = (1 - self.d, x, self.g)
        self.core = (self.d, self.h * 2 + 1 - self.c, self.g)
        h, c = (self.h, 1 - self.h), (self.c, 1 - self.c)
        every = [(d, hh * 2 + cc, self.g) for d in (self.d, 1 - self.d) for hh in h for cc in c]
        self.plane = every[1:]

    def greet(self):
        barrier = pltpu.get_barrier_semaphore()
        peers = self.z + self.plane
        for peer in peers:
            pl.semaphore_signal(barrier, inc=1, device_id=peer, device_id_type=MESH)
        pl.semaphore_wait(barrier, len(peers))


def stops(plan, **stages):
    steps = iter(plan)

    def stop():
        for token in next(steps):
            stages[token[0]](int(token[1:]))

    return stop


class Gather:
    def __init__(self, at, shards, views, sems):
        self.at, self.shards, self.views, self.n = at, shards, views, len(shards)
        self.loc, self.zsend, self.zrecv, self.bsend, self.brecv = sems
        self.zs, self.bs, self.fs, self.cs = {}, {}, {}, {}

    @staticmethod
    def semaphores(n, ny):
        return [pltpu.SemaphoreType.DMA(s) for s in ((n,), (n, ny - 1), (n, ny - 1), (n, 8), (n, 8))]

    def push(self, t, i, ref, dev):
        cp = remote(ref, ref, self.bsend.at[t, i], self.brecv.at[t, i], dev)
        cp.start()
        return cp

    def z(self, t):
        at = self.at
        own = self.views[t](at.d, at.h, at.c, at.g, 1)
        local = pltpu.make_async_copy(self.shards[t], own, self.loc.at[t])
        local.start()
        copies = []
        for k, dev in enumerate(at.z):
            cp = remote(self.shards[t], own, self.zsend.at[t, k], self.zrecv.at[t, k], dev)
            cp.start()
            copies.append(cp)
        self.zs[t] = local, copies

    def b(self, t):
        at = self.at
        self.zs[t][0].wait()
        for cp in self.zs[t][1]:
            cp.wait_recv()
        b = self.views[t](at.d, at.h, at.c, 0, at.ny)
        self.bs[t] = [self.push(t, i, b, dev) for i, dev in enumerate((at.y, at.x, at.core))]

    def f(self, t):
        at, view = self.at, self.views[t]
        half = at.ny // 2
        self.bs[t][0].wait_recv()
        f1 = self.push(t, 3, view(at.d, 1 - at.h, at.c, 0, half), at.x)
        c1 = self.push(t, 4, view(at.d, 1 - at.h, at.c, 0, at.ny), at.core)
        self.bs[t][1].wait_recv()
        f2 = self.push(t, 5, view(1 - at.d, at.h, at.c, half, at.ny - half), at.y)
        c2 = self.push(t, 6, view(1 - at.d, at.h, at.c, 0, at.ny), at.core)
        self.fs[t] = [f1, c1, f2, c2]

    def c(self, t):
        at = self.at
        self.fs[t][0].wait_recv()
        self.fs[t][2].wait_recv()
        self.cs[t] = self.push(t, 7, self.views[t](1 - at.d, 1 - at.h, at.c, 0, at.ny), at.core)

    def arrived(self, t):
        for cp in (self.bs[t][2], self.fs[t][1], self.fs[t][3], self.cs[t]):
            cp.wait_recv()

    def sent(self, t):
        for cp in self.zs[t][1] + self.bs[t] + self.fs[t] + [self.cs[t]]:
            cp.wait_send()


class Table:
    def __init__(self, at, total, landing, send, recv):
        self.at, self.total, self.landing, self.send, self.recv = at, total, landing, send, recv
        self.stages = [at.plane, at.z]
        self.flight, self.slot = [], 0

    @staticmethod
    def scratch(shape, ny, dtype):
        return [
            pltpu.VMEM((ny + 6,) + shape, dtype), pltpu.VMEM((2,) + shape, dtype),
            pltpu.SemaphoreType.DMA((ny + 6,)), pltpu.SemaphoreType.DMA((ny + 6,)),
        ]

    def step(self, k):
        if k > 0:
            value = self.total[k - 1].astype(F32)
            for cp, slot in self.flight[k - 1]:
                cp.wait_recv()
                value = value + self.landing[slot].astype(F32)
            if k < len(self.stages):
                self.total[k] = value.astype(self.total.dtype)
            else:
                self.result = value
                return
        copies = []
        for dev in self.stages[k]:
            slot = self.slot
            self.slot += 1
            cp = remote(self.total.at[k], self.landing.at[slot], self.send.at[slot], self.recv.at[slot], dev)
            cp.start()
            copies.append((cp, slot))
        self.flight.append(copies)

    def sent(self):
        for copies in self.flight:
            for cp, _ in copies:
                cp.wait_send()


class Scatter:
    def __init__(self, at, units, buffers, sems):
        self.at, self.units, self.n = at, units, len(units)
        self.bufs = buffers
        self.lsem, self.csend, self.crecv, self.bsend, self.brecv, self.zsend, self.zrecv = sems
        d, h = at.d, at.h
        self.quads = [(1 - d, 1 - h), (d, 1 - h), (1 - d, h), (d, h)]
        self.cs, self.fars, self.nears, self.zs = {}, {}, {}, {}

    @staticmethod
    def buffers(k, rows, cols, ny):
        return [
            pltpu.VMEM((lead, n * k, rows, cols), BF)
            for lead, n in ((4, ny), (4, ny), (2, ny // 2), (2, ny), (ny - 1, 1))
        ]

    @staticmethod
    def semaphores(n, ny):
        lead = (4, 4, 4, 4, 4, ny - 1, ny - 1)
        return [pltpu.SemaphoreType.DMA((n, k)) for k in lead]

    def add(self, dst, src, pieces):
        lead = dst.shape[0] // pieces

        def body(i, carry):
            part = pl.ds(i * lead, lead)
            dst[part] = (dst[part].astype(F32) + src[part].astype(F32)).astype(dst.dtype)
            return carry

        lax.fori_loop(0, pieces, body, 0)

    def core(self, t):
        view, (sums, rc) = self.units[t][0], self.bufs[t][:2]
        c = self.at.c
        res = []
        for q, (d, h) in enumerate(self.quads):
            cp = remote(
                view(d, h, 1 - c), rc.at[q], self.csend.at[t, q], self.crecv.at[t, q], self.at.core
            )
            cp.start()
            lc = pltpu.make_async_copy(view(d, h, c), sums.at[q], self.lsem.at[t, q])
            lc.start()
            res.append((cp, lc))
        self.cs[t] = res

    def far(self, t):
        sums, rc, rs = self.bufs[t][:3]
        ny, k = self.at.ny, self.units[t][1]
        cut = ny // 2 * k
        res = []
        for q in range(4):
            self.cs[t][q][0].wait_recv()
            self.cs[t][q][1].wait()
            self.add(sums.at[q], rc.at[q], ny)
            if q == 0:
                for i, (lo, dev) in enumerate(((0, self.at.x), (cut, self.at.y))):
                    cp = remote(
                        sums.at[0, lo : lo + cut], rs.at[i], self.bsend.at[t, i], self.brecv.at[t, i], dev
                    )
                    cp.start()
                    res.append(cp)
        self.fars[t] = res

    def near(self, t):
        sums, _, rs, rl = self.bufs[t][:4]
        ny, k = self.at.ny, self.units[t][1]
        cut = ny // 2 * k
        res = []
        for i, (lo, dev) in enumerate(((0, self.at.y), (cut, self.at.x))):
            self.fars[t][i].wait_recv()
            self.add(sums.at[1 + i, lo : lo + cut], rs.at[i], ny // 2)
            cp = remote(sums.at[1 + i], rl.at[i], self.bsend.at[t, 2 + i], self.brecv.at[t, 2 + i], dev)
            cp.start()
            res.append(cp)
        self.nears[t] = res

    def z(self, t):
        sums, rl, rz = self.bufs[t][0], self.bufs[t][3], self.bufs[t][4]
        at, n = self.at, self.units[t][1]
        for i in range(2):
            self.nears[t][i].wait_recv()
            self.add(sums.at[3], rl.at[i], at.ny)
        res = []
        for k, dev in enumerate(at.z):
            cp = remote(
                sums.at[3, pl.ds(dev[2] * n, n)], rz.at[k], self.zsend.at[t, k], self.zrecv.at[t, k], dev
            )
            cp.start()
            res.append(cp)
        self.zs[t] = res

    def finish(self, t):
        sums, rz = self.bufs[t][0], self.bufs[t][4]
        n = self.units[t][1]
        total = sums[3, pl.ds(self.at.g * n, n)].astype(F32)
        for k, cp in enumerate(self.zs[t]):
            cp.wait_recv()
            total = total + rz[k].astype(F32)
        self.units[t][2](total)

    def sent(self, t):
        for q in range(4):
            self.cs[t][q][0].wait_send()
        for cp in self.fars[t] + self.nears[t] + self.zs[t]:
            cp.wait_send()


GROUPS = ((0, 128), (128, 256), (384, 256), (640, 128))
NG = len(GROUPS)
PARTS = 3


def att_view(ref, tiles, sizes):
    nd, nh, ny = sizes

    def view(d, h, c, lo, n):
        return ref.at[pl.ds((((d * nh + h) * 2 + c) * ny + lo) * tiles, n * tiles)]

    return view


def ff_view(ref, part):
    def view(d, h, c, lo, n):
        start = pl.multiple_of((h * 2 + c) * part, part)
        return ref.at[d, pl.ds(lo, n), :, pl.ds(start, part)]

    return view


def copies_of(sem, *pairs):
    made = [pltpu.make_async_copy(a, b, sem.at[i]) for i, (a, b) in enumerate(pairs)]
    for cp in made:
        cp.start()
    return made


def columns_of(seg_row):
    return jnp.broadcast_to(seg_row, (128, seg_row.shape[1])).T[:, 0:1]


def turn(dst_ref, src_ref):
    total, width = src_ref.shape
    step = 256
    eye = jnp.where(
        lax.broadcasted_iota(jnp.int32, (step, step), 0) == lax.broadcasted_iota(jnp.int32, (step, step), 1), 1.0, 0.0
    ).astype(BF)
    for lo, size in row_pieces(total, step):
        for j in range(width // step):
            cols = slice(j * step, (j + 1) * step)
            dst_ref[cols, lo : lo + size] = nt(eye, src_ref[lo : lo + size, cols]).astype(BF)


def mask_into(bias_ref, segp_ref, s):
    row = segp_ref[s : s + 1, :]
    bias_ref[...] = jnp.where(columns_of(row) == row, 0.0, -1e30).astype(F32)


def segments_into(segp_ref, seg_ref):
    strips, length = seg_ref.shape
    segp_ref[...] = jnp.full(segp_ref.shape, -1.0, F32)
    segp_ref[0:strips, 0:length] = seg_ref[...].astype(F32)


def attend_pair(qkv_ref, o_ref, lse_ref, bias_ref, s, lp, base, gw, out_col):
    head = out_col // HD
    qrows = lp // 2
    lane = lax.broadcasted_iota(jnp.int32, (qrows, 128), 1)
    first = lane < HD
    scale = 0.125 * LOG2E
    off = s * lp
    k = qkv_ref[off : off + lp, base + gw : base + gw + 128]
    v = qkv_ref[off : off + lp, base + 2 * gw : base + 2 * gw + 128]
    for part in range(2):
        lo = part * qrows
        q = qkv_ref[off + lo : off + lo + qrows, base : base + 128]
        lse = lse_ref[s, lo : lo + qrows, :]
        res = []
        for j in range(2):
            keep = first if j == 0 else jnp.logical_not(first)
            z = nt(jnp.where(keep, q, jnp.zeros_like(q)), k) * scale + bias_ref[s, lo : lo + qrows, :]
            top = jnp.max(z, axis=-1, keepdims=True)
            e = jnp.exp2(z - top)
            total = jnp.sum(e, axis=-1, keepdims=True)
            res.append(nn(e.astype(BF), v) / total)
            lse = jnp.where(lane == head + j, top + jnp.log2(total), lse)
        o_ref[off + lo : off + lo + qrows, out_col : out_col + 128] = jnp.where(first, res[0], res[1]).astype(BF)
        lse_ref[s, lo : lo + qrows, :] = lse


def front_kernel(
    sizes, x_hbm, do_hbm, seg_ref, wq, wk, wv, wo, up, down, small_ref,
    lt_ref, table_ref, gsum_ref, qkv_out, mixed_out, nT_out, dout_out, doutT_out, watt_out, wo_out, up_out, down_out,
    x_ref, do_ref, xhat_ref, norm_ref, shard_ref, watt_ref, bias_row, lse_ref, bias_ref, segp_ref,
    qkv_ref, mixed_ref, nT_ref, dout_ref, doutT_ref,
    land_ref, tot_ref, tsend, trecv, lsem, osem, s_loc, s_zs, s_zr, s_bs, s_br, *land_w,
):
    nd, nh, ny = sizes
    strips, length, width = x_ref.shape
    lp = norm_ref.shape[0] // strips
    tiles = wq.shape[0]
    at = Place(ny)
    loads = [pltpu.make_async_copy(x_hbm, x_ref, lsem.at[0]), pltpu.make_async_copy(do_hbm, do_ref, lsem.at[1])]
    pieces = []
    for i, (first, gw) in enumerate(GROUPS):
        for j, w in enumerate((wq, wk, wv)):
            to = 3 * first + j * gw
            pieces.append(
                pltpu.make_async_copy(
                    w.at[:, :, first : first + gw], shard_ref.at[:, :, to : to + gw], lsem.at[2 + 3 * i + j]
                )
            )
    for cp in pieces + loads:
        cp.start()
    at.greet()
    tab = Table(at, tot_ref, land_ref, tsend, trecv)
    tot_ref[0] = small_ref[...].astype(BF)
    for cp in pieces:
        cp.wait()
    pw = up.shape[-1] // PARTS
    views = [att_view(land, tiles, sizes) for land in land_w] + [att_view(wo_out, tiles, sizes)]
    shards = [shard_ref.at[:, :, 3 * first : 3 * (first + gw)] for first, gw in GROUPS]
    shards += [wo, up.at[:, :, 0:pw], down.at[:, :, 0:pw]]
    views += [ff_view(up_out, pw), ff_view(down_out, pw)]
    gat = Gather(at, shards, views, (s_loc, s_zs, s_zr, s_bs, s_br))

    stop = stops(FRONT_PLAN, z=gat.z, b=gat.b, f=gat.f, c=gat.c, A=gat.arrived, t=tab.step)

    def hats(s):
        for lo, size in row_pieces(length, 136):
            xhat, _ = normalise(x_ref[s, lo : lo + size, :].astype(F32))
            xhat_ref[s * lp + lo : s * lp + lo + size, :] = xhat

    stop()
    for cp in loads:
        cp.wait()
    hats(0)
    stop()
    for s in range(1, strips):
        hats(s)
    stop()
    segments_into(segp_ref, seg_ref)
    for s in range(strips):
        mask_into(bias_ref.at[s], segp_ref, s)
    lse_ref[...] = jnp.zeros(lse_ref.shape, F32)
    stop()
    gsum = jnp.zeros((1, width), F32)
    for s in range(strips):
        dout_ref[s * lp : s * lp + length, :] = do_ref[s]
        dout_ref[s * lp + length : (s + 1) * lp, :] = jnp.zeros((lp - length, width), BF)
        gsum = gsum + colsum(do_ref[s].astype(F32))
    gsum_ref[...] = jnp.broadcast_to(gsum, gsum_ref.shape)
    stop()
    turn(doutT_ref, dout_ref)
    outs = copies_of(osem, (dout_ref, dout_out), (doutT_ref, doutT_out))
    stop()
    table = tab.result
    table_ref[...] = table
    gain, shift = table[G1 : G1 + 1, :], table[S1 : S1 + 1, :]
    for s in range(strips):
        for lo, size in row_pieces(length, 136):
            part = slice(s * lp + lo, s * lp + lo + size)
            norm_ref[part, :] = (xhat_ref[part, :] * gain + shift).astype(BF)
        norm_ref[s * lp + length : (s + 1) * lp, :] = jnp.zeros((lp - length, width), BF)
    for first, gw in GROUPS:
        cols = slice(first, first + gw)
        bias_row[0:1, 3 * first : 3 * first + gw] = table[QB : QB + 1, cols]
        bias_row[0:1, 3 * first + gw : 3 * first + 2 * gw] = jnp.zeros((1, gw), F32)
        bias_row[0:1, 3 * first + 2 * gw : 3 * (first + gw)] = table[VB : VB + 1, cols]
    for i, (first, gw) in enumerate(GROUPS):
        stop()
        wide = slice(3 * first, 3 * (first + gw))

        def settle(n, carry):
            rows = pl.ds(pl.multiple_of(n * 64, 64), 64)
            watt_ref[rows, wide] = land_w[i][pl.ds(n * 8, 8)].astype(F32).reshape(64, 3 * gw).astype(BF)
            return carry

        lax.fori_loop(0, width // 64, settle, 0)

        def project(n, carry):
            cols = pl.ds(pl.multiple_of(3 * first + n * gw, 128), gw)
            qkv_ref[:, cols] = (nn(norm_ref[...], watt_ref[:, cols]) + bias_row[0:1, cols]).astype(BF)
            return carry

        lax.fori_loop(0, 3, project, 0)
        outs += copies_of(
            osem.at[2 + 2 * i : 4 + 2 * i],
            (qkv_ref.at[:, wide], qkv_out.at[:, wide]), (watt_ref.at[:, wide], watt_out.at[:, wide]),
        )
        for s in range(strips):
            for p in range(gw // 128):
                stop()
                attend_pair(
                    qkv_ref, mixed_ref, lse_ref, bias_ref, s, lp, 3 * first + p * 128, gw, first + p * 128
                )
        if i == 0:
            stop()
            turn(nT_ref, norm_ref)
            outs += copies_of(osem.at[2 + 2 * NG : 3 + 2 * NG], (nT_ref, nT_out))
    stop()
    outs += copies_of(osem.at[3 + 2 * NG :], (mixed_ref, mixed_out))
    for s in range(strips):
        lt_ref[s] = lse_ref[s].T[0:16, :]
    stop()
    for t in range(gat.n):
        gat.sent(t)
    tab.sent()
    for cp in outs:
        cp.wait()


FRONT_PLAN = (
    ("z0", "z2"), ("t0",), ("z1", "t1", "z3", "b0"), ("b2", "z6", "f0"), ("b1", "t2"), ("b3", "z5", "c0"),
    ("A0", "f1"), ("f2", "f3"), ("z4",), ("b6", "c1"),
    ("A1",), ("b5", "c3"), (), ("b4",), ("c2", "f6"),
    ("A2",), ("A3",), ("f5",), (), (),
    ("f4",), ("c6",), ("c5", "A6"), ("A5", "c4"), ("A4",),
)


MIDDLE_PLAN = (
    ("z0",), ("z1",), (), ("z3",),
    ("b0", "z2"), ("b1",), ("f0",), ("f1", "c0", "b3", "K0"), ("b2",),
    ("c1", "A0", "F0", "A1"), ("K1",), ("f3", "f2"), ("F1", "N0"), ("c3", "c2"),
    ("A2", "A3"), ("N1",), ("Z0",), (), ("Z1",),
    (), (), ("E0",), ("E1",),
)


def middle_kernel(
    sizes, x_ref, mix_ref, wo_ref, v_ref, gsum_ref, dout_hbm, doutT_hbm, u0, d0, up, down,
    mg_ref, gwo_ref, gv_ref, gu_ref, gd_ref, y_out, rg_out, *out_parts_and_scratch,
):
    middle_body(
        sizes, x_ref, mix_ref, wo_ref, v_ref, gsum_ref, dout_hbm, doutT_hbm, u0, d0, up, down,
        mg_ref, gwo_ref, gv_ref, gu_ref, gd_ref, y_out, rg_out,
        out_parts_and_scratch[: 2 * (PARTS - 1)], *out_parts_and_scratch[2 * (PARTS - 1) :],
    )


def middle_body(
    sizes, x_ref, mix_ref, wo_ref, v_ref, gsum_ref, dout_hbm, doutT_hbm, u0, d0, up, down,
    mg_ref, gwo_ref, gv_ref, gu_ref, gd_ref, y_out, rg_out, later,
    dout_ref, doutT_ref, sec_ref, secT_ref, res_ref, acc_ref, rg_ref, hid_ref, pre_ref, y_ref, wu, wd, pu, pd,
    lsem, osem, s_loc, s_zs, s_zr, s_bs, s_br, *rest,
):
    nd, nh, ny = sizes
    nq = nh * 2
    strips, length, width = x_ref.shape
    lp = mix_ref.shape[0] // strips
    rows, part = up.shape[1], up.shape[2] // PARTS
    at = Place(ny)
    loads = copies_of(lsem, (dout_hbm, dout_ref), (doutT_hbm, doutT_ref), (u0, wu.at[0]), (d0, wd.at[0]))
    at.greet()
    n_sc = 2
    shards, views, units = [], [], []
    for b in range(1, PARTS):
        cols = slice(b * part, (b + 1) * part)
        shards += [up.at[:, :, cols], down.at[:, :, cols]]
        views += [ff_view(wu.at[b], part), ff_view(wd.at[b], part)]
    for src, dst in ((pu, gu_ref), (pd, gd_ref)):

        def put(total, dst=dst):
            dst[...] = total[0]

        whole = ff_view(src, part)
        units.append(((lambda d, h, c, whole=whole: whole(d, h, c, 0, ny)), 1, put))
    gat = Gather(at, shards, views, (s_loc, s_zs, s_zr, s_bs, s_br))
    sca = Scatter(at, units, [rest[5 * t : 5 * t + 5] for t in range(n_sc)], rest[5 * n_sc :])
    stop = stops(
        MIDDLE_PLAN, z=gat.z, b=gat.b, f=gat.f, c=gat.c, A=gat.arrived,
        K=sca.core, F=sca.far, N=sca.near, Z=sca.z, E=sca.finish,
    )
    stop()

    step = 256
    bias_o, gain, shift = v_ref[OB : OB + 1, :], v_ref[G2 : G2 + 1, :], v_ref[S2 : S2 + 1, :]
    gv_ref[...] = jnp.zeros(gv_ref.shape, F32)
    gv_ref[DB : DB + 1, :] = gsum_ref[0:1, :]

    def proj(i, carry):
        cols = pl.ds(pl.multiple_of(i * step, step), step)
        acc_ref[:, cols] = nn(mix_ref[...], wo_ref[:, cols])
        return carry

    lax.fori_loop(0, width // step, proj, 0)
    for s in range(strips):
        stop()
        for lo, size in row_pieces(length, 136):
            sel = slice(s * lp + lo, s * lp + lo + size)
            residual = x_ref[s, lo : lo + size, :].astype(F32) + (acc_ref[sel, :] + bias_o)
            res_ref[sel, :] = residual
            xhat, _ = normalise(residual)
            sec_ref[sel, :] = (xhat * gain + shift).astype(BF)
            acc_ref[sel, :] = residual + v_ref[DB : DB + 1, :]
        sec_ref[s * lp + length : (s + 1) * lp, :] = jnp.zeros((lp - length, width), BF)
    stop()
    turn(secT_ref, sec_ref)
    for cp in loads:
        cp.wait()

    outs = []
    for b in range(PARTS):

        def hidden(q, carry):
            cols = pl.ds(pl.multiple_of(q * part, part), part)
            w_up = wu[b, :, :, :, cols].reshape(width, part)
            w_down = wd[b, :, :, :, cols].reshape(width, part)
            pre = nn(sec_ref[...], w_up) + v_ref[pl.ds(UB0 + q, 1), b * part : (b + 1) * part]
            hg = nn(dout_ref[...], w_down)
            cdf = 0.5 + 0.5 * lax.erf(pre * INV_SQRT2)
            pdf = jnp.exp(-0.5 * pre * pre) * INV_SQRT_2PI
            hid_ref[:, cols] = (pre * cdf).astype(BF)
            pg = (hg * (cdf + pre * pdf)).astype(BF)
            pre_ref[:, cols] = pg
            gv_ref[pl.ds(UB0 + q, 1), b * part : (b + 1) * part] = colsum(pg.astype(F32))
            return carry

        g_up, g_down = (pu, pd) if b == 0 else (wu.at[b - 1], wd.at[b - 1])

        def grads(q, carry):
            cols = pl.ds(pl.multiple_of(q * part, part), part)
            shape = (nd, ny, rows, part)
            g_down[:, :, :, cols] = nn(doutT_ref[...], hid_ref[:, cols]).astype(BF).reshape(shape)
            g_up[:, :, :, cols] = nn(secT_ref[...], pre_ref[:, cols]).astype(BF).reshape(shape)
            return carry

        stop()
        lax.fori_loop(0, nq // 2, hidden, 0)
        stop()
        lax.fori_loop(nq // 2, nq, hidden, 0)
        stop()
        if b > 1:
            gat.sent(2 * b - 4)
            gat.sent(2 * b - 3)
        lax.fori_loop(0, nq, grads, 0)
        if b > 0:
            outs += copies_of(
                osem.at[2 * b : 2 * b + 2], (g_up, later[2 * b - 2]), (g_down, later[2 * b - 1])
            )
        stop()
        w_down = wd[b].reshape(width, nq * part)
        for n in range(width // step):
            cols = slice(n * step, (n + 1) * step)
            acc_ref[:, cols] += nt(hid_ref[...], w_down[cols, :])
        stop()
        w_up = wu[b].reshape(width, nq * part)
        for n in range(width // step):
            cols = slice(n * step, (n + 1) * step)
            value = nt(pre_ref[...], w_up[cols, :])
            rg_ref[:, cols] = value if b == 0 else rg_ref[:, cols] + value

    for s in range(strips):
        stop()
        for lo, size in row_pieces(length, 136):
            sel = slice(s * lp + lo, s * lp + lo + size)
            y_ref[lo : lo + size, s, :] = acc_ref[sel, :].astype(BF)
            xhat, scale = normalise(res_ref[sel, :])
            grad = rg_ref[sel, :]
            gv_ref[G2 : G2 + 1, :] += colsum(grad * xhat)
            gv_ref[S2 : S2 + 1, :] += colsum(grad)
            rg = dout_ref[sel, :].astype(F32) + norm_back(grad, gain, xhat, scale)
            rg_ref[sel, :] = rg
            low = rg.astype(BF)
            sec_ref[sel, :] = low
            gv_ref[OB : OB + 1, :] += colsum(low.astype(F32))
        tail = slice(s * lp + length, (s + 1) * lp)
        sec_ref[tail, :] = jnp.zeros((lp - length, width), BF)
        rg_ref[tail, :] = jnp.zeros((lp - length, width), F32)
    outs += copies_of(osem.at[0:2], (rg_ref, rg_out), (y_ref, y_out))
    turn(secT_ref, mix_ref)
    stop()

    def last(i, carry):
        sel = pl.ds(pl.multiple_of(i * step, step), step)
        mg_ref[:, sel] = nt(sec_ref[...], wo_ref[sel, :]).astype(BF)
        gwo_ref[sel, :] = nn(secT_ref[sel, :], sec_ref[...]).astype(BF)
        return carry

    lax.fori_loop(0, width // step, last, 0)
    stop()
    for t in range(2 * (PARTS - 2), gat.n):
        gat.sent(t)
    for t in range(n_sc):
        sca.sent(t)
    for cp in outs:
        cp.wait()


def attend_back_pair(
    qkv_ref, mg_ref, dz_ref, bias_ref, lt_ref, dt_ref, kt_ref, s, lp, base, gw, out_col, dst
):
    head = out_col // HD
    krows = lp // 2
    first = lax.broadcasted_iota(jnp.int32, (krows, 128), 1) < HD
    scale = 0.125 * LOG2E
    off = s * lp
    q = qkv_ref[off : off + lp, base : base + 128]
    do = mg_ref[off : off + lp, out_col : out_col + 128]
    kt_ref[...] = qkv_ref[off : off + lp, base + gw : base + gw + 128].astype(F32).T.astype(BF)
    dq = [jnp.zeros((HD, lp), F32), jnp.zeros((HD, lp), F32)]
    for part in range(2):
        lo = off + part * krows
        k = qkv_ref[lo : lo + krows, base + gw : base + gw + 128]
        v = qkv_ref[lo : lo + krows, base + 2 * gw : base + 2 * gw + 128]
        dv, dk = [], []
        for j in range(2):
            keep = first if j == 0 else jnp.logical_not(first)
            lse = lt_ref[s, head + j : head + j + 1, :]
            delta = dt_ref[s, head + j : head + j + 1, :]
            mask = bias_ref[s, part * krows : (part + 1) * krows, :]
            z = nt(jnp.where(keep, k, jnp.zeros_like(k)), q) * scale + mask
            prob = jnp.exp2(z - lse)
            pg = nt(jnp.where(keep, v, jnp.zeros_like(v)), do)
            sg = (prob * (pg - delta)).astype(BF)
            dv.append(nn(prob.astype(BF), do))
            dk.append(nn(sg, q))
            dq[j] = dq[j] + nn(kt_ref[j * HD : (j + 1) * HD, part * krows : (part + 1) * krows], sg)
        dz_ref[lo : lo + krows, dst + 2 * gw : dst + 2 * gw + 128] = jnp.where(first, dv[0], dv[1]).astype(BF)
        dz_ref[lo : lo + krows, dst + gw : dst + gw + 128] = (0.125 * jnp.where(first, dk[0], dk[1])).astype(BF)
    dz_ref[off : off + lp, dst : dst + 128] = (0.125 * jnp.concatenate(dq, axis=0)).T.astype(BF)


BACK_PLAN = (
    ("K0", "K1"), ("K7", "F0"),
    ("t0", "F1", "K8", "F7"), ("N0",), (), ("K3", "K2"),
    (), ("N7", "F2"), ("F3",), ("F8", "N1"), ("Z7",), (),
    ("N2", "Z0"), (), ("K4", "N8"), ("Z1",), (), ("K5", "F4", "N3", "t1", "Z2"),
    ("F5",), ("N4", "Z8"), ("N5",), ("K6", "Z3"),
    ("F6", "E7", "Z4"), (), ("u0", "Z5", "N6", "E0", "u1", "Z6"), ("E1", "E4", "E2", "t2", "E5", "E3", "E8", "u2", "E6"),
)


def back_kernel(
    sizes, gu1, gd1, gu2, gd2, gwo, seg_ref, lt_ref, v_ref, gvm_ref, gu0_ref, gd0_ref,
    mg_hbm, mix_hbm, qkv_hbm, nT_hbm, watt_hbm, x_hbm, rg_hbm,
    gx_ref, gq_ref, gk_ref, gv_ref, go_ref, gu_ref, gd_ref, gtab_ref,
    mg_ref, mix_ref, qkv_ref, nT_ref, watt_ref, x_ref, rg_ref,
    dz_ref, ng_ref, bias_ref, segp_ref, dt_ref, kt_ref, tab_ref,
    land_ref, tot_ref, tsend, trecv, land2_ref, tot2_ref, tsend2, trecv2, isem,
    *rest,
):
    nd, nh, ny = sizes
    strips, length, width = x_ref.shape
    lp = qkv_ref.shape[0] // strips
    parts, rest = rest[:NG], rest[NG:]
    loads = copies_of(
        isem, (mg_hbm, mg_ref), (mix_hbm, mix_ref),
        *[
            (qkv_hbm.at[:, 3 * first : 3 * (first + gw)], qkv_ref.at[:, 3 * first : 3 * (first + gw)])
            for first, gw in GROUPS
        ],
        (nT_hbm, nT_ref), (watt_hbm, watt_ref), (x_hbm, x_ref), (rg_hbm, rg_ref),
    )
    at = Place(ny)
    at.greet()
    n = 5 + NG
    bufs = [rest[5 * t : 5 * t + 5] for t in range(n)]
    sems = rest[5 * n :]
    pw = gu1.shape[-1] // (2 * nh)
    units = []

    def ff_unit(src, dst, cols):
        whole = ff_view(src, pw)

        def put(total):
            dst[:, cols] = total[0]

        return lambda d, h, c: whole(d, h, c, 0, ny), 1, put

    one, two = slice(pw, 2 * pw), slice(2 * pw, 3 * pw)
    units += [ff_unit(gu2, gu_ref, two), ff_unit(gd2, gd_ref, two)]
    tiles = gq_ref.shape[0] // 8

    def att_unit(src, put):
        inner = att_view(src, tiles, sizes)
        return lambda d, h, c: inner(d, h, c, 0, ny), tiles, put

    def put_out(total):
        go_ref[...] = total.reshape(go_ref.shape)

    units.append(att_unit(gwo, put_out))
    for i, (first, gw) in enumerate(GROUPS):

        def put_group(total, first=first, gw=gw):
            for j, ref in enumerate((gq_ref, gk_ref, gv_ref)):
                ref[:, first : first + gw] = total[:, :, j * gw : (j + 1) * gw].reshape(-1, gw)

        units.append(att_unit(parts[i], put_group))
    units += [ff_unit(gu1, gu_ref, one), ff_unit(gd1, gd_ref, one)]
    sca = Scatter(at, units, bufs, sems)
    early = Table(at, tot_ref, land_ref, tsend, trecv)
    late = Table(at, tot2_ref, land2_ref, tsend2, trecv2)
    stop = stops(
        BACK_PLAN, K=sca.core, F=sca.far, N=sca.near, Z=sca.z, E=sca.finish, t=early.step, u=late.step
    )
    stop()
    gu_ref[:, 0:pw] = gu0_ref[...]
    gd_ref[:, 0:pw] = gd0_ref[...]
    tot_ref[0] = jnp.concatenate([gvm_ref[OB : DB + 1, :], gvm_ref[UB0 : UB0 + 4, :]]).astype(BF)
    segments_into(segp_ref, seg_ref)
    heads = lax.broadcasted_iota(jnp.int32, (16, width), 0)
    pick = jnp.where(heads == lax.broadcasted_iota(jnp.int32, (16, width), 1) // HD, 1.0, 0.0).astype(BF)
    for s in range(strips):
        mask_into(bias_ref.at[s], segp_ref, s)
    loads[0].wait()
    loads[1].wait()
    stop()
    for s in range(strips):
        part = slice(s * lp, (s + 1) * lp)
        prod = mg_ref[part, :].astype(F32) * mix_ref[part, :].astype(F32)
        high = prod.astype(BF)
        dt_ref[s] = nt(pick, high) + nt(pick, (prod - high.astype(F32)).astype(BF))
    for i, (first, gw) in enumerate(GROUPS):
        loads[2 + i].wait()
        for s in range(strips):
            for p in range(gw // 128):
                stop()
                attend_back_pair(
                    qkv_ref, mg_ref, dz_ref, bias_ref, lt_ref, dt_ref, kt_ref, s, lp,
                    3 * first + p * 128, gw, first + p * 128, p * 128,
                )
        cols = slice(first, first + gw)
        tab_ref[QB : QB + 1, cols] = colsum(dz_ref[:, 0:gw].astype(F32))
        tab_ref[VB : VB + 1, cols] = colsum(dz_ref[:, 2 * gw : 3 * gw].astype(F32))
        if i == 0:
            loads[2 + NG].wait()
            loads[3 + NG].wait()

        def grads(j, carry):
            c = pl.ds(pl.multiple_of(j * gw, gw), gw)
            parts[i][:, :, c] = nn(nT_ref[...], dz_ref[:, c]).reshape(width // 8, 8, gw).astype(BF)
            return carry

        stop()
        lax.fori_loop(0, 3, grads, 0)
        stop()

        def to_norm(j, carry):
            c = pl.ds(pl.multiple_of(j * 256, 256), 256)
            value = nt(dz_ref[:, 0 : 3 * gw], watt_ref[c, 3 * first : 3 * (first + gw)])
            ng_ref[:, c] = value if i == 0 else ng_ref[:, c] + value
            return carry

        lax.fori_loop(0, width // 256, to_norm, 0)
    gain = v_ref[G1 : G1 + 1, :]
    loads[4 + NG].wait()
    loads[5 + NG].wait()
    g_gain, g_shift = jnp.zeros((1, width), F32), jnp.zeros((1, width), F32)
    for s in range(strips):
        stop()
        for lo, size in row_pieces(length, 136):
            part = slice(s * lp + lo, s * lp + lo + size)
            xhat, scale = normalise(x_ref[s, lo : lo + size, :].astype(F32))
            grad = ng_ref[part, :]
            g_gain = g_gain + colsum(grad * xhat)
            g_shift = g_shift + colsum(grad)
            term = norm_back(grad, gain, xhat, scale)
            gx_ref[lo : lo + size, s, :] = (rg_ref[part, :] + term).astype(BF)
    tot2_ref[0] = jnp.concatenate(
        [g_gain, g_shift, tab_ref[QB : VB + 1, :], jnp.zeros((4, width), F32)]
    ).astype(BF)
    stop()
    stop()
    sums, ends = early.result, late.result
    gtab_ref[G1 : VB + 1, :] = ends[0:4]
    gtab_ref[OB : DB + 1, :] = sums[0:4]
    gtab_ref[UB0 : UB0 + 4, :] = sums[4:8]
    gtab_ref[UB0 + 4 :, :] = jnp.zeros((gtab_ref.shape[0] - UB0 - 4, width), F32)
    for t in range(n):
        sca.sent(t)
    early.sent()
    late.sent()


def own_path(sizes, args):
    (
        block_input, segment_ids, out_grad, query_weight, key_weight, value_weight, output_weight, small,
        up_weight, down_weight,
    ) = args
    nd, nx, ny = sizes
    nh = nx // 2
    grid3 = (nd, nh, ny)
    strips, length, width = block_input.shape
    units = up_weight.shape[1]
    att_rows, ff_rows = query_weight.shape[0], up_weight.shape[0]
    lp = padded(length)
    tiles = att_rows // 8
    part = units // PARTS
    total = strips * lp
    full, wide, turned = (total, width), (total, 3 * width), (width, total)
    n_tab = small.shape[0]
    ff_shape = (nd, ny, ff_rows, nx * part)
    x_shape = block_input.shape
    t_shape = (length, strips, width)
    watt_shape = (width, 3 * width)
    lt_shape = (strips, 16, lp)
    dma = pltpu.SemaphoreType.DMA
    ups, downs = up_weight[None], down_weight[None]
    (
        lt, table, gsum, qkv, mixed, nT, dout, doutT, watt, wo, u0, d0,
    ) = pl.pallas_call(
        functools.partial(front_kernel, grid3),
        out_shape=[
            sds(lt_shape, F32), sds((n_tab, width), F32), sds((8, width), F32), sds(wide, BF), sds(full, BF),
            sds(turned, BF), sds(full, BF), sds(turned, BF), sds(watt_shape, BF), sds((width // 8, 8, width), BF),
            sds(ff_shape, BF), sds(ff_shape, BF),
        ],
        in_specs=[ANY, ANY, VM] + [ANY] * 6 + [VM],
        out_specs=[VM] * 3 + [ANY] * 9,
        scratch_shapes=[
            pltpu.VMEM(x_shape, BF), pltpu.VMEM(x_shape, BF), pltpu.VMEM(full, F32), pltpu.VMEM(full, BF),
            pltpu.VMEM((tiles, 8, 3 * width), BF), pltpu.VMEM(watt_shape, BF), pltpu.VMEM((8, 3 * width), F32), pltpu.VMEM((strips, lp, 128), F32),
            pltpu.VMEM((strips, lp, lp), F32), pltpu.VMEM((8, lp), F32),
            pltpu.VMEM(wide, BF), pltpu.VMEM(full, BF), pltpu.VMEM(turned, BF), pltpu.VMEM(full, BF),
            pltpu.VMEM(turned, BF),
        ]
        + Table.scratch((n_tab, width), ny, BF)
        + [dma((2 + 3 * NG,)), dma((4 + 2 * NG,))]
        + Gather.semaphores(NG + 3, ny)
        + [pltpu.VMEM((width // 8, 8, 3 * gw), BF) for _, gw in GROUPS],
        compiler_params=pltpu.CompilerParams(collective_id=0, has_side_effects=True, vmem_limit_bytes=LIMIT),
    )(
        block_input, out_grad, segment_ids,
        *(w.reshape(tiles, 8, width) for w in (query_weight, key_weight, value_weight, output_weight)),
        ups, downs, small,
    )

    n_sc, n_later = 2, 2 * (PARTS - 1)
    some = (ff_rows, part)
    buffers = []
    for _ in range(n_sc):
        buffers += Scatter.buffers(1, ff_rows, part, ny)
    mg, gwo, gvm, gu0, gd0, y, rg, gu1, gd1, gu2, gd2 = pl.pallas_call(
        functools.partial(middle_kernel, grid3),
        out_shape=[
            sds(full, BF), sds((width, width), BF), sds((n_tab, width), F32), sds(some, F32), sds(some, F32),
            sds(t_shape, BF), sds(full, F32),
        ]
        + [sds(ff_shape, BF)] * n_later,
        in_specs=[VM] * 5 + [ANY] * 6,
        out_specs=[VM] * 5 + [ANY] * (2 + n_later),
        scratch_shapes=[
            pltpu.VMEM(full, BF), pltpu.VMEM(turned, BF), pltpu.VMEM(full, BF), pltpu.VMEM(turned, BF),
            pltpu.VMEM(full, F32), pltpu.VMEM(full, F32), pltpu.VMEM(full, F32),
            pltpu.VMEM((total, nx * part), BF), pltpu.VMEM((total, nx * part), BF), pltpu.VMEM(t_shape, BF),
        ]
        + [pltpu.VMEM((PARTS,) + ff_shape, BF)] * 2
        + [pltpu.VMEM(ff_shape, BF)] * 2
        + [dma((4,)), dma((2 + n_later,))]
        + Gather.semaphores(n_later, ny)
        + buffers
        + Scatter.semaphores(n_sc, ny),
        compiler_params=pltpu.CompilerParams(collective_id=1, has_side_effects=True, vmem_limit_bytes=LIMIT),
    )(block_input, mixed, wo.reshape(width, width), table, gsum, dout, doutT, u0, d0, ups, downs)

    n_units = 5 + NG
    buffers = []
    for _ in range(2):
        buffers += Scatter.buffers(1, ff_rows, part, ny)
    for cols in [width] + [3 * gw for _, gw in GROUPS]:
        buffers += Scatter.buffers(tiles, 8, cols, ny)
    for _ in range(2):
        buffers += Scatter.buffers(1, ff_rows, part, ny)
    gx, gq, gk, gv, go, gu, gd, gtab = pl.pallas_call(
        functools.partial(back_kernel, grid3),
        out_shape=[sds(t_shape, BF)] + [sds((att_rows, width), F32)] * 4 + [sds((ff_rows, units), F32)] * 2
        + [sds((n_tab, width), F32)],
        in_specs=[ANY] * 5 + [VM] * 6 + [ANY] * 7,
        out_specs=[VM] * 8,
        scratch_shapes=[
            pltpu.VMEM(full, BF), pltpu.VMEM(full, BF), pltpu.VMEM(wide, BF), pltpu.VMEM(turned, BF),
            pltpu.VMEM(watt_shape, BF), pltpu.VMEM(x_shape, BF), pltpu.VMEM(full, F32),
            pltpu.VMEM(full, BF), pltpu.VMEM(full, F32), pltpu.VMEM((strips, lp, lp), F32), pltpu.VMEM((8, lp), F32), pltpu.VMEM(lt_shape, F32),
            pltpu.VMEM((128, lp), BF), pltpu.VMEM((n_tab, width), F32),
        ]
        + Table.scratch((8, width), ny, BF)
        + Table.scratch((8, width), ny, BF)
        + [dma((6 + NG,))]
        + [pltpu.VMEM((width // 8, 8, 3 * gw), BF) for _, gw in GROUPS]
        + buffers
        + Scatter.semaphores(n_units, ny),
        compiler_params=pltpu.CompilerParams(collective_id=2, has_side_effects=True, vmem_limit_bytes=LIMIT),
    )(
        gu1, gd1, gu2, gd2, gwo.reshape(width // 8, 8, width), segment_ids, lt, table, gvm, gu0, gd0,
        mg, mixed, qkv, nT, watt, block_input, rg,
    )
    return y.transpose(1, 0, 2), gx.transpose(1, 0, 2), gq, gk, gv, go, gu, gd, gtab


def wide_path(sizes, args):
    (
        block_input, segment_ids, out_grad, query_weight, key_weight, value_weight, output_weight, table,
        up_weight, down_weight,
    ) = args
    nd, nx, ny = sizes
    strips, length, width = block_input.shape
    units = up_weight.shape[1]
    lp = padded(length)
    att = jnp.concatenate([query_weight, key_weight, value_weight, output_weight], axis=1)
    att = lax.all_gather(att, ALL, axis=0, tiled=True)
    up, down = (
        lax.all_gather(lax.all_gather(a, ("dp", "gy"), axis=0, tiled=True), "gx", axis=0)
        for a in (up_weight, down_weight)
    )
    w_qkv, w_out = att[:, : 3 * width], att[:, 3 * width :]
    seg = jnp.pad(segment_ids, ((0, 0), (0, lp - length)), constant_values=-1)
    seg_row, seg_col = seg[:, None, :], seg[:, :, None]
    full = (strips, lp, width)
    wide = (strips, lp, 3 * width)
    turned = (strips, width, lp)
    qkv, normed = call(
        qkv_kernel, [sds(wide, BF), sds(full, BF)], 3, [pltpu.VMEM((8, 3 * width), F32)]
    )(block_input, w_qkv, table)
    mixed, lse = call(
        attend_kernel, [sds(full, BF), sds((strips, lp, 128), F32)], 3, [pltpu.VMEM((lp, lp), F32)]
    )(qkv, seg_row, seg_col)
    y, res_grad, mixed_grad, g_up, g_down, g_out, g_tab = call(
        ff_kernel,
        [
            sds(block_input.shape, BF), sds(full, F32), sds(full, BF), sds(up.shape, BF),
            sds(down.shape, BF), sds((width, width), BF), sds(table.shape, F32),
        ],
        7,
        [
            pltpu.VMEM(full, BF), pltpu.VMEM(turned, BF), pltpu.VMEM(full, BF), pltpu.VMEM(turned, BF),
            pltpu.VMEM(full, F32), pltpu.VMEM(full, F32), pltpu.VMEM(full, F32),
            pltpu.VMEM((strips, lp, units), BF), pltpu.VMEM((strips, lp, units), BF),
        ],
    )(block_input, mixed, out_grad, w_out, up, down, table)
    (dqkv,) = call(
        attend_back_kernel,
        [sds(wide, BF)],
        6,
        [
            pltpu.VMEM((lp, lp), F32), pltpu.VMEM((128, lp), F32), pltpu.VMEM((16, lp), F32),
            pltpu.VMEM((128, lp), BF),
        ],
    )(qkv, mixed_grad, mixed, lse, seg_row, seg_col)
    x_grad, g_qkv, g_tab1 = call(
        qkv_back_kernel,
        [sds(block_input.shape, BF), sds((width, 3 * width), BF), sds(table.shape, F32)],
        6,
        [pltpu.VMEM(turned, BF), pltpu.VMEM(full, F32)],
    )(block_input, normed, dqkv, res_grad, w_qkv, table)
    g_tab = lax.psum(g_tab + g_tab1, ALL)
    g_qkv, g_out = (
        lax.psum_scatter(a.astype(F32), ALL, scatter_dimension=0, tiled=True) for a in (g_qkv, g_out)
    )
    g_up, g_down = (
        lax.psum_scatter(
            lax.psum_scatter(a.astype(F32), "gx", scatter_dimension=0, tiled=True)[0],
            ("dp", "gy"),
            scatter_dimension=0,
            tiled=True,
        )
        for a in (g_up, g_down)
    )
    g_att = (g_qkv[:, :width], g_qkv[:, width : 2 * width], g_qkv[:, 2 * width :], g_out)
    return y, x_grad, g_att, g_up, g_down, g_tab


def per_device(
    sizes, block_input, segment_ids, out_grad, query_weight, key_weight, value_weight, output_weight,
    first_gain, first_shift, query_bias, value_bias, output_bias, second_gain, second_shift,
    up_weight, up_bias, down_weight, down_bias,
):
    nd, nx, ny = sizes
    n_dev = nd * nx * ny
    strips, length, width = block_input.shape
    units = up_weight.shape[1]
    att_rows, ff_rows = query_weight.shape[0], up_weight.shape[0]
    own = nd == 2 and nx == 4 and ny % 2 == 0 and att_rows % 8 == 0 and ff_rows % 8 == 0

    vecs = [first_gain, first_shift, query_bias, value_bias, output_bias, second_gain, second_shift, down_bias]
    n_vec = len(vecs)
    me = (lax.axis_index("dp") * nx + lax.axis_index("gx")) * ny + lax.axis_index("gy")
    n_tab = n_vec + up_bias.shape[0] * n_dev // width
    pieces = jnp.stack(vecs).astype(F32)
    lane = lax.broadcasted_iota(jnp.int32, (n_vec, width), 1) // att_rows
    top = jnp.where(lane == me, jnp.tile(pieces, (1, n_dev)), 0.0)
    flat = jnp.tile(up_bias.astype(F32), n_dev).reshape(n_tab - n_vec, width)
    index = lax.broadcasted_iota(jnp.int32, flat.shape, 0) * width + lax.broadcasted_iota(jnp.int32, flat.shape, 1)
    small = jnp.concatenate([top, jnp.where(index // up_bias.shape[0] == me, flat, 0.0)])
    rows_up = (n_tab + 7) // 8 * 8
    small = jnp.pad(small, ((0, rows_up - n_tab), (0, 0)))
    if own:
        y, x_grad, gq, gk, gv_, go, g_up, g_down, g_tab = own_path(
            sizes,
            (
                block_input, segment_ids, out_grad, query_weight, key_weight, value_weight, output_weight,
                small, up_weight, down_weight,
            ),
        )
        g_att = (gq, gk, gv_, go)
    else:
        table = lax.psum(small, ALL)
        y, x_grad, g_att, g_up, g_down, g_tab = wide_path(
            sizes,
            (
                block_input, segment_ids, out_grad, query_weight, key_weight, value_weight, output_weight,
                table, up_weight, down_weight,
            ),
        )
    mine = lax.dynamic_slice(g_tab, (0, me * att_rows), (n_vec, att_rows))
    g_bias = lax.dynamic_slice(
        g_tab[n_vec:n_tab].reshape(-1), (me * up_bias.shape[0],), (up_bias.shape[0],)
    )
    return (
        y, x_grad, *g_att, mine[G1], mine[S1], mine[QB], mine[VB], mine[OB], mine[G2], mine[S2],
        g_up, g_bias, g_down, mine[DB],
    )


def solution(mesh):
    rows, cols = P(ALL, None), P(ALL)
    cube = P(ALL, None, None)
    ff = P(("dp", "gy"), "gx")
    sizes = (mesh.shape["dp"], mesh.shape["gx"], mesh.shape["gy"])
    return jax.shard_map(
        functools.partial(per_device, sizes),
        mesh=mesh,
        in_specs=(cube, rows, cube) + (rows,) * 4 + (cols,) * 7 + (ff, cols, ff, cols),
        out_specs=(cube, cube) + (rows,) * 4 + (cols,) * 7 + (ff, cols, ff, cols),
        check_vma=False,
    )
```

```python
import functools
import math

import jax
import jax.numpy as jnp
from jax import lax
from jax.experimental import pallas as pl
from jax.experimental.pallas import tpu as pltpu
from jax.sharding import PartitionSpec as P

H = 12
HD = 64
BF = jnp.bfloat16
F32 = jnp.float32
ALL = ("dp", "gx", "gy")
MESH = pl.DeviceIdType.MESH
LOG2E = 1.4426950408889634
INV_SQRT2 = 0.7071067811865476
INV_SQRT_2PI = 0.3989422804014327
ANY = pl.BlockSpec(memory_space=pl.ANY)
VM = pl.BlockSpec(memory_space=pltpu.VMEM)
LIMIT = 61 << 20

G1, S1, QB, VB, OB, G2, S2, DB, UB0 = 0, 1, 2, 3, 4, 5, 6, 7, 8


def nn(a, b):
    return lax.dot_general(a, b, (((1,), (0,)), ((), ())), preferred_element_type=F32)


def nt(a, b):
    return lax.dot_general(a, b, (((1,), (1,)), ((), ())), preferred_element_type=F32)


def padded(length):
    return (length + 31) // 32 * 32


def row_pieces(length, step):
    return [(lo, min(step, length - lo)) for lo in range(0, length, step)]


def normalise(rows):
    centred = rows - jnp.mean(rows, axis=-1, keepdims=True)
    scale = lax.rsqrt(jnp.mean(centred * centred, axis=-1, keepdims=True) + 1e-06)
    return centred * scale, scale


def norm_back(grad, gain, xhat, scale):
    t = grad * gain
    return scale * (
        t
        - jnp.mean(t, axis=-1, keepdims=True)
        - xhat * jnp.mean(t * xhat, axis=-1, keepdims=True)
    )


def colsum(rows):
    return jnp.sum(rows, axis=0, keepdims=True)


def qkv_kernel(x_ref, w_ref, v_ref, qkv_ref, n_ref, bias_ref):
    strips, length, width = x_ref.shape
    lp = n_ref.shape[1]
    gain, shift = v_ref[G1 : G1 + 1, :], v_ref[S1 : S1 + 1, :]
    for s in range(strips):
        for lo, size in row_pieces(length, 136):
            xhat, _ = normalise(x_ref[s, lo : lo + size, :].astype(F32))
            n_ref[s, lo : lo + size, :] = (xhat * gain + shift).astype(BF)
        n_ref[s, length:lp, :] = jnp.zeros((lp - length, width), BF)
    bias_ref[0:1, 0:width] = v_ref[QB : QB + 1, :]
    bias_ref[0:1, width : 2 * width] = jnp.zeros((1, width), F32)
    bias_ref[0:1, 2 * width : 3 * width] = v_ref[VB : VB + 1, :]
    step = 256

    def body(i, carry):
        cols = pl.ds(pl.multiple_of(i * step, step), step)
        w = w_ref[:, cols]
        for s in range(strips):
            qkv_ref[s, :, cols] = (nn(n_ref[s], w) + bias_ref[0:1, cols]).astype(BF)
        return carry

    lax.fori_loop(0, 3 * width // step, body, 0)


def fill_bias(bias_ref, row, col):
    bias_ref[...] = jnp.where(row == col, 0.0, -1e30).astype(F32)


def attend_kernel(qkv_ref, sr_ref, sc_ref, o_ref, lse_ref, bias_ref):
    strips, lp, width = o_ref.shape
    qrows = lp // 2
    first = lax.broadcasted_iota(jnp.int32, (qrows, 128), 1) < HD
    lane = lax.broadcasted_iota(jnp.int32, (qrows, 128), 1)
    scale = 0.125 * LOG2E
    for s in range(strips):
        fill_bias(bias_ref, sc_ref[s], sr_ref[s])
        lse_ref[s] = jnp.zeros((lp, 128), F32)

        def body(p, carry):
            cq = pl.ds(pl.multiple_of(p * 128, 128), 128)
            ck = pl.ds(pl.multiple_of(width + p * 128, 128), 128)
            cv = pl.ds(pl.multiple_of(2 * width + p * 128, 128), 128)
            k, v = qkv_ref[s, :, ck], qkv_ref[s, :, cv]
            for part in range(2):
                rows = pl.ds(part * qrows, qrows)
                q = qkv_ref[s, rows, cq]
                lse = lse_ref[s, rows, :]
                res = []
                for j in range(2):
                    keep = first if j == 0 else jnp.logical_not(first)
                    z = nt(jnp.where(keep, q, jnp.zeros_like(q)), k) * scale + bias_ref[rows, :]
                    top = jnp.max(z, axis=-1, keepdims=True)
                    e = jnp.exp2(z - top)
                    total = jnp.sum(e, axis=-1, keepdims=True)
                    res.append(nn(e.astype(BF), v) / total)
                    lse = jnp.where(lane == 2 * p + j, top + jnp.log2(total), lse)
                o_ref[s, rows, cq] = jnp.where(first, res[0], res[1]).astype(BF)
                lse_ref[s, rows, :] = lse
            return carry

        lax.fori_loop(0, H // 2, body, 0)


def transpose_into(dst_ref, src_ref, lp):
    strips, _, width = src_ref.shape
    for s in range(strips):

        def body(i, carry):
            cols = pl.ds(pl.multiple_of(i * 128, 128), 128)
            dst_ref[s, cols, :] = src_ref[s, :, cols].astype(F32).T.astype(BF)
            return carry

        lax.fori_loop(0, width // 128, body, 0)


def ff_kernel(
    x_ref, mix_ref, dout_in_ref, wo_ref, up_ref, down_ref, v_ref,
    y_ref, rg_ref, mg_ref, gup_ref, gdown_ref, gwo_ref, gv_ref,
    dout_ref, doutT_ref, sec_ref, secT_ref, res_ref, acc_ref, sg_ref, hid_ref, pre_ref,
):
    strips, length, width = x_ref.shape
    lp = mix_ref.shape[1]
    groups = up_ref.shape[0]
    units = up_ref.shape[2]
    gv_ref[...] = jnp.zeros(gv_ref.shape, F32)
    bias_o, gain, shift = v_ref[OB : OB + 1, :], v_ref[G2 : G2 + 1, :], v_ref[S2 : S2 + 1, :]
    step = 256
    for s in range(strips):
        dout_ref[s, 0:length, :] = dout_in_ref[s]
        dout_ref[s, length:lp, :] = jnp.zeros((lp - length, width), BF)

        def proj(i, carry):
            cols = pl.ds(pl.multiple_of(i * step, step), step)
            acc_ref[s, :, cols] = nn(mix_ref[s], wo_ref[:, cols])
            return carry

        lax.fori_loop(0, width // step, proj, 0)
        for lo, size in row_pieces(length, 136):
            rows = pl.ds(lo, size)
            residual = x_ref[s, rows, :].astype(F32) + (acc_ref[s, rows, :] + bias_o)
            res_ref[s, rows, :] = residual
            xhat, _ = normalise(residual)
            sec_ref[s, rows, :] = (xhat * gain + shift).astype(BF)
            acc_ref[s, rows, :] = residual + v_ref[DB : DB + 1, :]
        sec_ref[s, length:lp, :] = jnp.zeros((lp - length, width), BF)
        res_ref[s, length:lp, :] = jnp.zeros((lp - length, width), F32)
        gv_ref[DB : DB + 1, :] += colsum(dout_in_ref[s].astype(F32))
    sg_ref[...] = jnp.zeros(sg_ref.shape, F32)
    transpose_into(doutT_ref, dout_ref, lp)
    transpose_into(secT_ref, sec_ref, lp)

    def group(gi, carry):
        def hidden(i, carry):
            cols = pl.ds(pl.multiple_of(i * step, step), step)
            up, down = up_ref[gi, :, cols], down_ref[gi, :, cols]
            ub = v_ref[pl.ds(UB0 + gi, 1), cols]
            total = jnp.zeros((1, step), F32)
            for s in range(strips):
                pre = nn(sec_ref[s], up) + ub
                hg = nn(dout_ref[s], down)
                cdf = 0.5 + 0.5 * lax.erf(pre * INV_SQRT2)
                pdf = jnp.exp(-0.5 * pre * pre) * INV_SQRT_2PI
                hid_ref[s, :, cols] = (pre * cdf).astype(BF)
                pg = (hg * (cdf + pre * pdf)).astype(BF)
                pre_ref[s, :, cols] = pg
                total = total + colsum(pg.astype(F32))
            gv_ref[pl.ds(UB0 + gi, 1), cols] = total
            return carry

        lax.fori_loop(0, units // step, hidden, 0)

        def back(i, carry):
            rows = pl.ds(pl.multiple_of(i * step, step), step)
            for s in range(strips):
                acc_ref[s, :, rows] += nt(hid_ref[s], down_ref[gi, rows, :])
                sg_ref[s, :, rows] += nt(pre_ref[s], up_ref[gi, rows, :])
            gd = nn(doutT_ref[0, rows, :], hid_ref[0])
            gu = nn(secT_ref[0, rows, :], pre_ref[0])
            for s in range(1, strips):
                gd = gd + nn(doutT_ref[s, rows, :], hid_ref[s])
                gu = gu + nn(secT_ref[s, rows, :], pre_ref[s])
            gdown_ref[gi, rows, :] = gd.astype(BF)
            gup_ref[gi, rows, :] = gu.astype(BF)
            return carry

        lax.fori_loop(0, width // step, back, 0)
        return carry

    lax.fori_loop(0, groups, group, 0)
    for s in range(strips):
        for lo, size in row_pieces(length, 136):
            rows = pl.ds(lo, size)
            y_ref[s, rows, :] = acc_ref[s, rows, :].astype(BF)
            xhat, scale = normalise(res_ref[s, rows, :])
            grad = sg_ref[s, rows, :]
            gv_ref[G2 : G2 + 1, :] += colsum(grad * xhat)
            gv_ref[S2 : S2 + 1, :] += colsum(grad)
            rg = dout_ref[s, rows, :].astype(F32) + norm_back(grad, gain, xhat, scale)
            rg_ref[s, rows, :] = rg
            low = rg.astype(BF)
            sec_ref[s, rows, :] = low
            gv_ref[OB : OB + 1, :] += colsum(low.astype(F32))
        sec_ref[s, length:lp, :] = jnp.zeros((lp - length, width), BF)
        rg_ref[s, length:lp, :] = jnp.zeros((lp - length, width), F32)
    transpose_into(secT_ref, mix_ref, lp)

    def last(i, carry):
        rows = pl.ds(pl.multiple_of(i * step, step), step)
        for s in range(strips):
            mg_ref[s, :, rows] = nt(sec_ref[s], wo_ref[rows, :]).astype(BF)
        gw = nn(secT_ref[0, rows, :], sec_ref[0])
        for s in range(1, strips):
            gw = gw + nn(secT_ref[s, rows, :], sec_ref[s])
        gwo_ref[rows, :] = gw.astype(BF)
        return carry

    lax.fori_loop(0, width // step, last, 0)


def attend_back_kernel(
    qkv_ref, mg_ref, mix_ref, lse_ref, sr_ref, sc_ref, dqkv_ref, bias_ref, lt_ref, dt_ref, kt_ref
):
    strips, lp, width = mg_ref.shape
    krows = lp // 2
    first = lax.broadcasted_iota(jnp.int32, (krows, 128), 1) < HD
    scale = 0.125 * LOG2E
    heads = lax.broadcasted_iota(jnp.int32, (16, width), 0)
    owner = lax.broadcasted_iota(jnp.int32, (16, width), 1) // HD
    pick = jnp.where(heads == owner, 1.0, 0.0).astype(BF)
    for s in range(strips):
        fill_bias(bias_ref, sc_ref[s], sr_ref[s])
        lt_ref[...] = lse_ref[s].T
        prod = mg_ref[s].astype(F32) * mix_ref[s].astype(F32)
        high = prod.astype(BF)
        rest = (prod - high.astype(F32)).astype(BF)
        dt_ref[...] = nt(pick, high) + nt(pick, rest)

        def body(p, carry):
            cq = pl.ds(pl.multiple_of(p * 128, 128), 128)
            ck = pl.ds(pl.multiple_of(width + p * 128, 128), 128)
            cv = pl.ds(pl.multiple_of(2 * width + p * 128, 128), 128)
            q, do = qkv_ref[s, :, cq], mg_ref[s, :, cq]
            kt_ref[...] = qkv_ref[s, :, ck].astype(F32).T.astype(BF)
            dq = [jnp.zeros((HD, lp), F32), jnp.zeros((HD, lp), F32)]
            for part in range(2):
                rows = pl.ds(part * krows, krows)
                k, v = qkv_ref[s, rows, ck], qkv_ref[s, rows, cv]
                dv, dk = [], []
                for j in range(2):
                    keep = first if j == 0 else jnp.logical_not(first)
                    lse = lt_ref[pl.ds(2 * p + j, 1), :]
                    delta = dt_ref[pl.ds(2 * p + j, 1), :]
                    z = nt(jnp.where(keep, k, jnp.zeros_like(k)), q) * scale + bias_ref[rows, :]
                    prob = jnp.exp2(z - lse)
                    pg = nt(jnp.where(keep, v, jnp.zeros_like(v)), do)
                    sg = (prob * (pg - delta)).astype(BF)
                    dv.append(nn(prob.astype(BF), do))
                    dk.append(nn(sg, q))
                    dq[j] = dq[j] + nn(kt_ref[j * HD : (j + 1) * HD, part * krows : (part + 1) * krows], sg)
                dqkv_ref[s, rows, cv] = jnp.where(first, dv[0], dv[1]).astype(BF)
                dqkv_ref[s, rows, ck] = (0.125 * jnp.where(first, dk[0], dk[1])).astype(BF)
            dqkv_ref[s, :, cq] = (0.125 * jnp.concatenate(dq, axis=0)).T.astype(BF)
            return carry

        lax.fori_loop(0, H // 2, body, 0)


def qkv_back_kernel(
    x_ref, n_ref, dqkv_ref, rg_ref, w_ref, v_ref, gx_ref, gw_ref, gv_ref, nT_ref, ng_ref
):
    strips, length, width = x_ref.shape
    lp = n_ref.shape[1]
    step = 256
    gv_ref[...] = jnp.zeros(gv_ref.shape, F32)
    gain = v_ref[G1 : G1 + 1, :]
    transpose_into(nT_ref, n_ref, lp)
    for s in range(strips):
        gv_ref[QB : QB + 1, :] += colsum(dqkv_ref[s, :, 0:width].astype(F32))
        gv_ref[VB : VB + 1, :] += colsum(dqkv_ref[s, :, 2 * width : 3 * width].astype(F32))

        def body(i, carry):
            rows = pl.ds(pl.multiple_of(i * step, step), step)
            ng_ref[s, :, rows] = nt(dqkv_ref[s], w_ref[rows, :])
            return carry

        lax.fori_loop(0, width // step, body, 0)

    def grads(i, carry):
        cols = pl.ds(pl.multiple_of(i * step, step), step)
        gw = nn(nT_ref[0], dqkv_ref[0, :, cols])
        for s in range(1, strips):
            gw = gw + nn(nT_ref[s], dqkv_ref[s, :, cols])
        gw_ref[:, cols] = gw.astype(BF)
        return carry

    lax.fori_loop(0, 3 * width // step, grads, 0)
    for s in range(strips):
        for lo, size in row_pieces(length, 136):
            rows = pl.ds(lo, size)
            xhat, scale = normalise(x_ref[s, rows, :].astype(F32))
            grad = ng_ref[s, rows, :]
            gv_ref[G1 : G1 + 1, :] += colsum(grad * xhat)
            gv_ref[S1 : S1 + 1, :] += colsum(grad)
            term = norm_back(grad, gain, xhat, scale)
            gx_ref[s, rows, :] = (rg_ref[s, rows, :] + term).astype(BF)


def call(kernel, outs, n_in, scratch=()):
    return pl.pallas_call(
        kernel,
        out_shape=outs,
        in_specs=[VM] * n_in,
        out_specs=[VM] * len(outs),
        scratch_shapes=list(scratch),
        compiler_params=pltpu.CompilerParams(vmem_limit_bytes=LIMIT),
    )


def sds(shape, dtype):
    return jax.ShapeDtypeStruct(shape, dtype)


def remote(src, dst, send, recv, dev):
    return pltpu.make_async_remote_copy(
        src_ref=src, dst_ref=dst, send_sem=send, recv_sem=recv, device_id=dev, device_id_type=MESH
    )


class Place:
    def __init__(self, ny):
        self.ny = ny
        self.d, x, self.g = lax.axis_index("dp"), lax.axis_index("gx"), lax.axis_index("gy")
        self.h, self.c = x // 2, x % 2
        self.z = [(self.d, x, lax.rem(self.g + k, ny)) for k in range(1, ny)]
        self.y = (self.d, (1 - self.h) * 2 + self.c, self.g)
        self.x = (1 - self.d, x, self.g)
        self.core = (self.d, self.h * 2 + 1 - self.c, self.g)
        h, c = (self.h, 1 - self.h), (self.c, 1 - self.c)
        every = [(d, hh * 2 + cc, self.g) for d in (self.d, 1 - self.d) for hh in h for cc in c]
        self.plane = every[1:]

    def greet(self):
        barrier = pltpu.get_barrier_semaphore()
        peers = self.z + self.plane
        for peer in peers:
            pl.semaphore_signal(barrier, inc=1, device_id=peer, device_id_type=MESH)
        pl.semaphore_wait(barrier, len(peers))


def stops(plan, **stages):
    steps = iter(plan)

    def stop():
        for token in next(steps):
            stages[token[0]](int(token[1:]))

    return stop


class Gather:
    def __init__(self, at, shards, views, sems):
        self.at, self.shards, self.views, self.n = at, shards, views, len(shards)
        self.loc, self.zsend, self.zrecv, self.bsend, self.brecv = sems
        self.zs, self.bs, self.fs, self.cs = {}, {}, {}, {}

    @staticmethod
    def semaphores(n, ny):
        return [pltpu.SemaphoreType.DMA(s) for s in ((n,), (n, ny - 1), (n, ny - 1), (n, 8), (n, 8))]

    def push(self, t, i, ref, dev):
        cp = remote(ref, ref, self.bsend.at[t, i], self.brecv.at[t, i], dev)
        cp.start()
        return cp

    def z(self, t):
        at = self.at
        own = self.views[t](at.d, at.h, at.c, at.g, 1)
        local = pltpu.make_async_copy(self.shards[t], own, self.loc.at[t])
        local.start()
        copies = []
        for k, dev in enumerate(at.z):
            cp = remote(self.shards[t], own, self.zsend.at[t, k], self.zrecv.at[t, k], dev)
            cp.start()
            copies.append(cp)
        self.zs[t] = local, copies

    def b(self, t):
        at = self.at
        self.zs[t][0].wait()
        for cp in self.zs[t][1]:
            cp.wait_recv()
        b = self.views[t](at.d, at.h, at.c, 0, at.ny)
        self.bs[t] = [self.push(t, i, b, dev) for i, dev in enumerate((at.y, at.x, at.core))]

    def f(self, t):
        at, view = self.at, self.views[t]
        half = at.ny // 2
        self.bs[t][0].wait_recv()
        f1 = self.push(t, 3, view(at.d, 1 - at.h, at.c, 0, half), at.x)
        c1 = self.push(t, 4, view(at.d, 1 - at.h, at.c, 0, at.ny), at.core)
        self.bs[t][1].wait_recv()
        f2 = self.push(t, 5, view(1 - at.d, at.h, at.c, half, at.ny - half), at.y)
        c2 = self.push(t, 6, view(1 - at.d, at.h, at.c, 0, at.ny), at.core)
        self.fs[t] = [f1, c1, f2, c2]

    def c(self, t):
        at = self.at
        self.fs[t][0].wait_recv()
        self.fs[t][2].wait_recv()
        self.cs[t] = self.push(t, 7, self.views[t](1 - at.d, 1 - at.h, at.c, 0, at.ny), at.core)

    def arrived(self, t):
        for cp in (self.bs[t][2], self.fs[t][1], self.fs[t][3], self.cs[t]):
            cp.wait_recv()

    def sent(self, t):
        for cp in self.zs[t][1] + self.bs[t] + self.fs[t] + [self.cs[t]]:
            cp.wait_send()


class Table:
    def __init__(self, at, total, landing, send, recv):
        self.at, self.total, self.landing, self.send, self.recv = at, total, landing, send, recv
        self.stages = [at.plane, at.z]
        self.flight, self.slot = [], 0

    @staticmethod
    def scratch(shape, ny, dtype):
        return [
            pltpu.VMEM((ny + 6,) + shape, dtype), pltpu.VMEM((2,) + shape, dtype),
            pltpu.SemaphoreType.DMA((ny + 6,)), pltpu.SemaphoreType.DMA((ny + 6,)),
        ]

    def step(self, k):
        if k > 0:
            value = self.total[k - 1].astype(F32)
            for cp, slot in self.flight[k - 1]:
                cp.wait_recv()
                value = value + self.landing[slot].astype(F32)
            if k < len(self.stages):
                self.total[k] = value.astype(self.total.dtype)
            else:
                self.result = value
                return
        copies = []
        for dev in self.stages[k]:
            slot = self.slot
            self.slot += 1
            cp = remote(self.total.at[k], self.landing.at[slot], self.send.at[slot], self.recv.at[slot], dev)
            cp.start()
            copies.append((cp, slot))
        self.flight.append(copies)

    def sent(self):
        for copies in self.flight:
            for cp, _ in copies:
                cp.wait_send()


class Scatter:
    def __init__(self, at, units, buffers, sems):
        self.at, self.units, self.n = at, units, len(units)
        self.bufs = buffers
        self.lsem, self.csend, self.crecv, self.bsend, self.brecv, self.zsend, self.zrecv = sems
        d, h = at.d, at.h
        self.quads = [(1 - d, 1 - h), (d, 1 - h), (1 - d, h), (d, h)]
        self.cs, self.fars, self.nears, self.zs = {}, {}, {}, {}

    @staticmethod
    def buffers(k, rows, cols, ny):
        return [
            pltpu.VMEM((lead, n * k, rows, cols), BF)
            for lead, n in ((4, ny), (4, ny), (2, ny // 2), (2, ny), (ny - 1, 1))
        ]

    @staticmethod
    def semaphores(n, ny):
        lead = (4, 4, 4, 4, 4, ny - 1, ny - 1)
        return [pltpu.SemaphoreType.DMA((n, k)) for k in lead]

    def add(self, dst, src, pieces):
        lead = dst.shape[0] // pieces

        def body(i, carry):
            part = pl.ds(i * lead, lead)
            dst[part] = (dst[part].astype(F32) + src[part].astype(F32)).astype(dst.dtype)
            return carry

        lax.fori_loop(0, pieces, body, 0)

    def core(self, t):
        view, (sums, rc) = self.units[t][0], self.bufs[t][:2]
        c = self.at.c
        res = []
        for q, (d, h) in enumerate(self.quads):
            cp = remote(
                view(d, h, 1 - c), rc.at[q], self.csend.at[t, q], self.crecv.at[t, q], self.at.core
            )
            cp.start()
            lc = pltpu.make_async_copy(view(d, h, c), sums.at[q], self.lsem.at[t, q])
            lc.start()
            res.append((cp, lc))
        self.cs[t] = res

    def far(self, t):
        sums, rc, rs = self.bufs[t][:3]
        ny, k = self.at.ny, self.units[t][1]
        cut = ny // 2 * k
        res = []
        for q in range(4):
            self.cs[t][q][0].wait_recv()
            self.cs[t][q][1].wait()
            self.add(sums.at[q], rc.at[q], ny)
            if q == 0:
                for i, (lo, dev) in enumerate(((0, self.at.x), (cut, self.at.y))):
                    cp = remote(
                        sums.at[0, lo : lo + cut], rs.at[i], self.bsend.at[t, i], self.brecv.at[t, i], dev
                    )
                    cp.start()
                    res.append(cp)
        self.fars[t] = res

    def near(self, t):
        sums, _, rs, rl = self.bufs[t][:4]
        ny, k = self.at.ny, self.units[t][1]
        cut = ny // 2 * k
        res = []
        for i, (lo, dev) in enumerate(((0, self.at.y), (cut, self.at.x))):
            self.fars[t][i].wait_recv()
            self.add(sums.at[1 + i, lo : lo + cut], rs.at[i], ny // 2)
            cp = remote(sums.at[1 + i], rl.at[i], self.bsend.at[t, 2 + i], self.brecv.at[t, 2 + i], dev)
            cp.start()
            res.append(cp)
        self.nears[t] = res

    def z(self, t):
        sums, rl, rz = self.bufs[t][0], self.bufs[t][3], self.bufs[t][4]
        at, n = self.at, self.units[t][1]
        for i in range(2):
            self.nears[t][i].wait_recv()
            self.add(sums.at[3], rl.at[i], at.ny)
        res = []
        for k, dev in enumerate(at.z):
            cp = remote(
                sums.at[3, pl.ds(dev[2] * n, n)], rz.at[k], self.zsend.at[t, k], self.zrecv.at[t, k], dev
            )
            cp.start()
            res.append(cp)
        self.zs[t] = res

    def finish(self, t):
        sums, rz = self.bufs[t][0], self.bufs[t][4]
        n = self.units[t][1]
        total = sums[3, pl.ds(self.at.g * n, n)].astype(F32)
        for k, cp in enumerate(self.zs[t]):
            cp.wait_recv()
            total = total + rz[k].astype(F32)
        self.units[t][2](total)

    def sent(self, t):
        for q in range(4):
            self.cs[t][q][0].wait_send()
        for cp in self.fars[t] + self.nears[t] + self.zs[t]:
            cp.wait_send()


GROUPS = ((0, 128), (128, 256), (384, 256), (640, 128))
NG = len(GROUPS)
PARTS = 3


def att_view(ref, tiles, sizes):
    nd, nh, ny = sizes

    def view(d, h, c, lo, n):
        return ref.at[pl.ds((((d * nh + h) * 2 + c) * ny + lo) * tiles, n * tiles)]

    return view


def ff_view(ref, part):
    def view(d, h, c, lo, n):
        start = pl.multiple_of((h * 2 + c) * part, part)
        return ref.at[d, pl.ds(lo, n), :, pl.ds(start, part)]

    return view


def copies_of(sem, *pairs):
    made = [pltpu.make_async_copy(a, b, sem.at[i]) for i, (a, b) in enumerate(pairs)]
    for cp in made:
        cp.start()
    return made


def columns_of(seg_row):
    return jnp.broadcast_to(seg_row, (128, seg_row.shape[1])).T[:, 0:1]


def turn(dst_ref, src_ref):
    total, width = src_ref.shape
    step = 256
    eye = jnp.where(
        lax.broadcasted_iota(jnp.int32, (step, step), 0) == lax.broadcasted_iota(jnp.int32, (step, step), 1), 1.0, 0.0
    ).astype(BF)
    for lo, size in row_pieces(total, step):
        for j in range(width // step):
            cols = slice(j * step, (j + 1) * step)
            dst_ref[cols, lo : lo + size] = nt(eye, src_ref[lo : lo + size, cols]).astype(BF)


def mask_into(bias_ref, segp_ref, s):
    row = segp_ref[s : s + 1, :]
    bias_ref[...] = jnp.where(columns_of(row) == row, 0.0, -1e30).astype(F32)


def segments_into(segp_ref, seg_ref):
    strips, length = seg_ref.shape
    segp_ref[...] = jnp.full(segp_ref.shape, -1.0, F32)
    segp_ref[0:strips, 0:length] = seg_ref[...].astype(F32)


def attend_pair(qkv_ref, o_ref, lse_ref, bias_ref, s, lp, base, gw, out_col):
    head = out_col // HD
    qrows = lp // 2
    lane = lax.broadcasted_iota(jnp.int32, (qrows, 128), 1)
    first = lane < HD
    scale = 0.125 * LOG2E
    off = s * lp
    k = qkv_ref[off : off + lp, base + gw : base + gw + 128]
    v = qkv_ref[off : off + lp, base + 2 * gw : base + 2 * gw + 128]
    for part in range(2):
        lo = part * qrows
        q = qkv_ref[off + lo : off + lo + qrows, base : base + 128]
        lse = lse_ref[s, lo : lo + qrows, :]
        res = []
        for j in range(2):
            keep = first if j == 0 else jnp.logical_not(first)
            z = nt(jnp.where(keep, q, jnp.zeros_like(q)), k) * scale + bias_ref[s, lo : lo + qrows, :]
            top = jnp.max(z, axis=-1, keepdims=True)
            e = jnp.exp2(z - top)
            total = jnp.sum(e, axis=-1, keepdims=True)
            res.append(nn(e.astype(BF), v) / total)
            lse = jnp.where(lane == head + j, top + jnp.log2(total), lse)
        o_ref[off + lo : off + lo + qrows, out_col : out_col + 128] = jnp.where(first, res[0], res[1]).astype(BF)
        lse_ref[s, lo : lo + qrows, :] = lse


def front_kernel(
    sizes, x_hbm, do_hbm, seg_ref, wq, wk, wv, wo, up, down, small_ref,
    lt_ref, table_ref, gsum_ref, qkv_out, mixed_out, nT_out, dout_out, doutT_out, watt_out, wo_out, up_out, down_out,
    x_ref, do_ref, xhat_ref, norm_ref, shard_ref, watt_ref, bias_row, lse_ref, bias_ref, segp_ref,
    qkv_ref, mixed_ref, nT_ref, dout_ref, doutT_ref,
    land_ref, tot_ref, tsend, trecv, lsem, osem, s_loc, s_zs, s_zr, s_bs, s_br, *land_w,
):
    nd, nh, ny = sizes
    strips, length, width = x_ref.shape
    lp = norm_ref.shape[0] // strips
    tiles = wq.shape[0]
    at = Place(ny)
    loads = [pltpu.make_async_copy(x_hbm, x_ref, lsem.at[0]), pltpu.make_async_copy(do_hbm, do_ref, lsem.at[1])]
    pieces = []
    for i, (first, gw) in enumerate(GROUPS):
        for j, w in enumerate((wq, wk, wv)):
            to = 3 * first + j * gw
            pieces.append(
                pltpu.make_async_copy(
                    w.at[:, :, first : first + gw], shard_ref.at[:, :, to : to + gw], lsem.at[2 + 3 * i + j]
                )
            )
    for cp in pieces + loads:
        cp.start()
    at.greet()
    tab = Table(at, tot_ref, land_ref, tsend, trecv)
    tot_ref[0] = small_ref[...].astype(BF)
    for cp in pieces:
        cp.wait()
    pw = up.shape[-1] // PARTS
    views = [att_view(land, tiles, sizes) for land in land_w] + [att_view(wo_out, tiles, sizes)]
    shards = [shard_ref.at[:, :, 3 * first : 3 * (first + gw)] for first, gw in GROUPS]
    shards += [wo, up.at[:, :, 0:pw], down.at[:, :, 0:pw]]
    views += [ff_view(up_out, pw), ff_view(down_out, pw)]
    gat = Gather(at, shards, views, (s_loc, s_zs, s_zr, s_bs, s_br))

    stop = stops(FRONT_PLAN, z=gat.z, b=gat.b, f=gat.f, c=gat.c, A=gat.arrived, t=tab.step)

    def hats(s):
        for lo, size in row_pieces(length, 136):
            xhat, _ = normalise(x_ref[s, lo : lo + size, :].astype(F32))
            xhat_ref[s * lp + lo : s * lp + lo + size, :] = xhat

    stop()
    for cp in loads:
        cp.wait()
    hats(0)
    stop()
    for s in range(1, strips):
        hats(s)
    stop()
    segments_into(segp_ref, seg_ref)
    for s in range(strips):
        mask_into(bias_ref.at[s], segp_ref, s)
    lse_ref[...] = jnp.zeros(lse_ref.shape, F32)
    stop()
    gsum = jnp.zeros((1, width), F32)
    for s in range(strips):
        dout_ref[s * lp : s * lp + length, :] = do_ref[s]
        dout_ref[s * lp + length : (s + 1) * lp, :] = jnp.zeros((lp - length, width), BF)
        gsum = gsum + colsum(do_ref[s].astype(F32))
    gsum_ref[...] = jnp.broadcast_to(gsum, gsum_ref.shape)
    stop()
    turn(doutT_ref, dout_ref)
    outs = copies_of(osem, (dout_ref, dout_out), (doutT_ref, doutT_out))
    stop()
    table = tab.result
    table_ref[...] = table
    gain, shift = table[G1 : G1 + 1, :], table[S1 : S1 + 1, :]
    for s in range(strips):
        for lo, size in row_pieces(length, 136):
            part = slice(s * lp + lo, s * lp + lo + size)
            norm_ref[part, :] = (xhat_ref[part, :] * gain + shift).astype(BF)
        norm_ref[s * lp + length : (s + 1) * lp, :] = jnp.zeros((lp - length, width), BF)
    for first, gw in GROUPS:
        cols = slice(first, first + gw)
        bias_row[0:1, 3 * first : 3 * first + gw] = table[QB : QB + 1, cols]
        bias_row[0:1, 3 * first + gw : 3 * first + 2 * gw] = jnp.zeros((1, gw), F32)
        bias_row[0:1, 3 * first + 2 * gw : 3 * (first + gw)] = table[VB : VB + 1, cols]
    for i, (first, gw) in enumerate(GROUPS):
        stop()
        wide = slice(3 * first, 3 * (first + gw))

        def settle(n, carry):
            rows = pl.ds(pl.multiple_of(n * 64, 64), 64)
            watt_ref[rows, wide] = land_w[i][pl.ds(n * 8, 8)].astype(F32).reshape(64, 3 * gw).astype(BF)
            return carry

        lax.fori_loop(0, width // 64, settle, 0)

        def project(n, carry):
            cols = pl.ds(pl.multiple_of(3 * first + n * gw, 128), gw)
            qkv_ref[:, cols] = (nn(norm_ref[...], watt_ref[:, cols]) + bias_row[0:1, cols]).astype(BF)
            return carry

        lax.fori_loop(0, 3, project, 0)
        outs += copies_of(
            osem.at[2 + 2 * i : 4 + 2 * i],
            (qkv_ref.at[:, wide], qkv_out.at[:, wide]), (watt_ref.at[:, wide], watt_out.at[:, wide]),
        )
        for s in range(strips):
            for p in range(gw // 128):
                stop()
                attend_pair(
                    qkv_ref, mixed_ref, lse_ref, bias_ref, s, lp, 3 * first + p * 128, gw, first + p * 128
                )
        if i == 0:
            stop()
            turn(nT_ref, norm_ref)
            outs += copies_of(osem.at[2 + 2 * NG : 3 + 2 * NG], (nT_ref, nT_out))
    stop()
    outs += copies_of(osem.at[3 + 2 * NG :], (mixed_ref, mixed_out))
    for s in range(strips):
        lt_ref[s] = lse_ref[s].T[0:16, :]
    stop()
    for t in range(gat.n):
        gat.sent(t)
    tab.sent()
    for cp in outs:
        cp.wait()


FRONT_PLAN = (
    ("z0", "z2"), ("t0",), ("z1", "t1", "z3", "b0"), ("b2", "z6", "f0"), ("b1", "t2"), ("b3", "z5", "c0"),
    ("A0", "f1"), ("f2", "f3"), ("z4",), ("b6", "c1"),
    ("A1",), ("b5", "c3"), (), ("b4",), ("c2", "f6"),
    ("A2",), ("A3",), ("f5",), (), (),
    ("f4",), ("c6",), ("c5", "A6"), ("A5", "c4"), ("A4",),
)


MIDDLE_PLAN = (
    ("z0",), ("z1",), (), ("z3",),
    ("b0", "z2"), ("b1",), ("f0",), ("f1", "c0", "b3", "K0"), ("b2",),
    ("c1", "A0", "F0", "A1"), ("K1",), ("f3", "f2"), ("F1", "N0"), ("c3", "c2"),
    ("A2", "A3"), ("N1",), ("Z0",), (), ("Z1",),
    (), (), ("E0",), ("E1",),
)


def middle_kernel(
    sizes, x_ref, mix_ref, wo_ref, v_ref, gsum_ref, dout_hbm, doutT_hbm, u0, d0, up, down,
    mg_ref, gwo_ref, gv_ref, gu_ref, gd_ref, y_out, rg_out, *out_parts_and_scratch,
):
    middle_body(
        sizes, x_ref, mix_ref, wo_ref, v_ref, gsum_ref, dout_hbm, doutT_hbm, u0, d0, up, down,
        mg_ref, gwo_ref, gv_ref, gu_ref, gd_ref, y_out, rg_out,
        out_parts_and_scratch[: 2 * (PARTS - 1)], *out_parts_and_scratch[2 * (PARTS - 1) :],
    )


def middle_body(
    sizes, x_ref, mix_ref, wo_ref, v_ref, gsum_ref, dout_hbm, doutT_hbm, u0, d0, up, down,
    mg_ref, gwo_ref, gv_ref, gu_ref, gd_ref, y_out, rg_out, later,
    dout_ref, doutT_ref, sec_ref, secT_ref, res_ref, acc_ref, rg_ref, hid_ref, pre_ref, y_ref, wu, wd, pu, pd,
    lsem, osem, s_loc, s_zs, s_zr, s_bs, s_br, *rest,
):
    nd, nh, ny = sizes
    nq = nh * 2
    strips, length, width = x_ref.shape
    lp = mix_ref.shape[0] // strips
    rows, part = up.shape[1], up.shape[2] // PARTS
    at = Place(ny)
    loads = copies_of(lsem, (dout_hbm, dout_ref), (doutT_hbm, doutT_ref), (u0, wu.at[0]), (d0, wd.at[0]))
    at.greet()
    n_sc = 2
    shards, views, units = [], [], []
    for b in range(1, PARTS):
        cols = slice(b * part, (b + 1) * part)
        shards += [up.at[:, :, cols], down.at[:, :, cols]]
        views += [ff_view(wu.at[b], part), ff_view(wd.at[b], part)]
    for src, dst in ((pu, gu_ref), (pd, gd_ref)):

        def put(total, dst=dst):
            dst[...] = total[0]

        whole = ff_view(src, part)
        units.append(((lambda d, h, c, whole=whole: whole(d, h, c, 0, ny)), 1, put))
    gat = Gather(at, shards, views, (s_loc, s_zs, s_zr, s_bs, s_br))
    sca = Scatter(at, units, [rest[5 * t : 5 * t + 5] for t in range(n_sc)], rest[5 * n_sc :])
    stop = stops(
        MIDDLE_PLAN, z=gat.z, b=gat.b, f=gat.f, c=gat.c, A=gat.arrived,
        K=sca.core, F=sca.far, N=sca.near, Z=sca.z, E=sca.finish,
    )
    stop()

    step = 256
    bias_o, gain, shift = v_ref[OB : OB + 1, :], v_ref[G2 : G2 + 1, :], v_ref[S2 : S2 + 1, :]
    gv_ref[...] = jnp.zeros(gv_ref.shape, F32)
    gv_ref[DB : DB + 1, :] = gsum_ref[0:1, :]

    def proj(i, carry):
        cols = pl.ds(pl.multiple_of(i * step, step), step)
        acc_ref[:, cols] = nn(mix_ref[...], wo_ref[:, cols])
        return carry

    lax.fori_loop(0, width // step, proj, 0)
    for s in range(strips):
        stop()
        for lo, size in row_pieces(length, 136):
            sel = slice(s * lp + lo, s * lp + lo + size)
            residual = x_ref[s, lo : lo + size, :].astype(F32) + (acc_ref[sel, :] + bias_o)
            res_ref[sel, :] = residual
            xhat, _ = normalise(residual)
            sec_ref[sel, :] = (xhat * gain + shift).astype(BF)
            acc_ref[sel, :] = residual + v_ref[DB : DB + 1, :]
        sec_ref[s * lp + length : (s + 1) * lp, :] = jnp.zeros((lp - length, width), BF)
    stop()
    turn(secT_ref, sec_ref)
    for cp in loads:
        cp.wait()

    outs = []
    block = strips * lp // 8
    for b in range(PARTS):

        def hidden(q, carry):
            cols = pl.ds(pl.multiple_of(q * part, part), part)
            w_up = wu[b, :, :, :, cols].reshape(width, part)
            w_down = wd[b, :, :, :, cols].reshape(width, part)
            csum = jnp.zeros((1, part), F32)
            for r in range(8):
                rs = slice(r * block, (r + 1) * block)
                pre = nn(sec_ref[rs, :], w_up) + v_ref[pl.ds(UB0 + q, 1), b * part : (b + 1) * part]
                hg = nn(dout_ref[rs, :], w_down)
                cdf = 0.5 + 0.5 * lax.erf(pre * INV_SQRT2)
                pdf = jnp.exp(-0.5 * pre * pre) * INV_SQRT_2PI
                hid_ref[rs, cols] = (pre * cdf).astype(BF)
                pg = (hg * (cdf + pre * pdf)).astype(BF)
                pre_ref[rs, cols] = pg
                csum = csum + colsum(pg.astype(F32))
            gv_ref[pl.ds(UB0 + q, 1), b * part : (b + 1) * part] = csum
            return carry

        g_up, g_down = (pu, pd) if b == 0 else (wu.at[b - 1], wd.at[b - 1])

        def grads(d):
            rs = slice(d * ny * rows, (d + 1) * ny * rows)
            g_down[d] = nn(doutT_ref[rs, :], hid_ref[...]).astype(BF).reshape((ny, rows, nq * part))
            g_up[d] = nn(secT_ref[rs, :], pre_ref[...]).astype(BF).reshape((ny, rows, nq * part))

        stop()
        lax.fori_loop(0, nq // 2, hidden, 0)
        stop()
        lax.fori_loop(nq // 2, nq, hidden, 0)
        stop()
        if b > 1:
            gat.sent(2 * b - 4)
            gat.sent(2 * b - 3)
        for q in range(nd):
            grads(q)
        if b > 0:
            outs += copies_of(
                osem.at[2 * b : 2 * b + 2], (g_up, later[2 * b - 2]), (g_down, later[2 * b - 1])
            )
        stop()
        w_down = wd[b].reshape(width, nq * part)
        for n in range(strips):
            rs = slice(n * lp, (n + 1) * lp)
            acc_ref[rs, :] += nt(hid_ref[rs, :], w_down)
        stop()
        w_up = wu[b].reshape(width, nq * part)
        for n in range(strips):
            rs = slice(n * lp, (n + 1) * lp)
            value = nt(pre_ref[rs, :], w_up)
            rg_ref[rs, :] = value if b == 0 else rg_ref[rs, :] + value

    for s in range(strips):
        stop()
        for lo, size in row_pieces(length, 136):
            sel = slice(s * lp + lo, s * lp + lo + size)
            y_ref[lo : lo + size, s, :] = acc_ref[sel, :].astype(BF)
            xhat, scale = normalise(res_ref[sel, :])
            grad = rg_ref[sel, :]
            gv_ref[G2 : G2 + 1, :] += colsum(grad * xhat)
            gv_ref[S2 : S2 + 1, :] += colsum(grad)
            rg = dout_ref[sel, :].astype(F32) + norm_back(grad, gain, xhat, scale)
            rg_ref[sel, :] = rg
            low = rg.astype(BF)
            sec_ref[sel, :] = low
            gv_ref[OB : OB + 1, :] += colsum(low.astype(F32))
        tail = slice(s * lp + length, (s + 1) * lp)
        sec_ref[tail, :] = jnp.zeros((lp - length, width), BF)
        rg_ref[tail, :] = jnp.zeros((lp - length, width), F32)
    outs += copies_of(osem.at[0:2], (rg_ref, rg_out), (y_ref, y_out))
    turn(secT_ref, mix_ref)
    stop()

    def last(i, carry):
        sel = pl.ds(pl.multiple_of(i * step, step), step)
        mg_ref[:, sel] = nt(sec_ref[...], wo_ref[sel, :]).astype(BF)
        gwo_ref[sel, :] = nn(secT_ref[sel, :], sec_ref[...]).astype(BF)
        return carry

    lax.fori_loop(0, width // step, last, 0)
    stop()
    for t in range(2 * (PARTS - 2), gat.n):
        gat.sent(t)
    for t in range(n_sc):
        sca.sent(t)
    for cp in outs:
        cp.wait()


def attend_back_pair(
    qkv_ref, mg_ref, dz_ref, bias_ref, lt_ref, dt_ref, kt_ref, s, lp, base, gw, out_col, dst
):
    head = out_col // HD
    first = lax.broadcasted_iota(jnp.int32, (lp, 128), 1) < HD
    scale = 0.125 * LOG2E
    rows = slice(s * lp, (s + 1) * lp)
    q = qkv_ref[rows, base : base + 128]
    k = qkv_ref[rows, base + gw : base + gw + 128]
    v = qkv_ref[rows, base + 2 * gw : base + 2 * gw + 128]
    do = mg_ref[rows, out_col : out_col + 128]
    kt_ref[...] = k.astype(F32).T.astype(BF)
    dq, dk, dv = [], [], []
    for j in range(2):
        keep = first if j == 0 else jnp.logical_not(first)
        lse = lt_ref[s, head + j : head + j + 1, :]
        delta = dt_ref[s, head + j : head + j + 1, :]
        z = nt(jnp.where(keep, k, jnp.zeros_like(k)), q) * scale + bias_ref[s]
        prob = jnp.exp2(z - lse)
        pg = nt(jnp.where(keep, v, jnp.zeros_like(v)), do)
        sg = (prob * (pg - delta)).astype(BF)
        dv.append(nn(prob.astype(BF), do))
        dk.append(nn(sg, q))
        dq.append(nn(kt_ref[j * HD : (j + 1) * HD, :], sg))
    dz_ref[rows, dst + 2 * gw : dst + 2 * gw + 128] = jnp.where(first, dv[0], dv[1]).astype(BF)
    dz_ref[rows, dst + gw : dst + gw + 128] = (0.125 * jnp.where(first, dk[0], dk[1])).astype(BF)
    dz_ref[rows, dst : dst + 128] = (0.125 * jnp.concatenate(dq, axis=0)).T.astype(BF)


BACK_PLAN = (
    ("K0", "K1"), ("K7", "F0"),
    ("t0", "F1", "K8", "F7"), ("N0",), (), ("K3", "K2"),
    (), ("N7", "F2"), ("F3",), ("F8", "N1"), ("Z7",), (),
    ("N2", "Z0"), (), ("K4", "N8"), ("Z1",), (), ("K5", "F4", "N3", "t1", "Z2"),
    ("F5",), ("N4", "Z8"), ("N5",), ("K6", "Z3"),
    ("F6", "E7", "Z4"), (), ("u0", "Z5", "N6", "E0", "u1", "Z6"), ("E1", "E4", "E2", "t2", "E5", "E3", "E8", "u2", "E6"),
)


def back_kernel(
    sizes, gu1, gd1, gu2, gd2, gwo, seg_ref, lt_ref, v_ref, gvm_ref, gu0_ref, gd0_ref,
    mg_hbm, mix_hbm, qkv_hbm, nT_hbm, watt_hbm, x_hbm, rg_hbm,
    gx_ref, gq_ref, gk_ref, gv_ref, go_ref, gu_ref, gd_ref, gtab_ref,
    mg_ref, mix_ref, qkv_ref, nT_ref, watt_ref, x_ref, rg_ref,
    dz_ref, ng_ref, bias_ref, segp_ref, dt_ref, kt_ref, tab_ref,
    land_ref, tot_ref, tsend, trecv, land2_ref, tot2_ref, tsend2, trecv2, isem,
    *rest,
):
    nd, nh, ny = sizes
    strips, length, width = x_ref.shape
    lp = qkv_ref.shape[0] // strips
    parts, rest = rest[:NG], rest[NG:]
    loads = copies_of(
        isem, (mg_hbm, mg_ref), (mix_hbm, mix_ref),
        *[
            (qkv_hbm.at[:, 3 * first : 3 * (first + gw)], qkv_ref.at[:, 3 * first : 3 * (first + gw)])
            for first, gw in GROUPS
        ],
        (nT_hbm, nT_ref), (watt_hbm, watt_ref), (x_hbm, x_ref), (rg_hbm, rg_ref),
    )
    at = Place(ny)
    at.greet()
    n = 5 + NG
    bufs = [rest[5 * t : 5 * t + 5] for t in range(n)]
    sems = rest[5 * n :]
    pw = gu1.shape[-1] // (2 * nh)
    units = []

    def ff_unit(src, dst, cols):
        whole = ff_view(src, pw)

        def put(total):
            dst[:, cols] = total[0]

        return lambda d, h, c: whole(d, h, c, 0, ny), 1, put

    one, two = slice(pw, 2 * pw), slice(2 * pw, 3 * pw)
    units += [ff_unit(gu2, gu_ref, two), ff_unit(gd2, gd_ref, two)]
    tiles = gq_ref.shape[0] // 8

    def att_unit(src, put):
        inner = att_view(src, tiles, sizes)
        return lambda d, h, c: inner(d, h, c, 0, ny), tiles, put

    def put_out(total):
        go_ref[...] = total.reshape(go_ref.shape)

    units.append(att_unit(gwo, put_out))
    for i, (first, gw) in enumerate(GROUPS):

        def put_group(total, first=first, gw=gw):
            for j, ref in enumerate((gq_ref, gk_ref, gv_ref)):
                ref[:, first : first + gw] = total[:, :, j * gw : (j + 1) * gw].reshape(-1, gw)

        units.append(att_unit(parts[i], put_group))
    units += [ff_unit(gu1, gu_ref, one), ff_unit(gd1, gd_ref, one)]
    sca = Scatter(at, units, bufs, sems)
    early = Table(at, tot_ref, land_ref, tsend, trecv)
    late = Table(at, tot2_ref, land2_ref, tsend2, trecv2)
    stop = stops(
        BACK_PLAN, K=sca.core, F=sca.far, N=sca.near, Z=sca.z, E=sca.finish, t=early.step, u=late.step
    )
    stop()
    gu_ref[:, 0:pw] = gu0_ref[...]
    gd_ref[:, 0:pw] = gd0_ref[...]
    tot_ref[0] = jnp.concatenate([gvm_ref[OB : DB + 1, :], gvm_ref[UB0 : UB0 + 4, :]]).astype(BF)
    segments_into(segp_ref, seg_ref)
    heads = lax.broadcasted_iota(jnp.int32, (16, width), 0)
    pick = jnp.where(heads == lax.broadcasted_iota(jnp.int32, (16, width), 1) // HD, 1.0, 0.0).astype(BF)
    for s in range(strips):
        mask_into(bias_ref.at[s], segp_ref, s)
    loads[0].wait()
    loads[1].wait()
    stop()
    for s in range(strips):
        part = slice(s * lp, (s + 1) * lp)
        prod = mg_ref[part, :].astype(F32) * mix_ref[part, :].astype(F32)
        high = prod.astype(BF)
        dt_ref[s] = nt(pick, high) + nt(pick, (prod - high.astype(F32)).astype(BF))
    for i, (first, gw) in enumerate(GROUPS):
        loads[2 + i].wait()
        for s in range(strips):
            for p in range(gw // 128):
                stop()
                attend_back_pair(
                    qkv_ref, mg_ref, dz_ref, bias_ref, lt_ref, dt_ref, kt_ref, s, lp,
                    3 * first + p * 128, gw, first + p * 128, p * 128,
                )
        cols = slice(first, first + gw)
        tab_ref[QB : QB + 1, cols] = colsum(dz_ref[:, 0:gw].astype(F32))
        tab_ref[VB : VB + 1, cols] = colsum(dz_ref[:, 2 * gw : 3 * gw].astype(F32))
        if i == 0:
            loads[2 + NG].wait()
            loads[3 + NG].wait()

        def grads(j, carry):
            c = pl.ds(pl.multiple_of(j * gw, gw), gw)
            parts[i][:, :, c] = nn(nT_ref[...], dz_ref[:, c]).reshape(width // 8, 8, gw).astype(BF)
            return carry

        stop()
        lax.fori_loop(0, 3, grads, 0)
        stop()

        def to_norm(j, carry):
            c = pl.ds(pl.multiple_of(j * 256, 256), 256)
            value = nt(dz_ref[:, 0 : 3 * gw], watt_ref[c, 3 * first : 3 * (first + gw)])
            ng_ref[:, c] = value if i == 0 else ng_ref[:, c] + value
            return carry

        lax.fori_loop(0, width // 256, to_norm, 0)
    gain = v_ref[G1 : G1 + 1, :]
    loads[4 + NG].wait()
    loads[5 + NG].wait()
    g_gain, g_shift = jnp.zeros((1, width), F32), jnp.zeros((1, width), F32)
    for s in range(strips):
        stop()
        for lo, size in row_pieces(length, 136):
            part = slice(s * lp + lo, s * lp + lo + size)
            xhat, scale = normalise(x_ref[s, lo : lo + size, :].astype(F32))
            grad = ng_ref[part, :]
            g_gain = g_gain + colsum(grad * xhat)
            g_shift = g_shift + colsum(grad)
            term = norm_back(grad, gain, xhat, scale)
            gx_ref[lo : lo + size, s, :] = (rg_ref[part, :] + term).astype(BF)
    tot2_ref[0] = jnp.concatenate(
        [g_gain, g_shift, tab_ref[QB : VB + 1, :], jnp.zeros((4, width), F32)]
    ).astype(BF)
    stop()
    stop()
    sums, ends = early.result, late.result
    gtab_ref[G1 : VB + 1, :] = ends[0:4]
    gtab_ref[OB : DB + 1, :] = sums[0:4]
    gtab_ref[UB0 : UB0 + 4, :] = sums[4:8]
    gtab_ref[UB0 + 4 :, :] = jnp.zeros((gtab_ref.shape[0] - UB0 - 4, width), F32)
    for t in range(n):
        sca.sent(t)
    early.sent()
    late.sent()


def own_path(sizes, args):
    (
        block_input, segment_ids, out_grad, query_weight, key_weight, value_weight, output_weight, small,
        up_weight, down_weight,
    ) = args
    nd, nx, ny = sizes
    nh = nx // 2
    grid3 = (nd, nh, ny)
    strips, length, width = block_input.shape
    units = up_weight.shape[1]
    att_rows, ff_rows = query_weight.shape[0], up_weight.shape[0]
    lp = padded(length)
    tiles = att_rows // 8
    part = units // PARTS
    total = strips * lp
    full, wide, turned = (total, width), (total, 3 * width), (width, total)
    n_tab = small.shape[0]
    ff_shape = (nd, ny, ff_rows, nx * part)
    x_shape = block_input.shape
    t_shape = (length, strips, width)
    watt_shape = (width, 3 * width)
    lt_shape = (strips, 16, lp)
    dma = pltpu.SemaphoreType.DMA
    ups, downs = up_weight[None], down_weight[None]
    (
        lt, table, gsum, qkv, mixed, nT, dout, doutT, watt, wo, u0, d0,
    ) = pl.pallas_call(
        functools.partial(front_kernel, grid3),
        out_shape=[
            sds(lt_shape, F32), sds((n_tab, width), F32), sds((8, width), F32), sds(wide, BF), sds(full, BF),
            sds(turned, BF), sds(full, BF), sds(turned, BF), sds(watt_shape, BF), sds((width // 8, 8, width), BF),
            sds(ff_shape, BF), sds(ff_shape, BF),
        ],
        in_specs=[ANY, ANY, VM] + [ANY] * 6 + [VM],
        out_specs=[VM] * 3 + [ANY] * 9,
        scratch_shapes=[
            pltpu.VMEM(x_shape, BF), pltpu.VMEM(x_shape, BF), pltpu.VMEM(full, F32), pltpu.VMEM(full, BF),
            pltpu.VMEM((tiles, 8, 3 * width), BF), pltpu.VMEM(watt_shape, BF), pltpu.VMEM((8, 3 * width), F32), pltpu.VMEM((strips, lp, 128), F32),
            pltpu.VMEM((strips, lp, lp), F32), pltpu.VMEM((8, lp), F32),
            pltpu.VMEM(wide, BF), pltpu.VMEM(full, BF), pltpu.VMEM(turned, BF), pltpu.VMEM(full, BF),
            pltpu.VMEM(turned, BF),
        ]
        + Table.scratch((n_tab, width), ny, BF)
        + [dma((2 + 3 * NG,)), dma((4 + 2 * NG,))]
        + Gather.semaphores(NG + 3, ny)
        + [pltpu.VMEM((width // 8, 8, 3 * gw), BF) for _, gw in GROUPS],
        compiler_params=pltpu.CompilerParams(collective_id=0, has_side_effects=True, vmem_limit_bytes=LIMIT),
    )(
        block_input, out_grad, segment_ids,
        *(w.reshape(tiles, 8, width) for w in (query_weight, key_weight, value_weight, output_weight)),
        ups, downs, small,
    )

    n_sc, n_later = 2, 2 * (PARTS - 1)
    some = (ff_rows, part)
    buffers = []
    for _ in range(n_sc):
        buffers += Scatter.buffers(1, ff_rows, part, ny)
    mg, gwo, gvm, gu0, gd0, y, rg, gu1, gd1, gu2, gd2 = pl.pallas_call(
        functools.partial(middle_kernel, grid3),
        out_shape=[
            sds(full, BF), sds((width, width), BF), sds((n_tab, width), F32), sds(some, F32), sds(some, F32),
            sds(t_shape, BF), sds(full, F32),
        ]
        + [sds(ff_shape, BF)] * n_later,
        in_specs=[VM] * 5 + [ANY] * 6,
        out_specs=[VM] * 5 + [ANY] * (2 + n_later),
        scratch_shapes=[
            pltpu.VMEM(full, BF), pltpu.VMEM(turned, BF), pltpu.VMEM(full, BF), pltpu.VMEM(turned, BF),
            pltpu.VMEM(full, F32), pltpu.VMEM(full, F32), pltpu.VMEM(full, F32),
            pltpu.VMEM((total, nx * part), BF), pltpu.VMEM((total, nx * part), BF), pltpu.VMEM(t_shape, BF),
        ]
        + [pltpu.VMEM((PARTS,) + ff_shape, BF)] * 2
        + [pltpu.VMEM(ff_shape, BF)] * 2
        + [dma((4,)), dma((2 + n_later,))]
        + Gather.semaphores(n_later, ny)
        + buffers
        + Scatter.semaphores(n_sc, ny),
        compiler_params=pltpu.CompilerParams(collective_id=1, has_side_effects=True, vmem_limit_bytes=LIMIT),
    )(block_input, mixed, wo.reshape(width, width), table, gsum, dout, doutT, u0, d0, ups, downs)

    n_units = 5 + NG
    buffers = []
    for _ in range(2):
        buffers += Scatter.buffers(1, ff_rows, part, ny)
    for cols in [width] + [3 * gw for _, gw in GROUPS]:
        buffers += Scatter.buffers(tiles, 8, cols, ny)
    for _ in range(2):
        buffers += Scatter.buffers(1, ff_rows, part, ny)
    gx, gq, gk, gv, go, gu, gd, gtab = pl.pallas_call(
        functools.partial(back_kernel, grid3),
        out_shape=[sds(t_shape, BF)] + [sds((att_rows, width), F32)] * 4 + [sds((ff_rows, units), F32)] * 2
        + [sds((n_tab, width), F32)],
        in_specs=[ANY] * 5 + [VM] * 6 + [ANY] * 7,
        out_specs=[VM] * 8,
        scratch_shapes=[
            pltpu.VMEM(full, BF), pltpu.VMEM(full, BF), pltpu.VMEM(wide, BF), pltpu.VMEM(turned, BF),
            pltpu.VMEM(watt_shape, BF), pltpu.VMEM(x_shape, BF), pltpu.VMEM(full, F32),
            pltpu.VMEM(full, BF), pltpu.VMEM(full, F32), pltpu.VMEM((strips, lp, lp), F32), pltpu.VMEM((8, lp), F32), pltpu.VMEM(lt_shape, F32),
            pltpu.VMEM((128, lp), BF), pltpu.VMEM((n_tab, width), F32),
        ]
        + Table.scratch((8, width), ny, BF)
        + Table.scratch((8, width), ny, BF)
        + [dma((6 + NG,))]
        + [pltpu.VMEM((width // 8, 8, 3 * gw), BF) for _, gw in GROUPS]
        + buffers
        + Scatter.semaphores(n_units, ny),
        compiler_params=pltpu.CompilerParams(collective_id=2, has_side_effects=True, vmem_limit_bytes=LIMIT),
    )(
        gu1, gd1, gu2, gd2, gwo.reshape(width // 8, 8, width), segment_ids, lt, table, gvm, gu0, gd0,
        mg, mixed, qkv, nT, watt, block_input, rg,
    )
    return y.transpose(1, 0, 2), gx.transpose(1, 0, 2), gq, gk, gv, go, gu, gd, gtab


def wide_path(sizes, args):
    (
        block_input, segment_ids, out_grad, query_weight, key_weight, value_weight, output_weight, table,
        up_weight, down_weight,
    ) = args
    nd, nx, ny = sizes
    strips, length, width = block_input.shape
    units = up_weight.shape[1]
    lp = padded(length)
    att = jnp.concatenate([query_weight, key_weight, value_weight, output_weight], axis=1)
    att = lax.all_gather(att, ALL, axis=0, tiled=True)
    up, down = (
        lax.all_gather(lax.all_gather(a, ("dp", "gy"), axis=0, tiled=True), "gx", axis=0)
        for a in (up_weight, down_weight)
    )
    w_qkv, w_out = att[:, : 3 * width], att[:, 3 * width :]
    seg = jnp.pad(segment_ids, ((0, 0), (0, lp - length)), constant_values=-1)
    seg_row, seg_col = seg[:, None, :], seg[:, :, None]
    full = (strips, lp, width)
    wide = (strips, lp, 3 * width)
    turned = (strips, width, lp)
    qkv, normed = call(
        qkv_kernel, [sds(wide, BF), sds(full, BF)], 3, [pltpu.VMEM((8, 3 * width), F32)]
    )(block_input, w_qkv, table)
    mixed, lse = call(
        attend_kernel, [sds(full, BF), sds((strips, lp, 128), F32)], 3, [pltpu.VMEM((lp, lp), F32)]
    )(qkv, seg_row, seg_col)
    y, res_grad, mixed_grad, g_up, g_down, g_out, g_tab = call(
        ff_kernel,
        [
            sds(block_input.shape, BF), sds(full, F32), sds(full, BF), sds(up.shape, BF),
            sds(down.shape, BF), sds((width, width), BF), sds(table.shape, F32),
        ],
        7,
        [
            pltpu.VMEM(full, BF), pltpu.VMEM(turned, BF), pltpu.VMEM(full, BF), pltpu.VMEM(turned, BF),
            pltpu.VMEM(full, F32), pltpu.VMEM(full, F32), pltpu.VMEM(full, F32),
            pltpu.VMEM((strips, lp, units), BF), pltpu.VMEM((strips, lp, units), BF),
        ],
    )(block_input, mixed, out_grad, w_out, up, down, table)
    (dqkv,) = call(
        attend_back_kernel,
        [sds(wide, BF)],
        6,
        [
            pltpu.VMEM((lp, lp), F32), pltpu.VMEM((128, lp), F32), pltpu.VMEM((16, lp), F32),
            pltpu.VMEM((128, lp), BF),
        ],
    )(qkv, mixed_grad, mixed, lse, seg_row, seg_col)
    x_grad, g_qkv, g_tab1 = call(
        qkv_back_kernel,
        [sds(block_input.shape, BF), sds((width, 3 * width), BF), sds(table.shape, F32)],
        6,
        [pltpu.VMEM(turned, BF), pltpu.VMEM(full, F32)],
    )(block_input, normed, dqkv, res_grad, w_qkv, table)
    g_tab = lax.psum(g_tab + g_tab1, ALL)
    g_qkv, g_out = (
        lax.psum_scatter(a.astype(F32), ALL, scatter_dimension=0, tiled=True) for a in (g_qkv, g_out)
    )
    g_up, g_down = (
        lax.psum_scatter(
            lax.psum_scatter(a.astype(F32), "gx", scatter_dimension=0, tiled=True)[0],
            ("dp", "gy"),
            scatter_dimension=0,
            tiled=True,
        )
        for a in (g_up, g_down)
    )
    g_att = (g_qkv[:, :width], g_qkv[:, width : 2 * width], g_qkv[:, 2 * width :], g_out)
    return y, x_grad, g_att, g_up, g_down, g_tab


def per_device(
    sizes, block_input, segment_ids, out_grad, query_weight, key_weight, value_weight, output_weight,
    first_gain, first_shift, query_bias, value_bias, output_bias, second_gain, second_shift,
    up_weight, up_bias, down_weight, down_bias,
):
    nd, nx, ny = sizes
    n_dev = nd * nx * ny
    strips, length, width = block_input.shape
    units = up_weight.shape[1]
    att_rows, ff_rows = query_weight.shape[0], up_weight.shape[0]
    own = nd == 2 and nx == 4 and ny % 2 == 0 and att_rows % 8 == 0 and ff_rows % 8 == 0

    vecs = [first_gain, first_shift, query_bias, value_bias, output_bias, second_gain, second_shift, down_bias]
    n_vec = len(vecs)
    me = (lax.axis_index("dp") * nx + lax.axis_index("gx")) * ny + lax.axis_index("gy")
    n_tab = n_vec + up_bias.shape[0] * n_dev // width
    pieces = jnp.stack(vecs).astype(F32)
    lane = lax.broadcasted_iota(jnp.int32, (n_vec, width), 1) // att_rows
    top = jnp.where(lane == me, jnp.tile(pieces, (1, n_dev)), 0.0)
    flat = jnp.tile(up_bias.astype(F32), n_dev).reshape(n_tab - n_vec, width)
    index = lax.broadcasted_iota(jnp.int32, flat.shape, 0) * width + lax.broadcasted_iota(jnp.int32, flat.shape, 1)
    small = jnp.concatenate([top, jnp.where(index // up_bias.shape[0] == me, flat, 0.0)])
    rows_up = (n_tab + 7) // 8 * 8
    small = jnp.pad(small, ((0, rows_up - n_tab), (0, 0)))
    if own:
        y, x_grad, gq, gk, gv_, go, g_up, g_down, g_tab = own_path(
            sizes,
            (
                block_input, segment_ids, out_grad, query_weight, key_weight, value_weight, output_weight,
                small, up_weight, down_weight,
            ),
        )
        g_att = (gq, gk, gv_, go)
    else:
        table = lax.psum(small, ALL)
        y, x_grad, g_att, g_up, g_down, g_tab = wide_path(
            sizes,
            (
                block_input, segment_ids, out_grad, query_weight, key_weight, value_weight, output_weight,
                table, up_weight, down_weight,
            ),
        )
    mine = lax.dynamic_slice(g_tab, (0, me * att_rows), (n_vec, att_rows))
    g_bias = lax.dynamic_slice(
        g_tab[n_vec:n_tab].reshape(-1), (me * up_bias.shape[0],), (up_bias.shape[0],)
    )
    return (
        y, x_grad, *g_att, mine[G1], mine[S1], mine[QB], mine[VB], mine[OB], mine[G2], mine[S2],
        g_up, g_bias, g_down, mine[DB],
    )


def solution(mesh):
    rows, cols = P(ALL, None), P(ALL)
    cube = P(ALL, None, None)
    ff = P(("dp", "gy"), "gx")
    sizes = (mesh.shape["dp"], mesh.shape["gx"], mesh.shape["gy"])
    return jax.shard_map(
        functools.partial(per_device, sizes),
        mesh=mesh,
        in_specs=(cube, rows, cube) + (rows,) * 4 + (cols,) * 7 + (ff, cols, ff, cols),
        out_specs=(cube, cube) + (rows,) * 4 + (cols,) * 7 + (ff, cols, ff, cols),
        check_vma=False,
    )
```

```python
import functools
import math

import jax
import jax.numpy as jnp
from jax import lax
from jax.experimental import pallas as pl
from jax.experimental.pallas import tpu as pltpu
from jax.sharding import PartitionSpec as P

H = 12
HD = 64
BF = jnp.bfloat16
F32 = jnp.float32
ALL = ("dp", "gx", "gy")
MESH = pl.DeviceIdType.MESH
LOG2E = 1.4426950408889634
INV_SQRT2 = 0.7071067811865476
INV_SQRT_2PI = 0.3989422804014327
ANY = pl.BlockSpec(memory_space=pl.ANY)
VM = pl.BlockSpec(memory_space=pltpu.VMEM)
LIMIT = 61 << 20

G1, S1, QB, VB, OB, G2, S2, DB, UB0 = 0, 1, 2, 3, 4, 5, 6, 7, 8


def nn(a, b):
    return lax.dot_general(a, b, (((1,), (0,)), ((), ())), preferred_element_type=F32)


def nt(a, b):
    return lax.dot_general(a, b, (((1,), (1,)), ((), ())), preferred_element_type=F32)


def padded(length):
    return (length + 31) // 32 * 32


def row_pieces(length, step):
    return [(lo, min(step, length - lo)) for lo in range(0, length, step)]


def normalise(rows):
    centred = rows - jnp.mean(rows, axis=-1, keepdims=True)
    scale = lax.rsqrt(jnp.mean(centred * centred, axis=-1, keepdims=True) + 1e-06)
    return centred * scale, scale


def norm_back(grad, gain, xhat, scale):
    t = grad * gain
    return scale * (
        t
        - jnp.mean(t, axis=-1, keepdims=True)
        - xhat * jnp.mean(t * xhat, axis=-1, keepdims=True)
    )


def colsum(rows):
    return jnp.sum(rows, axis=0, keepdims=True)


def qkv_kernel(x_ref, w_ref, v_ref, qkv_ref, n_ref, bias_ref):
    strips, length, width = x_ref.shape
    lp = n_ref.shape[1]
    gain, shift = v_ref[G1 : G1 + 1, :], v_ref[S1 : S1 + 1, :]
    for s in range(strips):
        for lo, size in row_pieces(length, 136):
            xhat, _ = normalise(x_ref[s, lo : lo + size, :].astype(F32))
            n_ref[s, lo : lo + size, :] = (xhat * gain + shift).astype(BF)
        n_ref[s, length:lp, :] = jnp.zeros((lp - length, width), BF)
    bias_ref[0:1, 0:width] = v_ref[QB : QB + 1, :]
    bias_ref[0:1, width : 2 * width] = jnp.zeros((1, width), F32)
    bias_ref[0:1, 2 * width : 3 * width] = v_ref[VB : VB + 1, :]
    step = 256

    def body(i, carry):
        cols = pl.ds(pl.multiple_of(i * step, step), step)
        w = w_ref[:, cols]
        for s in range(strips):
            qkv_ref[s, :, cols] = (nn(n_ref[s], w) + bias_ref[0:1, cols]).astype(BF)
        return carry

    lax.fori_loop(0, 3 * width // step, body, 0)


def fill_bias(bias_ref, row, col):
    bias_ref[...] = jnp.where(row == col, 0.0, -1e30).astype(F32)


def attend_kernel(qkv_ref, sr_ref, sc_ref, o_ref, lse_ref, bias_ref):
    strips, lp, width = o_ref.shape
    qrows = lp // 2
    first = lax.broadcasted_iota(jnp.int32, (qrows, 128), 1) < HD
    lane = lax.broadcasted_iota(jnp.int32, (qrows, 128), 1)
    scale = 0.125 * LOG2E
    for s in range(strips):
        fill_bias(bias_ref, sc_ref[s], sr_ref[s])
        lse_ref[s] = jnp.zeros((lp, 128), F32)

        def body(p, carry):
            cq = pl.ds(pl.multiple_of(p * 128, 128), 128)
            ck = pl.ds(pl.multiple_of(width + p * 128, 128), 128)
            cv = pl.ds(pl.multiple_of(2 * width + p * 128, 128), 128)
            k, v = qkv_ref[s, :, ck], qkv_ref[s, :, cv]
            for part in range(2):
                rows = pl.ds(part * qrows, qrows)
                q = qkv_ref[s, rows, cq]
                lse = lse_ref[s, rows, :]
                res = []
                for j in range(2):
                    keep = first if j == 0 else jnp.logical_not(first)
                    z = nt(jnp.where(keep, q, jnp.zeros_like(q)), k) * scale + bias_ref[rows, :]
                    top = jnp.max(z, axis=-1, keepdims=True)
                    e = jnp.exp2(z - top)
                    total = jnp.sum(e, axis=-1, keepdims=True)
                    res.append(nn(e.astype(BF), v) / total)
                    lse = jnp.where(lane == 2 * p + j, top + jnp.log2(total), lse)
                o_ref[s, rows, cq] = jnp.where(first, res[0], res[1]).astype(BF)
                lse_ref[s, rows, :] = lse
            return carry

        lax.fori_loop(0, H // 2, body, 0)


def transpose_into(dst_ref, src_ref, lp):
    strips, _, width = src_ref.shape
    for s in range(strips):

        def body(i, carry):
            cols = pl.ds(pl.multiple_of(i * 128, 128), 128)
            dst_ref[s, cols, :] = src_ref[s, :, cols].astype(F32).T.astype(BF)
            return carry

        lax.fori_loop(0, width // 128, body, 0)


def ff_kernel(
    x_ref, mix_ref, dout_in_ref, wo_ref, up_ref, down_ref, v_ref,
    y_ref, rg_ref, mg_ref, gup_ref, gdown_ref, gwo_ref, gv_ref,
    dout_ref, doutT_ref, sec_ref, secT_ref, res_ref, acc_ref, sg_ref, hid_ref, pre_ref,
):
    strips, length, width = x_ref.shape
    lp = mix_ref.shape[1]
    groups = up_ref.shape[0]
    units = up_ref.shape[2]
    gv_ref[...] = jnp.zeros(gv_ref.shape, F32)
    bias_o, gain, shift = v_ref[OB : OB + 1, :], v_ref[G2 : G2 + 1, :], v_ref[S2 : S2 + 1, :]
    step = 256
    for s in range(strips):
        dout_ref[s, 0:length, :] = dout_in_ref[s]
        dout_ref[s, length:lp, :] = jnp.zeros((lp - length, width), BF)

        def proj(i, carry):
            cols = pl.ds(pl.multiple_of(i * step, step), step)
            acc_ref[s, :, cols] = nn(mix_ref[s], wo_ref[:, cols])
            return carry

        lax.fori_loop(0, width // step, proj, 0)
        for lo, size in row_pieces(length, 136):
            rows = pl.ds(lo, size)
            residual = x_ref[s, rows, :].astype(F32) + (acc_ref[s, rows, :] + bias_o)
            res_ref[s, rows, :] = residual
            xhat, _ = normalise(residual)
            sec_ref[s, rows, :] = (xhat * gain + shift).astype(BF)
            acc_ref[s, rows, :] = residual + v_ref[DB : DB + 1, :]
        sec_ref[s, length:lp, :] = jnp.zeros((lp - length, width), BF)
        res_ref[s, length:lp, :] = jnp.zeros((lp - length, width), F32)
        gv_ref[DB : DB + 1, :] += colsum(dout_in_ref[s].astype(F32))
    sg_ref[...] = jnp.zeros(sg_ref.shape, F32)
    transpose_into(doutT_ref, dout_ref, lp)
    transpose_into(secT_ref, sec_ref, lp)

    def group(gi, carry):
        def hidden(i, carry):
            cols = pl.ds(pl.multiple_of(i * step, step), step)
            up, down = up_ref[gi, :, cols], down_ref[gi, :, cols]
            ub = v_ref[pl.ds(UB0 + gi, 1), cols]
            total = jnp.zeros((1, step), F32)
            for s in range(strips):
                pre = nn(sec_ref[s], up) + ub
                hg = nn(dout_ref[s], down)
                cdf = 0.5 + 0.5 * lax.erf(pre * INV_SQRT2)
                pdf = jnp.exp(-0.5 * pre * pre) * INV_SQRT_2PI
                hid_ref[s, :, cols] = (pre * cdf).astype(BF)
                pg = (hg * (cdf + pre * pdf)).astype(BF)
                pre_ref[s, :, cols] = pg
                total = total + colsum(pg.astype(F32))
            gv_ref[pl.ds(UB0 + gi, 1), cols] = total
            return carry

        lax.fori_loop(0, units // step, hidden, 0)

        def back(i, carry):
            rows = pl.ds(pl.multiple_of(i * step, step), step)
            for s in range(strips):
                acc_ref[s, :, rows] += nt(hid_ref[s], down_ref[gi, rows, :])
                sg_ref[s, :, rows] += nt(pre_ref[s], up_ref[gi, rows, :])
            gd = nn(doutT_ref[0, rows, :], hid_ref[0])
            gu = nn(secT_ref[0, rows, :], pre_ref[0])
            for s in range(1, strips):
                gd = gd + nn(doutT_ref[s, rows, :], hid_ref[s])
                gu = gu + nn(secT_ref[s, rows, :], pre_ref[s])
            gdown_ref[gi, rows, :] = gd.astype(BF)
            gup_ref[gi, rows, :] = gu.astype(BF)
            return carry

        lax.fori_loop(0, width // step, back, 0)
        return carry

    lax.fori_loop(0, groups, group, 0)
    for s in range(strips):
        for lo, size in row_pieces(length, 136):
            rows = pl.ds(lo, size)
            y_ref[s, rows, :] = acc_ref[s, rows, :].astype(BF)
            xhat, scale = normalise(res_ref[s, rows, :])
            grad = sg_ref[s, rows, :]
            gv_ref[G2 : G2 + 1, :] += colsum(grad * xhat)
            gv_ref[S2 : S2 + 1, :] += colsum(grad)
            rg = dout_ref[s, rows, :].astype(F32) + norm_back(grad, gain, xhat, scale)
            rg_ref[s, rows, :] = rg
            low = rg.astype(BF)
            sec_ref[s, rows, :] = low
            gv_ref[OB : OB + 1, :] += colsum(low.astype(F32))
        sec_ref[s, length:lp, :] = jnp.zeros((lp - length, width), BF)
        rg_ref[s, length:lp, :] = jnp.zeros((lp - length, width), F32)
    transpose_into(secT_ref, mix_ref, lp)

    def last(i, carry):
        rows = pl.ds(pl.multiple_of(i * step, step), step)
        for s in range(strips):
            mg_ref[s, :, rows] = nt(sec_ref[s], wo_ref[rows, :]).astype(BF)
        gw = nn(secT_ref[0, rows, :], sec_ref[0])
        for s in range(1, strips):
            gw = gw + nn(secT_ref[s, rows, :], sec_ref[s])
        gwo_ref[rows, :] = gw.astype(BF)
        return carry

    lax.fori_loop(0, width // step, last, 0)


def attend_back_kernel(
    qkv_ref, mg_ref, mix_ref, lse_ref, sr_ref, sc_ref, dqkv_ref, bias_ref, lt_ref, dt_ref, kt_ref
):
    strips, lp, width = mg_ref.shape
    krows = lp // 2
    first = lax.broadcasted_iota(jnp.int32, (krows, 128), 1) < HD
    scale = 0.125 * LOG2E
    heads = lax.broadcasted_iota(jnp.int32, (16, width), 0)
    owner = lax.broadcasted_iota(jnp.int32, (16, width), 1) // HD
    pick = jnp.where(heads == owner, 1.0, 0.0).astype(BF)
    for s in range(strips):
        fill_bias(bias_ref, sc_ref[s], sr_ref[s])
        lt_ref[...] = lse_ref[s].T
        prod = mg_ref[s].astype(F32) * mix_ref[s].astype(F32)
        high = prod.astype(BF)
        rest = (prod - high.astype(F32)).astype(BF)
        dt_ref[...] = nt(pick, high) + nt(pick, rest)

        def body(p, carry):
            cq = pl.ds(pl.multiple_of(p * 128, 128), 128)
            ck = pl.ds(pl.multiple_of(width + p * 128, 128), 128)
            cv = pl.ds(pl.multiple_of(2 * width + p * 128, 128), 128)
            q, do = qkv_ref[s, :, cq], mg_ref[s, :, cq]
            kt_ref[...] = qkv_ref[s, :, ck].astype(F32).T.astype(BF)
            dq = [jnp.zeros((HD, lp), F32), jnp.zeros((HD, lp), F32)]
            for part in range(2):
                rows = pl.ds(part * krows, krows)
                k, v = qkv_ref[s, rows, ck], qkv_ref[s, rows, cv]
                dv, dk = [], []
                for j in range(2):
                    keep = first if j == 0 else jnp.logical_not(first)
                    lse = lt_ref[pl.ds(2 * p + j, 1), :]
                    delta = dt_ref[pl.ds(2 * p + j, 1), :]
                    z = nt(jnp.where(keep, k, jnp.zeros_like(k)), q) * scale + bias_ref[rows, :]
                    prob = jnp.exp2(z - lse)
                    pg = nt(jnp.where(keep, v, jnp.zeros_like(v)), do)
                    sg = (prob * (pg - delta)).astype(BF)
                    dv.append(nn(prob.astype(BF), do))
                    dk.append(nn(sg, q))
                    dq[j] = dq[j] + nn(kt_ref[j * HD : (j + 1) * HD, part * krows : (part + 1) * krows], sg)
                dqkv_ref[s, rows, cv] = jnp.where(first, dv[0], dv[1]).astype(BF)
                dqkv_ref[s, rows, ck] = (0.125 * jnp.where(first, dk[0], dk[1])).astype(BF)
            dqkv_ref[s, :, cq] = (0.125 * jnp.concatenate(dq, axis=0)).T.astype(BF)
            return carry

        lax.fori_loop(0, H // 2, body, 0)


def qkv_back_kernel(
    x_ref, n_ref, dqkv_ref, rg_ref, w_ref, v_ref, gx_ref, gw_ref, gv_ref, nT_ref, ng_ref
):
    strips, length, width = x_ref.shape
    lp = n_ref.shape[1]
    step = 256
    gv_ref[...] = jnp.zeros(gv_ref.shape, F32)
    gain = v_ref[G1 : G1 + 1, :]
    transpose_into(nT_ref, n_ref, lp)
    for s in range(strips):
        gv_ref[QB : QB + 1, :] += colsum(dqkv_ref[s, :, 0:width].astype(F32))
        gv_ref[VB : VB + 1, :] += colsum(dqkv_ref[s, :, 2 * width : 3 * width].astype(F32))

        def body(i, carry):
            rows = pl.ds(pl.multiple_of(i * step, step), step)
            ng_ref[s, :, rows] = nt(dqkv_ref[s], w_ref[rows, :])
            return carry

        lax.fori_loop(0, width // step, body, 0)

    def grads(i, carry):
        cols = pl.ds(pl.multiple_of(i * step, step), step)
        gw = nn(nT_ref[0], dqkv_ref[0, :, cols])
        for s in range(1, strips):
            gw = gw + nn(nT_ref[s], dqkv_ref[s, :, cols])
        gw_ref[:, cols] = gw.astype(BF)
        return carry

    lax.fori_loop(0, 3 * width // step, grads, 0)
    for s in range(strips):
        for lo, size in row_pieces(length, 136):
            rows = pl.ds(lo, size)
            xhat, scale = normalise(x_ref[s, rows, :].astype(F32))
            grad = ng_ref[s, rows, :]
            gv_ref[G1 : G1 + 1, :] += colsum(grad * xhat)
            gv_ref[S1 : S1 + 1, :] += colsum(grad)
            term = norm_back(grad, gain, xhat, scale)
            gx_ref[s, rows, :] = (rg_ref[s, rows, :] + term).astype(BF)


def call(kernel, outs, n_in, scratch=()):
    return pl.pallas_call(
        kernel,
        out_shape=outs,
        in_specs=[VM] * n_in,
        out_specs=[VM] * len(outs),
        scratch_shapes=list(scratch),
        compiler_params=pltpu.CompilerParams(vmem_limit_bytes=LIMIT),
    )


def sds(shape, dtype):
    return jax.ShapeDtypeStruct(shape, dtype)


def remote(src, dst, send, recv, dev):
    return pltpu.make_async_remote_copy(
        src_ref=src, dst_ref=dst, send_sem=send, recv_sem=recv, device_id=dev, device_id_type=MESH
    )


class Place:
    def __init__(self, ny):
        self.ny = ny
        self.d, x, self.g = lax.axis_index("dp"), lax.axis_index("gx"), lax.axis_index("gy")
        self.h, self.c = x // 2, x % 2
        self.z = [(self.d, x, lax.rem(self.g + k, ny)) for k in range(1, ny)]
        self.y = (self.d, (1 - self.h) * 2 + self.c, self.g)
        self.x = (1 - self.d, x, self.g)
        self.core = (self.d, self.h * 2 + 1 - self.c, self.g)
        h, c = (self.h, 1 - self.h), (self.c, 1 - self.c)
        every = [(d, hh * 2 + cc, self.g) for d in (self.d, 1 - self.d) for hh in h for cc in c]
        self.plane = every[1:]

    def greet(self):
        for peer in self.z + self.plane:
            pl.semaphore_signal(pltpu.get_barrier_semaphore(), inc=1, device_id=peer, device_id_type=MESH)

    def greeted(self):
        pl.semaphore_wait(pltpu.get_barrier_semaphore(), len(self.z + self.plane))


def stops(plan, **stages):
    steps = iter(plan)

    def stop():
        for token in next(steps):
            stages[token[0]](int(token[1:]))

    return stop


class Gather:
    def __init__(self, at, shards, views, sems):
        self.at, self.shards, self.views, self.n = at, shards, views, len(shards)
        self.loc, self.zsend, self.zrecv, self.bsend, self.brecv = sems
        self.zs, self.bs, self.fs, self.cs = {}, {}, {}, {}

    @staticmethod
    def semaphores(n, ny, only_z=0):
        m = n + only_z
        return [pltpu.SemaphoreType.DMA(s) for s in ((m,), (m, ny - 1), (m, ny - 1), (n, 8), (n, 8))]

    def push(self, t, i, ref, dev):
        cp = remote(ref, ref, self.bsend.at[t, i], self.brecv.at[t, i], dev)
        cp.start()
        return cp

    def z(self, t):
        at = self.at
        own = self.views[t](at.d, at.h, at.c, at.g, 1)
        local = pltpu.make_async_copy(self.shards[t], own, self.loc.at[t])
        local.start()
        copies = []
        for k, dev in enumerate(at.z):
            cp = remote(self.shards[t], own, self.zsend.at[t, k], self.zrecv.at[t, k], dev)
            cp.start()
            copies.append(cp)
        self.zs[t] = local, copies

    def ready(self, t, source):
        at = self.at
        local = pltpu.make_async_copy(source, self.views[t](at.d, at.h, at.c, 0, at.ny), self.loc.at[t])
        local.start()
        self.zs[t] = local, []

    def along_z(self, t):
        self.zs[t][0].wait()
        for cp in self.zs[t][1]:
            cp.wait_recv()
        for cp in self.zs[t][1]:
            cp.wait_send()

    def b(self, t):
        at = self.at
        self.zs[t][0].wait()
        for cp in self.zs[t][1]:
            cp.wait_recv()
        b = self.views[t](at.d, at.h, at.c, 0, at.ny)
        self.bs[t] = [self.push(t, i, b, dev) for i, dev in enumerate((at.y, at.x, at.core))]

    def f(self, t):
        at, view = self.at, self.views[t]
        half = at.ny // 2
        self.bs[t][0].wait_recv()
        f1 = self.push(t, 3, view(at.d, 1 - at.h, at.c, 0, half), at.x)
        c1 = self.push(t, 4, view(at.d, 1 - at.h, at.c, 0, at.ny), at.core)
        self.bs[t][1].wait_recv()
        f2 = self.push(t, 5, view(1 - at.d, at.h, at.c, half, at.ny - half), at.y)
        c2 = self.push(t, 6, view(1 - at.d, at.h, at.c, 0, at.ny), at.core)
        self.fs[t] = [f1, c1, f2, c2]

    def c(self, t):
        at = self.at
        self.fs[t][0].wait_recv()
        self.fs[t][2].wait_recv()
        self.cs[t] = self.push(t, 7, self.views[t](1 - at.d, 1 - at.h, at.c, 0, at.ny), at.core)

    def arrived(self, t):
        for cp in (self.bs[t][2], self.fs[t][1], self.fs[t][3], self.cs[t]):
            cp.wait_recv()

    def sent(self, t):
        for cp in self.zs[t][1] + self.bs[t] + self.fs[t] + [self.cs[t]]:
            cp.wait_send()


class Table:
    def __init__(self, at, total, landing, send, recv):
        self.at, self.total, self.landing, self.send, self.recv = at, total, landing, send, recv
        self.stages = [at.plane, at.z]
        self.flight, self.slot = [], 0

    @staticmethod
    def scratch(shape, ny, dtype):
        return [
            pltpu.VMEM((ny + 6,) + shape, dtype), pltpu.VMEM((2,) + shape, dtype),
            pltpu.SemaphoreType.DMA((ny + 6,)), pltpu.SemaphoreType.DMA((ny + 6,)),
        ]

    def step(self, k):
        if k > 0:
            value = self.total[k - 1].astype(F32)
            for cp, slot in self.flight[k - 1]:
                cp.wait_recv()
                value = value + self.landing[slot].astype(F32)
            if k < len(self.stages):
                self.total[k] = value.astype(self.total.dtype)
            else:
                self.result = value
                return
        copies = []
        for dev in self.stages[k]:
            slot = self.slot
            self.slot += 1
            cp = remote(self.total.at[k], self.landing.at[slot], self.send.at[slot], self.recv.at[slot], dev)
            cp.start()
            copies.append((cp, slot))
        self.flight.append(copies)

    def sent(self):
        for copies in self.flight:
            for cp, _ in copies:
                cp.wait_send()


class Scatter:
    def __init__(self, at, units, buffers, sems):
        self.at, self.units, self.n = at, units, len(units)
        self.bufs = buffers
        self.lsem, self.csend, self.crecv, self.bsend, self.brecv, self.zsend, self.zrecv = sems
        d, h = at.d, at.h
        self.quads = [(1 - d, 1 - h), (d, 1 - h), (1 - d, h), (d, h)]
        self.cs, self.fars, self.nears, self.zs = {}, {}, {}, {}

    @staticmethod
    def buffers(k, rows, cols, ny):
        return [
            pltpu.VMEM((lead, n * k, rows, cols), BF)
            for lead, n in ((4, ny), (4, ny), (2, ny // 2), (2, ny), (ny - 1, 1))
        ]

    @staticmethod
    def semaphores(n, ny):
        lead = (4, 4, 4, 4, 4, ny - 1, ny - 1)
        return [pltpu.SemaphoreType.DMA((n, k)) for k in lead]

    def add(self, dst, src, pieces):
        lead = dst.shape[0] // pieces

        def body(i, carry):
            part = pl.ds(i * lead, lead)
            dst[part] = (dst[part].astype(F32) + src[part].astype(F32)).astype(dst.dtype)
            return carry

        lax.fori_loop(0, pieces, body, 0)

    def core(self, t):
        view, (sums, rc) = self.units[t][0], self.bufs[t][:2]
        c = self.at.c
        res = []
        for q, (d, h) in enumerate(self.quads):
            cp = remote(
                view(d, h, 1 - c), rc.at[q], self.csend.at[t, q], self.crecv.at[t, q], self.at.core
            )
            cp.start()
            lc = pltpu.make_async_copy(view(d, h, c), sums.at[q], self.lsem.at[t, q])
            lc.start()
            res.append((cp, lc))
        self.cs[t] = res

    def far(self, t):
        sums, rc, rs = self.bufs[t][:3]
        ny, k = self.at.ny, self.units[t][1]
        cut = ny // 2 * k
        res = []
        for q in range(4):
            self.cs[t][q][0].wait_recv()
            self.cs[t][q][1].wait()
            self.add(sums.at[q], rc.at[q], ny)
            if q == 0:
                for i, (lo, dev) in enumerate(((0, self.at.x), (cut, self.at.y))):
                    cp = remote(
                        sums.at[0, lo : lo + cut], rs.at[i], self.bsend.at[t, i], self.brecv.at[t, i], dev
                    )
                    cp.start()
                    res.append(cp)
        self.fars[t] = res

    def near(self, t):
        sums, _, rs, rl = self.bufs[t][:4]
        ny, k = self.at.ny, self.units[t][1]
        cut = ny // 2 * k
        res = []
        for i, (lo, dev) in enumerate(((0, self.at.y), (cut, self.at.x))):
            self.fars[t][i].wait_recv()
            self.add(sums.at[1 + i, lo : lo + cut], rs.at[i], ny // 2)
            cp = remote(sums.at[1 + i], rl.at[i], self.bsend.at[t, 2 + i], self.brecv.at[t, 2 + i], dev)
            cp.start()
            res.append(cp)
        self.nears[t] = res

    def z(self, t):
        sums, rl, rz = self.bufs[t][0], self.bufs[t][3], self.bufs[t][4]
        at, n = self.at, self.units[t][1]
        for i in range(2):
            self.nears[t][i].wait_recv()
            self.add(sums.at[3], rl.at[i], at.ny)
        res = []
        for k, dev in enumerate(at.z):
            cp = remote(
                sums.at[3, pl.ds(dev[2] * n, n)], rz.at[k], self.zsend.at[t, k], self.zrecv.at[t, k], dev
            )
            cp.start()
            res.append(cp)
        self.zs[t] = res

    def finish(self, t):
        sums, rz = self.bufs[t][0], self.bufs[t][4]
        n = self.units[t][1]
        total = sums[3, pl.ds(self.at.g * n, n)].astype(F32)
        for k, cp in enumerate(self.zs[t]):
            cp.wait_recv()
            total = total + rz[k].astype(F32)
        self.units[t][2](total)

    def sent(self, t):
        for q in range(4):
            self.cs[t][q][0].wait_send()
        for cp in self.fars[t] + self.nears[t] + self.zs[t]:
            cp.wait_send()


GROUPS = ((0, 128), (128, 256), (384, 256), (640, 128))
NG = len(GROUPS)
PARTS = 3


def att_view(ref, tiles, sizes):
    nd, nh, ny = sizes

    def view(d, h, c, lo, n):
        return ref.at[pl.ds((((d * nh + h) * 2 + c) * ny + lo) * tiles, n * tiles)]

    return view


def ff_view(ref, part):
    def view(d, h, c, lo, n):
        start = pl.multiple_of((h * 2 + c) * part, part)
        return ref.at[d, pl.ds(lo, n), :, pl.ds(start, part)]

    return view


def copies_of(sem, *pairs):
    made = [pltpu.make_async_copy(a, b, sem.at[i]) for i, (a, b) in enumerate(pairs)]
    for cp in made:
        cp.start()
    return made


def columns_of(seg_row):
    return jnp.broadcast_to(seg_row, (128, seg_row.shape[1])).T[:, 0:1]


def turn(dst_ref, src_ref):
    total, width = src_ref.shape
    step = 256
    eye = jnp.where(
        lax.broadcasted_iota(jnp.int32, (step, step), 0) == lax.broadcasted_iota(jnp.int32, (step, step), 1), 1.0, 0.0
    ).astype(BF)
    for lo, size in row_pieces(total, step):
        for j in range(width // step):
            cols = slice(j * step, (j + 1) * step)
            dst_ref[cols, lo : lo + size] = nt(eye, src_ref[lo : lo + size, cols]).astype(BF)


def mask_into(bias_ref, segp_ref, s):
    row = segp_ref[s : s + 1, :]
    bias_ref[...] = jnp.where(columns_of(row) == row, 0.0, -1e30).astype(F32)


def segments_into(segp_ref, seg_ref):
    strips, length = seg_ref.shape
    segp_ref[...] = jnp.full(segp_ref.shape, -1.0, F32)
    segp_ref[0:strips, 0:length] = seg_ref[...].astype(F32)


def attend_pair(qkv_ref, o_ref, lse_ref, bias_ref, s, lp, base, gw, out_col):
    head = out_col // HD
    qrows = lp // 2
    lane = lax.broadcasted_iota(jnp.int32, (qrows, 128), 1)
    first = lane < HD
    scale = 0.125 * LOG2E
    off = s * lp
    k = qkv_ref[off : off + lp, base + gw : base + gw + 128]
    v = qkv_ref[off : off + lp, base + 2 * gw : base + 2 * gw + 128]
    for part in range(2):
        lo = part * qrows
        q = qkv_ref[off + lo : off + lo + qrows, base : base + 128]
        lse = lse_ref[s, lo : lo + qrows, :]
        res = []
        for j in range(2):
            keep = first if j == 0 else jnp.logical_not(first)
            z = nt(jnp.where(keep, q, jnp.zeros_like(q)), k) * scale + bias_ref[s, lo : lo + qrows, :]
            top = jnp.max(z, axis=-1, keepdims=True)
            e = jnp.exp2(z - top)
            total = jnp.sum(e, axis=-1, keepdims=True)
            res.append(nn(e.astype(BF), v) / total)
            lse = jnp.where(lane == head + j, top + jnp.log2(total), lse)
        o_ref[off + lo : off + lo + qrows, out_col : out_col + 128] = jnp.where(first, res[0], res[1]).astype(BF)
        lse_ref[s, lo : lo + qrows, :] = lse


def front_kernel(
    sizes, x_hbm, do_hbm, seg_ref, wq, wk, wv, wo, up, down, small_ref,
    lt_ref, table_ref, gsum_ref, qkv_out, mixed_out, nT_out, dout_out, doutT_out, xp_out, watt_out, wo_out, up_out, down_out, zb_out,
    x_ref, do_ref, xhat_ref, norm_ref, shard_ref, watt_ref, bias_row, lse_ref, bias_ref, segp_ref,
    qkv_ref, mixed_ref, nT_ref, dout_ref, doutT_ref, xp_ref,
    land_ref, tot_ref, tsend, trecv, lsem, osem, s_loc, s_zs, s_zr, s_bs, s_br, *land_w,
):
    nd, nh, ny = sizes
    length, strips, width = x_ref.shape
    lp = norm_ref.shape[0] // strips
    tiles = wq.shape[0]
    at = Place(ny)
    loads = [pltpu.make_async_copy(x_hbm, x_ref, lsem.at[0]), pltpu.make_async_copy(do_hbm, do_ref, lsem.at[1])]
    pieces = []
    for i, (first, gw) in enumerate(GROUPS):
        for j, w in enumerate((wq, wk, wv)):
            to = 3 * first + j * gw
            pieces.append(
                pltpu.make_async_copy(
                    w.at[:, :, first : first + gw], shard_ref.at[:, :, to : to + gw], lsem.at[2 + 3 * i + j]
                )
            )
    at.greet()
    for cp in pieces + loads:
        cp.start()
    at.greeted()
    tab = Table(at, tot_ref, land_ref, tsend, trecv)
    tot_ref[0] = small_ref[...].astype(BF)
    for cp in pieces:
        cp.wait()
    pw = up.shape[-1] // PARTS
    views = [att_view(land, tiles, sizes) for land in land_w] + [att_view(wo_out, tiles, sizes)]
    shards = [shard_ref.at[:, :, 3 * first : 3 * (first + gw)] for first, gw in GROUPS]
    shards += [wo, up.at[:, :, 0:pw], down.at[:, :, 0:pw]]
    views += [ff_view(up_out, pw), ff_view(down_out, pw)]
    n_full = len(shards)
    for b in range(1, PARTS):
        for w in (up, down):
            views.append(lambda d, h, c, lo, n, t=len(shards) - n_full: zb_out.at[t, pl.ds(lo, n)])
            shards.append(w.at[:, :, b * pw : (b + 1) * pw])
    gat = Gather(at, shards, views, (s_loc, s_zs, s_zr, s_bs, s_br))

    stop = stops(FRONT_PLAN, z=gat.z, b=gat.b, f=gat.f, c=gat.c, A=gat.arrived, t=tab.step, Y=gat.along_z)

    def hats(s):
        for lo, size in row_pieces(length, 136):
            part = slice(s * lp + lo, s * lp + lo + size)
            rows = x_ref[lo : lo + size, s, :]
            xp_ref[part, :] = rows
            xhat_ref[part, :], _ = normalise(rows.astype(F32))

    stop()
    for cp in loads:
        cp.wait()
    hats(0)
    stop()
    for s in range(1, strips):
        hats(s)
    stop()
    segments_into(segp_ref, seg_ref)
    for s in range(strips):
        mask_into(bias_ref.at[s], segp_ref, s)
    lse_ref[...] = jnp.zeros(lse_ref.shape, F32)
    stop()
    gsum = jnp.zeros((1, width), F32)
    for s in range(strips):
        for lo, size in row_pieces(length, 136):
            rows = do_ref[lo : lo + size, s, :]
            dout_ref[s * lp + lo : s * lp + lo + size, :] = rows
            gsum = gsum + colsum(rows.astype(F32))
        tail = slice(s * lp + length, (s + 1) * lp)
        dout_ref[tail, :] = jnp.zeros((lp - length, width), BF)
        xp_ref[tail, :] = jnp.zeros((lp - length, width), BF)
    gsum_ref[...] = jnp.broadcast_to(gsum, gsum_ref.shape)
    stop()
    turn(doutT_ref, dout_ref)
    outs = copies_of(osem, (dout_ref, dout_out), (doutT_ref, doutT_out))
    outs += copies_of(osem.at[4 + 2 * NG :], (xp_ref, xp_out))
    stop()
    table = tab.result
    table_ref[...] = table
    gain, shift = table[G1 : G1 + 1, :], table[S1 : S1 + 1, :]
    for s in range(strips):
        for lo, size in row_pieces(length, 136):
            part = slice(s * lp + lo, s * lp + lo + size)
            norm_ref[part, :] = (xhat_ref[part, :] * gain + shift).astype(BF)
        norm_ref[s * lp + length : (s + 1) * lp, :] = jnp.zeros((lp - length, width), BF)
    for first, gw in GROUPS:
        cols = slice(first, first + gw)
        bias_row[0:1, 3 * first : 3 * first + gw] = table[QB : QB + 1, cols]
        bias_row[0:1, 3 * first + gw : 3 * first + 2 * gw] = jnp.zeros((1, gw), F32)
        bias_row[0:1, 3 * first + 2 * gw : 3 * (first + gw)] = table[VB : VB + 1, cols]
    for i, (first, gw) in enumerate(GROUPS):
        stop()
        wide = slice(3 * first, 3 * (first + gw))

        def settle(n, carry):
            rows = pl.ds(pl.multiple_of(n * 64, 64), 64)
            watt_ref[rows, wide] = land_w[i][pl.ds(n * 8, 8)].astype(F32).reshape(64, 3 * gw).astype(BF)
            return carry

        lax.fori_loop(0, width // 64, settle, 0)

        def project(n, carry):
            cols = pl.ds(pl.multiple_of(3 * first + n * gw, 128), gw)
            qkv_ref[:, cols] = (nn(norm_ref[...], watt_ref[:, cols]) + bias_row[0:1, cols]).astype(BF)
            return carry

        lax.fori_loop(0, 3, project, 0)
        outs += copies_of(
            osem.at[2 + 2 * i : 4 + 2 * i],
            (qkv_ref.at[:, wide], qkv_out.at[:, wide]), (watt_ref.at[:, wide], watt_out.at[:, wide]),
        )
        for s in range(strips):
            for p in range(gw // 128):
                stop()
                attend_pair(
                    qkv_ref, mixed_ref, lse_ref, bias_ref, s, lp, 3 * first + p * 128, gw, first + p * 128
                )
        if i == 0:
            stop()
            turn(nT_ref, norm_ref)
            outs += copies_of(osem.at[2 + 2 * NG : 3 + 2 * NG], (nT_ref, nT_out))
    stop()
    outs += copies_of(osem.at[3 + 2 * NG : 4 + 2 * NG], (mixed_ref, mixed_out))
    for s in range(strips):
        lt_ref[s] = lse_ref[s].T[0:16, :]
    stop()
    for t in range(n_full):
        gat.sent(t)
    tab.sent()
    for cp in outs:
        cp.wait()


FRONT_PLAN = (
    ("z0", "t0", "z1"), ("z2", "b0"), ("b1", "z3", "t1"), ("f0", "z5", "b2"), ("b3",), ("z6", "f1", "c0", "t2"),
    ("f2", "A0"), ("z4",), ("b5",), ("c1",),
    ("c2", "f3", "A1"), ("b6",), ("z7",), ("b4", "A2"), ("z8",),
    (), ("f5",), ("f6", "z9"), ("c3",), ("A3", "z10"),
    ("f4",), ("c5",), ("c6", "A5"), ("A6", "c4"), ("A4", "Y7", "Y8", "Y9", "Y10"),
)


MIDDLE_PLAN = (
    ("b1",), ("b0",), (),
    (), (), ("f1", "f0", "b3"), ("c1", "b2", "K1"), ("A1", "c0"),
    ("A0",), ("f3", "F1"), ("f2", "K0"), ("F0", "c3"), ("A3", "c2", "N1"),
    ("A2",), ("N0",), ("Z1",), (), (),
    ("Z0",), (), ("E1",), ("E0",),
)


def middle_kernel(
    sizes, x_ref, mix_ref, wo_ref, v_ref, gsum_ref, dout_hbm, doutT_hbm, u0, d0, zb,
    mg_ref, gwo_ref, gv_ref, gu_ref, gd_ref, y_out, rg_out, *out_parts_and_scratch,
):
    middle_body(
        sizes, x_ref, mix_ref, wo_ref, v_ref, gsum_ref, dout_hbm, doutT_hbm, u0, d0, zb,
        mg_ref, gwo_ref, gv_ref, gu_ref, gd_ref, y_out, rg_out,
        out_parts_and_scratch[: 2 * (PARTS - 1)], *out_parts_and_scratch[2 * (PARTS - 1) :],
    )


def middle_body(
    sizes, x_ref, mix_ref, wo_ref, v_ref, gsum_ref, dout_hbm, doutT_hbm, u0, d0, zb,
    mg_ref, gwo_ref, gv_ref, gu_ref, gd_ref, y_out, rg_out, later,
    dout_ref, doutT_ref, sec_ref, secT_ref, res_ref, acc_ref, rg_ref, hid_ref, pre_ref, y_ref, wu, wd, pu, pd,
    lsem, osem, s_loc, s_zs, s_zr, s_bs, s_br, *rest,
):
    nd, nh, ny = sizes
    nq = nh * 2
    length, strips, width = y_ref.shape
    lp = mix_ref.shape[0] // strips
    rows, part = zb.shape[2], zb.shape[3]
    at = Place(ny)
    at.greet()
    loads = copies_of(lsem, (dout_hbm, dout_ref), (doutT_hbm, doutT_ref), (u0, wu.at[0]), (d0, wd.at[0]))
    n_sc = 2
    views, units = [], []
    for b in range(1, PARTS):
        views += [ff_view(wu.at[b], part), ff_view(wd.at[b], part)]
    for src, dst in ((pu, gu_ref), (pd, gd_ref)):

        def put(total, dst=dst):
            dst[...] = total[0]

        whole = ff_view(src, part)
        units.append(((lambda d, h, c, whole=whole: whole(d, h, c, 0, ny)), 1, put))
    gat = Gather(at, views, views, (s_loc, s_zs, s_zr, s_bs, s_br))
    for t in range(gat.n):
        gat.ready(t, zb.at[t])
    sca = Scatter(at, units, [rest[5 * t : 5 * t + 5] for t in range(n_sc)], rest[5 * n_sc :])
    stop = stops(
        MIDDLE_PLAN, b=gat.b, f=gat.f, c=gat.c, A=gat.arrived,
        K=sca.core, F=sca.far, N=sca.near, Z=sca.z, E=sca.finish,
    )

    step = 256
    bias_o, gain, shift = v_ref[OB : OB + 1, :], v_ref[G2 : G2 + 1, :], v_ref[S2 : S2 + 1, :]
    gv_ref[...] = jnp.zeros(gv_ref.shape, F32)
    gv_ref[DB : DB + 1, :] = gsum_ref[0:1, :]

    def proj(i, carry):
        cols = pl.ds(pl.multiple_of(i * step, step), step)
        acc_ref[:, cols] = nn(mix_ref[...], wo_ref[:, cols])
        return carry

    lax.fori_loop(0, width // step, proj, 0)
    at.greeted()
    for s in range(strips):
        stop()
        for lo, size in row_pieces(length, 136):
            sel = slice(s * lp + lo, s * lp + lo + size)
            residual = x_ref[sel, :].astype(F32) + (acc_ref[sel, :] + bias_o)
            res_ref[sel, :] = residual
            xhat, _ = normalise(residual)
            sec_ref[sel, :] = (xhat * gain + shift).astype(BF)
            acc_ref[sel, :] = residual + v_ref[DB : DB + 1, :]
        sec_ref[s * lp + length : (s + 1) * lp, :] = jnp.zeros((lp - length, width), BF)
    stop()
    turn(secT_ref, sec_ref)
    for cp in loads:
        cp.wait()

    outs = []
    block = strips * lp // 8
    for b in range(PARTS):

        def hidden(q, carry):
            cols = pl.ds(pl.multiple_of(q * part, part), part)
            w_up = wu[b, :, :, :, cols].reshape(width, part)
            w_down = wd[b, :, :, :, cols].reshape(width, part)
            csum = jnp.zeros((1, part), F32)
            for r in range(8):
                rs = slice(r * block, (r + 1) * block)
                pre = nn(sec_ref[rs, :], w_up) + v_ref[pl.ds(UB0 + q, 1), b * part : (b + 1) * part]
                hg = nn(dout_ref[rs, :], w_down)
                cdf = 0.5 + 0.5 * lax.erf(pre * INV_SQRT2)
                pdf = jnp.exp(-0.5 * pre * pre) * INV_SQRT_2PI
                hid_ref[rs, cols] = (pre * cdf).astype(BF)
                pg = (hg * (cdf + pre * pdf)).astype(BF)
                pre_ref[rs, cols] = pg
                csum = csum + colsum(pg.astype(F32))
            gv_ref[pl.ds(UB0 + q, 1), b * part : (b + 1) * part] = csum
            return carry

        g_up, g_down = (pu, pd) if b == 0 else (wu.at[b - 1], wd.at[b - 1])

        def grads(d):
            rs = slice(d * ny * rows, (d + 1) * ny * rows)
            g_down[d] = nn(doutT_ref[rs, :], hid_ref[...]).astype(BF).reshape((ny, rows, nq * part))
            g_up[d] = nn(secT_ref[rs, :], pre_ref[...]).astype(BF).reshape((ny, rows, nq * part))

        stop()
        lax.fori_loop(0, nq // 2, hidden, 0)
        stop()
        lax.fori_loop(nq // 2, nq, hidden, 0)
        stop()
        if b > 1:
            gat.sent(2 * b - 4)
            gat.sent(2 * b - 3)
        for q in range(nd):
            grads(q)
        if b > 0:
            outs += copies_of(
                osem.at[2 * b : 2 * b + 2], (g_up, later[2 * b - 2]), (g_down, later[2 * b - 1])
            )
        stop()
        w_down = wd[b].reshape(width, nq * part)
        for n in range(strips):
            rs = slice(n * lp, (n + 1) * lp)
            acc_ref[rs, :] += nt(hid_ref[rs, :], w_down)
        stop()
        w_up = wu[b].reshape(width, nq * part)
        for n in range(strips):
            rs = slice(n * lp, (n + 1) * lp)
            value = nt(pre_ref[rs, :], w_up)
            rg_ref[rs, :] = value if b == 0 else rg_ref[rs, :] + value

    for s in range(strips):
        stop()
        for lo, size in row_pieces(length, 136):
            sel = slice(s * lp + lo, s * lp + lo + size)
            y_ref[lo : lo + size, s, :] = acc_ref[sel, :].astype(BF)
            xhat, scale = normalise(res_ref[sel, :])
            grad = rg_ref[sel, :]
            gv_ref[G2 : G2 + 1, :] += colsum(grad * xhat)
            gv_ref[S2 : S2 + 1, :] += colsum(grad)
            rg = dout_ref[sel, :].astype(F32) + norm_back(grad, gain, xhat, scale)
            rg_ref[sel, :] = rg
            low = rg.astype(BF)
            sec_ref[sel, :] = low
            gv_ref[OB : OB + 1, :] += colsum(low.astype(F32))
        tail = slice(s * lp + length, (s + 1) * lp)
        sec_ref[tail, :] = jnp.zeros((lp - length, width), BF)
        rg_ref[tail, :] = jnp.zeros((lp - length, width), F32)
    outs += copies_of(osem.at[0:2], (rg_ref, rg_out), (y_ref, y_out))
    turn(secT_ref, mix_ref)
    stop()

    def last(i, carry):
        sel = pl.ds(pl.multiple_of(i * step, step), step)
        mg_ref[:, sel] = nt(sec_ref[...], wo_ref[sel, :]).astype(BF)
        gwo_ref[sel, :] = nn(secT_ref[sel, :], sec_ref[...]).astype(BF)
        return carry

    lax.fori_loop(0, width // step, last, 0)
    stop()
    for t in range(2 * (PARTS - 2), gat.n):
        gat.sent(t)
    for t in range(n_sc):
        sca.sent(t)
    for cp in outs:
        cp.wait()


def attend_back_pair(
    qkv_ref, mg_ref, dz_ref, bias_ref, lt_ref, dt_ref, kt_ref, s, lp, base, gw, out_col, dst
):
    head = out_col // HD
    first = lax.broadcasted_iota(jnp.int32, (lp, 128), 1) < HD
    scale = 0.125 * LOG2E
    rows = slice(s * lp, (s + 1) * lp)
    q = qkv_ref[rows, base : base + 128]
    k = qkv_ref[rows, base + gw : base + gw + 128]
    v = qkv_ref[rows, base + 2 * gw : base + 2 * gw + 128]
    do = mg_ref[rows, out_col : out_col + 128]
    kt_ref[...] = k.astype(F32).T.astype(BF)
    dq, dk, dv = [], [], []
    for j in range(2):
        keep = first if j == 0 else jnp.logical_not(first)
        lse = lt_ref[s, head + j : head + j + 1, :]
        delta = dt_ref[s, head + j : head + j + 1, :]
        z = nt(jnp.where(keep, k, jnp.zeros_like(k)), q) * scale + bias_ref[s]
        prob = jnp.exp2(z - lse)
        pg = nt(jnp.where(keep, v, jnp.zeros_like(v)), do)
        sg = (prob * (pg - delta)).astype(BF)
        dv.append(nn(prob.astype(BF), do))
        dk.append(nn(sg, q))
        dq.append(nn(kt_ref[j * HD : (j + 1) * HD, :], sg))
    dz_ref[rows, dst + 2 * gw : dst + 2 * gw + 128] = jnp.where(first, dv[0], dv[1]).astype(BF)
    dz_ref[rows, dst + gw : dst + gw + 128] = (0.125 * jnp.where(first, dk[0], dk[1])).astype(BF)
    dz_ref[rows, dst : dst + 128] = (0.125 * jnp.concatenate(dq, axis=0)).T.astype(BF)


BACK_PLAN = (
    ("K0", "t0"), ("K1", "F0"), ("K7", "F1"), ("K3",),
    ("F7", "F3"), ("K8", "K2", "N1"), (), ("F8", "N7"), ("t1",), ("N3",),
    ("N8", "Z1"), ("K4",), ("F2", "Z7"), ("N0",), ("F4", "Z3"), ("N2", "K5", "Z8"),
    ("F5",), ("Z0", "N4"), ("E3",), ("K6", "t2", "N5", "Z2"),
    (), ("Z4", "F6", "E0"), ("E8", "u0", "Z5", "E7", "N6", "u1"), ("E1", "E2", "E4", "Z6", "E5", "u2", "E6"),
)


def back_kernel(
    sizes, gu1, gd1, gu2, gd2, gwo, seg_ref, lt_ref, v_ref, gvm_ref, gu0_ref, gd0_ref,
    mg_hbm, mix_hbm, qkv_hbm, nT_hbm, watt_hbm, x_hbm, rg_hbm,
    gx_ref, gq_ref, gk_ref, gv_ref, go_ref, gu_ref, gd_ref, gtab_ref,
    mg_ref, mix_ref, qkv_ref, nT_ref, watt_ref, x_ref, rg_ref,
    dz_ref, ng_ref, bias_ref, segp_ref, dt_ref, kt_ref, tab_ref,
    land_ref, tot_ref, tsend, trecv, land2_ref, tot2_ref, tsend2, trecv2, isem,
    *rest,
):
    nd, nh, ny = sizes
    length, strips, width = gx_ref.shape
    lp = qkv_ref.shape[0] // strips
    parts, rest = rest[:NG], rest[NG:]
    at = Place(ny)
    at.greet()
    loads = copies_of(
        isem, (mg_hbm, mg_ref), (mix_hbm, mix_ref),
        *[
            (qkv_hbm.at[:, 3 * first : 3 * (first + gw)], qkv_ref.at[:, 3 * first : 3 * (first + gw)])
            for first, gw in GROUPS
        ],
        (nT_hbm, nT_ref), (watt_hbm, watt_ref), (x_hbm, x_ref), (rg_hbm, rg_ref),
    )
    n = 5 + NG
    bufs = [rest[5 * t : 5 * t + 5] for t in range(n)]
    sems = rest[5 * n :]
    pw = gu1.shape[-1] // (2 * nh)
    units = []

    def ff_unit(src, dst, cols):
        whole = ff_view(src, pw)

        def put(total):
            dst[:, cols] = total[0]

        return lambda d, h, c: whole(d, h, c, 0, ny), 1, put

    one, two = slice(pw, 2 * pw), slice(2 * pw, 3 * pw)
    units += [ff_unit(gu2, gu_ref, two), ff_unit(gd2, gd_ref, two)]
    tiles = gq_ref.shape[0] // 8

    def att_unit(src, put):
        inner = att_view(src, tiles, sizes)
        return lambda d, h, c: inner(d, h, c, 0, ny), tiles, put

    def put_out(total):
        go_ref[...] = total.reshape(go_ref.shape)

    units.append(att_unit(gwo, put_out))
    for i, (first, gw) in enumerate(GROUPS):

        def put_group(total, first=first, gw=gw):
            for j, ref in enumerate((gq_ref, gk_ref, gv_ref)):
                ref[:, first : first + gw] = total[:, :, j * gw : (j + 1) * gw].reshape(-1, gw)

        units.append(att_unit(parts[i], put_group))
    units += [ff_unit(gu1, gu_ref, one), ff_unit(gd1, gd_ref, one)]
    sca = Scatter(at, units, bufs, sems)
    early = Table(at, tot_ref, land_ref, tsend, trecv)
    late = Table(at, tot2_ref, land2_ref, tsend2, trecv2)
    stop = stops(
        BACK_PLAN, K=sca.core, F=sca.far, N=sca.near, Z=sca.z, E=sca.finish, t=early.step, u=late.step
    )
    tot_ref[0] = jnp.concatenate([gvm_ref[OB : DB + 1, :], gvm_ref[UB0 : UB0 + 4, :]]).astype(BF)
    gu_ref[:, 0:pw] = gu0_ref[...]
    gd_ref[:, 0:pw] = gd0_ref[...]
    segments_into(segp_ref, seg_ref)
    heads = lax.broadcasted_iota(jnp.int32, (16, width), 0)
    pick = jnp.where(heads == lax.broadcasted_iota(jnp.int32, (16, width), 1) // HD, 1.0, 0.0).astype(BF)
    for s in range(strips):
        mask_into(bias_ref.at[s], segp_ref, s)
    loads[0].wait()
    loads[1].wait()
    for s in range(strips):
        part = slice(s * lp, (s + 1) * lp)
        prod = mg_ref[part, :].astype(F32) * mix_ref[part, :].astype(F32)
        high = prod.astype(BF)
        dt_ref[s] = nt(pick, high) + nt(pick, (prod - high.astype(F32)).astype(BF))
    at.greeted()
    for i, (first, gw) in enumerate(GROUPS):
        loads[2 + i].wait()
        for s in range(strips):
            for p in range(gw // 128):
                stop()
                attend_back_pair(
                    qkv_ref, mg_ref, dz_ref, bias_ref, lt_ref, dt_ref, kt_ref, s, lp,
                    3 * first + p * 128, gw, first + p * 128, p * 128,
                )
        cols = slice(first, first + gw)
        tab_ref[QB : QB + 1, cols] = colsum(dz_ref[:, 0:gw].astype(F32))
        tab_ref[VB : VB + 1, cols] = colsum(dz_ref[:, 2 * gw : 3 * gw].astype(F32))
        if i == 0:
            loads[2 + NG].wait()
            loads[3 + NG].wait()

        def grads(j, carry):
            c = pl.ds(pl.multiple_of(j * gw, gw), gw)
            parts[i][:, :, c] = nn(nT_ref[...], dz_ref[:, c]).reshape(width // 8, 8, gw).astype(BF)
            return carry

        stop()
        lax.fori_loop(0, 3, grads, 0)
        stop()

        def to_norm(j, carry):
            c = pl.ds(pl.multiple_of(j * 256, 256), 256)
            value = nt(dz_ref[:, 0 : 3 * gw], watt_ref[c, 3 * first : 3 * (first + gw)])
            ng_ref[:, c] = value if i == 0 else ng_ref[:, c] + value
            return carry

        lax.fori_loop(0, width // 256, to_norm, 0)
    gain = v_ref[G1 : G1 + 1, :]
    loads[4 + NG].wait()
    loads[5 + NG].wait()
    g_gain, g_shift = jnp.zeros((1, width), F32), jnp.zeros((1, width), F32)
    for s in range(strips):
        stop()
        for lo, size in row_pieces(length, 136):
            part = slice(s * lp + lo, s * lp + lo + size)
            xhat, scale = normalise(x_ref[part, :].astype(F32))
            grad = ng_ref[part, :]
            g_gain = g_gain + colsum(grad * xhat)
            g_shift = g_shift + colsum(grad)
            term = norm_back(grad, gain, xhat, scale)
            gx_ref[lo : lo + size, s, :] = (rg_ref[part, :] + term).astype(BF)
    tot2_ref[0] = jnp.concatenate(
        [g_gain, g_shift, tab_ref[QB : VB + 1, :], jnp.zeros((4, width), F32)]
    ).astype(BF)
    stop()
    stop()
    sums, ends = early.result, late.result
    gtab_ref[G1 : VB + 1, :] = ends[0:4]
    gtab_ref[OB : DB + 1, :] = sums[0:4]
    gtab_ref[UB0 : UB0 + 4, :] = sums[4:8]
    gtab_ref[UB0 + 4 :, :] = jnp.zeros((gtab_ref.shape[0] - UB0 - 4, width), F32)
    for t in range(n):
        sca.sent(t)
    early.sent()
    late.sent()


def own_path(sizes, args):
    (
        block_input, segment_ids, out_grad, query_weight, key_weight, value_weight, output_weight, small,
        up_weight, down_weight,
    ) = args
    nd, nx, ny = sizes
    nh = nx // 2
    grid3 = (nd, nh, ny)
    strips, length, width = block_input.shape
    units = up_weight.shape[1]
    att_rows, ff_rows = query_weight.shape[0], up_weight.shape[0]
    lp = padded(length)
    tiles = att_rows // 8
    part = units // PARTS
    total = strips * lp
    full, wide, turned = (total, width), (total, 3 * width), (width, total)
    n_tab = small.shape[0]
    ff_shape = (nd, ny, ff_rows, nx * part)
    n_later = 2 * (PARTS - 1)
    t_shape = (length, strips, width)
    watt_shape = (width, 3 * width)
    lt_shape = (strips, 16, lp)
    dma = pltpu.SemaphoreType.DMA
    ups, downs = up_weight[None], down_weight[None]
    (
        lt, table, gsum, qkv, mixed, nT, dout, doutT, xp, watt, wo, u0, d0, zb,
    ) = pl.pallas_call(
        functools.partial(front_kernel, grid3),
        out_shape=[
            sds(lt_shape, F32), sds((n_tab, width), F32), sds((8, width), F32), sds(wide, BF), sds(full, BF),
            sds(turned, BF), sds(full, BF), sds(turned, BF), sds(full, BF), sds(watt_shape, BF),
            sds((width // 8, 8, width), BF), sds(ff_shape, BF), sds(ff_shape, BF),
            sds((n_later, ny, ff_rows, part), BF),
        ],
        in_specs=[ANY, ANY, VM] + [ANY] * 6 + [VM],
        out_specs=[VM] * 3 + [ANY] * 11,
        scratch_shapes=[
            pltpu.VMEM(t_shape, BF), pltpu.VMEM(t_shape, BF), pltpu.VMEM(full, F32), pltpu.VMEM(full, BF),
            pltpu.VMEM((tiles, 8, 3 * width), BF), pltpu.VMEM(watt_shape, BF), pltpu.VMEM((8, 3 * width), F32), pltpu.VMEM((strips, lp, 128), F32),
            pltpu.VMEM((strips, lp, lp), F32), pltpu.VMEM((8, lp), F32),
            pltpu.VMEM(wide, BF), pltpu.VMEM(full, BF), pltpu.VMEM(turned, BF), pltpu.VMEM(full, BF),
            pltpu.VMEM(turned, BF), pltpu.VMEM(full, BF),
        ]
        + Table.scratch((n_tab, width), ny, BF)
        + [dma((2 + 3 * NG,)), dma((5 + 2 * NG,))]
        + Gather.semaphores(NG + 3, ny, n_later)
        + [pltpu.VMEM((width // 8, 8, 3 * gw), BF) for _, gw in GROUPS],
        compiler_params=pltpu.CompilerParams(collective_id=0, has_side_effects=True, vmem_limit_bytes=LIMIT),
    )(
        block_input.transpose(1, 0, 2), out_grad.transpose(1, 0, 2), segment_ids,
        *(w.reshape(tiles, 8, width) for w in (query_weight, key_weight, value_weight, output_weight)),
        ups, downs, small,
    )

    n_sc = 2
    some = (ff_rows, part)
    buffers = []
    for _ in range(n_sc):
        buffers += Scatter.buffers(1, ff_rows, part, ny)
    mg, gwo, gvm, gu0, gd0, y, rg, gu1, gd1, gu2, gd2 = pl.pallas_call(
        functools.partial(middle_kernel, grid3),
        out_shape=[
            sds(full, BF), sds((width, width), BF), sds((n_tab, width), F32), sds(some, F32), sds(some, F32),
            sds(t_shape, BF), sds(full, F32),
        ]
        + [sds(ff_shape, BF)] * n_later,
        in_specs=[VM] * 5 + [ANY] * 5,
        out_specs=[VM] * 5 + [ANY] * (2 + n_later),
        scratch_shapes=[
            pltpu.VMEM(full, BF), pltpu.VMEM(turned, BF), pltpu.VMEM(full, BF), pltpu.VMEM(turned, BF),
            pltpu.VMEM(full, F32), pltpu.VMEM(full, F32), pltpu.VMEM(full, F32),
            pltpu.VMEM((total, nx * part), BF), pltpu.VMEM((total, nx * part), BF), pltpu.VMEM(t_shape, BF),
        ]
        + [pltpu.VMEM((PARTS,) + ff_shape, BF)] * 2
        + [pltpu.VMEM(ff_shape, BF)] * 2
        + [dma((4,)), dma((2 + n_later,))]
        + Gather.semaphores(n_later, ny)
        + buffers
        + Scatter.semaphores(n_sc, ny),
        compiler_params=pltpu.CompilerParams(collective_id=1, has_side_effects=True, vmem_limit_bytes=LIMIT),
    )(xp, mixed, wo.reshape(width, width), table, gsum, dout, doutT, u0, d0, zb)

    n_units = 5 + NG
    buffers = []
    for _ in range(2):
        buffers += Scatter.buffers(1, ff_rows, part, ny)
    for cols in [width] + [3 * gw for _, gw in GROUPS]:
        buffers += Scatter.buffers(tiles, 8, cols, ny)
    for _ in range(2):
        buffers += Scatter.buffers(1, ff_rows, part, ny)
    gx, gq, gk, gv, go, gu, gd, gtab = pl.pallas_call(
        functools.partial(back_kernel, grid3),
        out_shape=[sds(t_shape, BF)] + [sds((att_rows, width), F32)] * 4 + [sds((ff_rows, units), F32)] * 2
        + [sds((n_tab, width), F32)],
        in_specs=[ANY] * 5 + [VM] * 6 + [ANY] * 7,
        out_specs=[VM] * 8,
        scratch_shapes=[
            pltpu.VMEM(full, BF), pltpu.VMEM(full, BF), pltpu.VMEM(wide, BF), pltpu.VMEM(turned, BF),
            pltpu.VMEM(watt_shape, BF), pltpu.VMEM(full, BF), pltpu.VMEM(full, F32),
            pltpu.VMEM(full, BF), pltpu.VMEM(full, F32), pltpu.VMEM((strips, lp, lp), F32), pltpu.VMEM((8, lp), F32), pltpu.VMEM(lt_shape, F32),
            pltpu.VMEM((128, lp), BF), pltpu.VMEM((n_tab, width), F32),
        ]
        + Table.scratch((8, width), ny, BF)
        + Table.scratch((8, width), ny, BF)
        + [dma((6 + NG,))]
        + [pltpu.VMEM((width // 8, 8, 3 * gw), BF) for _, gw in GROUPS]
        + buffers
        + Scatter.semaphores(n_units, ny),
        compiler_params=pltpu.CompilerParams(collective_id=2, has_side_effects=True, vmem_limit_bytes=LIMIT),
    )(
        gu1, gd1, gu2, gd2, gwo.reshape(width // 8, 8, width), segment_ids, lt, table, gvm, gu0, gd0,
        mg, mixed, qkv, nT, watt, xp, rg,
    )
    return y.transpose(1, 0, 2), gx.transpose(1, 0, 2), gq, gk, gv, go, gu, gd, gtab


def wide_path(sizes, args):
    (
        block_input, segment_ids, out_grad, query_weight, key_weight, value_weight, output_weight, table,
        up_weight, down_weight,
    ) = args
    nd, nx, ny = sizes
    strips, length, width = block_input.shape
    units = up_weight.shape[1]
    lp = padded(length)
    att = jnp.concatenate([query_weight, key_weight, value_weight, output_weight], axis=1)
    att = lax.all_gather(att, ALL, axis=0, tiled=True)
    up, down = (
        lax.all_gather(lax.all_gather(a, ("dp", "gy"), axis=0, tiled=True), "gx", axis=0)
        for a in (up_weight, down_weight)
    )
    w_qkv, w_out = att[:, : 3 * width], att[:, 3 * width :]
    seg = jnp.pad(segment_ids, ((0, 0), (0, lp - length)), constant_values=-1)
    seg_row, seg_col = seg[:, None, :], seg[:, :, None]
    full = (strips, lp, width)
    wide = (strips, lp, 3 * width)
    turned = (strips, width, lp)
    qkv, normed = call(
        qkv_kernel, [sds(wide, BF), sds(full, BF)], 3, [pltpu.VMEM((8, 3 * width), F32)]
    )(block_input, w_qkv, table)
    mixed, lse = call(
        attend_kernel, [sds(full, BF), sds((strips, lp, 128), F32)], 3, [pltpu.VMEM((lp, lp), F32)]
    )(qkv, seg_row, seg_col)
    y, res_grad, mixed_grad, g_up, g_down, g_out, g_tab = call(
        ff_kernel,
        [
            sds(block_input.shape, BF), sds(full, F32), sds(full, BF), sds(up.shape, BF),
            sds(down.shape, BF), sds((width, width), BF), sds(table.shape, F32),
        ],
        7,
        [
            pltpu.VMEM(full, BF), pltpu.VMEM(turned, BF), pltpu.VMEM(full, BF), pltpu.VMEM(turned, BF),
            pltpu.VMEM(full, F32), pltpu.VMEM(full, F32), pltpu.VMEM(full, F32),
            pltpu.VMEM((strips, lp, units), BF), pltpu.VMEM((strips, lp, units), BF),
        ],
    )(block_input, mixed, out_grad, w_out, up, down, table)
    (dqkv,) = call(
        attend_back_kernel,
        [sds(wide, BF)],
        6,
        [
            pltpu.VMEM((lp, lp), F32), pltpu.VMEM((128, lp), F32), pltpu.VMEM((16, lp), F32),
            pltpu.VMEM((128, lp), BF),
        ],
    )(qkv, mixed_grad, mixed, lse, seg_row, seg_col)
    x_grad, g_qkv, g_tab1 = call(
        qkv_back_kernel,
        [sds(block_input.shape, BF), sds((width, 3 * width), BF), sds(table.shape, F32)],
        6,
        [pltpu.VMEM(turned, BF), pltpu.VMEM(full, F32)],
    )(block_input, normed, dqkv, res_grad, w_qkv, table)
    g_tab = lax.psum(g_tab + g_tab1, ALL)
    g_qkv, g_out = (
        lax.psum_scatter(a.astype(F32), ALL, scatter_dimension=0, tiled=True) for a in (g_qkv, g_out)
    )
    g_up, g_down = (
        lax.psum_scatter(
            lax.psum_scatter(a.astype(F32), "gx", scatter_dimension=0, tiled=True)[0],
            ("dp", "gy"),
            scatter_dimension=0,
            tiled=True,
        )
        for a in (g_up, g_down)
    )
    g_att = (g_qkv[:, :width], g_qkv[:, width : 2 * width], g_qkv[:, 2 * width :], g_out)
    return y, x_grad, g_att, g_up, g_down, g_tab


def per_device(
    sizes, block_input, segment_ids, out_grad, query_weight, key_weight, value_weight, output_weight,
    first_gain, first_shift, query_bias, value_bias, output_bias, second_gain, second_shift,
    up_weight, up_bias, down_weight, down_bias,
):
    nd, nx, ny = sizes
    n_dev = nd * nx * ny
    strips, length, width = block_input.shape
    units = up_weight.shape[1]
    att_rows, ff_rows = query_weight.shape[0], up_weight.shape[0]
    own = nd == 2 and nx == 4 and ny % 2 == 0 and att_rows % 8 == 0 and ff_rows % 8 == 0

    vecs = [first_gain, first_shift, query_bias, value_bias, output_bias, second_gain, second_shift, down_bias]
    n_vec = len(vecs)
    me = (lax.axis_index("dp") * nx + lax.axis_index("gx")) * ny + lax.axis_index("gy")
    n_tab = n_vec + up_bias.shape[0] * n_dev // width
    pieces = jnp.stack(vecs).astype(F32)
    lane = lax.broadcasted_iota(jnp.int32, (n_vec, width), 1) // att_rows
    top = jnp.where(lane == me, jnp.tile(pieces, (1, n_dev)), 0.0)
    flat = jnp.tile(up_bias.astype(F32), n_dev).reshape(n_tab - n_vec, width)
    index = lax.broadcasted_iota(jnp.int32, flat.shape, 0) * width + lax.broadcasted_iota(jnp.int32, flat.shape, 1)
    small = jnp.concatenate([top, jnp.where(index // up_bias.shape[0] == me, flat, 0.0)])
    rows_up = (n_tab + 7) // 8 * 8
    small = jnp.pad(small, ((0, rows_up - n_tab), (0, 0)))
    if own:
        y, x_grad, gq, gk, gv_, go, g_up, g_down, g_tab = own_path(
            sizes,
            (
                block_input, segment_ids, out_grad, query_weight, key_weight, value_weight, output_weight,
                small, up_weight, down_weight,
            ),
        )
        g_att = (gq, gk, gv_, go)
    else:
        table = lax.psum(small, ALL)
        y, x_grad, g_att, g_up, g_down, g_tab = wide_path(
            sizes,
            (
                block_input, segment_ids, out_grad, query_weight, key_weight, value_weight, output_weight,
                table, up_weight, down_weight,
            ),
        )
    mine = lax.dynamic_slice(g_tab, (0, me * att_rows), (n_vec, att_rows))
    g_bias = lax.dynamic_slice(
        g_tab[n_vec:n_tab].reshape(-1), (me * up_bias.shape[0],), (up_bias.shape[0],)
    )
    return (
        y, x_grad, *g_att, mine[G1], mine[S1], mine[QB], mine[VB], mine[OB], mine[G2], mine[S2],
        g_up, g_bias, g_down, mine[DB],
    )


def solution(mesh):
    rows, cols = P(ALL, None), P(ALL)
    cube = P(ALL, None, None)
    ff = P(("dp", "gy"), "gx")
    sizes = (mesh.shape["dp"], mesh.shape["gx"], mesh.shape["gy"])
    return jax.shard_map(
        functools.partial(per_device, sizes),
        mesh=mesh,
        in_specs=(cube, rows, cube) + (rows,) * 4 + (cols,) * 7 + (ff, cols, ff, cols),
        out_specs=(cube, cube) + (rows,) * 4 + (cols,) * 7 + (ff, cols, ff, cols),
        check_vma=False,
    )
```

```python
import functools
import math

import jax
import jax.numpy as jnp
from jax import lax
from jax.experimental import pallas as pl
from jax.experimental.pallas import tpu as pltpu
from jax.sharding import PartitionSpec as P

H = 12
HD = 64
BF = jnp.bfloat16
F32 = jnp.float32
ALL = ("dp", "gx", "gy")
MESH = pl.DeviceIdType.MESH
LOG2E = 1.4426950408889634
INV_SQRT2 = 0.7071067811865476
INV_SQRT_2PI = 0.3989422804014327
ANY = pl.BlockSpec(memory_space=pl.ANY)
VM = pl.BlockSpec(memory_space=pltpu.VMEM)
LIMIT = 61 << 20

G1, S1, QB, VB, OB, G2, S2, DB, UB0 = 0, 1, 2, 3, 4, 5, 6, 7, 8


def nn(a, b):
    return lax.dot_general(a, b, (((1,), (0,)), ((), ())), preferred_element_type=F32)


def nt(a, b):
    return lax.dot_general(a, b, (((1,), (1,)), ((), ())), preferred_element_type=F32)


def padded(length):
    return (length + 31) // 32 * 32


def row_pieces(length, step):
    return [(lo, min(step, length - lo)) for lo in range(0, length, step)]


def normalise(rows):
    centred = rows - jnp.mean(rows, axis=-1, keepdims=True)
    scale = lax.rsqrt(jnp.mean(centred * centred, axis=-1, keepdims=True) + 1e-06)
    return centred * scale, scale


def norm_back(grad, gain, xhat, scale):
    t = grad * gain
    return scale * (
        t
        - jnp.mean(t, axis=-1, keepdims=True)
        - xhat * jnp.mean(t * xhat, axis=-1, keepdims=True)
    )


def colsum(rows):
    return jnp.sum(rows, axis=0, keepdims=True)


def qkv_kernel(x_ref, w_ref, v_ref, qkv_ref, n_ref, bias_ref):
    strips, length, width = x_ref.shape
    lp = n_ref.shape[1]
    gain, shift = v_ref[G1 : G1 + 1, :], v_ref[S1 : S1 + 1, :]
    for s in range(strips):
        for lo, size in row_pieces(length, 136):
            xhat, _ = normalise(x_ref[s, lo : lo + size, :].astype(F32))
            n_ref[s, lo : lo + size, :] = (xhat * gain + shift).astype(BF)
        n_ref[s, length:lp, :] = jnp.zeros((lp - length, width), BF)
    bias_ref[0:1, 0:width] = v_ref[QB : QB + 1, :]
    bias_ref[0:1, width : 2 * width] = jnp.zeros((1, width), F32)
    bias_ref[0:1, 2 * width : 3 * width] = v_ref[VB : VB + 1, :]
    step = 256

    def body(i, carry):
        cols = pl.ds(pl.multiple_of(i * step, step), step)
        w = w_ref[:, cols]
        for s in range(strips):
            qkv_ref[s, :, cols] = (nn(n_ref[s], w) + bias_ref[0:1, cols]).astype(BF)
        return carry

    lax.fori_loop(0, 3 * width // step, body, 0)


def fill_bias(bias_ref, row, col):
    bias_ref[...] = jnp.where(row == col, 0.0, -1e30).astype(F32)


def attend_kernel(qkv_ref, sr_ref, sc_ref, o_ref, lse_ref, bias_ref):
    strips, lp, width = o_ref.shape
    qrows = lp // 2
    first = lax.broadcasted_iota(jnp.int32, (qrows, 128), 1) < HD
    lane = lax.broadcasted_iota(jnp.int32, (qrows, 128), 1)
    scale = 0.125 * LOG2E
    for s in range(strips):
        fill_bias(bias_ref, sc_ref[s], sr_ref[s])
        lse_ref[s] = jnp.zeros((lp, 128), F32)

        def body(p, carry):
            cq = pl.ds(pl.multiple_of(p * 128, 128), 128)
            ck = pl.ds(pl.multiple_of(width + p * 128, 128), 128)
            cv = pl.ds(pl.multiple_of(2 * width + p * 128, 128), 128)
            k, v = qkv_ref[s, :, ck], qkv_ref[s, :, cv]
            for part in range(2):
                rows = pl.ds(part * qrows, qrows)
                q = qkv_ref[s, rows, cq]
                lse = lse_ref[s, rows, :]
                res = []
                for j in range(2):
                    keep = first if j == 0 else jnp.logical_not(first)
                    z = nt(jnp.where(keep, q, jnp.zeros_like(q)), k) * scale + bias_ref[rows, :]
                    top = jnp.max(z, axis=-1, keepdims=True)
                    e = jnp.exp2(z - top)
                    total = jnp.sum(e, axis=-1, keepdims=True)
                    res.append(nn(e.astype(BF), v) / total)
                    lse = jnp.where(lane == 2 * p + j, top + jnp.log2(total), lse)
                o_ref[s, rows, cq] = jnp.where(first, res[0], res[1]).astype(BF)
                lse_ref[s, rows, :] = lse
            return carry

        lax.fori_loop(0, H // 2, body, 0)


def transpose_into(dst_ref, src_ref, lp):
    strips, _, width = src_ref.shape
    for s in range(strips):

        def body(i, carry):
            cols = pl.ds(pl.multiple_of(i * 128, 128), 128)
            dst_ref[s, cols, :] = src_ref[s, :, cols].astype(F32).T.astype(BF)
            return carry

        lax.fori_loop(0, width // 128, body, 0)


def ff_kernel(
    x_ref, mix_ref, dout_in_ref, wo_ref, up_ref, down_ref, v_ref,
    y_ref, rg_ref, mg_ref, gup_ref, gdown_ref, gwo_ref, gv_ref,
    dout_ref, doutT_ref, sec_ref, secT_ref, res_ref, acc_ref, sg_ref, hid_ref, pre_ref,
):
    strips, length, width = x_ref.shape
    lp = mix_ref.shape[1]
    groups = up_ref.shape[0]
    units = up_ref.shape[2]
    gv_ref[...] = jnp.zeros(gv_ref.shape, F32)
    bias_o, gain, shift = v_ref[OB : OB + 1, :], v_ref[G2 : G2 + 1, :], v_ref[S2 : S2 + 1, :]
    step = 256
    for s in range(strips):
        dout_ref[s, 0:length, :] = dout_in_ref[s]
        dout_ref[s, length:lp, :] = jnp.zeros((lp - length, width), BF)

        def proj(i, carry):
            cols = pl.ds(pl.multiple_of(i * step, step), step)
            acc_ref[s, :, cols] = nn(mix_ref[s], wo_ref[:, cols])
            return carry

        lax.fori_loop(0, width // step, proj, 0)
        for lo, size in row_pieces(length, 136):
            rows = pl.ds(lo, size)
            residual = x_ref[s, rows, :].astype(F32) + (acc_ref[s, rows, :] + bias_o)
            res_ref[s, rows, :] = residual
            xhat, _ = normalise(residual)
            sec_ref[s, rows, :] = (xhat * gain + shift).astype(BF)
            acc_ref[s, rows, :] = residual + v_ref[DB : DB + 1, :]
        sec_ref[s, length:lp, :] = jnp.zeros((lp - length, width), BF)
        res_ref[s, length:lp, :] = jnp.zeros((lp - length, width), F32)
        gv_ref[DB : DB + 1, :] += colsum(dout_in_ref[s].astype(F32))
    sg_ref[...] = jnp.zeros(sg_ref.shape, F32)
    transpose_into(doutT_ref, dout_ref, lp)
    transpose_into(secT_ref, sec_ref, lp)

    def group(gi, carry):
        def hidden(i, carry):
            cols = pl.ds(pl.multiple_of(i * step, step), step)
            up, down = up_ref[gi, :, cols], down_ref[gi, :, cols]
            ub = v_ref[pl.ds(UB0 + gi, 1), cols]
            total = jnp.zeros((1, step), F32)
            for s in range(strips):
                pre = nn(sec_ref[s], up) + ub
                hg = nn(dout_ref[s], down)
                cdf = 0.5 + 0.5 * lax.erf(pre * INV_SQRT2)
                pdf = jnp.exp(-0.5 * pre * pre) * INV_SQRT_2PI
                hid_ref[s, :, cols] = (pre * cdf).astype(BF)
                pg = (hg * (cdf + pre * pdf)).astype(BF)
                pre_ref[s, :, cols] = pg
                total = total + colsum(pg.astype(F32))
            gv_ref[pl.ds(UB0 + gi, 1), cols] = total
            return carry

        lax.fori_loop(0, units // step, hidden, 0)

        def back(i, carry):
            rows = pl.ds(pl.multiple_of(i * step, step), step)
            for s in range(strips):
                acc_ref[s, :, rows] += nt(hid_ref[s], down_ref[gi, rows, :])
                sg_ref[s, :, rows] += nt(pre_ref[s], up_ref[gi, rows, :])
            gd = nn(doutT_ref[0, rows, :], hid_ref[0])
            gu = nn(secT_ref[0, rows, :], pre_ref[0])
            for s in range(1, strips):
                gd = gd + nn(doutT_ref[s, rows, :], hid_ref[s])
                gu = gu + nn(secT_ref[s, rows, :], pre_ref[s])
            gdown_ref[gi, rows, :] = gd.astype(BF)
            gup_ref[gi, rows, :] = gu.astype(BF)
            return carry

        lax.fori_loop(0, width // step, back, 0)
        return carry

    lax.fori_loop(0, groups, group, 0)
    for s in range(strips):
        for lo, size in row_pieces(length, 136):
            rows = pl.ds(lo, size)
            y_ref[s, rows, :] = acc_ref[s, rows, :].astype(BF)
            xhat, scale = normalise(res_ref[s, rows, :])
            grad = sg_ref[s, rows, :]
            gv_ref[G2 : G2 + 1, :] += colsum(grad * xhat)
            gv_ref[S2 : S2 + 1, :] += colsum(grad)
            rg = dout_ref[s, rows, :].astype(F32) + norm_back(grad, gain, xhat, scale)
            rg_ref[s, rows, :] = rg
            low = rg.astype(BF)
            sec_ref[s, rows, :] = low
            gv_ref[OB : OB + 1, :] += colsum(low.astype(F32))
        sec_ref[s, length:lp, :] = jnp.zeros((lp - length, width), BF)
        rg_ref[s, length:lp, :] = jnp.zeros((lp - length, width), F32)
    transpose_into(secT_ref, mix_ref, lp)

    def last(i, carry):
        rows = pl.ds(pl.multiple_of(i * step, step), step)
        for s in range(strips):
            mg_ref[s, :, rows] = nt(sec_ref[s], wo_ref[rows, :]).astype(BF)
        gw = nn(secT_ref[0, rows, :], sec_ref[0])
        for s in range(1, strips):
            gw = gw + nn(secT_ref[s, rows, :], sec_ref[s])
        gwo_ref[rows, :] = gw.astype(BF)
        return carry

    lax.fori_loop(0, width // step, last, 0)


def attend_back_kernel(
    qkv_ref, mg_ref, mix_ref, lse_ref, sr_ref, sc_ref, dqkv_ref, bias_ref, lt_ref, dt_ref, kt_ref
):
    strips, lp, width = mg_ref.shape
    krows = lp // 2
    first = lax.broadcasted_iota(jnp.int32, (krows, 128), 1) < HD
    scale = 0.125 * LOG2E
    heads = lax.broadcasted_iota(jnp.int32, (16, width), 0)
    owner = lax.broadcasted_iota(jnp.int32, (16, width), 1) // HD
    pick = jnp.where(heads == owner, 1.0, 0.0).astype(BF)
    for s in range(strips):
        fill_bias(bias_ref, sc_ref[s], sr_ref[s])
        lt_ref[...] = lse_ref[s].T
        prod = mg_ref[s].astype(F32) * mix_ref[s].astype(F32)
        high = prod.astype(BF)
        rest = (prod - high.astype(F32)).astype(BF)
        dt_ref[...] = nt(pick, high) + nt(pick, rest)

        def body(p, carry):
            cq = pl.ds(pl.multiple_of(p * 128, 128), 128)
            ck = pl.ds(pl.multiple_of(width + p * 128, 128), 128)
            cv = pl.ds(pl.multiple_of(2 * width + p * 128, 128), 128)
            q, do = qkv_ref[s, :, cq], mg_ref[s, :, cq]
            kt_ref[...] = qkv_ref[s, :, ck].astype(F32).T.astype(BF)
            dq = [jnp.zeros((HD, lp), F32), jnp.zeros((HD, lp), F32)]
            for part in range(2):
                rows = pl.ds(part * krows, krows)
                k, v = qkv_ref[s, rows, ck], qkv_ref[s, rows, cv]
                dv, dk = [], []
                for j in range(2):
                    keep = first if j == 0 else jnp.logical_not(first)
                    lse = lt_ref[pl.ds(2 * p + j, 1), :]
                    delta = dt_ref[pl.ds(2 * p + j, 1), :]
                    z = nt(jnp.where(keep, k, jnp.zeros_like(k)), q) * scale + bias_ref[rows, :]
                    prob = jnp.exp2(z - lse)
                    pg = nt(jnp.where(keep, v, jnp.zeros_like(v)), do)
                    sg = (prob * (pg - delta)).astype(BF)
                    dv.append(nn(prob.astype(BF), do))
                    dk.append(nn(sg, q))
                    dq[j] = dq[j] + nn(kt_ref[j * HD : (j + 1) * HD, part * krows : (part + 1) * krows], sg)
                dqkv_ref[s, rows, cv] = jnp.where(first, dv[0], dv[1]).astype(BF)
                dqkv_ref[s, rows, ck] = (0.125 * jnp.where(first, dk[0], dk[1])).astype(BF)
            dqkv_ref[s, :, cq] = (0.125 * jnp.concatenate(dq, axis=0)).T.astype(BF)
            return carry

        lax.fori_loop(0, H // 2, body, 0)


def qkv_back_kernel(
    x_ref, n_ref, dqkv_ref, rg_ref, w_ref, v_ref, gx_ref, gw_ref, gv_ref, nT_ref, ng_ref
):
    strips, length, width = x_ref.shape
    lp = n_ref.shape[1]
    step = 256
    gv_ref[...] = jnp.zeros(gv_ref.shape, F32)
    gain = v_ref[G1 : G1 + 1, :]
    transpose_into(nT_ref, n_ref, lp)
    for s in range(strips):
        gv_ref[QB : QB + 1, :] += colsum(dqkv_ref[s, :, 0:width].astype(F32))
        gv_ref[VB : VB + 1, :] += colsum(dqkv_ref[s, :, 2 * width : 3 * width].astype(F32))

        def body(i, carry):
            rows = pl.ds(pl.multiple_of(i * step, step), step)
            ng_ref[s, :, rows] = nt(dqkv_ref[s], w_ref[rows, :])
            return carry

        lax.fori_loop(0, width // step, body, 0)

    def grads(i, carry):
        cols = pl.ds(pl.multiple_of(i * step, step), step)
        gw = nn(nT_ref[0], dqkv_ref[0, :, cols])
        for s in range(1, strips):
            gw = gw + nn(nT_ref[s], dqkv_ref[s, :, cols])
        gw_ref[:, cols] = gw.astype(BF)
        return carry

    lax.fori_loop(0, 3 * width // step, grads, 0)
    for s in range(strips):
        for lo, size in row_pieces(length, 136):
            rows = pl.ds(lo, size)
            xhat, scale = normalise(x_ref[s, rows, :].astype(F32))
            grad = ng_ref[s, rows, :]
            gv_ref[G1 : G1 + 1, :] += colsum(grad * xhat)
            gv_ref[S1 : S1 + 1, :] += colsum(grad)
            term = norm_back(grad, gain, xhat, scale)
            gx_ref[s, rows, :] = (rg_ref[s, rows, :] + term).astype(BF)


def call(kernel, outs, n_in, scratch=()):
    return pl.pallas_call(
        kernel,
        out_shape=outs,
        in_specs=[VM] * n_in,
        out_specs=[VM] * len(outs),
        scratch_shapes=list(scratch),
        compiler_params=pltpu.CompilerParams(vmem_limit_bytes=LIMIT),
    )


def sds(shape, dtype):
    return jax.ShapeDtypeStruct(shape, dtype)


def remote(src, dst, send, recv, dev):
    return pltpu.make_async_remote_copy(
        src_ref=src, dst_ref=dst, send_sem=send, recv_sem=recv, device_id=dev, device_id_type=MESH
    )


class Place:
    def __init__(self, ny):
        self.ny = ny
        self.d, x, self.g = lax.axis_index("dp"), lax.axis_index("gx"), lax.axis_index("gy")
        self.h, self.c = x // 2, x % 2
        self.z = [(self.d, x, lax.rem(self.g + k, ny)) for k in range(1, ny)]
        self.y = (self.d, (1 - self.h) * 2 + self.c, self.g)
        self.x = (1 - self.d, x, self.g)
        self.core = (self.d, self.h * 2 + 1 - self.c, self.g)
        h, c = (self.h, 1 - self.h), (self.c, 1 - self.c)
        every = [(d, hh * 2 + cc, self.g) for d in (self.d, 1 - self.d) for hh in h for cc in c]
        self.plane = every[1:]

    def greet(self):
        for peer in self.z + self.plane:
            pl.semaphore_signal(pltpu.get_barrier_semaphore(), inc=1, device_id=peer, device_id_type=MESH)

    def greeted(self):
        pl.semaphore_wait(pltpu.get_barrier_semaphore(), len(self.z + self.plane))


def stops(plan, **stages):
    steps = iter(plan)

    def stop():
        for token in next(steps):
            stages[token[0]](int(token[1:]))

    return stop


class Gather:
    def __init__(self, at, shards, views, sems):
        self.at, self.shards, self.views, self.n = at, shards, views, len(shards)
        self.loc, self.zsend, self.zrecv, self.bsend, self.brecv = sems
        self.zs, self.bs, self.fs, self.cs = {}, {}, {}, {}

    @staticmethod
    def semaphores(n, ny, only_z=0):
        m = n + only_z
        return [pltpu.SemaphoreType.DMA(s) for s in ((m,), (m, ny - 1), (m, ny - 1), (n, 8), (n, 8))]

    def push(self, t, i, ref, dev):
        cp = remote(ref, ref, self.bsend.at[t, i], self.brecv.at[t, i], dev)
        cp.start()
        return cp

    def z(self, t):
        at = self.at
        own = self.views[t](at.d, at.h, at.c, at.g, 1)
        local = pltpu.make_async_copy(self.shards[t], own, self.loc.at[t])
        local.start()
        copies = []
        for k, dev in enumerate(at.z):
            cp = remote(self.shards[t], own, self.zsend.at[t, k], self.zrecv.at[t, k], dev)
            cp.start()
            copies.append(cp)
        self.zs[t] = local, copies

    def ready(self, t, source):
        at = self.at
        local = pltpu.make_async_copy(source, self.views[t](at.d, at.h, at.c, 0, at.ny), self.loc.at[t])
        local.start()
        self.zs[t] = local, []

    def along_z(self, t):
        self.zs[t][0].wait()
        for cp in self.zs[t][1]:
            cp.wait_recv()
        for cp in self.zs[t][1]:
            cp.wait_send()

    def b(self, t):
        at = self.at
        self.zs[t][0].wait()
        for cp in self.zs[t][1]:
            cp.wait_recv()
        b = self.views[t](at.d, at.h, at.c, 0, at.ny)
        self.bs[t] = [self.push(t, i, b, dev) for i, dev in enumerate((at.y, at.x, at.core))]

    def f(self, t):
        at, view = self.at, self.views[t]
        half = at.ny // 2
        self.bs[t][0].wait_recv()
        f1 = self.push(t, 3, view(at.d, 1 - at.h, at.c, 0, half), at.x)
        c1 = self.push(t, 4, view(at.d, 1 - at.h, at.c, 0, at.ny), at.core)
        self.bs[t][1].wait_recv()
        f2 = self.push(t, 5, view(1 - at.d, at.h, at.c, half, at.ny - half), at.y)
        c2 = self.push(t, 6, view(1 - at.d, at.h, at.c, 0, at.ny), at.core)
        self.fs[t] = [f1, c1, f2, c2]

    def c(self, t):
        at = self.at
        self.fs[t][0].wait_recv()
        self.fs[t][2].wait_recv()
        self.cs[t] = self.push(t, 7, self.views[t](1 - at.d, 1 - at.h, at.c, 0, at.ny), at.core)

    def arrived(self, t):
        for cp in (self.bs[t][2], self.fs[t][1], self.fs[t][3], self.cs[t]):
            cp.wait_recv()

    def sent(self, t):
        for cp in self.zs[t][1] + self.bs[t] + self.fs[t] + [self.cs[t]]:
            cp.wait_send()


class Table:
    def __init__(self, at, total, landing, send, recv):
        self.at, self.total, self.landing, self.send, self.recv = at, total, landing, send, recv
        self.stages = [at.plane, at.z]
        self.flight, self.slot = [], 0

    @staticmethod
    def scratch(shape, ny, dtype):
        return [
            pltpu.VMEM((ny + 6,) + shape, dtype), pltpu.VMEM((2,) + shape, dtype),
            pltpu.SemaphoreType.DMA((ny + 6,)), pltpu.SemaphoreType.DMA((ny + 6,)),
        ]

    def step(self, k):
        if k > 0:
            value = self.total[k - 1].astype(F32)
            for cp, slot in self.flight[k - 1]:
                cp.wait_recv()
                value = value + self.landing[slot].astype(F32)
            if k < len(self.stages):
                self.total[k] = value.astype(self.total.dtype)
            else:
                self.result = value
                return
        copies = []
        for dev in self.stages[k]:
            slot = self.slot
            self.slot += 1
            cp = remote(self.total.at[k], self.landing.at[slot], self.send.at[slot], self.recv.at[slot], dev)
            cp.start()
            copies.append((cp, slot))
        self.flight.append(copies)

    def sent(self):
        for copies in self.flight:
            for cp, _ in copies:
                cp.wait_send()


class Scatter:
    def __init__(self, at, units, buffers, sems):
        self.at, self.units, self.n = at, units, len(units)
        self.bufs = buffers
        self.lsem, self.csend, self.crecv, self.bsend, self.brecv, self.zsend, self.zrecv = sems
        d, h = at.d, at.h
        self.quads = [(1 - d, 1 - h), (d, 1 - h), (1 - d, h), (d, h)]
        self.cs, self.fars, self.nears, self.zs = {}, {}, {}, {}

    @staticmethod
    def buffers(k, rows, cols, ny):
        return [
            pltpu.VMEM((lead, n * k, rows, cols), BF)
            for lead, n in ((4, ny), (4, ny), (2, ny // 2), (2, ny), (ny - 1, 1))
        ]

    @staticmethod
    def semaphores(n, ny):
        lead = (4, 4, 4, 4, 4, ny - 1, ny - 1)
        return [pltpu.SemaphoreType.DMA((n, k)) for k in lead]

    def add(self, dst, src, pieces):
        lead = dst.shape[0] // pieces

        def body(i, carry):
            part = pl.ds(i * lead, lead)
            dst[part] = (dst[part].astype(F32) + src[part].astype(F32)).astype(dst.dtype)
            return carry

        lax.fori_loop(0, pieces, body, 0)

    def core(self, t):
        view, (sums, rc) = self.units[t][0], self.bufs[t][:2]
        c = self.at.c
        res = []
        for q, (d, h) in enumerate(self.quads):
            cp = remote(
                view(d, h, 1 - c), rc.at[q], self.csend.at[t, q], self.crecv.at[t, q], self.at.core
            )
            cp.start()
            lc = pltpu.make_async_copy(view(d, h, c), sums.at[q], self.lsem.at[t, q])
            lc.start()
            res.append((cp, lc))
        self.cs[t] = res

    def far(self, t):
        sums, rc, rs = self.bufs[t][:3]
        ny, k = self.at.ny, self.units[t][1]
        cut = ny // 2 * k
        res = []
        for q in range(4):
            self.cs[t][q][0].wait_recv()
            self.cs[t][q][1].wait()
            self.add(sums.at[q], rc.at[q], ny)
            if q == 0:
                for i, (lo, dev) in enumerate(((0, self.at.x), (cut, self.at.y))):
                    cp = remote(
                        sums.at[0, lo : lo + cut], rs.at[i], self.bsend.at[t, i], self.brecv.at[t, i], dev
                    )
                    cp.start()
                    res.append(cp)
        self.fars[t] = res

    def near(self, t):
        sums, _, rs, rl = self.bufs[t][:4]
        ny, k = self.at.ny, self.units[t][1]
        cut = ny // 2 * k
        res = []
        for i, (lo, dev) in enumerate(((0, self.at.y), (cut, self.at.x))):
            self.fars[t][i].wait_recv()
            self.add(sums.at[1 + i, lo : lo + cut], rs.at[i], ny // 2)
            cp = remote(sums.at[1 + i], rl.at[i], self.bsend.at[t, 2 + i], self.brecv.at[t, 2 + i], dev)
            cp.start()
            res.append(cp)
        self.nears[t] = res

    def z(self, t):
        sums, rl, rz = self.bufs[t][0], self.bufs[t][3], self.bufs[t][4]
        at, n = self.at, self.units[t][1]
        for i in range(2):
            self.nears[t][i].wait_recv()
            self.add(sums.at[3], rl.at[i], at.ny)
        res = []
        for k, dev in enumerate(at.z):
            cp = remote(
                sums.at[3, pl.ds(dev[2] * n, n)], rz.at[k], self.zsend.at[t, k], self.zrecv.at[t, k], dev
            )
            cp.start()
            res.append(cp)
        self.zs[t] = res

    def finish(self, t):
        sums, rz = self.bufs[t][0], self.bufs[t][4]
        n = self.units[t][1]
        total = sums[3, pl.ds(self.at.g * n, n)].astype(F32)
        for k, cp in enumerate(self.zs[t]):
            cp.wait_recv()
            total = total + rz[k].astype(F32)
        self.units[t][2](total)

    def sent(self, t):
        for q in range(4):
            self.cs[t][q][0].wait_send()
        for cp in self.fars[t] + self.nears[t] + self.zs[t]:
            cp.wait_send()


GROUPS = ((0, 128), (128, 256), (384, 256), (640, 128))
NG = len(GROUPS)
PARTS = 3


def att_view(ref, tiles, sizes):
    nd, nh, ny = sizes

    def view(d, h, c, lo, n):
        return ref.at[pl.ds((((d * nh + h) * 2 + c) * ny + lo) * tiles, n * tiles)]

    return view


def ff_view(ref, part):
    def view(d, h, c, lo, n):
        start = pl.multiple_of((h * 2 + c) * part, part)
        return ref.at[d, pl.ds(lo, n), :, pl.ds(start, part)]

    return view


def copies_of(sem, *pairs):
    made = [pltpu.make_async_copy(a, b, sem.at[i]) for i, (a, b) in enumerate(pairs)]
    for cp in made:
        cp.start()
    return made


def columns_of(seg_row):
    return jnp.broadcast_to(seg_row, (128, seg_row.shape[1])).T[:, 0:1]


def turn(dst_ref, src_ref):
    total, width = src_ref.shape
    step = 256
    eye = jnp.where(
        lax.broadcasted_iota(jnp.int32, (step, step), 0) == lax.broadcasted_iota(jnp.int32, (step, step), 1), 1.0, 0.0
    ).astype(BF)
    for lo, size in row_pieces(total, step):
        for j in range(width // step):
            cols = slice(j * step, (j + 1) * step)
            dst_ref[cols, lo : lo + size] = nt(eye, src_ref[lo : lo + size, cols]).astype(BF)


def mask_into(bias_ref, segp_ref, s):
    row = segp_ref[s : s + 1, :]
    bias_ref[...] = jnp.where(columns_of(row) == row, 0.0, -1e30).astype(F32)


def segments_into(segp_ref, seg_ref):
    strips, length = seg_ref.shape
    segp_ref[...] = jnp.full(segp_ref.shape, -1.0, F32)
    segp_ref[0:strips, 0:length] = seg_ref[...].astype(F32)


def attend_pair(qkv_ref, o_ref, lse_ref, bias_ref, s, lp, base, gw, out_col):
    head = out_col // HD
    qrows = lp // 2
    lane = lax.broadcasted_iota(jnp.int32, (qrows, 128), 1)
    first = lane < HD
    scale = 0.125 * LOG2E
    off = s * lp
    k = qkv_ref[off : off + lp, base + gw : base + gw + 128]
    v = qkv_ref[off : off + lp, base + 2 * gw : base + 2 * gw + 128]
    for part in range(2):
        lo = part * qrows
        q = qkv_ref[off + lo : off + lo + qrows, base : base + 128]
        lse = lse_ref[s, lo : lo + qrows, :]
        res = []
        for j in range(2):
            keep = first if j == 0 else jnp.logical_not(first)
            z = nt(jnp.where(keep, q, jnp.zeros_like(q)), k) * scale + bias_ref[s, lo : lo + qrows, :]
            top = jnp.max(z, axis=-1, keepdims=True)
            e = jnp.exp2(z - top)
            total = jnp.sum(e, axis=-1, keepdims=True)
            res.append(nn(e.astype(BF), v) / total)
            lse = jnp.where(lane == head + j, top + jnp.log2(total), lse)
        o_ref[off + lo : off + lo + qrows, out_col : out_col + 128] = jnp.where(first, res[0], res[1]).astype(BF)
        lse_ref[s, lo : lo + qrows, :] = lse


def front_kernel(
    sizes, x_hbm, do_hbm, seg_ref, wq, wk, wv, wo, up, down, small_ref,
    lt_ref, table_ref, gsum_ref, qkv_out, mixed_out, nT_out, dout_out, doutT_out, xp_out, watt_out, wo_out, up_out, down_out, zb_out,
    x_ref, do_ref, xhat_ref, norm_ref, shard_ref, watt_ref, bias_row, lse_ref, bias_ref, segp_ref,
    qkv_ref, mixed_ref, nT_ref, dout_ref, doutT_ref, xp_ref,
    land_ref, tot_ref, tsend, trecv, lsem, osem, s_loc, s_zs, s_zr, s_bs, s_br, *land_w,
):
    nd, nh, ny = sizes
    length, strips, width = x_ref.shape
    lp = norm_ref.shape[0] // strips
    tiles = wq.shape[0]
    at = Place(ny)
    loads = [pltpu.make_async_copy(x_hbm, x_ref, lsem.at[0]), pltpu.make_async_copy(do_hbm, do_ref, lsem.at[1])]
    pieces = []
    for i, (first, gw) in enumerate(GROUPS):
        for j, w in enumerate((wq, wk, wv)):
            to = 3 * first + j * gw
            pieces.append(
                pltpu.make_async_copy(
                    w.at[:, :, first : first + gw], shard_ref.at[:, :, to : to + gw], lsem.at[2 + 3 * i + j]
                )
            )
    at.greet()
    for cp in pieces + loads:
        cp.start()
    at.greeted()
    tab = Table(at, tot_ref, land_ref, tsend, trecv)
    tot_ref[0] = small_ref[...].astype(BF)
    for cp in pieces:
        cp.wait()
    pw = up.shape[-1] // PARTS
    views = [att_view(land, tiles, sizes) for land in land_w] + [att_view(wo_out, tiles, sizes)]
    shards = [shard_ref.at[:, :, 3 * first : 3 * (first + gw)] for first, gw in GROUPS]
    shards += [wo, up.at[:, :, 0:pw], down.at[:, :, 0:pw]]
    views += [ff_view(up_out, pw), ff_view(down_out, pw)]
    n_full = len(shards)
    for b in range(1, PARTS):
        for w in (up, down):
            views.append(lambda d, h, c, lo, n, t=len(shards) - n_full: zb_out.at[t, pl.ds(lo, n)])
            shards.append(w.at[:, :, b * pw : (b + 1) * pw])
    gat = Gather(at, shards, views, (s_loc, s_zs, s_zr, s_bs, s_br))

    stop = stops(FRONT_PLAN, z=gat.z, b=gat.b, f=gat.f, c=gat.c, A=gat.arrived, t=tab.step, Y=gat.along_z)

    def hats(s):
        for lo, size in row_pieces(length, 136):
            part = slice(s * lp + lo, s * lp + lo + size)
            rows = x_ref[lo : lo + size, s, :]
            xp_ref[part, :] = rows
            xhat_ref[part, :], _ = normalise(rows.astype(F32))

    stop()
    for cp in loads:
        cp.wait()
    hats(0)
    stop()
    for s in range(1, strips):
        hats(s)
    stop()
    segments_into(segp_ref, seg_ref)
    for s in range(strips):
        mask_into(bias_ref.at[s], segp_ref, s)
    lse_ref[...] = jnp.zeros(lse_ref.shape, F32)
    stop()
    gsum = jnp.zeros((1, width), F32)
    for s in range(strips):
        for lo, size in row_pieces(length, 136):
            rows = do_ref[lo : lo + size, s, :]
            dout_ref[s * lp + lo : s * lp + lo + size, :] = rows
            gsum = gsum + colsum(rows.astype(F32))
        tail = slice(s * lp + length, (s + 1) * lp)
        dout_ref[tail, :] = jnp.zeros((lp - length, width), BF)
        xp_ref[tail, :] = jnp.zeros((lp - length, width), BF)
    gsum_ref[...] = jnp.broadcast_to(gsum, gsum_ref.shape)
    stop()
    turn(doutT_ref, dout_ref)
    outs = copies_of(osem, (dout_ref, dout_out), (doutT_ref, doutT_out))
    outs += copies_of(osem.at[4 + 2 * NG :], (xp_ref, xp_out))
    stop()
    table = tab.result
    table_ref[...] = table
    gain, shift = table[G1 : G1 + 1, :], table[S1 : S1 + 1, :]
    for s in range(strips):
        for lo, size in row_pieces(length, 136):
            part = slice(s * lp + lo, s * lp + lo + size)
            norm_ref[part, :] = (xhat_ref[part, :] * gain + shift).astype(BF)
        norm_ref[s * lp + length : (s + 1) * lp, :] = jnp.zeros((lp - length, width), BF)
    for first, gw in GROUPS:
        cols = slice(first, first + gw)
        bias_row[0:1, 3 * first : 3 * first + gw] = table[QB : QB + 1, cols]
        bias_row[0:1, 3 * first + gw : 3 * first + 2 * gw] = jnp.zeros((1, gw), F32)
        bias_row[0:1, 3 * first + 2 * gw : 3 * (first + gw)] = table[VB : VB + 1, cols]
    for i, (first, gw) in enumerate(GROUPS):
        stop()
        wide = slice(3 * first, 3 * (first + gw))

        def settle(n, carry):
            rows = pl.ds(pl.multiple_of(n * 64, 64), 64)
            watt_ref[rows, wide] = land_w[i][pl.ds(n * 8, 8)].astype(F32).reshape(64, 3 * gw).astype(BF)
            return carry

        lax.fori_loop(0, width // 64, settle, 0)

        def project(n, carry):
            cols = pl.ds(pl.multiple_of(3 * first + n * gw, 128), gw)
            qkv_ref[:, cols] = (nn(norm_ref[...], watt_ref[:, cols]) + bias_row[0:1, cols]).astype(BF)
            return carry

        lax.fori_loop(0, 3, project, 0)
        outs += copies_of(
            osem.at[2 + 2 * i : 4 + 2 * i],
            (qkv_ref.at[:, wide], qkv_out.at[:, wide]), (watt_ref.at[:, wide], watt_out.at[:, wide]),
        )
        for s in range(strips):
            for p in range(gw // 128):
                stop()
                attend_pair(
                    qkv_ref, mixed_ref, lse_ref, bias_ref, s, lp, 3 * first + p * 128, gw, first + p * 128
                )
        if i == 0:
            stop()
            turn(nT_ref, norm_ref)
            outs += copies_of(osem.at[2 + 2 * NG : 3 + 2 * NG], (nT_ref, nT_out))
    stop()
    outs += copies_of(osem.at[3 + 2 * NG : 4 + 2 * NG], (mixed_ref, mixed_out))
    for s in range(strips):
        lt_ref[s] = lse_ref[s].T[0:16, :]
    stop()
    for t in range(n_full):
        gat.sent(t)
    tab.sent()
    for cp in outs:
        cp.wait()


FRONT_PLAN = (
    ("z0", "t0", "z1"), ("z2", "b0"), ("b1", "z3", "t1"), ("f0", "z5", "b2"), ("b3",), ("z6", "f1", "c0", "t2"),
    ("f2", "A0"), ("z4",), ("b5",), ("c1",),
    ("c2", "f3", "A1"), ("b6",), ("z7",), ("b4", "A2"), ("z8",),
    (), ("f5",), ("f6", "z9"), ("c3",), ("A3", "z10"),
    ("f4",), ("c5",), ("c6", "A5"), ("A6", "c4"), ("A4", "Y7", "Y8", "Y9", "Y10"),
)


MIDDLE_PLAN = (
    ("b1",), ("b0",), (),
    (), (), ("f1", "f0", "b3"), ("c1", "b2", "K1"), ("A1", "c0"),
    ("A0",), ("f3", "F1"), ("f2", "K0"), ("F0", "c3"), ("A3", "c2", "N1"),
    ("A2",), ("N0",), ("Z1",), (), (),
    ("Z0",), (), ("E1",), ("E0",),
)


def middle_kernel(
    sizes, x_ref, mix_ref, wo_ref, v_ref, gsum_ref, dout_hbm, doutT_hbm, u0, d0, zb,
    mg_ref, gwo_ref, gv_ref, gu_ref, gd_ref, y_out, rg_out, *out_parts_and_scratch,
):
    middle_body(
        sizes, x_ref, mix_ref, wo_ref, v_ref, gsum_ref, dout_hbm, doutT_hbm, u0, d0, zb,
        mg_ref, gwo_ref, gv_ref, gu_ref, gd_ref, y_out, rg_out,
        out_parts_and_scratch[: 2 * (PARTS - 1)], *out_parts_and_scratch[2 * (PARTS - 1) :],
    )


def middle_body(
    sizes, x_ref, mix_ref, wo_ref, v_ref, gsum_ref, dout_hbm, doutT_hbm, u0, d0, zb,
    mg_ref, gwo_ref, gv_ref, gu_ref, gd_ref, y_out, rg_out, later,
    dout_ref, doutT_ref, sec_ref, secT_ref, res_ref, acc_ref, rg_ref, hid_ref, pre_ref, y_ref, wu, wd, pu, pd,
    lsem, osem, s_loc, s_zs, s_zr, s_bs, s_br, *rest,
):
    nd, nh, ny = sizes
    nq = nh * 2
    length, strips, width = y_ref.shape
    lp = mix_ref.shape[0] // strips
    rows, part = zb.shape[2], zb.shape[3]
    at = Place(ny)
    at.greet()
    loads = copies_of(lsem, (dout_hbm, dout_ref), (doutT_hbm, doutT_ref), (u0, wu.at[0]), (d0, wd.at[0]))
    n_sc = 2
    views, units = [], []
    for b in range(1, PARTS):
        views += [ff_view(wu.at[b], part), ff_view(wd.at[b], part)]
    for src, dst in ((pu, gu_ref), (pd, gd_ref)):

        def put(total, dst=dst):
            dst[...] = total[0]

        whole = ff_view(src, part)
        units.append(((lambda d, h, c, whole=whole: whole(d, h, c, 0, ny)), 1, put))
    gat = Gather(at, views, views, (s_loc, s_zs, s_zr, s_bs, s_br))
    for t in range(gat.n):
        gat.ready(t, zb.at[t])
    sca = Scatter(at, units, [rest[5 * t : 5 * t + 5] for t in range(n_sc)], rest[5 * n_sc :])
    stop = stops(
        MIDDLE_PLAN, b=gat.b, f=gat.f, c=gat.c, A=gat.arrived,
        K=sca.core, F=sca.far, N=sca.near, Z=sca.z, E=sca.finish,
    )

    step = 256
    bias_o, gain, shift = v_ref[OB : OB + 1, :], v_ref[G2 : G2 + 1, :], v_ref[S2 : S2 + 1, :]
    gv_ref[...] = jnp.zeros(gv_ref.shape, F32)
    gv_ref[DB : DB + 1, :] = gsum_ref[0:1, :]

    def proj(i, carry):
        cols = pl.ds(pl.multiple_of(i * step, step), step)
        acc_ref[:, cols] = nn(mix_ref[...], wo_ref[:, cols])
        return carry

    lax.fori_loop(0, width // step, proj, 0)
    at.greeted()
    for s in range(strips):
        stop()
        for lo, size in row_pieces(length, 136):
            sel = slice(s * lp + lo, s * lp + lo + size)
            residual = x_ref[sel, :].astype(F32) + (acc_ref[sel, :] + bias_o)
            res_ref[sel, :] = residual
            xhat, _ = normalise(residual)
            sec_ref[sel, :] = (xhat * gain + shift).astype(BF)
            acc_ref[sel, :] = residual + v_ref[DB : DB + 1, :]
        sec_ref[s * lp + length : (s + 1) * lp, :] = jnp.zeros((lp - length, width), BF)
    stop()
    turn(secT_ref, sec_ref)
    for cp in loads:
        cp.wait()

    outs = []
    block = strips * lp // 4
    for b in range(PARTS):

        def hidden(q):
            cols = slice(q * part, (q + 1) * part)
            w_up = wu[b, :, :, :, cols].reshape(width, part)
            w_down = wd[b, :, :, :, cols].reshape(width, part)
            csum = jnp.zeros((1, part), F32)
            for r in range(4):
                rs = slice(r * block, (r + 1) * block)
                pre = nn(sec_ref[rs, :], w_up) + v_ref[UB0 + q : UB0 + q + 1, b * part : (b + 1) * part]
                hg = nn(dout_ref[rs, :], w_down)
                cdf = 0.5 + 0.5 * lax.erf(pre * INV_SQRT2)
                pdf = jnp.exp(-0.5 * pre * pre) * INV_SQRT_2PI
                hid_ref[rs, cols] = (pre * cdf).astype(BF)
                pg = (hg * (cdf + pre * pdf)).astype(BF)
                pre_ref[rs, cols] = pg
                csum = csum + colsum(pg.astype(F32))
            gv_ref[UB0 + q : UB0 + q + 1, b * part : (b + 1) * part] = csum

        g_up, g_down = (pu, pd) if b == 0 else (wu.at[b - 1], wd.at[b - 1])

        def grads(d):
            rs = slice(d * ny * rows, (d + 1) * ny * rows)
            g_down[d] = nn(doutT_ref[rs, :], hid_ref[...]).astype(BF).reshape((ny, rows, nq * part))
            g_up[d] = nn(secT_ref[rs, :], pre_ref[...]).astype(BF).reshape((ny, rows, nq * part))

        stop()
        for q in range(nq // 2):
            hidden(q)
        stop()
        for q in range(nq // 2, nq):
            hidden(q)
        stop()
        if b > 1:
            gat.sent(2 * b - 4)
            gat.sent(2 * b - 3)
        for q in range(nd):
            grads(q)
        if b > 0:
            outs += copies_of(
                osem.at[2 * b : 2 * b + 2], (g_up, later[2 * b - 2]), (g_down, later[2 * b - 1])
            )
        stop()
        w_down = wd[b].reshape(width, nq * part)
        for n in range(strips):
            rs = slice(n * lp, (n + 1) * lp)
            acc_ref[rs, :] += nt(hid_ref[rs, :], w_down)
        stop()
        w_up = wu[b].reshape(width, nq * part)
        for n in range(strips):
            rs = slice(n * lp, (n + 1) * lp)
            value = nt(pre_ref[rs, :], w_up)
            rg_ref[rs, :] = value if b == 0 else rg_ref[rs, :] + value

    for s in range(strips):
        stop()
        for lo, size in row_pieces(length, 136):
            sel = slice(s * lp + lo, s * lp + lo + size)
            y_ref[lo : lo + size, s, :] = acc_ref[sel, :].astype(BF)
            xhat, scale = normalise(res_ref[sel, :])
            grad = rg_ref[sel, :]
            gv_ref[G2 : G2 + 1, :] += colsum(grad * xhat)
            gv_ref[S2 : S2 + 1, :] += colsum(grad)
            rg = dout_ref[sel, :].astype(F32) + norm_back(grad, gain, xhat, scale)
            rg_ref[sel, :] = rg
            low = rg.astype(BF)
            sec_ref[sel, :] = low
            gv_ref[OB : OB + 1, :] += colsum(low.astype(F32))
        tail = slice(s * lp + length, (s + 1) * lp)
        sec_ref[tail, :] = jnp.zeros((lp - length, width), BF)
        rg_ref[tail, :] = jnp.zeros((lp - length, width), F32)
    outs += copies_of(osem.at[0:2], (rg_ref, rg_out), (y_ref, y_out))
    turn(secT_ref, mix_ref)
    stop()

    def last(i, carry):
        sel = pl.ds(pl.multiple_of(i * step, step), step)
        mg_ref[:, sel] = nt(sec_ref[...], wo_ref[sel, :]).astype(BF)
        gwo_ref[sel, :] = nn(secT_ref[sel, :], sec_ref[...]).astype(BF)
        return carry

    lax.fori_loop(0, width // step, last, 0)
    stop()
    for t in range(2 * (PARTS - 2), gat.n):
        gat.sent(t)
    for t in range(n_sc):
        sca.sent(t)
    for cp in outs:
        cp.wait()


def attend_back_pair(qkv_ref, mg_ref, bias_ref, lt_ref, dt_ref, kt_ref, s, lp, base, gw, out_col):
    head = out_col // HD
    first = lax.broadcasted_iota(jnp.int32, (lp, 128), 1) < HD
    scale = 0.125 * LOG2E
    rows = slice(s * lp, (s + 1) * lp)
    q = qkv_ref[rows, base : base + 128]
    k = qkv_ref[rows, base + gw : base + gw + 128]
    v = qkv_ref[rows, base + 2 * gw : base + 2 * gw + 128]
    do = mg_ref[rows, out_col : out_col + 128]
    kt_ref[...] = k.astype(F32).T.astype(BF)
    dq, dk, dv = [], [], []
    for j in range(2):
        keep = first if j == 0 else jnp.logical_not(first)
        lse = lt_ref[s, head + j : head + j + 1, :]
        delta = dt_ref[s, head + j : head + j + 1, :]
        z = nt(jnp.where(keep, k, jnp.zeros_like(k)), q) * scale + bias_ref[s]
        prob = jnp.exp2(z - lse)
        pg = nt(jnp.where(keep, v, jnp.zeros_like(v)), do)
        sg = (prob * (pg - delta)).astype(BF)
        dv.append(nn(prob.astype(BF), do))
        dk.append(nn(sg, q))
        dq.append(nn(kt_ref[j * HD : (j + 1) * HD, :], sg))
    qkv_ref[rows, base + 2 * gw : base + 2 * gw + 128] = jnp.where(first, dv[0], dv[1]).astype(BF)
    qkv_ref[rows, base + gw : base + gw + 128] = (0.125 * jnp.where(first, dk[0], dk[1])).astype(BF)
    qkv_ref[rows, base : base + 128] = (0.125 * jnp.concatenate(dq, axis=0)).T.astype(BF)


BACK_PLAN = (
    ("K7", "t0"), ("K0", "F7"), ("K8", "F0"), ("K3", "K1", "F8"),
    ("N7",), (), ("N0",), ("F3",), ("F1", "N8"), (),
    ("Z7",), ("K4",), ("F4",), ("Z0", "K2", "N3"), ("N1",), ("K5", "Z8", "t1", "F5"),
    ("N4",), ("E0", "Z3"), ("Z1", "F2"), ("N5", "E7"),
    ("E8", "K6", "E3", "Z4", "N2"), (), ("Z5", "F6", "t2"),
    ("u0", "E4", "Z2"), ("N6", "u1", "E1", "E5", "Z6", "u2", "E2", "E6"),
)


def back_kernel(
    sizes, gu1, gd1, gu2, gd2, gwo, seg_ref, lt_ref, v_ref, gvm_ref, gu0_ref, gd0_ref,
    mg_hbm, mix_hbm, qkv_hbm, nT_hbm, watt_hbm, x_hbm, rg_hbm,
    gx_ref, gq_ref, gk_ref, gv_ref, go_ref, gu_ref, gd_ref, gtab_ref,
    mg_ref, mix_ref, qkv_ref, nT_ref, watt_ref, x_ref, rg_ref,
    ng_ref, bias_ref, segp_ref, dt_ref, kt_ref, tab_ref,
    land_ref, tot_ref, tsend, trecv, land2_ref, tot2_ref, tsend2, trecv2, isem,
    *rest,
):
    nd, nh, ny = sizes
    length, strips, width = gx_ref.shape
    lp = qkv_ref.shape[0] // strips
    parts, rest = rest[:NG], rest[NG:]
    at = Place(ny)
    at.greet()
    loads = copies_of(
        isem, (mg_hbm, mg_ref), (mix_hbm, mix_ref),
        *[
            (qkv_hbm.at[:, 3 * first : 3 * (first + gw)], qkv_ref.at[:, 3 * first : 3 * (first + gw)])
            for first, gw in GROUPS
        ],
        (nT_hbm, nT_ref), (watt_hbm, watt_ref), (x_hbm, x_ref), (rg_hbm, rg_ref),
    )
    n = 5 + NG
    bufs = [rest[5 * t : 5 * t + 5] for t in range(n)]
    sems = rest[5 * n :]
    pw = gu1.shape[-1] // (2 * nh)
    units = []

    def ff_unit(src, dst, cols):
        whole = ff_view(src, pw)

        def put(total):
            dst[:, cols] = total[0]

        return lambda d, h, c: whole(d, h, c, 0, ny), 1, put

    one, two = slice(pw, 2 * pw), slice(2 * pw, 3 * pw)
    units += [ff_unit(gu2, gu_ref, two), ff_unit(gd2, gd_ref, two)]
    tiles = gq_ref.shape[0] // 8

    def att_unit(src, put):
        inner = att_view(src, tiles, sizes)
        return lambda d, h, c: inner(d, h, c, 0, ny), tiles, put

    def put_out(total):
        go_ref[...] = total.reshape(go_ref.shape)

    units.append(att_unit(gwo, put_out))
    for i, (first, gw) in enumerate(GROUPS):

        def put_group(total, first=first, gw=gw):
            for j, ref in enumerate((gq_ref, gk_ref, gv_ref)):
                ref[:, first : first + gw] = total[:, :, j * gw : (j + 1) * gw].reshape(-1, gw)

        units.append(att_unit(parts[i], put_group))
    units += [ff_unit(gu1, gu_ref, one), ff_unit(gd1, gd_ref, one)]
    sca = Scatter(at, units, bufs, sems)
    early = Table(at, tot_ref, land_ref, tsend, trecv)
    late = Table(at, tot2_ref, land2_ref, tsend2, trecv2)
    stop = stops(
        BACK_PLAN, K=sca.core, F=sca.far, N=sca.near, Z=sca.z, E=sca.finish, t=early.step, u=late.step
    )
    tot_ref[0] = jnp.concatenate([gvm_ref[OB : DB + 1, :], gvm_ref[UB0 : UB0 + 4, :]]).astype(BF)
    gu_ref[:, 0:pw] = gu0_ref[...]
    gd_ref[:, 0:pw] = gd0_ref[...]
    segments_into(segp_ref, seg_ref)
    heads = lax.broadcasted_iota(jnp.int32, (16, width), 0)
    pick = jnp.where(heads == lax.broadcasted_iota(jnp.int32, (16, width), 1) // HD, 1.0, 0.0).astype(BF)
    for s in range(strips):
        mask_into(bias_ref.at[s], segp_ref, s)
    loads[0].wait()
    loads[1].wait()
    for s in range(strips):
        part = slice(s * lp, (s + 1) * lp)
        prod = mg_ref[part, :].astype(F32) * mix_ref[part, :].astype(F32)
        high = prod.astype(BF)
        dt_ref[s] = nt(pick, high) + nt(pick, (prod - high.astype(F32)).astype(BF))
    at.greeted()
    for i, (first, gw) in enumerate(GROUPS):
        loads[2 + i].wait()
        for s in range(strips):
            for p in range(gw // 128):
                stop()
                attend_back_pair(
                    qkv_ref, mg_ref, bias_ref, lt_ref, dt_ref, kt_ref, s, lp,
                    3 * first + p * 128, gw, first + p * 128,
                )
        cols = slice(first, first + gw)
        tab_ref[QB : QB + 1, cols] = colsum(qkv_ref[:, 3 * first : 3 * first + gw].astype(F32))
        tab_ref[VB : VB + 1, cols] = colsum(qkv_ref[:, 3 * first + 2 * gw : 3 * (first + gw)].astype(F32))
        if i == 0:
            loads[2 + NG].wait()
            loads[3 + NG].wait()

        def grads(j, carry):
            c = pl.ds(pl.multiple_of(j * gw, gw), gw)
            dz = qkv_ref[:, pl.ds(pl.multiple_of(3 * first + j * gw, 128), gw)]
            parts[i][:, :, c] = nn(nT_ref[...], dz).reshape(width // 8, 8, gw).astype(BF)
            return carry

        stop()
        lax.fori_loop(0, 3, grads, 0)
        stop()
    gain = v_ref[G1 : G1 + 1, :]
    loads[4 + NG].wait()
    loads[5 + NG].wait()
    g_gain, g_shift = jnp.zeros((1, width), F32), jnp.zeros((1, width), F32)
    for s in range(strips):
        if s > 0:
            stop()
        rows = slice(s * lp, (s + 1) * lp)

        def to_norm(j, carry):
            c = pl.ds(pl.multiple_of(j * 256, 256), 256)
            ng_ref[rows, c] = nt(qkv_ref[rows, :], watt_ref[c, :])
            return carry

        lax.fori_loop(0, width // 256, to_norm, 0)
        stop()
        for lo, size in row_pieces(length, 136):
            part = slice(s * lp + lo, s * lp + lo + size)
            xhat, scale = normalise(x_ref[part, :].astype(F32))
            grad = ng_ref[part, :]
            g_gain = g_gain + colsum(grad * xhat)
            g_shift = g_shift + colsum(grad)
            term = norm_back(grad, gain, xhat, scale)
            gx_ref[lo : lo + size, s, :] = (rg_ref[part, :] + term).astype(BF)
    tot2_ref[0] = jnp.concatenate(
        [g_gain, g_shift, tab_ref[QB : VB + 1, :], jnp.zeros((4, width), F32)]
    ).astype(BF)
    stop()
    stop()
    sums, ends = early.result, late.result
    gtab_ref[G1 : VB + 1, :] = ends[0:4]
    gtab_ref[OB : DB + 1, :] = sums[0:4]
    gtab_ref[UB0 : UB0 + 4, :] = sums[4:8]
    gtab_ref[UB0 + 4 :, :] = jnp.zeros((gtab_ref.shape[0] - UB0 - 4, width), F32)
    for t in range(n):
        sca.sent(t)
    early.sent()
    late.sent()


def own_path(sizes, args):
    (
        block_input, segment_ids, out_grad, query_weight, key_weight, value_weight, output_weight, small,
        up_weight, down_weight,
    ) = args
    nd, nx, ny = sizes
    nh = nx // 2
    grid3 = (nd, nh, ny)
    strips, length, width = block_input.shape
    units = up_weight.shape[1]
    att_rows, ff_rows = query_weight.shape[0], up_weight.shape[0]
    lp = padded(length)
    tiles = att_rows // 8
    part = units // PARTS
    total = strips * lp
    full, wide, turned = (total, width), (total, 3 * width), (width, total)
    n_tab = small.shape[0]
    ff_shape = (nd, ny, ff_rows, nx * part)
    n_later = 2 * (PARTS - 1)
    t_shape = (length, strips, width)
    watt_shape = (width, 3 * width)
    lt_shape = (strips, 16, lp)
    dma = pltpu.SemaphoreType.DMA
    ups, downs = up_weight[None], down_weight[None]
    (
        lt, table, gsum, qkv, mixed, nT, dout, doutT, xp, watt, wo, u0, d0, zb,
    ) = pl.pallas_call(
        functools.partial(front_kernel, grid3),
        out_shape=[
            sds(lt_shape, F32), sds((n_tab, width), F32), sds((8, width), F32), sds(wide, BF), sds(full, BF),
            sds(turned, BF), sds(full, BF), sds(turned, BF), sds(full, BF), sds(watt_shape, BF),
            sds((width // 8, 8, width), BF), sds(ff_shape, BF), sds(ff_shape, BF),
            sds((n_later, ny, ff_rows, part), BF),
        ],
        in_specs=[ANY, ANY, VM] + [ANY] * 6 + [VM],
        out_specs=[VM] * 3 + [ANY] * 11,
        scratch_shapes=[
            pltpu.VMEM(t_shape, BF), pltpu.VMEM(t_shape, BF), pltpu.VMEM(full, F32), pltpu.VMEM(full, BF),
            pltpu.VMEM((tiles, 8, 3 * width), BF), pltpu.VMEM(watt_shape, BF), pltpu.VMEM((8, 3 * width), F32), pltpu.VMEM((strips, lp, 128), F32),
            pltpu.VMEM((strips, lp, lp), F32), pltpu.VMEM((8, lp), F32),
            pltpu.VMEM(wide, BF), pltpu.VMEM(full, BF), pltpu.VMEM(turned, BF), pltpu.VMEM(full, BF),
            pltpu.VMEM(turned, BF), pltpu.VMEM(full, BF),
        ]
        + Table.scratch((n_tab, width), ny, BF)
        + [dma((2 + 3 * NG,)), dma((5 + 2 * NG,))]
        + Gather.semaphores(NG + 3, ny, n_later)
        + [pltpu.VMEM((width // 8, 8, 3 * gw), BF) for _, gw in GROUPS],
        compiler_params=pltpu.CompilerParams(collective_id=0, has_side_effects=True, vmem_limit_bytes=LIMIT),
    )(
        block_input.transpose(1, 0, 2), out_grad.transpose(1, 0, 2), segment_ids,
        *(w.reshape(tiles, 8, width) for w in (query_weight, key_weight, value_weight, output_weight)),
        ups, downs, small,
    )

    n_sc = 2
    some = (ff_rows, part)
    buffers = []
    for _ in range(n_sc):
        buffers += Scatter.buffers(1, ff_rows, part, ny)
    mg, gwo, gvm, gu0, gd0, y, rg, gu1, gd1, gu2, gd2 = pl.pallas_call(
        functools.partial(middle_kernel, grid3),
        out_shape=[
            sds(full, BF), sds((width, width), BF), sds((n_tab, width), F32), sds(some, F32), sds(some, F32),
            sds(t_shape, BF), sds(full, F32),
        ]
        + [sds(ff_shape, BF)] * n_later,
        in_specs=[VM] * 5 + [ANY] * 5,
        out_specs=[VM] * 5 + [ANY] * (2 + n_later),
        scratch_shapes=[
            pltpu.VMEM(full, BF), pltpu.VMEM(turned, BF), pltpu.VMEM(full, BF), pltpu.VMEM(turned, BF),
            pltpu.VMEM(full, F32), pltpu.VMEM(full, F32), pltpu.VMEM(full, F32),
            pltpu.VMEM((total, nx * part), BF), pltpu.VMEM((total, nx * part), BF), pltpu.VMEM(t_shape, BF),
        ]
        + [pltpu.VMEM((PARTS,) + ff_shape, BF)] * 2
        + [pltpu.VMEM(ff_shape, BF)] * 2
        + [dma((4,)), dma((2 + n_later,))]
        + Gather.semaphores(n_later, ny)
        + buffers
        + Scatter.semaphores(n_sc, ny),
        compiler_params=pltpu.CompilerParams(collective_id=1, has_side_effects=True, vmem_limit_bytes=LIMIT),
    )(xp, mixed, wo.reshape(width, width), table, gsum, dout, doutT, u0, d0, zb)

    n_units = 5 + NG
    buffers = []
    for _ in range(2):
        buffers += Scatter.buffers(1, ff_rows, part, ny)
    for cols in [width] + [3 * gw for _, gw in GROUPS]:
        buffers += Scatter.buffers(tiles, 8, cols, ny)
    for _ in range(2):
        buffers += Scatter.buffers(1, ff_rows, part, ny)
    gx, gq, gk, gv, go, gu, gd, gtab = pl.pallas_call(
        functools.partial(back_kernel, grid3),
        out_shape=[sds(t_shape, BF)] + [sds((att_rows, width), F32)] * 4 + [sds((ff_rows, units), F32)] * 2
        + [sds((n_tab, width), F32)],
        in_specs=[ANY] * 5 + [VM] * 6 + [ANY] * 7,
        out_specs=[VM] * 8,
        scratch_shapes=[
            pltpu.VMEM(full, BF), pltpu.VMEM(full, BF), pltpu.VMEM(wide, BF), pltpu.VMEM(turned, BF),
            pltpu.VMEM(watt_shape, BF), pltpu.VMEM(full, BF), pltpu.VMEM(full, F32),
            pltpu.VMEM(full, F32), pltpu.VMEM((strips, lp, lp), F32), pltpu.VMEM((8, lp), F32), pltpu.VMEM(lt_shape, F32),
            pltpu.VMEM((128, lp), BF), pltpu.VMEM((n_tab, width), F32),
        ]
        + Table.scratch((8, width), ny, BF)
        + Table.scratch((8, width), ny, BF)
        + [dma((6 + NG,))]
        + [pltpu.VMEM((width // 8, 8, 3 * gw), BF) for _, gw in GROUPS]
        + buffers
        + Scatter.semaphores(n_units, ny),
        compiler_params=pltpu.CompilerParams(collective_id=2, has_side_effects=True, vmem_limit_bytes=LIMIT),
    )(
        gu1, gd1, gu2, gd2, gwo.reshape(width // 8, 8, width), segment_ids, lt, table, gvm, gu0, gd0,
        mg, mixed, qkv, nT, watt, xp, rg,
    )
    return y.transpose(1, 0, 2), gx.transpose(1, 0, 2), gq, gk, gv, go, gu, gd, gtab


def wide_path(sizes, args):
    (
        block_input, segment_ids, out_grad, query_weight, key_weight, value_weight, output_weight, table,
        up_weight, down_weight,
    ) = args
    nd, nx, ny = sizes
    strips, length, width = block_input.shape
    units = up_weight.shape[1]
    lp = padded(length)
    att = jnp.concatenate([query_weight, key_weight, value_weight, output_weight], axis=1)
    att = lax.all_gather(att, ALL, axis=0, tiled=True)
    up, down = (
        lax.all_gather(lax.all_gather(a, ("dp", "gy"), axis=0, tiled=True), "gx", axis=0)
        for a in (up_weight, down_weight)
    )
    w_qkv, w_out = att[:, : 3 * width], att[:, 3 * width :]
    seg = jnp.pad(segment_ids, ((0, 0), (0, lp - length)), constant_values=-1)
    seg_row, seg_col = seg[:, None, :], seg[:, :, None]
    full = (strips, lp, width)
    wide = (strips, lp, 3 * width)
    turned = (strips, width, lp)
    qkv, normed = call(
        qkv_kernel, [sds(wide, BF), sds(full, BF)], 3, [pltpu.VMEM((8, 3 * width), F32)]
    )(block_input, w_qkv, table)
    mixed, lse = call(
        attend_kernel, [sds(full, BF), sds((strips, lp, 128), F32)], 3, [pltpu.VMEM((lp, lp), F32)]
    )(qkv, seg_row, seg_col)
    y, res_grad, mixed_grad, g_up, g_down, g_out, g_tab = call(
        ff_kernel,
        [
            sds(block_input.shape, BF), sds(full, F32), sds(full, BF), sds(up.shape, BF),
            sds(down.shape, BF), sds((width, width), BF), sds(table.shape, F32),
        ],
        7,
        [
            pltpu.VMEM(full, BF), pltpu.VMEM(turned, BF), pltpu.VMEM(full, BF), pltpu.VMEM(turned, BF),
            pltpu.VMEM(full, F32), pltpu.VMEM(full, F32), pltpu.VMEM(full, F32),
            pltpu.VMEM((strips, lp, units), BF), pltpu.VMEM((strips, lp, units), BF),
        ],
    )(block_input, mixed, out_grad, w_out, up, down, table)
    (dqkv,) = call(
        attend_back_kernel,
        [sds(wide, BF)],
        6,
        [
            pltpu.VMEM((lp, lp), F32), pltpu.VMEM((128, lp), F32), pltpu.VMEM((16, lp), F32),
            pltpu.VMEM((128, lp), BF),
        ],
    )(qkv, mixed_grad, mixed, lse, seg_row, seg_col)
    x_grad, g_qkv, g_tab1 = call(
        qkv_back_kernel,
        [sds(block_input.shape, BF), sds((width, 3 * width), BF), sds(table.shape, F32)],
        6,
        [pltpu.VMEM(turned, BF), pltpu.VMEM(full, F32)],
    )(block_input, normed, dqkv, res_grad, w_qkv, table)
    g_tab = lax.psum(g_tab + g_tab1, ALL)
    g_qkv, g_out = (
        lax.psum_scatter(a.astype(F32), ALL, scatter_dimension=0, tiled=True) for a in (g_qkv, g_out)
    )
    g_up, g_down = (
        lax.psum_scatter(
            lax.psum_scatter(a.astype(F32), "gx", scatter_dimension=0, tiled=True)[0],
            ("dp", "gy"),
            scatter_dimension=0,
            tiled=True,
        )
        for a in (g_up, g_down)
    )
    g_att = (g_qkv[:, :width], g_qkv[:, width : 2 * width], g_qkv[:, 2 * width :], g_out)
    return y, x_grad, g_att, g_up, g_down, g_tab


def per_device(
    sizes, block_input, segment_ids, out_grad, query_weight, key_weight, value_weight, output_weight,
    first_gain, first_shift, query_bias, value_bias, output_bias, second_gain, second_shift,
    up_weight, up_bias, down_weight, down_bias,
):
    nd, nx, ny = sizes
    n_dev = nd * nx * ny
    strips, length, width = block_input.shape
    units = up_weight.shape[1]
    att_rows, ff_rows = query_weight.shape[0], up_weight.shape[0]
    own = nd == 2 and nx == 4 and ny % 2 == 0 and att_rows % 8 == 0 and ff_rows % 8 == 0

    vecs = [first_gain, first_shift, query_bias, value_bias, output_bias, second_gain, second_shift, down_bias]
    n_vec = len(vecs)
    me = (lax.axis_index("dp") * nx + lax.axis_index("gx")) * ny + lax.axis_index("gy")
    n_tab = n_vec + up_bias.shape[0] * n_dev // width
    pieces = jnp.stack(vecs).astype(F32)
    lane = lax.broadcasted_iota(jnp.int32, (n_vec, width), 1) // att_rows
    top = jnp.where(lane == me, jnp.tile(pieces, (1, n_dev)), 0.0)
    flat = jnp.tile(up_bias.astype(F32), n_dev).reshape(n_tab - n_vec, width)
    index = lax.broadcasted_iota(jnp.int32, flat.shape, 0) * width + lax.broadcasted_iota(jnp.int32, flat.shape, 1)
    small = jnp.concatenate([top, jnp.where(index // up_bias.shape[0] == me, flat, 0.0)])
    rows_up = (n_tab + 7) // 8 * 8
    small = jnp.pad(small, ((0, rows_up - n_tab), (0, 0)))
    if own:
        y, x_grad, gq, gk, gv_, go, g_up, g_down, g_tab = own_path(
            sizes,
            (
                block_input, segment_ids, out_grad, query_weight, key_weight, value_weight, output_weight,
                small, up_weight, down_weight,
            ),
        )
        g_att = (gq, gk, gv_, go)
    else:
        table = lax.psum(small, ALL)
        y, x_grad, g_att, g_up, g_down, g_tab = wide_path(
            sizes,
            (
                block_input, segment_ids, out_grad, query_weight, key_weight, value_weight, output_weight,
                table, up_weight, down_weight,
            ),
        )
    mine = lax.dynamic_slice(g_tab, (0, me * att_rows), (n_vec, att_rows))
    g_bias = lax.dynamic_slice(
        g_tab[n_vec:n_tab].reshape(-1), (me * up_bias.shape[0],), (up_bias.shape[0],)
    )
    return (
        y, x_grad, *g_att, mine[G1], mine[S1], mine[QB], mine[VB], mine[OB], mine[G2], mine[S2],
        g_up, g_bias, g_down, mine[DB],
    )


def solution(mesh):
    rows, cols = P(ALL, None), P(ALL)
    cube = P(ALL, None, None)
    ff = P(("dp", "gy"), "gx")
    sizes = (mesh.shape["dp"], mesh.shape["gx"], mesh.shape["gy"])
    return jax.shard_map(
        functools.partial(per_device, sizes),
        mesh=mesh,
        in_specs=(cube, rows, cube) + (rows,) * 4 + (cols,) * 7 + (ff, cols, ff, cols),
        out_specs=(cube, cube) + (rows,) * 4 + (cols,) * 7 + (ff, cols, ff, cols),
        check_vma=False,
    )
```
